32 devices in a mesh: batch: 16 (over z, y, core), tensor: 2 (over x).
Axes of the slice: x: 2, y: 2, z: 4, core: 2. Of those that a mesh axis runs over, the one named last changes fastest.
Arguments:
- block_in: bfloat16 [2, 16384, 1024], P(None, ('batch', 'tensor')), may hold values from -6 to 6
- lengths: int32 [2, 16, 4], P(None, 'batch'), may hold values from 1 to 512, 1024 in all within a row
- norm_gains: float32 [3, 1024], replicated, may hold values from 0.5 to 1.5
- qkv_weight: bfloat16 [3, 1024, 1024], P(None, 'batch', 'tensor'), may hold values from -0.1875 to 0.1875
- head_scale: float32 [16], P('tensor'), may hold values from 0.5 to 2
- out_weight: bfloat16 [1024, 1024], P('tensor', 'batch'), may hold values from -0.1875 to 0.1875
- up_weight: bfloat16 [1024, 4096], P('batch', 'tensor'), may hold values from -0.7875 to 0.7875
- mid_gain: float32 [4096], P('tensor'), may hold values from 0.5 to 1.5
- down_weight: bfloat16 [4096, 1024], P('tensor', 'batch'), may hold values from -0.39375 to 0.39375
- cotangent: bfloat16 [2, 16384, 1024], P(None, ('batch', 'tensor')), may hold values from -6 to 6
Outputs:
- block_out: bfloat16 [2, 16384, 1024], P(None, ('batch', 'tensor'))
- grad_in: bfloat16 [2, 16384, 1024], P(None, ('batch', 'tensor'))
- grad_gains: float32 [3, 1024], replicated
- grad_qkv: float32 [3, 1024, 1024], P(None, 'batch', 'tensor')
- grad_scale: float32 [16], P('tensor')
- grad_proj: float32 [1024, 1024], P('tensor', 'batch')
- grad_up: float32 [1024, 4096], P('batch', 'tensor')
- grad_mid: float32 [4096], P('tensor')
- grad_down: float32 [4096, 1024], P('tensor', 'batch')
The draws below stay inside these ranges and needn't reach their ends.
Inputs may be any that keep to these rules, and one draw needn't show every extreme that they name: lengths[m, b] holds the lengths of the 4 sequences packed in order into the 1024 rows of group b in micro-batch m; they sum to 1024.
All inputs are finite; a program needn't handle non-finite values.
Results may differ from the reference program's by a relative error of at most 0.019.
Values may be sent and summed in bfloat16 or wider, within the bound.
No kernel may reach another device: no remote copies, remote signals or barrier semaphores. Data moves between devices by JAX's collectives and lax.ppermute only.
A program may use at most 256 MiB of HBM per device.

```python
import math
import jax
import jax.numpy as jnp
import numpy as np
from jax import lax

D = 1024
HEADS = 16
HEAD_DIM = 64
FF = 4096
TOK_GRP = 1024
SEQS = 4
MICRO = 2
SEQ_MOST = 512
GROUPS = 16
TOKENS = 16384
N_BATCH = 16


def unit_scales(key, count):
    place = jnp.arange(count, dtype=jnp.float32) / max(count - 1, 1)
    low_end, high_end = (0.4, 2.0)
    rising = jnp.exp(jnp.log(low_end) + (jnp.log(high_end) - jnp.log(low_end)) * place)
    rough = jax.random.uniform(jax.random.fold_in(key, 11), (count,), jnp.float32, 0.7, 1.4)
    return rising * rough


def draw_up_weight(key, part):
    entries = jnp.clip(jax.random.normal(jax.random.fold_in(key, 3), (D, FF), jnp.float32), -6.0, 6.0)
    scales = unit_scales(jax.random.fold_in(key, 5), FF)
    return (entries * scales[None, :] * D ** (-0.5)).astype(jnp.bfloat16)


def draw_down_weight(key, part):
    entries = jnp.clip(jax.random.normal(jax.random.fold_in(key, 7), (FF, D), jnp.float32), -6.0, 6.0)
    scales = unit_scales(jax.random.fold_in(key, 9), FF)
    return (entries * scales[:, None] * FF ** (-0.5)).astype(jnp.bfloat16)


def shard_levels(own_key, shape, split, least, top_value):
    gain = 1.0
    for axis_at, blocks in split:
        heights = jax.random.uniform(jax.random.fold_in(jax.random.fold_in(own_key, 6), axis_at), (blocks,), jnp.float32, least / len(split), top_value / len(split))
        gain = gain * jnp.repeat(jnp.exp(heights), shape[axis_at] // blocks).reshape((-1,) + (1,) * (len(shape) - 1 - axis_at))
    return gain


def split_up(amount, total, most, slope):
    weights = [(1 << 20) // math.isqrt(grade ** slope) + 1 for grade in range(2, amount + 1)]
    rest, holding = total - most - (amount - 1), [1] * (amount - 1)
    while rest > 0:
        candidates = [i for i in range(amount - 1) if holding[i] < most]
        whole, left = sum([weights[i] for i in candidates]), rest
        for i in candidates:
            extra = min(most - holding[i], max(1, left * weights[i] // whole), rest)
            holding[i] = holding[i] + extra
            rest = rest - extra
    return np.array([most] + holding)


def ragged(rng, number_of, total, most, skew):
    if number_of == 2:
        one = jax.random.randint(rng, (), max(1, total - most), min(most, total - 1) + 1)
        return jnp.stack([one, total - one])
    sizes = jnp.asarray(split_up(number_of, total, most, skew), jnp.int32)
    couples = (number_of - 1) // 2
    source_of, taker = sizes[1:1 + 2 * couples:2], sizes[2:2 + 2 * couples:2]
    slack = jnp.minimum(source_of - 1, most - taker)
    moved = jax.random.randint(jax.random.fold_in(rng, 1), (couples,), 0, 1 << 20) % (slack + 1)
    sizes = sizes.at[1:1 + 2 * couples:2].set(source_of - moved).at[2:2 + 2 * couples:2].set(taker + moved)
    return sizes[jax.random.permutation(jax.random.fold_in(rng, 2), number_of)]


def normal_values(rng, extent, spread, bound, shards=(), kind=jnp.bfloat16):
    level = shard_levels(rng, extent, shards, -0.22, 0.18) if shards else 1.0
    values = jax.random.normal(rng, extent, jnp.float32) * spread * level
    return jnp.minimum(jnp.maximum(values, -bound), bound).astype(kind)


def setup_inputs(seed: int = 0) -> dict:
    keys = jax.random.split(jax.random.key(seed), 11)
    return {
        "block_in": normal_values(keys[0], (MICRO, TOKENS, D), 1.0, 6.0, ((1, 32),)),
        "lengths": jax.vmap(lambda own: ragged(own, SEQS, TOK_GRP, SEQ_MOST, 2))(jax.random.split(keys[1], MICRO * GROUPS)).reshape((MICRO, GROUPS, SEQS)).astype(jnp.int32),
        "norm_gains": jnp.clip(1.0 + 0.1 * jax.random.normal(keys[2], (3, D), jnp.float32), 0.5, 1.5),
        "qkv_weight": normal_values(keys[3], (3, D, D), D ** -0.5, 0.1875, ((1, 16), (2, 2))),
        "head_scale": jnp.clip(jnp.exp(math.log(2.0) - 1.3862944 * jax.random.uniform(keys[4], (HEADS,), jnp.float32) ** shard_levels(keys[4], (HEADS,), ((0, 2),), -0.2, 0.2)), 0.5, 2.0),
        "out_weight": normal_values(keys[5], (D, D), D ** -0.5, 0.1875, ((0, 2), (1, 16))),
        "up_weight": draw_up_weight(jax.random.fold_in(keys[10], 71), 0),
        "mid_gain": jnp.clip(1.0 + 0.1 * jax.random.normal(keys[7], (FF,), jnp.float32), 0.5, 1.5),
        "down_weight": draw_down_weight(jax.random.fold_in(keys[10], 71), 0),
        "cotangent": normal_values(keys[9], (MICRO, TOKENS, D), 1.0, 6.0, ((1, 32),)),
    }


eps = 1e-05
highest = lax.Precision.HIGHEST

@jax.custom_vjp
def low(v):
    return lax.optimization_barrier(v.astype(jnp.bfloat16)).astype(jnp.float32)

@jax.custom_vjp
def low_back(v):
    return v

def low_keep(v):
    return (low(v), None)

def low_pass(kept, grad):
    return (grad,)

def back_keep(v):
    return (v, None)

def back_low(kept, grad):
    return (low(grad),)
low.defvjp(low_keep, low_pass)
low_back.defvjp(back_keep, back_low)

def normalize(values):
    centred = values - lax.optimization_barrier(jnp.mean(values, axis=-1, keepdims=True))
    return centred * lax.rsqrt(lax.optimization_barrier(jnp.mean(centred * centred, axis=-1, keepdims=True)) + eps)

def segment_ids(seq_lengths, group_rows):
    places = jnp.arange(group_rows, dtype=jnp.int32)
    ends = jnp.cumsum(seq_lengths.astype(jnp.int32)).astype(jnp.int32)
    seg_ids = lax.optimization_barrier(jnp.sum((places[:, None] >= ends[None, :]).astype(jnp.int32), axis=1)).astype(jnp.int32)
    return (seg_ids, places)

def attention(queries, all_keys, values, seg_ids, places):
    group_rows = queries.shape[0]
    block_rows = min(512, group_rows)
    factor = queries.shape[2] ** (-0.5)

    @jax.checkpoint
    def one_block(first_row):
        query_block = lax.dynamic_slice_in_dim(queries, first_row, block_rows, 0)
        seg_block = lax.dynamic_slice_in_dim(seg_ids, first_row, block_rows, 0)
        place_block = lax.dynamic_slice_in_dim(places, first_row, block_rows, 0)
        scores = low_back(jnp.einsum('qhd,khd->hqk', query_block, all_keys, precision=highest) * factor)
        visible = (seg_block[:, None] == seg_ids[None, :]) & (place_block[:, None] >= places[None, :])
        scores = jnp.where(visible[None], scores, -1e+30)
        row_max = lax.optimization_barrier(jnp.max(scores, axis=-1, keepdims=True))
        shifted = jnp.exp(scores - row_max)
        weights_low = low(shifted / lax.optimization_barrier(jnp.sum(shifted, axis=-1, keepdims=True)))
        return jnp.einsum('hqk,khd->qhd', weights_low, values, precision=highest)
    firsts = jnp.arange(group_rows // block_rows, dtype=jnp.int32) * block_rows
    return lax.map(one_block, firsts).reshape(queries.shape)

def block_forward(block_x, norm_gains, qkv_weight, head_scale, out_weight, up_weight, mid_gain, down_weight, seg_ids, places):
    group_rows = block_x.shape[0]
    first_norm = low(normalize(block_x) * norm_gains[0])
    projected = low(low_back(jnp.einsum('gd,cde->cge', first_norm, qkv_weight, precision=highest)))
    heads_shape = (group_rows, HEADS, HEAD_DIM)
    attended = attention(projected[0].reshape(heads_shape), projected[1].reshape(heads_shape), projected[2].reshape(heads_shape), seg_ids, places)
    scaled = low(low_back(attended) * head_scale[None, :, None]).reshape(group_rows, D)
    mixed = low_back(jnp.dot(scaled, out_weight, precision=highest))
    resid = block_x + normalize(mixed) * norm_gains[1]
    third_norm = low(normalize(resid) * norm_gains[2])
    hidden = low_back(jnp.dot(third_norm, up_weight, precision=highest))
    narrow = low(normalize(jax.nn.gelu(hidden)) * mid_gain)
    return resid + low_back(jnp.dot(narrow, down_weight, precision=highest))

def reference(block_in, lengths, norm_gains, qkv_weight, head_scale, out_weight, up_weight, mid_gain, down_weight, cotangent):
    item_count = MICRO * N_BATCH
    inputs = block_in.reshape(item_count, TOK_GRP, D)
    cot_rows = cotangent.reshape(item_count, TOK_GRP, D)
    seq_table = lengths.reshape(item_count, SEQS)
    params = (norm_gains.astype(jnp.float32), qkv_weight.astype(jnp.float32), head_scale.astype(jnp.float32), out_weight.astype(jnp.float32), up_weight.astype(jnp.float32), mid_gain.astype(jnp.float32), down_weight.astype(jnp.float32))

    def one_group(totals, group_item):
        group_x, group_cot, group_len = group_item
        seg_ids, places = segment_ids(group_len, TOK_GRP)

        def forward(block_x, *weights):
            return block_forward(block_x, *weights, seg_ids, places)
        result, pullback = jax.vjp(forward, group_x.astype(jnp.float32), *params)
        gradients = pullback(group_cot.astype(jnp.float32))
        totals = tuple((running + fresh for running, fresh in zip(totals, gradients[1:])))
        return (totals, (result.astype(jnp.bfloat16), gradients[0].astype(jnp.bfloat16)))
    zero_grads = tuple((jnp.zeros(weight.shape, jnp.float32) for weight in params))
    totals, (outputs, input_grads) = lax.scan(one_group, zero_grads, (inputs, cot_rows, seq_table))
    return (outputs.reshape(MICRO, TOKENS, D), input_grads.reshape(MICRO, TOKENS, D), totals[0], totals[1], totals[2], totals[3], totals[4], totals[5], totals[6])
```

```python
import functools
import math

import jax
import jax.numpy as jnp
from jax import lax
from jax.experimental import pallas as pl
from jax.experimental.pallas import tpu as pltpu
from jax.sharding import PartitionSpec as P

eps = 1e-05
SEQ_MOST = 512
F32 = jnp.float32
BF = jnp.bfloat16
ALL = ("batch", "tensor")
GELU_C = math.sqrt(2.0 / math.pi)
GELU_A = 0.044715


def dotf(a, b, ca, cb):
    return lax.dot_general(a, b, (((ca,), (cb,)), ((), ())), preferred_element_type=F32)


def row_loop(rows, step, fn):
    def one(i, carry):
        fn(pl.multiple_of(i * step, step))
        return carry

    lax.fori_loop(0, rows // step, one, 0)


def normalize(values):
    centred = values - jnp.mean(values, axis=-1, keepdims=True)
    factor = lax.rsqrt(jnp.mean(centred * centred, axis=-1, keepdims=True) + eps)
    return (centred * factor, factor)


def norm_back(unit, factor, grad):
    return factor * (
        grad
        - jnp.mean(grad, axis=-1, keepdims=True)
        - unit * jnp.mean(grad * unit, axis=-1, keepdims=True)
    )


def fold8(values):
    rows, width = values.shape
    return jnp.sum(values.reshape(rows // 8, 8, width), axis=0)


def bits_of(count):
    return count.bit_length() - 1


def rel_table(batch_count, tensor_count):
    batch_bits = bits_of(batch_count)
    table = []
    for core in range(2):
        for tensor in range(tensor_count):
            for rest in range(batch_count // 2):
                batch = core
                for k in range(1, batch_bits):
                    batch |= ((rest >> (batch_bits - 1 - k)) & 1) << k
                table.append((batch, tensor))
    return table


def exchange_steps(batch_count, tensor_count):
    steps = [("batch", 1)]
    steps += [("tensor", 1 << k) for k in reversed(range(bits_of(tensor_count)))]
    steps += [("batch", 1 << k) for k in range(1, bits_of(batch_count))]
    return steps


def swap(value, axis, flip):
    count = lax.axis_size(axis)
    return lax.ppermute(value, axis, [(i, i ^ flip) for i in range(count)])


def reduce_scatter(buffer, steps):
    for axis, flip in steps:
        half = buffer.shape[0] // 2
        arrived = swap(buffer[half:], axis, flip)
        buffer = (buffer[:half].astype(F32) + arrived.astype(F32)).astype(BF)
    return buffer[0].astype(F32)


def all_sum(vector, steps):
    for axis, flip in steps:
        vector = vector + swap(vector, axis, flip)
    return vector


def load_shards(src, dst, sem, table, ids_ref, lead=None, col=0):
    height, cols = dst.shape[1] // (len(table) // dst.shape[0]), dst.shape[2]
    for p, (batch, tensor) in enumerate(table):
        b = lax.bitwise_xor(jnp.int32(batch), ids_ref[0])
        t = lax.bitwise_xor(jnp.int32(tensor), ids_ref[1])
        piece = src.at[p] if lead is None else src.at[p, lead]
        pltpu.make_async_copy(
            piece.at[:, pl.ds(col, cols)],
            dst.at[t, pl.ds(pl.multiple_of(b * height, height), height), :],
            sem,
        ).start()


def wait_shards(dst, sem):
    pltpu.make_async_copy(dst, dst, sem).wait()


def qkv_kernel(table, factor, ids_ref, x_ref, gain_ref, w_hbm, h1_ref, q_ref, k_ref, v_ref, w, sem):
    first = pl.program_id(0) == 0

    @pl.when(first)
    def _():
        for c in range(3):
            load_shards(w_hbm, w.at[c], sem.at[c], table, ids_ref, lead=c)

    def chunk(r):
        unit, _ = normalize(x_ref[pl.ds(r, 32), :].astype(F32))
        h1_ref[pl.ds(r, 32), :] = (unit * gain_ref[0:1, :]).astype(BF)

    row_loop(x_ref.shape[0], 32, chunk)
    tensor_count, _, cols = w.shape[1:]
    for c, out in enumerate((q_ref, k_ref, v_ref)):

        @pl.when(first)
        def _(c=c):
            wait_shards(w.at[c], sem.at[c])

        for t in range(tensor_count):
            part = dotf(h1_ref[...], w[c, t], 1, 0).astype(BF)
            out[:, t * cols : (t + 1) * cols] = part * BF(factor) if c == 0 else part


def project(ids, x, gains, w_all, table, tensor_count, factor):
    rows, width = x.shape
    block = min(256, rows)
    cols = width // tensor_count
    row = pl.BlockSpec((block, width), lambda i, e: (i, 0))
    return pl.pallas_call(
        functools.partial(qkv_kernel, table, factor),
        grid_spec=pltpu.PrefetchScalarGridSpec(
            num_scalar_prefetch=1,
            grid=(rows // block,),
            in_specs=[
                row,
                pl.BlockSpec((3, width), lambda i, e: (0, 0)),
                pl.BlockSpec(memory_space=pl.ANY),
            ],
            out_specs=[row] * 4,
            scratch_shapes=[
                pltpu.VMEM((3, tensor_count, width, cols), BF),
                pltpu.SemaphoreType.DMA((3,)),
            ],
        ),
        out_shape=[jax.ShapeDtypeStruct((rows, width), BF)] * 4,
        compiler_params=pltpu.CompilerParams(vmem_limit_bytes=32 << 20),
        cost_estimate=pl.CostEstimate(
            flops=6 * rows * width * width, transcendentals=0, bytes_accessed=16 << 20
        ),
        name="project",
    )(ids, x, gains, w_all)


def spans(rows, block):
    return [
        (first, max(0, (first - SEQ_MOST + 1) // block * block), first + block)
        for first in range(0, rows, block)
    ]


def fill_bias(ends_ref, bias, parts, block):
    for (first, low, high), ref in zip(parts, bias):
        shape = (high - low, block)
        keys = low + lax.broadcasted_iota(jnp.int32, shape, 0)
        queries = first + lax.broadcasted_iota(jnp.int32, shape, 1)
        start = jnp.zeros(shape, jnp.int32)
        for n in range(ends_ref.shape[0]):
            end = ends_ref[n]
            start = jnp.where(queries >= end, end, start)
        ref[...] = jnp.where((keys <= queries) & (keys >= start), 0.0, -1e30).astype(F32)


def attend_kernel(rows, block, ends_ref, q_ref, k_ref, v_ref, scale_ref, o_ref, lse_ref, *bias):
    parts = spans(rows, block)

    @pl.when(pl.program_id(0) == 0)
    def _():
        fill_bias(ends_ref, bias, parts, block)

    lower = lax.broadcasted_iota(jnp.int32, (1, 128), 1) < 64
    for n, (first, low, high) in enumerate(parts):
        q = q_ref[pl.ds(first, block), :]
        heads = []
        for h in range(2):
            own = jnp.where(lower if h == 0 else ~lower, q, jnp.zeros_like(q))
            s = dotf(k_ref[pl.ds(low, high - low), :], own, 1, 1) + bias[n][...]
            most = jnp.max(s, axis=0, keepdims=True)
            p = jnp.exp(s - most)
            total = jnp.sum(p, axis=0, keepdims=True)
            probs = (p * (1.0 / total)).astype(BF)
            lse_ref[0, pl.ds(h, 1), pl.ds(first, block)] = most + jnp.log(total)
            heads.append(dotf(probs, v_ref[pl.ds(low, high - low), :], 0, 0))
        out = jnp.where(lower, heads[0], heads[1]) * scale_ref[...]
        o_ref[pl.ds(first, block), :] = out.astype(BF)


def attend_back_kernel(
    rows, block, factor, ends_ref, q_ref, k_ref, v_ref, da_ref, lse_ref,
    dq_ref, dk_ref, dv_ref, inner_ref, dk_acc, dv_acc, *bias
):
    parts = spans(rows, block)

    @pl.when(pl.program_id(0) == 0)
    def _():
        fill_bias(ends_ref, bias, parts, block)

    lower = lax.broadcasted_iota(jnp.int32, (1, 128), 1) < 64
    dk_acc[...] = jnp.zeros_like(dk_acc)
    dv_acc[...] = jnp.zeros_like(dv_acc)
    for n, (first, low, high) in enumerate(parts):
        here = pl.ds(first, block)
        keys = pl.ds(low, high - low)
        q, da, k, v = q_ref[here, :], da_ref[here, :], k_ref[keys, :], v_ref[keys, :]
        heads = []
        for h in range(2):
            mask = lower if h == 0 else ~lower
            q_own = jnp.where(mask, q, jnp.zeros_like(q))
            da_own = jnp.where(mask, da, jnp.zeros_like(da))
            s = dotf(k, q_own, 1, 1) + bias[n][...]
            p = jnp.exp(s - lse_ref[0, pl.ds(h, 1), here])
            product = p * dotf(v, da_own, 1, 1)
            inner = jnp.sum(product, axis=0, keepdims=True)
            inner_ref[0, pl.ds(h, 1), here] = inner
            ds = (product - p * inner).astype(BF)
            dv_acc[keys, :] += dotf(p.astype(BF), da_own, 1, 0)
            dk_acc[keys, :] += dotf(ds, q_own, 1, 0)
            heads.append(dotf(ds, k, 0, 0))
        dq_ref[here, :] = (jnp.where(lower, heads[0], heads[1]) * factor).astype(BF)
    dk_ref[...] = dk_acc[...].astype(BF)
    dv_ref[...] = dv_acc[...].astype(BF)


def bias_shapes(rows, block):
    return [pltpu.VMEM((high - low, block), F32) for _, low, high in spans(rows, block)]


def attend(q, k, v, scale_row, ends):
    rows, width = q.shape
    block = min(256, rows)
    pairs = width // 128
    col = pl.BlockSpec((rows, 128), lambda i, e: (0, i))
    return pl.pallas_call(
        functools.partial(attend_kernel, rows, block),
        grid_spec=pltpu.PrefetchScalarGridSpec(
            num_scalar_prefetch=1,
            grid=(pairs,),
            in_specs=[col, col, col, pl.BlockSpec((1, 128), lambda i, e: (0, i))],
            out_specs=[col, pl.BlockSpec((1, 2, rows), lambda i, e: (i, 0, 0))],
            scratch_shapes=bias_shapes(rows, block),
        ),
        out_shape=[
            jax.ShapeDtypeStruct((rows, width), BF),
            jax.ShapeDtypeStruct((pairs, 2, rows), F32),
        ],
        compiler_params=pltpu.CompilerParams(vmem_limit_bytes=40 << 20),
        cost_estimate=pl.CostEstimate(
            flops=28 * 10**9, transcendentals=0, bytes_accessed=8 << 20
        ),
        name="attend",
    )(ends, q, k, v, scale_row)


def attend_back(q, k, v, da, lse, ends, factor):
    rows, width = q.shape
    block = min(256, rows)
    pairs = width // 128
    col = pl.BlockSpec((rows, 128), lambda i, e: (0, i))
    row = pl.BlockSpec((1, 2, rows), lambda i, e: (i, 0, 0))
    out = jax.ShapeDtypeStruct((rows, width), BF)
    return pl.pallas_call(
        functools.partial(attend_back_kernel, rows, block, factor),
        grid_spec=pltpu.PrefetchScalarGridSpec(
            num_scalar_prefetch=1,
            grid=(pairs,),
            in_specs=[col, col, col, col, row],
            out_specs=[col, col, col, row],
            scratch_shapes=[pltpu.VMEM((rows, 128), F32)] * 2 + bias_shapes(rows, block),
        ),
        out_shape=[out, out, out, jax.ShapeDtypeStruct((pairs, 2, rows), F32)],
        compiler_params=pltpu.CompilerParams(vmem_limit_bytes=48 << 20),
        cost_estimate=pl.CostEstimate(
            flops=42 * 10**9, transcendentals=0, bytes_accessed=16 << 20
        ),
        name="attend_back",
    )(ends, q, k, v, da, lse)


def hidden_kernel(
    table, out_col, up_col, ids_ref, scaled_ref, x_ref, gain_ref, mid_ref, w_hbm,
    mixed_ref, h3_ref, hidden_ref, narrow_ref, stat_ref, out_w, up_w, act, sem
):
    first = pl.program_id(0) == 0
    block, width = x_ref.shape
    tensor_count, _, out_cols = out_w.shape
    up_cols = up_w.shape[2]
    total = tensor_count * up_cols

    @pl.when(first)
    def _():
        load_shards(w_hbm, out_w, sem.at[0], table, ids_ref, col=out_col)
        load_shards(w_hbm, up_w, sem.at[1], table, ids_ref, col=up_col)
        wait_shards(out_w, sem.at[0])

    mixed = dotf(scaled_ref[:, :out_cols], out_w[0], 1, 1)
    for t in range(1, tensor_count):
        mixed += dotf(scaled_ref[:, t * out_cols : (t + 1) * out_cols], out_w[t], 1, 1)
    mixed_ref[...] = mixed

    def norms(r):
        here = pl.ds(r, 32)
        unit, _ = normalize(mixed_ref[here, :])
        resid = x_ref[here, :].astype(F32) + unit * gain_ref[1:2, :]
        unit3, _ = normalize(resid)
        h3_ref[here, :] = (unit3 * gain_ref[2:3, :]).astype(BF)

    row_loop(block, 32, norms)

    @pl.when(first)
    def _():
        wait_shards(up_w, sem.at[1])

    chunk = min(512, up_cols)
    sums = jnp.zeros((block, 128), F32)
    squares = jnp.zeros((block, 128), F32)
    for c in range(total // chunk):
        t, off = divmod(c * chunk, up_cols)
        h = dotf(h3_ref[...], up_w[t, :, off : off + chunk], 1, 0)
        hidden_ref[:, c * chunk : (c + 1) * chunk] = h
        half = 0.5 * jnp.tanh(h * (GELU_C + (GELU_C * GELU_A) * (h * h))) + 0.5
        a = h * half
        act[:, c * chunk : (c + 1) * chunk] = a
        for j in range(chunk // 128):
            piece = a[:, j * 128 : (j + 1) * 128]
            sums += piece
            squares += piece * piece
    mean = jnp.sum(sums, axis=1, keepdims=True) / total
    spread = jnp.sum(squares, axis=1, keepdims=True) / total - mean * mean
    scale = lax.rsqrt(spread + eps)
    lane = lax.broadcasted_iota(jnp.int32, (1, 128), 1)
    stat_ref[...] = jnp.where(lane < 64, mean, scale)

    def narrow(r):
        here = pl.ds(r, 16)
        m = stat_ref[here, 0:1]
        s = stat_ref[here, 64:65]
        narrow_ref[here, :] = ((act[here, :] - m) * s * mid_ref[...]).astype(BF)

    row_loop(block, 16, narrow)


def hidden_forward(ids, scaled, x, gains, mid_row, w_all, table, tensor_count, cols):
    rows, width = x.shape
    block = min(256, rows)
    out_cols, up_cols, _ = cols
    total = up_cols * tensor_count
    row = pl.BlockSpec((block, width), lambda i, e: (i, 0))
    wide = pl.BlockSpec((block, total), lambda i, e: (i, 0))
    return pl.pallas_call(
        functools.partial(hidden_kernel, table, 0, out_cols),
        grid_spec=pltpu.PrefetchScalarGridSpec(
            num_scalar_prefetch=1,
            grid=(rows // block,),
            in_specs=[
                row,
                row,
                pl.BlockSpec((3, width), lambda i, e: (0, 0)),
                pl.BlockSpec((1, total), lambda i, e: (0, 0)),
                pl.BlockSpec(memory_space=pl.ANY),
            ],
            out_specs=[row, row, wide, wide, pl.BlockSpec((block, 128), lambda i, e: (i, 0))],
            scratch_shapes=[
                pltpu.VMEM((tensor_count, width, out_cols), BF),
                pltpu.VMEM((tensor_count, width, up_cols), BF),
                pltpu.VMEM((block, total), F32),
                pltpu.SemaphoreType.DMA((2,)),
            ],
        ),
        out_shape=[
            jax.ShapeDtypeStruct((rows, width), F32),
            jax.ShapeDtypeStruct((rows, width), BF),
            jax.ShapeDtypeStruct((rows, total), F32),
            jax.ShapeDtypeStruct((rows, total), BF),
            jax.ShapeDtypeStruct((rows, 128), F32),
        ],
        compiler_params=pltpu.CompilerParams(vmem_limit_bytes=48 << 20),
        cost_estimate=pl.CostEstimate(
            flops=20 * 10**9, transcendentals=0, bytes_accessed=40 << 20
        ),
        name="hidden_forward",
    )(ids, scaled, x, gains, mid_row, w_all)


def feed_kernel(
    table, offsets, ids_ref, narrow_ref, hidden_ref, stat_ref, mixed_ref, x_ref, cot_ref, gain_ref,
    mid_ref, scale_ref, w_hbm, out_ref, dhidden_ref, dresid_ref, dmixed_ref, dattended_ref,
    gains_ref, dmid_ref, out_w, up_w, down_w, grad, unit_s, slope_s, wide, sem
):
    first = pl.program_id(0) == 0
    block, width = x_ref.shape
    tensor_count, _, out_cols = out_w.shape
    up_cols = up_w.shape[2]
    total = tensor_count * up_cols

    @pl.when(first)
    def _():
        load_shards(w_hbm, down_w, sem.at[0], table, ids_ref, col=offsets[2])
        load_shards(w_hbm, up_w, sem.at[1], table, ids_ref, col=offsets[1])
        load_shards(w_hbm, out_w, sem.at[2], table, ids_ref, col=offsets[0])
        gains_ref[...] = jnp.zeros_like(gains_ref)
        dmid_ref[...] = jnp.zeros_like(dmid_ref)
        wait_shards(down_w, sem.at[0])

    feed = dotf(narrow_ref[:, :up_cols], down_w[0], 1, 1)
    for t in range(1, tensor_count):
        feed += dotf(narrow_ref[:, t * up_cols : (t + 1) * up_cols], down_w[t], 1, 1)
    wide[...] = feed

    def output(r):
        here = pl.ds(r, 32)
        unit, _ = normalize(mixed_ref[here, :])
        resid = x_ref[here, :].astype(F32) + unit * gain_ref[1:2, :]
        out_ref[here, :] = (resid + wide[here, :]).astype(BF)

    row_loop(block, 32, output)

    chunk = min(512, up_cols)
    mean = stat_ref[:, 0:1]
    scale = stat_ref[:, 64:65]
    back_sum = jnp.zeros((block, 128), F32)
    back_inner = jnp.zeros((block, 128), F32)
    for c in range(total // chunk):
        t, off = divmod(c * chunk, up_cols)
        here = slice(c * chunk, (c + 1) * chunk)
        dn = dotf(cot_ref[...], down_w[t, :, off : off + chunk], 1, 0)
        h = hidden_ref[:, here]
        square = h * h
        half = 0.5 * jnp.tanh(h * (GELU_C + (GELU_C * GELU_A) * square)) + 0.5
        a = h * half
        slope_s[:, here] = half + a * (1.0 - half) * (
            2.0 * GELU_C + (6.0 * GELU_C * GELU_A) * square
        )
        unit = (a - mean) * scale
        unit_s[:, here] = unit
        dmid_ref[:, here] += fold8(dn * unit)
        g = dn * mid_ref[:, here]
        grad[:, here] = g
        inner = g * unit
        for j in range(chunk // 128):
            back_sum += g[:, j * 128 : (j + 1) * 128]
            back_inner += inner[:, j * 128 : (j + 1) * 128]
    sum_col = jnp.sum(back_sum, axis=1, keepdims=True) / total
    inner_col = jnp.sum(back_inner, axis=1, keepdims=True) / total
    for c in range(total // chunk):
        here = slice(c * chunk, (c + 1) * chunk)
        act_grad = scale * (grad[:, here] - sum_col - unit_s[:, here] * inner_col)
        dhidden_ref[:, here] = (act_grad * slope_s[:, here]).astype(BF)

    @pl.when(first)
    def _():
        wait_shards(up_w, sem.at[1])
        wait_shards(out_w, sem.at[2])

    dh3 = dotf(dhidden_ref[:, :up_cols], up_w[0], 1, 1)
    for t in range(1, tensor_count):
        dh3 += dotf(dhidden_ref[:, t * up_cols : (t + 1) * up_cols], up_w[t], 1, 1)
    wide[...] = dh3

    def back(r):
        here = pl.ds(r, 32)
        unit, factor = normalize(mixed_ref[here, :])
        resid = x_ref[here, :].astype(F32) + unit * gain_ref[1:2, :]
        unit3, factor3 = normalize(resid)
        third = wide[here, :]
        gains_ref[8:16, :] += fold8(third * unit3)
        dresid = cot_ref[here, :].astype(F32) + norm_back(unit3, factor3, third * gain_ref[2:3, :])
        dresid_ref[here, :] = dresid
        gains_ref[0:8, :] += fold8(dresid * unit)
        dmixed_ref[here, :] = norm_back(unit, factor, dresid * gain_ref[1:2, :]).astype(BF)

    row_loop(block, 32, back)
    for t in range(tensor_count):
        here = slice(t * out_cols, (t + 1) * out_cols)
        dscaled = dotf(dmixed_ref[...], out_w[t], 1, 0)
        dattended_ref[:, here] = (dscaled * scale_ref[:, here]).astype(BF)


def feed_back(ids, narrow, hidden, stat, mixed, x, cot, gains, mid_row, scale_row, w_all, table, tensor_count, cols):
    rows, width = x.shape
    block = min(256, rows)
    out_cols, up_cols, _ = cols
    total = up_cols * tensor_count
    row = pl.BlockSpec((block, width), lambda i, e: (i, 0))
    wide = pl.BlockSpec((block, total), lambda i, e: (i, 0))
    return pl.pallas_call(
        functools.partial(feed_kernel, table, (0, out_cols, out_cols + up_cols)),
        grid_spec=pltpu.PrefetchScalarGridSpec(
            num_scalar_prefetch=1,
            grid=(rows // block,),
            in_specs=[
                wide,
                wide,
                pl.BlockSpec((block, 128), lambda i, e: (i, 0)),
                row,
                row,
                row,
                pl.BlockSpec((3, width), lambda i, e: (0, 0)),
                pl.BlockSpec((1, total), lambda i, e: (0, 0)),
                pl.BlockSpec((1, width), lambda i, e: (0, 0)),
                pl.BlockSpec(memory_space=pl.ANY),
            ],
            out_specs=[
                row,
                wide,
                row,
                row,
                row,
                pl.BlockSpec((16, width), lambda i, e: (0, 0)),
                pl.BlockSpec((8, total), lambda i, e: (0, 0)),
            ],
            scratch_shapes=[
                pltpu.VMEM((tensor_count, width, out_cols), BF),
                pltpu.VMEM((tensor_count, width, up_cols), BF),
                pltpu.VMEM((tensor_count, width, up_cols), BF),
                pltpu.VMEM((block, total), F32),
                pltpu.VMEM((block, total), F32),
                pltpu.VMEM((block, total), F32),
                pltpu.VMEM((block, width), F32),
                pltpu.SemaphoreType.DMA((3,)),
            ],
        ),
        out_shape=[
            jax.ShapeDtypeStruct((rows, width), BF),
            jax.ShapeDtypeStruct((rows, total), BF),
            jax.ShapeDtypeStruct((rows, width), F32),
            jax.ShapeDtypeStruct((rows, width), BF),
            jax.ShapeDtypeStruct((rows, width), BF),
            jax.ShapeDtypeStruct((16, width), F32),
            jax.ShapeDtypeStruct((8, total), F32),
        ],
        compiler_params=pltpu.CompilerParams(vmem_limit_bytes=60 << 20),
        cost_estimate=pl.CostEstimate(
            flops=45 * 10**9, transcendentals=0, bytes_accessed=60 << 20
        ),
        name="feed_back",
    )(ids, narrow, hidden, stat, mixed, x, cot, gains, mid_row, scale_row, w_all)


def grad_kernel(batch_table, count, ids_ref, a_ref, *refs):
    b_refs, o_ref, turned, acc = refs[:count], refs[count], refs[count + 1], refs[count + 2]
    step = pl.program_id(0)

    @pl.when(step == 0)
    def _():
        turned[...] = a_ref[...].T

    height = o_ref.shape[-2]
    for c, b_ref in enumerate(b_refs):
        acc[...] = dotf(turned[...], b_ref[...], 1, 0)
        for p, batch in enumerate(batch_table):
            b = lax.bitwise_xor(jnp.int32(batch), ids_ref[0])
            piece = acc[pl.ds(pl.multiple_of(b * height, height), height), :].astype(BF)
            core, rest = divmod(p, len(batch_table) // 2)
            if count == 1:
                o_ref[core, 0, rest] = piece
            else:
                o_ref[core, 0, rest, c] = piece


def weight_grad(ids, a, bs, table, batch_count, tensor_count, name):
    rows, width = a.shape
    cols = bs[0].shape[1] // tensor_count
    chunk = min(512, cols)
    per = cols // chunk
    height = width // batch_count
    half = batch_count // 2
    batch_table = [b for b, t in table if t == 0]
    count = len(bs)
    lead = () if count == 1 else (count,)
    zeros = (0,) * len(lead)
    return pl.pallas_call(
        functools.partial(grad_kernel, batch_table, count),
        grid_spec=pltpu.PrefetchScalarGridSpec(
            num_scalar_prefetch=1,
            grid=(tensor_count * per,),
            in_specs=[pl.BlockSpec((rows, width), lambda i, e: (0, 0))]
            + [
                pl.BlockSpec(
                    (rows, chunk),
                    lambda i, e: (0, lax.bitwise_xor(i // per, e[1]) * per + i % per),
                )
            ]
            * count,
            out_specs=pl.BlockSpec(
                (2, 1, half) + lead + (height, chunk),
                lambda i, e: (0, i // per, 0) + zeros + (0, i % per),
            ),
            scratch_shapes=[pltpu.VMEM((width, rows), BF), pltpu.VMEM((width, chunk), F32)],
        ),
        out_shape=jax.ShapeDtypeStruct((2, tensor_count, half) + lead + (height, cols), BF),
        compiler_params=pltpu.CompilerParams(vmem_limit_bytes=32 << 20),
        cost_estimate=pl.CostEstimate(
            flops=2 * rows * width * cols * tensor_count * count,
            transcendentals=0,
            bytes_accessed=2 * (rows * width + (rows + width) * cols * tensor_count * count),
        ),
        name=name,
    )(ids, a, *bs)


def input_kernel(table, ids_ref, dq_ref, dk_ref, dv_ref, x_ref, dresid_ref, gain_ref, w_hbm, out_ref, dgain_ref, w, wide, sem):
    first = pl.program_id(0) == 0
    tensor_count, _, cols = w.shape[1:]

    @pl.when(first)
    def _():
        for c in range(3):
            load_shards(w_hbm, w.at[c], sem.at[c], table, ids_ref, lead=c)
        dgain_ref[...] = jnp.zeros_like(dgain_ref)
        for c in range(3):
            wait_shards(w.at[c], sem.at[c])

    total = None
    for c, ref in enumerate((dq_ref, dk_ref, dv_ref)):
        for t in range(tensor_count):
            part = dotf(ref[:, t * cols : (t + 1) * cols], w[c, t], 1, 1)
            total = part if total is None else total + part
    wide[...] = total

    def back(r):
        here = pl.ds(r, 32)
        unit, factor = normalize(x_ref[here, :].astype(F32))
        grad = wide[here, :]
        dgain_ref[...] += fold8(grad * unit)
        out = dresid_ref[here, :] + norm_back(unit, factor, grad * gain_ref[0:1, :])
        out_ref[here, :] = out.astype(BF)

    row_loop(x_ref.shape[0], 32, back)


def input_grad(ids, dq, dk, dv, x, dresid, gains, w_all, table, tensor_count):
    rows, width = x.shape
    block = min(256, rows)
    cols = width // tensor_count
    row = pl.BlockSpec((block, width), lambda i, e: (i, 0))
    return pl.pallas_call(
        functools.partial(input_kernel, table),
        grid_spec=pltpu.PrefetchScalarGridSpec(
            num_scalar_prefetch=1,
            grid=(rows // block,),
            in_specs=[row] * 5
            + [
                pl.BlockSpec((3, width), lambda i, e: (0, 0)),
                pl.BlockSpec(memory_space=pl.ANY),
            ],
            out_specs=[row, pl.BlockSpec((8, width), lambda i, e: (0, 0))],
            scratch_shapes=[
                pltpu.VMEM((3, tensor_count, width, cols), BF),
                pltpu.VMEM((block, width), F32),
                pltpu.SemaphoreType.DMA((3,)),
            ],
        ),
        out_shape=[
            jax.ShapeDtypeStruct((rows, width), BF),
            jax.ShapeDtypeStruct((8, width), F32),
        ],
        compiler_params=pltpu.CompilerParams(vmem_limit_bytes=40 << 20),
        cost_estimate=pl.CostEstimate(
            flops=6 * rows * width * width, transcendentals=0, bytes_accessed=22 << 20
        ),
        name="input_grad",
    )(ids, dq, dk, dv, x, dresid, gains, w_all)


def take_micro(value, split):
    micro_count, own_rows, width = value.shape
    rank = lax.axis_index("tensor")
    if split == 1:
        out = jnp.zeros((micro_count, own_rows, width), value.dtype)
        mine = lax.dynamic_index_in_dim(value, rank, 0, keepdims=True)
        out = lax.dynamic_update_slice(out, mine, (rank, 0, 0))
        for flip in range(1, micro_count):
            other = lax.bitwise_xor(rank, flip)
            sent = lax.dynamic_index_in_dim(value, other, 0, keepdims=True)
            out = lax.dynamic_update_slice(out, swap(sent, "tensor", flip), (other, 0, 0))
        return out.reshape(micro_count * own_rows, width)
    whole = lax.all_gather(value, "tensor", axis=1, tiled=True)
    rows = micro_count * own_rows
    return lax.dynamic_slice(whole, (rank // split, rank % split * rows, 0), (1, rows, width))[0]


def give_micro(value, micro_count, split):
    rows, width = value.shape
    own_rows = rows // micro_count
    rank = lax.axis_index("tensor")
    if split == 1:
        pieces = value.reshape(micro_count, own_rows, width)
        out = jnp.zeros_like(pieces)
        mine = lax.dynamic_index_in_dim(pieces, rank, 0, keepdims=True)
        out = lax.dynamic_update_slice(out, mine, (rank, 0, 0))
        for flip in range(1, micro_count):
            other = lax.bitwise_xor(rank, flip)
            sent = lax.dynamic_index_in_dim(pieces, other, 0, keepdims=True)
            out = lax.dynamic_update_slice(out, swap(sent, "tensor", flip), (other, 0, 0))
        return out
    whole = lax.all_gather(value, "tensor", axis=0, tiled=True)
    whole = whole.reshape(micro_count, rows * split, width)
    return lax.dynamic_slice(whole, (0, rank * own_rows, 0), (micro_count, own_rows, width))


def gather_vector(value, tensor_count):
    rank = lax.axis_index("tensor")
    out = jnp.zeros((tensor_count,) + value.shape, value.dtype)
    for flip in range(tensor_count):
        part = value if flip == 0 else swap(value, "tensor", flip)
        out = lax.dynamic_update_slice(out, part[None], (lax.bitwise_xor(rank, flip), 0))
    return out


def body(
    block_in,
    lengths,
    norm_gains,
    qkv_weight,
    head_scale,
    out_weight,
    up_weight,
    mid_gain,
    down_weight,
    cotangent,
):
    tensor_count = lax.axis_size("tensor")
    batch_count = lax.axis_size("batch")
    tensor_rank = lax.axis_index("tensor")
    batch_rank = lax.axis_index("batch")
    micro_count, own_rows, width = block_in.shape
    if tensor_count % micro_count:
        raise NotImplementedError
    split = tensor_count // micro_count
    micro = tensor_rank // split
    local_heads = head_scale.shape[0]
    heads = local_heads * tensor_count
    head_size = width // heads
    local_hidden = mid_gain.shape[0]
    factor = head_size ** (-0.5)
    table = rel_table(batch_count, tensor_count)
    steps = exchange_steps(batch_count, tensor_count)
    own_ids = jnp.stack([batch_rank, tensor_rank]).astype(jnp.int32)
    plain = [(j // tensor_count, j % tensor_count) for j in range(batch_count * tensor_count)]
    zero_ids = jnp.zeros((2,), jnp.int32)
    out_cols = out_weight.shape[0]
    up_cols = local_hidden
    cols = (out_cols, up_cols, up_cols)

    qkv_all = lax.all_gather(qkv_weight, ALL, axis=0, tiled=False)
    rest = jnp.concatenate([out_weight.T, up_weight, down_weight.T], axis=1)
    rest_all = lax.all_gather(rest, ALL, axis=0, tiled=False)
    vectors = gather_vector(jnp.concatenate([mid_gain, head_scale]), tensor_count)
    mid_row = vectors[:, :local_hidden].reshape(1, -1)
    scale_all = vectors[:, local_hidden:].reshape(-1)
    scale_row = jnp.repeat(scale_all, head_size)[None]
    x = take_micro(block_in, split)
    cot = take_micro(cotangent, split)
    own_lengths = lax.dynamic_index_in_dim(lengths[:, 0], micro, 0, keepdims=False)
    ends = jnp.cumsum(own_lengths).astype(jnp.int32)

    def spread(value):
        if split == 1:
            return value
        groups = [[m * split + s for s in range(split)] for m in range(micro_count)]
        return lax.all_to_all(value, "tensor", 1, 0, tiled=True, axis_index_groups=groups)

    def collect(value):
        if split == 1:
            return value
        groups = [[m * split + s for s in range(split)] for m in range(micro_count)]
        return lax.all_to_all(value, "tensor", 0, 1, tiled=True, axis_index_groups=groups)

    h1, q, k, v = project(zero_ids, x, norm_gains, qkv_all, plain, tensor_count, factor)
    q, k, v = spread(q), spread(k), spread(v)
    part = width // split
    scale_part = lax.dynamic_slice(scale_row, (0, tensor_rank % split * part), (1, part))
    scaled, lse = attend(q, k, v, scale_part, ends)
    scaled = collect(scaled)
    mixed, h3, hidden, narrow, stat = hidden_forward(
        zero_ids, scaled, x, norm_gains, mid_row, rest_all, plain, tensor_count, cols
    )
    down_pieces = weight_grad(own_ids, cot, [narrow], table, batch_count, tensor_count, "grad_down")
    block_out, dhidden, dresid, dmixed, dattended, gain_sums, mid_sums = feed_back(
        zero_ids, narrow, hidden, stat, mixed, x, cot, norm_gains, mid_row, scale_row, rest_all,
        plain, tensor_count, cols,
    )
    up_pieces = weight_grad(own_ids, h3, [dhidden], table, batch_count, tensor_count, "grad_up")
    out_pieces = weight_grad(own_ids, dmixed, [scaled], table, batch_count, tensor_count, "grad_out")
    dq, dk, dv, inner = attend_back(q, k, v, spread(dattended), lse, ends, factor)
    dq, dk, dv = collect(dq), collect(dk), collect(dv)
    qkv_pieces = weight_grad(own_ids, h1, [dq, dk, dv], table, batch_count, tensor_count, "grad_qkv")
    grad_in, first_sums = input_grad(zero_ids, dq, dk, dv, x, dresid, norm_gains, qkv_all, plain, tensor_count)

    def scattered(pieces):
        return reduce_scatter(pieces.reshape((-1,) + pieces.shape[3:]), steps)

    down_grad = scattered(down_pieces).T
    up_grad = scattered(up_pieces)
    out_grad = scattered(out_pieces).T
    qkv_grad = scattered(qkv_pieces)
    head_sums = jnp.sum(inner, axis=2).reshape(-1) / lax.dynamic_slice(
        scale_all, (tensor_rank % split * (heads // split),), (heads // split,)
    )
    head_all = lax.dynamic_update_slice(
        jnp.zeros((heads,), F32), head_sums, (tensor_rank % split * (heads // split),)
    )
    gain_parts = [first_sums, gain_sums[:8], gain_sums[8:]]
    vector = jnp.concatenate(
        [jnp.sum(part, axis=0) for part in gain_parts] + [jnp.sum(mid_sums, axis=0), head_all]
    )
    vector = all_sum(vector, steps)
    gains_sum = vector[: 3 * width].reshape(3, width)
    mid_own = lax.dynamic_slice(vector, (3 * width + tensor_rank * local_hidden,), (local_hidden,))
    scale_own = lax.dynamic_slice(
        vector, (3 * width + tensor_count * local_hidden + tensor_rank * local_heads,), (local_heads,)
    )
    return (
        give_micro(block_out, micro_count, split),
        give_micro(grad_in, micro_count, split),
        gains_sum,
        qkv_grad,
        scale_own,
        out_grad,
        up_grad,
        mid_own,
        down_grad,
    )


def solution(mesh):
    in_specs = (
        P(None, ("batch", "tensor"), None),
        P(None, "batch", None),
        P(),
        P(None, "batch", "tensor"),
        P("tensor"),
        P("tensor", "batch"),
        P("batch", "tensor"),
        P("tensor"),
        P("tensor", "batch"),
        P(None, ("batch", "tensor"), None),
    )
    out_specs = (
        P(None, ("batch", "tensor"), None),
        P(None, ("batch", "tensor"), None),
        P(),
        P(None, "batch", "tensor"),
        P("tensor"),
        P("tensor", "batch"),
        P("batch", "tensor"),
        P("tensor"),
        P("tensor", "batch"),
    )
    return jax.shard_map(body, mesh=mesh, in_specs=in_specs, out_specs=out_specs, check_vma=False)
```

```python
import functools
import math

import jax
import jax.numpy as jnp
from jax import lax
from jax.experimental import pallas as pl
from jax.experimental.pallas import tpu as pltpu
from jax.sharding import PartitionSpec as P

eps = 1e-05
SEQ_MOST = 512
F32 = jnp.float32
BF = jnp.bfloat16
ALL = ("batch", "tensor")
GELU_C = math.sqrt(2.0 / math.pi)
GELU_A = 0.044715
STEP = 64


def cost(us):
    return pl.CostEstimate(flops=int(us * 1e9), transcendentals=0, bytes_accessed=1 << 20)


def dotf(a, b, ca, cb):
    return lax.dot_general(a, b, (((ca,), (cb,)), ((), ())), preferred_element_type=F32)


def row_loop(rows, step, fn):
    def one(i, carry):
        fn(pl.multiple_of(i * step, step))
        return carry

    lax.fori_loop(0, rows // step, one, 0)


def normalize(values):
    centred = values - jnp.mean(values, axis=-1, keepdims=True)
    factor = lax.rsqrt(jnp.mean(centred * centred, axis=-1, keepdims=True) + eps)
    return (centred * factor, factor)


def norm_back(unit, factor, grad):
    return factor * (
        grad
        - jnp.mean(grad, axis=-1, keepdims=True)
        - unit * jnp.mean(grad * unit, axis=-1, keepdims=True)
    )


def fold8(values):
    rows, width = values.shape
    return jnp.sum(values.reshape(rows // 8, 8, width), axis=0)


def bits_of(count):
    return count.bit_length() - 1


def gather_steps(batch_count, tensor_count, tensor_first):
    tensor = [("tensor", 1 << k) for k in range(bits_of(tensor_count))]
    plane = [("batch", 2)]
    far = [("batch", 1 << k) for k in reversed(range(2, bits_of(batch_count)))]
    return far + (tensor + plane if tensor_first else plane + tensor) + [("batch", 1)]


def place_table(steps, batch_count, tensor_count):
    batch = jnp.arange(batch_count * tensor_count, dtype=jnp.int32) // tensor_count
    tensor = jnp.arange(batch_count * tensor_count, dtype=jnp.int32) % tensor_count
    batch = jnp.bitwise_xor(batch, lax.axis_index("batch"))
    tensor = jnp.bitwise_xor(tensor, lax.axis_index("tensor"))
    place = jnp.zeros_like(batch)
    for k, (axis, flip) in enumerate(steps):
        apart = (jnp.bitwise_and(batch if axis == "batch" else tensor, flip) != 0).astype(jnp.int32)
        place = place + apart * (1 << k)
    return place


def swap(value, axis, flip):
    count = lax.axis_size(axis)
    return lax.ppermute(value, axis, [(i, i ^ flip) for i in range(count)])


def held(value, after):
    return lax.optimization_barrier((value, after))[0]


class Gather:
    def __init__(self, buffer, steps):
        self.own, self.steps, self.parts = buffer, list(steps), None

    def outgoing(self):
        return self.arrived if len(self.steps) == 1 else self.own

    def go(self, value):
        step = self.steps.pop(0)
        self.arrived = swap(value, *step)
        if not self.steps:
            self.parts[1] = value
        else:
            self.own = value
            if len(self.steps) == 1:
                self.parts = [value, None, swap(value, *self.steps[0]), None]

    def end(self):
        if self.parts is None:
            self.own = jnp.concatenate([self.own, self.arrived], axis=0)
        elif not self.steps:
            self.parts[3] = self.arrived

    def columns(self, start, count, steps):
        return Gather(self.own[..., start : start + count], steps)


class Scatter:
    def __init__(self, keep, send, steps):
        self.keep, self.send, self.steps = keep, send, list(reversed(steps))

    def outgoing(self):
        return (self.send, self.keep)

    def go(self, value):
        send, self.keep = value
        self.arrived = swap(send, *self.steps.pop(0))

    def end(self):
        keep, arrived = self.keep, self.arrived
        half = keep.shape[0] // 2
        if self.steps:
            self.send = (keep[half:].astype(F32) + arrived[half:].astype(F32)).astype(BF)
            self.keep = (keep[:half].astype(F32) + arrived[:half].astype(F32)).astype(BF)
        else:
            self.total = keep[0].astype(F32) + arrived[0].astype(F32)


class Total:
    def __init__(self, value, steps):
        self.value, self.steps = value, list(steps)

    def outgoing(self):
        return self.value

    def go(self, value):
        self.value = value
        self.arrived = swap(value, *self.steps.pop(0))

    def end(self):
        self.value = self.value + self.arrived


class Rows:
    def __init__(self, value, micro_count, split):
        self.value, self.micro_count, self.split = value, micro_count, split
        self.taken = value.ndim == 3
        self.steps = [None]
        self.rank = lax.axis_index("tensor")

    def pieces(self):
        if self.taken:
            return self.value
        return self.value.reshape(self.micro_count, -1, self.value.shape[1])

    def outgoing(self):
        if self.split > 1:
            return []
        return [
            lax.dynamic_index_in_dim(self.pieces(), lax.bitwise_xor(self.rank, flip), 0)
            for flip in range(1, self.micro_count)
        ]

    def go(self, value):
        self.steps = []
        if self.split == 1:
            self.arrived = [swap(one, "tensor", flip + 1) for flip, one in enumerate(value)]
        else:
            self.arrived = [
                lax.all_gather(self.value, "tensor", axis=1 if self.taken else 0, tiled=True)
            ]

    def end(self):
        if self.split == 1:
            pieces = self.pieces()
            out = lax.dynamic_update_slice(
                jnp.zeros_like(pieces),
                lax.dynamic_index_in_dim(pieces, self.rank, 0),
                (self.rank, 0, 0),
            )
            for flip, one in enumerate(self.arrived):
                out = lax.dynamic_update_slice(
                    out, one, (lax.bitwise_xor(self.rank, flip + 1), 0, 0)
                )
            self.result = out.reshape(-1, out.shape[2]) if self.taken else out
            return
        whole = self.arrived[0]
        width = whole.shape[-1]
        if self.taken:
            rows = self.value.shape[0] * self.value.shape[1]
            start = (self.rank // self.split, self.rank % self.split * rows, 0)
            self.result = lax.dynamic_slice(whole, start, (1, rows, width))[0]
        else:
            own = self.value.shape[0] // self.micro_count
            whole = whole.reshape(self.micro_count, -1, width)
            start = (0, self.rank * own, 0)
            self.result = lax.dynamic_slice(whole, start, (self.micro_count, own, width))


def launch(inputs, chains):
    inputs, values = lax.optimization_barrier((inputs, [chain.outgoing() for chain in chains]))
    for chain, value in zip(chains, values):
        chain.go(value)
    return inputs


def land(inputs, chains):
    inputs, values = lax.optimization_barrier((inputs, [chain.arrived for chain in chains]))
    for chain, value in zip(chains, values):
        chain.arrived = value
        chain.end()
    return inputs


def hop(chains, after=()):
    launch(after, chains)
    for chain in chains:
        chain.end()


def columns(parts, order_ref, batch_count, tensor_count, t, start, count, lead=None):
    for first, width, which, w_ref in parts:
        if first <= start < first + width:
            break
    pieces = []
    for b in range(batch_count):
        p = order_ref[(which * batch_count + b) * tensor_count + t]
        here = pl.ds(start - first, count)
        pieces.append(w_ref[p, :, here] if lead is None else w_ref[p, lead, :, here])
    return jnp.concatenate(pieces, axis=0)


def weights(*refs):
    out, first = [], 0
    for n, ref in enumerate(refs):
        out.append((first, ref.shape[-1], n % 2, ref))
        first += ref.shape[-1]
    return out


HBM = pl.BlockSpec(memory_space=pltpu.HBM)


def whole(chain):
    part = chain.parts[0].shape
    return pltpu.VMEM((4 * part[0],) + part[1:], BF)


def in_hbm(*values):
    return [pltpu.with_memory_space_constraint(value, pltpu.HBM) for value in values]


def parts_of(chains):
    return in_hbm(*[part for chain in chains for part in chain.parts])


def load_parts(refs, w, sem):
    count = w.shape[0] // 4
    for n in range(4):
        pltpu.make_async_copy(refs[n], w.at[pl.ds(n * count, count)], sem).start()


def wait_whole(w, sem):
    pltpu.make_async_copy(w, w, sem).wait()


def qkv_kernel(grid_of, factor, count, order_ref, x_ref, gain_ref, *refs):
    batch_count, tensor_count = grid_of
    w_hbm, refs = refs[: 4 * count], refs[4 * count :]
    turned_ref, q_ref, k_ref, v_ref, h1_ref = refs[:5]
    w_refs, sem = refs[5:-1], refs[-1]
    first = pl.program_id(0) == 0

    @pl.when(first)
    def _():
        for n in range(count):
            load_parts(w_hbm[4 * n : 4 * n + 4], w_refs[n], sem.at[n])

    def chunk(r):
        here = pl.ds(r, STEP)
        unit, _ = normalize(x_ref[here, :].astype(F32))
        h1_ref[here, :] = (unit * gain_ref[0:1, :]).astype(BF)

    row_loop(x_ref.shape[0], STEP, chunk)
    turned_ref[...] = h1_ref[...].T

    @pl.when(first)
    def _():
        for n in range(count):
            wait_whole(w_refs[n], sem.at[n])

    parts = weights(*w_refs)
    cols = sum(part[1] for part in parts)
    for c, out in enumerate((q_ref, k_ref, v_ref)):
        for t in range(tensor_count):
            for start, width, _, _ in parts:
                w = columns(parts, order_ref, batch_count, tensor_count, t, start, width, lead=c)
                value = dotf(h1_ref[...], w, 1, 0).astype(BF)
                here = slice(t * cols + start, t * cols + start + width)
                out[:, here] = value * BF(factor) if c == 0 else value


def project(orders, x, gains, chains, grid_of, factor):
    rows, width = x.shape
    block = min(256, rows)
    row = pl.BlockSpec((block, width), lambda i, e: (i, 0))
    return pl.pallas_call(
        functools.partial(qkv_kernel, grid_of, factor, len(chains)),
        grid_spec=pltpu.PrefetchScalarGridSpec(
            num_scalar_prefetch=1,
            grid=(rows // block,),
            in_specs=[row, pl.BlockSpec((3, width), lambda i, e: (0, 0))]
            + [HBM] * (4 * len(chains)),
            out_specs=[pl.BlockSpec((width, block), lambda i, e: (0, i))] + [row] * 3,
            scratch_shapes=[pltpu.VMEM((block, width), BF)]
            + [whole(chain) for chain in chains]
            + [pltpu.SemaphoreType.DMA((len(chains),))],
        ),
        out_shape=[jax.ShapeDtypeStruct((width, rows), BF)]
        + [jax.ShapeDtypeStruct((rows, width), BF)] * 3,
        compiler_params=pltpu.CompilerParams(vmem_limit_bytes=24 << 20),
        cost_estimate=cost(13),
        name="project",
    )(orders, *in_hbm(x), gains, *parts_of(chains))


def spans(rows, block):
    return [
        (first, max(0, (first - SEQ_MOST + 1) // block * block), first + block)
        for first in range(0, rows, block)
    ]


def fill_bias(ends_ref, bias, parts, block):
    for (first, low, high), ref in zip(parts, bias):
        shape = (high - low, block)
        keys = low + lax.broadcasted_iota(jnp.int32, shape, 0)
        queries = first + lax.broadcasted_iota(jnp.int32, shape, 1)
        start = jnp.zeros(shape, jnp.int32)
        for n in range(ends_ref.shape[0]):
            end = ends_ref[n]
            start = jnp.where(queries >= end, end, start)
        ref[...] = jnp.where((keys <= queries) & (keys >= start), 0.0, -1e30).astype(F32)


def attend_kernel(rows, block, ends_ref, q_ref, k_ref, v_ref, scale_ref, o_ref, lse_ref, *bias):
    parts = spans(rows, block)

    @pl.when(pl.program_id(0) == 0)
    def _():
        fill_bias(ends_ref, bias, parts, block)

    lower = lax.broadcasted_iota(jnp.int32, (1, 128), 1) < 64
    for n, (first, low, high) in enumerate(parts):
        q = q_ref[pl.ds(first, block), :]
        heads = []
        for h in range(2):
            own = jnp.where(lower if h == 0 else ~lower, q, jnp.zeros_like(q))
            s = dotf(k_ref[pl.ds(low, high - low), :], own, 1, 1) + bias[n][...]
            most = jnp.max(s, axis=0, keepdims=True)
            p = jnp.exp(s - most)
            total = jnp.sum(p, axis=0, keepdims=True)
            probs = (p * (1.0 / total)).astype(BF)
            lse_ref[0, pl.ds(h, 1), pl.ds(first, block)] = most + jnp.log(total)
            heads.append(dotf(probs, v_ref[pl.ds(low, high - low), :], 0, 0))
        out = jnp.where(lower, heads[0], heads[1]) * scale_ref[...]
        o_ref[pl.ds(first, block), :] = out.astype(BF)


def attend_back_kernel(
    rows, block, factor, ends_ref, q_ref, k_ref, v_ref, da_ref, lse_ref,
    dq_ref, dk_ref, dv_ref, inner_ref, dk_acc, dv_acc, *bias
):
    parts = spans(rows, block)

    @pl.when(pl.program_id(0) == 0)
    def _():
        fill_bias(ends_ref, bias, parts, block)

    lower = lax.broadcasted_iota(jnp.int32, (1, 128), 1) < 64
    dk_acc[...] = jnp.zeros_like(dk_acc)
    dv_acc[...] = jnp.zeros_like(dv_acc)
    for n, (first, low, high) in enumerate(parts):
        here = pl.ds(first, block)
        keys = pl.ds(low, high - low)
        q, da, k, v = q_ref[here, :], da_ref[here, :], k_ref[keys, :], v_ref[keys, :]
        heads = []
        for h in range(2):
            mask = lower if h == 0 else ~lower
            q_own = jnp.where(mask, q, jnp.zeros_like(q))
            da_own = jnp.where(mask, da, jnp.zeros_like(da))
            s = dotf(k, q_own, 1, 1) + bias[n][...]
            p = jnp.exp(s - lse_ref[0, pl.ds(h, 1), here])
            product = p * dotf(v, da_own, 1, 1)
            inner = jnp.sum(product, axis=0, keepdims=True)
            inner_ref[0, pl.ds(h, 1), here] = inner
            ds = (product - p * inner).astype(BF)
            dv_acc[keys, :] += dotf(p.astype(BF), da_own, 1, 0)
            dk_acc[keys, :] += dotf(ds, q_own, 1, 0)
            heads.append(dotf(ds, k, 0, 0))
        dq_ref[here, :] = (jnp.where(lower, heads[0], heads[1]) * factor).astype(BF)
    dk_ref[...] = dk_acc[...].astype(BF)
    dv_ref[...] = dv_acc[...].astype(BF)


def bias_shapes(rows, block):
    return [pltpu.VMEM((high - low, block), F32) for _, low, high in spans(rows, block)]


def pair_of(pairs, tensor_count, parts, n):
    if parts == 1:
        return pairs, lambda i: i
    per_tensor = pairs // tensor_count
    per = per_tensor // parts
    return pairs // parts, lambda i: i // per * per_tensor + n * per + i % per


def attend(q, k, v, scale_row, ends, tensor_count, parts, n, before_out, before_lse):
    rows, width = q.shape
    block = min(256, rows)
    pairs = width // 128
    steps, pair = pair_of(pairs, tensor_count, parts, n)
    col = pl.BlockSpec((rows, 128), lambda i, e: (0, pair(i)))
    earlier = [] if before_out is None else [before_out, before_lse]
    count = len(earlier)

    def kernel(ends_ref, q_ref, k_ref, v_ref, scale_ref, *refs):
        attend_kernel(rows, block, ends_ref, q_ref, k_ref, v_ref, scale_ref, *refs[count:])

    return pl.pallas_call(
        kernel,
        grid_spec=pltpu.PrefetchScalarGridSpec(
            num_scalar_prefetch=1,
            grid=(steps,),
            in_specs=[col, col, col, pl.BlockSpec((1, 128), lambda i, e: (0, pair(i)))]
            + [HBM] * count,
            out_specs=[col, pl.BlockSpec((1, 2, rows), lambda i, e: (pair(i), 0, 0))],
            scratch_shapes=bias_shapes(rows, block),
        ),
        out_shape=[
            jax.ShapeDtypeStruct((rows, width), BF),
            jax.ShapeDtypeStruct((pairs, 2, rows), F32),
        ],
        input_output_aliases={5 + j: j for j in range(count)},
        compiler_params=pltpu.CompilerParams(vmem_limit_bytes=32 << 20),
        cost_estimate=cost(24 / parts),
        name="attend",
    )(ends, *in_hbm(q, k, v), scale_row, *earlier)


def attend_back(q, k, v, da, lse, ends, factor, tensor_count, parts, n):
    rows, width = q.shape
    block = min(256, rows)
    pairs = width // 128
    steps, pair = pair_of(pairs, tensor_count, parts, n)
    col = pl.BlockSpec((rows, 128), lambda i, e: (0, pair(i)))
    out_col = pl.BlockSpec((rows, 128), lambda i, e: (0, i))
    out = jax.ShapeDtypeStruct((rows, width // parts), BF)
    return pl.pallas_call(
        functools.partial(attend_back_kernel, rows, block, factor),
        grid_spec=pltpu.PrefetchScalarGridSpec(
            num_scalar_prefetch=1,
            grid=(steps,),
            in_specs=[col] * 4 + [pl.BlockSpec((1, 2, rows), lambda i, e: (pair(i), 0, 0))],
            out_specs=[out_col] * 3 + [pl.BlockSpec((1, 2, rows), lambda i, e: (i, 0, 0))],
            scratch_shapes=[pltpu.VMEM((rows, 128), F32)] * 2 + bias_shapes(rows, block),
        ),
        out_shape=[out, out, out, jax.ShapeDtypeStruct((steps, 2, rows), F32)],
        compiler_params=pltpu.CompilerParams(vmem_limit_bytes=40 << 20),
        cost_estimate=cost(42 / parts),
        name="attend_back",
    )(ends, *in_hbm(q, k, v, da), lse)


def put_stats(ref, here, values):
    lane = lax.broadcasted_iota(jnp.int32, (1, 128), 1)
    out = values[-1]
    for n in reversed(range(len(values) - 1)):
        out = jnp.where(lane < 16 * (n + 1), values[n], out)
    ref[here, :] = jnp.broadcast_to(out, (values[0].shape[0], 128))


def hidden_kernel(
    grid_of, order_ref, scaled_ref, x_ref, gain_ref, mid_ref, a0, a1, a2, a3, b0, b1, b2, b3,
    unit_ref, turned_ref, hidden_ref, narrow_ref, stat_ref, act, norm_stat, wide, h3_ref, wa, wb, sem
):
    batch_count, tensor_count = grid_of
    block, width = x_ref.shape
    total = hidden_ref.shape[1]
    up_cols = total // tensor_count
    out_cols = width // tensor_count
    get = functools.partial(columns, weights(wa, wb), order_ref, batch_count, tensor_count)
    first = pl.program_id(0) == 0

    @pl.when(first)
    def _():
        load_parts((a0, a1, a2, a3), wa, sem.at[0])
        load_parts((b0, b1, b2, b3), wb, sem.at[1])
        wait_whole(wa, sem.at[0])

    mixed = None
    for t in range(tensor_count):
        part = dotf(scaled_ref[:, t * out_cols : (t + 1) * out_cols], get(t, 0, out_cols), 1, 1)
        mixed = part if mixed is None else mixed + part
    wide[...] = mixed

    def norms(r):
        here = pl.ds(r, STEP)
        unit, factor = normalize(wide[here, :])
        unit_ref[here, :] = unit
        resid = x_ref[here, :].astype(F32) + unit * gain_ref[1:2, :]
        mean3 = jnp.mean(resid, axis=-1, keepdims=True)
        centred = resid - mean3
        factor3 = lax.rsqrt(jnp.mean(centred * centred, axis=-1, keepdims=True) + eps)
        h3_ref[here, :] = (centred * factor3 * gain_ref[2:3, :]).astype(BF)
        put_stats(norm_stat, here, [factor, mean3, factor3])

    row_loop(block, STEP, norms)
    turned_ref[...] = h3_ref[...].T

    @pl.when(first)
    def _():
        wait_whole(wb, sem.at[1])

    chunk = min(256, up_cols // 2)
    sums = jnp.zeros((block, 128), F32)
    squares = jnp.zeros((block, 128), F32)
    for c in range(total // chunk):
        t, off = divmod(c * chunk, up_cols)
        h = dotf(h3_ref[...], get(t, out_cols + off, chunk), 1, 0)
        hidden_ref[:, c * chunk : (c + 1) * chunk] = h
        half = 0.5 * jnp.tanh(h * (GELU_C + (GELU_C * GELU_A) * (h * h))) + 0.5
        a = h * half
        act[:, c * chunk : (c + 1) * chunk] = a
        for j in range(chunk // 128):
            piece = a[:, j * 128 : (j + 1) * 128]
            sums += piece
            squares += piece * piece
    mean = jnp.sum(sums, axis=1, keepdims=True) / total
    spread = jnp.sum(squares, axis=1, keepdims=True) / total - mean * mean
    scale = lax.rsqrt(spread + eps)
    before = norm_stat[...]
    put_stats(stat_ref, slice(None), [mean, scale, before[:, 0:1], before[:, 16:17], before[:, 32:33]])

    def narrow(r):
        here = pl.ds(r, STEP)
        m = stat_ref[here, 0:1]
        s = stat_ref[here, 16:17]
        narrow_ref[here, :] = ((act[here, :] - m) * s * mid_ref[...]).astype(BF)

    row_loop(block, STEP, narrow)


def hidden_forward(orders, scaled, x, gains, mid_row, wa, wb, grid_of, share, earlier):
    rows, width = x.shape
    block = min(256, rows)
    total = mid_row.shape[1]
    blocks = rows // block // share[1]
    first = share[0] * blocks
    row = pl.BlockSpec((block, width), lambda i, e: (first + i, 0))
    wide = pl.BlockSpec((block, total), lambda i, e: (first + i, 0))

    def kernel(order_ref, *refs):
        hidden_kernel(grid_of, order_ref, *refs[:12], *refs[12 + len(earlier) :])

    return pl.pallas_call(
        kernel,
        grid_spec=pltpu.PrefetchScalarGridSpec(
            num_scalar_prefetch=1,
            grid=(blocks,),
            in_specs=[
                row,
                row,
                pl.BlockSpec((3, width), lambda i, e: (0, 0)),
                pl.BlockSpec((1, total), lambda i, e: (0, 0)),
            ]
            + [HBM] * (8 + len(earlier)),
            out_specs=[row, pl.BlockSpec((width, block), lambda i, e: (0, first + i)), wide, wide]
            + [pl.BlockSpec((block, 128), lambda i, e: (first + i, 0))],
            scratch_shapes=[
                pltpu.VMEM((block, total), F32),
                pltpu.VMEM((block, 128), F32),
                pltpu.VMEM((block, width), F32),
                pltpu.VMEM((block, width), BF),
                whole(wa),
                whole(wb),
                pltpu.SemaphoreType.DMA((2,)),
            ],
        ),
        out_shape=[
            jax.ShapeDtypeStruct((rows, width), F32),
            jax.ShapeDtypeStruct((width, rows), BF),
            jax.ShapeDtypeStruct((rows, total), F32),
            jax.ShapeDtypeStruct((rows, total), BF),
            jax.ShapeDtypeStruct((rows, 128), F32),
        ],
        input_output_aliases={13 + n: n for n in range(len(earlier))},
        compiler_params=pltpu.CompilerParams(vmem_limit_bytes=44 << 20),
        cost_estimate=cost(30 / share[1]),
        name="hidden_forward",
    )(orders, *in_hbm(scaled, x), gains, mid_row, *parts_of((wa, wb)), *earlier)


def feed_kernel(grid_of, order_ref, narrow_ref, unit_ref, x_ref, gain_ref, a0, a1, a2, a3, b0, b1, b2, b3, out_ref, wa, wb, sem):
    batch_count, tensor_count = grid_of
    up_cols = narrow_ref.shape[1] // tensor_count
    part_cols = wa.shape[2]
    parts = weights(wa, wb)

    @pl.when(pl.program_id(0) == 0)
    def _():
        load_parts((a0, a1, a2, a3), wa, sem.at[0])
        load_parts((b0, b1, b2, b3), wb, sem.at[1])
        wait_whole(wa, sem.at[0])
        wait_whole(wb, sem.at[1])

    out = x_ref[...].astype(F32) + unit_ref[...] * gain_ref[1:2, :]
    for start in range(0, up_cols, part_cols):
        for t in range(tensor_count):
            w = columns(parts, order_ref, batch_count, tensor_count, t, start, part_cols)
            off = t * up_cols + start
            out += dotf(narrow_ref[:, off : off + part_cols], w, 1, 1)
    out_ref[...] = out.astype(BF)


def feed_forward(orders, narrow, unit, x, gains, wa, wb, grid_of):
    rows, width = x.shape
    block = min(256, rows)
    total = narrow.shape[1]
    row = pl.BlockSpec((block, width), lambda i, e: (i, 0))
    return pl.pallas_call(
        functools.partial(feed_kernel, grid_of),
        grid_spec=pltpu.PrefetchScalarGridSpec(
            num_scalar_prefetch=1,
            grid=(rows // block,),
            in_specs=[pl.BlockSpec((block, total), lambda i, e: (i, 0)), row, row]
            + [pl.BlockSpec((3, width), lambda i, e: (0, 0))]
            + [HBM] * 8,
            out_specs=row,
            scratch_shapes=[whole(wa), whole(wb), pltpu.SemaphoreType.DMA((2,))],
        ),
        out_shape=jax.ShapeDtypeStruct((rows, width), BF),
        compiler_params=pltpu.CompilerParams(vmem_limit_bytes=28 << 20),
        cost_estimate=cost(14),
        name="feed_forward",
    )(orders, *in_hbm(narrow, unit, x), gains, *parts_of((wa, wb)))


def back_kernel(
    grid_of, order_ref, hidden_ref, stat_ref, unit_ref, x_ref, cot_ref, gain_ref, mid_ref,
    scale_ref, da0, da1, da2, da3, db0, db1, db2, db3, a0, a1, a2, a3, b0, b1, b2, b3, dhidden_ref, dresid_ref, turned_ref, dattended_ref,
    gains_ref, dmid_ref, grad, unit_s, slope_s, wide, dmixed_ref, wda, wdb, wa, wb, sem
):
    batch_count, tensor_count = grid_of
    block, width = x_ref.shape
    total = hidden_ref.shape[1]
    up_cols = total // tensor_count
    out_cols = width // tensor_count
    get = functools.partial(columns, weights(wa, wb), order_ref, batch_count, tensor_count)
    get_down = functools.partial(columns, weights(wda, wdb), order_ref, batch_count, tensor_count)
    first = pl.program_id(0) == 0

    @pl.when(first)
    def _():
        load_parts((da0, da1, da2, da3), wda, sem.at[0])
        load_parts((db0, db1, db2, db3), wdb, sem.at[1])
        load_parts((a0, a1, a2, a3), wa, sem.at[2])
        load_parts((b0, b1, b2, b3), wb, sem.at[3])
        gains_ref[...] = jnp.zeros_like(gains_ref)
        dmid_ref[...] = jnp.zeros_like(dmid_ref)
        wait_whole(wda, sem.at[0])
        wait_whole(wdb, sem.at[1])

    chunk = min(256, up_cols // 2)
    mean = stat_ref[:, 0:1]
    scale = stat_ref[:, 16:17]
    back_sum = jnp.zeros((block, 128), F32)
    back_inner = jnp.zeros((block, 128), F32)
    for c in range(total // chunk):
        t, off = divmod(c * chunk, up_cols)
        here = slice(c * chunk, (c + 1) * chunk)
        dn = dotf(cot_ref[...], get_down(t, off, chunk), 1, 0)
        h = hidden_ref[:, here]
        square = h * h
        half = 0.5 * jnp.tanh(h * (GELU_C + (GELU_C * GELU_A) * square)) + 0.5
        a = h * half
        slope_s[:, here] = half + a * (1.0 - half) * (
            2.0 * GELU_C + (6.0 * GELU_C * GELU_A) * square
        )
        unit = (a - mean) * scale
        unit_s[:, here] = unit
        dmid_ref[:, here] += fold8(dn * unit)
        g = dn * mid_ref[:, here]
        grad[:, here] = g
        inner = g * unit
        for j in range(chunk // 128):
            back_sum += g[:, j * 128 : (j + 1) * 128]
            back_inner += inner[:, j * 128 : (j + 1) * 128]
    sum_col = jnp.sum(back_sum, axis=1, keepdims=True) / total
    inner_col = jnp.sum(back_inner, axis=1, keepdims=True) / total

    @pl.when(first)
    def _():
        wait_whole(wa, sem.at[2])
        wait_whole(wb, sem.at[3])

    dh3 = None
    for c in range(total // chunk):
        t, off = divmod(c * chunk, up_cols)
        here = slice(c * chunk, (c + 1) * chunk)
        act_grad = scale * (grad[:, here] - sum_col - unit_s[:, here] * inner_col)
        dhidden = (act_grad * slope_s[:, here]).astype(BF)
        dhidden_ref[:, here] = dhidden
        part = dotf(dhidden, get(t, out_cols + off, chunk), 1, 1)
        dh3 = part if dh3 is None else dh3 + part
    wide[...] = dh3

    def back(r):
        here = pl.ds(r, STEP)
        unit = unit_ref[here, :]
        resid = x_ref[here, :].astype(F32) + unit * gain_ref[1:2, :]
        unit3 = (resid - stat_ref[here, 48:49]) * stat_ref[here, 64:65]
        third = wide[here, :]
        gains_ref[8:16, :] += fold8(third * unit3)
        dresid = cot_ref[here, :].astype(F32) + norm_back(
            unit3, stat_ref[here, 64:65], third * gain_ref[2:3, :]
        )
        dresid_ref[here, :] = dresid
        gains_ref[0:8, :] += fold8(dresid * unit)
        dmixed = norm_back(unit, stat_ref[here, 32:33], dresid * gain_ref[1:2, :])
        dmixed_ref[here, :] = dmixed.astype(BF)

    row_loop(block, STEP, back)
    turned_ref[...] = dmixed_ref[...].T
    for t in range(tensor_count):
        here = slice(t * out_cols, (t + 1) * out_cols)
        dscaled = dotf(dmixed_ref[...], get(t, 0, out_cols), 1, 0)
        dattended_ref[:, here] = (dscaled * scale_ref[:, here]).astype(BF)


def feed_back(orders, hidden, stat, unit, x, cot, gains, mid_row, scale_row, wda, wdb, wa, wb, grid_of):
    rows, width = x.shape
    block = min(256, rows)
    total = mid_row.shape[1]
    row = pl.BlockSpec((block, width), lambda i, e: (i, 0))
    wide = pl.BlockSpec((block, total), lambda i, e: (i, 0))
    return pl.pallas_call(
        functools.partial(back_kernel, grid_of),
        grid_spec=pltpu.PrefetchScalarGridSpec(
            num_scalar_prefetch=1,
            grid=(rows // block,),
            in_specs=[
                wide,
                pl.BlockSpec((block, 128), lambda i, e: (i, 0)),
                row,
                row,
                row,
                pl.BlockSpec((3, width), lambda i, e: (0, 0)),
                pl.BlockSpec((1, total), lambda i, e: (0, 0)),
                pl.BlockSpec((1, width), lambda i, e: (0, 0)),
            ]
            + [HBM] * 16,
            out_specs=[
                wide,
                row,
                pl.BlockSpec((width, block), lambda i, e: (0, i)),
                row,
                pl.BlockSpec((16, width), lambda i, e: (0, 0)),
                pl.BlockSpec((8, total), lambda i, e: (0, 0)),
            ],
            scratch_shapes=[
                pltpu.VMEM((block, total), F32),
                pltpu.VMEM((block, total), F32),
                pltpu.VMEM((block, total), F32),
                pltpu.VMEM((block, width), F32),
                pltpu.VMEM((block, width), BF),
            ]
            + [whole(chain) for chain in (wda, wdb, wa, wb)]
            + [pltpu.SemaphoreType.DMA((4,))],
        ),
        out_shape=[
            jax.ShapeDtypeStruct((rows, total), BF),
            jax.ShapeDtypeStruct((rows, width), F32),
            jax.ShapeDtypeStruct((width, rows), BF),
            jax.ShapeDtypeStruct((rows, width), BF),
            jax.ShapeDtypeStruct((16, width), F32),
            jax.ShapeDtypeStruct((8, total), F32),
        ],
        compiler_params=pltpu.CompilerParams(vmem_limit_bytes=60 << 20),
        cost_estimate=cost(60),
        name="feed_back",
    )(
        orders, *in_hbm(hidden, stat, unit, x, cot), gains, mid_row, scale_row,
        *parts_of((wda, wdb, wa, wb)),
    )


def grad_kernel(grid_of, count, turn, order_ref, a_ref, *refs):
    batch_count, tensor_count = grid_of
    b_refs, keep_ref, send_ref = refs[:count], refs[count], refs[count + 1]
    tensor = pl.program_id(1)
    if turn:
        turned = refs[count + 2]

        @pl.when((pl.program_id(0) == 0) & (tensor == 0))
        def _():
            turned[...] = a_ref[...].T

        a_ref = turned
    half = batch_count * tensor_count // 2
    height = keep_ref.shape[-2]
    second = order_ref[0] >= half
    for c, b_ref in enumerate(b_refs):
        acc = dotf(a_ref[...], b_ref[...], 1, 0).astype(BF)
        for core in range(2):

            @pl.when(second if core else jnp.logical_not(second))
            def _(acc=acc, core=core, c=c):
                for b in range(batch_count):
                    place = lax.bitwise_and(order_ref[b * tensor_count + tensor], half - 1)
                    ref = keep_ref if b % 2 == core else send_ref
                    ref[(place,) if count == 1 else (place, c)] = acc[b * height : (b + 1) * height]


def weight_grad(order, a, bs, grid_of, start, cols, name, turn=False):
    batch_count, tensor_count = grid_of
    width, rows = a.shape[::-1] if turn else a.shape
    part = bs[0].shape[1] // tensor_count
    chunk = min(512, cols)
    per = part // chunk
    height = width // batch_count
    count = len(bs)
    lead = (batch_count * tensor_count // 2,) + (() if count == 1 else (count,)) + (height,)
    zeros = (0,) * len(lead)
    out_spec = pl.BlockSpec(lead + (chunk,), lambda i, t, e: zeros + (i,))
    out = jax.ShapeDtypeStruct(lead + (cols,), BF)
    b_spec = pl.BlockSpec((rows, chunk), lambda i, t, e: (0, t * per + start // chunk + i))
    return pl.pallas_call(
        functools.partial(grad_kernel, grid_of, count, turn),
        grid_spec=pltpu.PrefetchScalarGridSpec(
            num_scalar_prefetch=1,
            grid=(cols // chunk, tensor_count),
            in_specs=[pl.BlockSpec(a.shape, lambda i, t, e: (0, 0))] + [b_spec] * count,
            out_specs=[out_spec, out_spec],
            scratch_shapes=[pltpu.VMEM((width, rows), BF)] if turn else [],
        ),
        out_shape=[out, out],
        compiler_params=pltpu.CompilerParams(vmem_limit_bytes=36 << 20),
        cost_estimate=cost(2.4 * count * cols * tensor_count / 1024),
        name=name,
    )(order, *in_hbm(a, *bs))


def input_kernel(grid_of, count, order_ref, *refs):
    batch_count, tensor_count = grid_of
    grads, refs = refs[: 3 * count], refs[3 * count :]
    x_ref, dresid_ref, gain_ref = refs[:3]
    w_hbm, refs = refs[3 : 3 + 4 * count], refs[3 + 4 * count :]
    out_ref, dgain_ref, wide = refs[:3]
    w_refs, sem = refs[3:-1], refs[-1]
    first = pl.program_id(0) == 0

    @pl.when(first)
    def _():
        for n in range(count):
            load_parts(w_hbm[4 * n : 4 * n + 4], w_refs[n], sem.at[n])
        dgain_ref[...] = jnp.zeros_like(dgain_ref)
        for n in range(count):
            wait_whole(w_refs[n], sem.at[n])

    parts = weights(*w_refs)
    total = None
    for n, (start, width, _, _) in enumerate(parts):
        for c in range(3):
            for t in range(tensor_count):
                w = columns(parts, order_ref, batch_count, tensor_count, t, start, width, lead=c)
                part = dotf(grads[3 * n + c][:, t * width : (t + 1) * width], w, 1, 1)
                total = part if total is None else total + part
    wide[...] = total

    def back(r):
        here = pl.ds(r, STEP)
        unit, factor = normalize(x_ref[here, :].astype(F32))
        grad = wide[here, :]
        dgain_ref[...] += fold8(grad * unit)
        out = dresid_ref[here, :] + norm_back(unit, factor, grad * gain_ref[0:1, :])
        out_ref[here, :] = out.astype(BF)

    row_loop(x_ref.shape[0], STEP, back)


def input_grad(orders, grads, x, dresid, gains, chains, grid_of):
    rows, width = x.shape
    block = min(256, rows)
    row = pl.BlockSpec((block, width), lambda i, e: (i, 0))
    part = pl.BlockSpec((block, width // len(chains)), lambda i, e: (i, 0))
    return pl.pallas_call(
        functools.partial(input_kernel, grid_of, len(chains)),
        grid_spec=pltpu.PrefetchScalarGridSpec(
            num_scalar_prefetch=1,
            grid=(rows // block,),
            in_specs=[part] * len(grads)
            + [row, row, pl.BlockSpec((3, width), lambda i, e: (0, 0))]
            + [HBM] * (4 * len(chains)),
            out_specs=[row, pl.BlockSpec((8, width), lambda i, e: (0, 0))],
            scratch_shapes=[pltpu.VMEM((block, width), F32)]
            + [whole(chain) for chain in chains]
            + [pltpu.SemaphoreType.DMA((len(chains),))],
        ),
        out_shape=[
            jax.ShapeDtypeStruct((rows, width), BF),
            jax.ShapeDtypeStruct((8, width), F32),
        ],
        compiler_params=pltpu.CompilerParams(vmem_limit_bytes=32 << 20),
        cost_estimate=cost(15),
        name="input_grad",
    )(orders, *in_hbm(*grads, x, dresid), gains, *parts_of(chains))


def gather_vector(value, tensor_count):
    rank = lax.axis_index("tensor")
    out = jnp.zeros((tensor_count,) + value.shape, value.dtype)
    for flip in range(tensor_count):
        part = value if flip == 0 else swap(value, "tensor", flip)
        out = lax.dynamic_update_slice(out, part[None], (lax.bitwise_xor(rank, flip), 0))
    return out


def body(
    block_in,
    lengths,
    norm_gains,
    qkv_weight,
    head_scale,
    out_weight,
    up_weight,
    mid_gain,
    down_weight,
    cotangent,
):
    tensor_count = lax.axis_size("tensor")
    batch_count = lax.axis_size("batch")
    tensor_rank = lax.axis_index("tensor")
    batch_rank = lax.axis_index("batch")
    micro_count, own_rows, width = block_in.shape
    if tensor_count % micro_count:
        raise NotImplementedError
    split = tensor_count // micro_count
    micro = tensor_rank // split
    local_heads = head_scale.shape[0]
    heads = local_heads * tensor_count
    head_size = width // heads
    local_hidden = mid_gain.shape[0]
    factor = head_size ** (-0.5)
    grid_of = (batch_count, tensor_count)
    half_cols = local_hidden // 2
    qkv_cols = width // tensor_count
    parts = 2 if qkv_cols % 256 == 0 and split == 1 else 1
    steps = [gather_steps(batch_count, tensor_count, first) for first in (True, False)]
    tables = [place_table(one, batch_count, tensor_count) for one in steps]
    orders = jnp.concatenate(tables)
    far = len(steps[0]) - 2 - bits_of(tensor_count)
    near = bits_of(tensor_count) + 1

    def more(chains, count):
        for _ in range(count):
            hop(chains)

    part_cols = qkv_cols // parts
    up_chunk = min(256, local_hidden // 2)
    out_cols = out_weight.shape[0]
    cut = out_cols + ((local_hidden - out_cols) // 2) // up_chunk * up_chunk
    rows_in = Rows(block_in, micro_count, split)
    qkv = Gather(qkv_weight[None], steps[0])
    launch((), [rows_in, qkv])
    qkv.end()
    for _ in range(far - 1):
        hop([qkv])
    qkv_chains = [
        qkv.columns(n * part_cols, part_cols, steps[n % 2][far:]) for n in range(parts)
    ]
    launch(rows_in.arrived, qkv_chains)
    vectors = gather_vector(
        held(jnp.concatenate([mid_gain, head_scale]), rows_in.arrived), tensor_count
    )
    out_up = Gather(
        held(jnp.concatenate([out_weight.T, up_weight], axis=1)[None], qkv.arrived), steps[0]
    )
    hop([out_up])
    for n in range(near - 1):
        for chain in qkv_chains:
            chain.end()
        launch((), qkv_chains)
    for _ in range(far - 1):
        hop([out_up])
    for chain in qkv_chains:
        chain.end()
    down = Gather(held(down_weight.T[None], out_up.arrived), steps[0])
    wa = out_up.columns(0, cut, steps[0][far:])
    wb = out_up.columns(cut, out_weight.shape[0] + local_hidden - cut, steps[1][far:])
    rows_in.end()
    x = launch(rows_in.result, qkv_chains)
    for chain in qkv_chains:
        chain.end()
    x = launch(x, [wa, wb])

    mid_row = vectors[:, :local_hidden].reshape(1, -1)
    scale_all = vectors[:, local_hidden:].reshape(-1)
    scale_row = jnp.repeat(scale_all, head_size)[None]
    own_lengths = lax.dynamic_index_in_dim(lengths[:, 0], micro, 0, keepdims=False)
    ends = jnp.cumsum(own_lengths).astype(jnp.int32)

    def spread(value):
        if split == 1:
            return value
        groups = [[m * split + s for s in range(split)] for m in range(micro_count)]
        return lax.all_to_all(value, "tensor", 1, 0, tiled=True, axis_index_groups=groups)

    def collect(value):
        if split == 1:
            return value
        groups = [[m * split + s for s in range(split)] for m in range(micro_count)]
        return lax.all_to_all(value, "tensor", 0, 1, tiled=True, axis_index_groups=groups)

    h1, q, k, v = project(orders, x, norm_gains, qkv_chains, grid_of, factor)
    q, k, v = land((q, k, v), [wa, wb])
    q, k, v = spread(q), spread(k), spread(v)
    more([wa, wb], near - 2)
    q = launch(q, [wa, wb, down])
    part = width // split
    scale_part = lax.dynamic_slice(scale_row, (0, tensor_rank % split * part), (1, part))
    scaled, lse = None, None
    for n in range(parts):
        scaled, lse = attend(q, k, v, scale_part, ends, tensor_count, parts, n, scaled, lse)
        if n == 0:
            scaled = land(scaled, [down])
            more([down], far - 2)
            scaled = launch(scaled, [down])
    scaled = land(scaled, [wa, wb, down])
    wda = down.columns(0, half_cols, steps[0][far:])
    wdb = down.columns(half_cols, half_cols, steps[1][far:])
    rows_cot = Rows(cotangent, micro_count, split)
    scaled = launch(scaled, [wa, wb])
    scaled = land(scaled, [wa, wb])
    scaled = collect(launch(scaled, [wda, wdb, rows_cot]))
    forward = []
    shares = 2 if x.shape[0] % 512 == 0 else 1
    for n in range(shares):
        if n:
            forward[0] = land(forward[0], [wda, wdb])
            more([wda, wdb], near - 2)
            forward[0] = launch(forward[0], [wda, wdb])
        forward = list(
            hidden_forward(orders, scaled, x, norm_gains, mid_row, wa, wb, grid_of, (n, shares), forward)
        )
    unit, h3, hidden, narrow, stat = forward
    if shares == 1:
        narrow = land(narrow, [wda, wdb])
        more([wda, wdb], near - 2)
        narrow = launch(narrow, [wda, wdb])
    narrow = land(narrow, [rows_cot, wda])
    cot = rows_cot.result

    def grad_half(n, a, b, name, turn=False):
        keep, send = weight_grad(tables[n], a, [b], grid_of, n * half_cols, half_cols, name, turn)
        return Scatter(keep, send, steps[n])

    def flush(chains):
        for chain in chains:
            while chain.steps:
                hop([chain])
        return [chain.total for chain in chains]

    cot_held = launch(cot, [wda])
    d0 = grad_half(0, cot_held, narrow, "grad_down", True)
    cot_held = launch(cot_held, [d0])
    d1 = grad_half(1, cot_held, narrow, "grad_down", True)
    d1.send = land(d1.send, [d0, wda, wdb])
    hidden = launch(hidden, [d1, d0, wdb])
    hidden = land(hidden, [d1, wdb])
    hidden = launch(hidden, [d1])
    dhidden, dresid, dmixed, dattended, gain_sums, mid_sums = feed_back(
        orders, hidden, stat, unit, x, cot, norm_gains, mid_row, scale_row, wda, wdb, wa, wb, grid_of
    )
    dhidden = land(dhidden, [d0, d1])
    more([d0, d1], near - 2)
    dhidden = launch(dhidden, [d0, d1])
    u0 = grad_half(0, h3, dhidden, "grad_up")
    dhidden = launch(dhidden, [u0])
    u1 = grad_half(1, h3, dhidden, "grad_up")
    u1.send = land(u1.send, [u0, d0, d1])
    narrow = launch(narrow, [u1, u0, d0, d1])
    block_out = feed_forward(orders, narrow, unit, x, norm_gains, wda, wdb, grid_of)
    rows_out = Rows(block_out, micro_count, split)
    dmixed, rows_out.value = land((dmixed, rows_out.value), [u1, d0, d1])
    dmixed = launch(dmixed, [u1, d0, d1])
    keep, send = weight_grad(
        tables[0], dmixed, [scaled], grid_of, 0, out_weight.shape[0], "grad_out"
    )
    o0 = Scatter(keep, send, steps[0])
    o0.send = land(o0.send, [u0])
    da = launch(spread(dattended), [u0, o0])
    halves, grads, inners = [], [], []
    for n in range(parts):
        *three, inner = attend_back(q, k, v, da, lse, ends, factor, tensor_count, parts, n)
        inners.append(inner)
        three = [collect(one) for one in three]
        if n == 0:
            three = land(three, [u0, u1, d0, d1, o0])
            three = launch(three, [o0])
        else:
            three = land(three, [rows_out, halves[0], u0, u1])
            three = launch(three, [halves[0], u0, u1, o0])
        keep, send = weight_grad(tables[n % 2], h1, three, grid_of, 0, part_cols, "grad_qkv")
        halves.append(Scatter(keep, send, steps[n % 2]))
        grads += three
        if n < parts - 1:
            da, halves[0].send = land((da, halves[0].send), [o0])
            da = launch(da, [halves[0], u0, u1, rows_out])
    q_last = halves[-1]
    beside = [u0, u1, o0] if parts > 1 else [o0]
    q_last.send = land(q_last.send, beside)
    dresid = launch(dresid, [q_last])
    dresid = land(dresid, [q_last])
    beside = [one for one in beside if one.steps]
    dresid = launch(dresid, [q_last] + beside)
    grad_in, first_sums = input_grad(orders, grads, x, dresid, norm_gains, qkv_chains, grid_of)
    local = heads // split
    if parts == 1:
        head_sums = jnp.sum(inners[0], axis=-1).reshape(-1)
    else:
        shaped = [jnp.sum(one, axis=-1).reshape(tensor_count, -1) for one in inners]
        head_sums = jnp.concatenate(shaped, axis=1).reshape(-1)
    first_head = tensor_rank % split * local
    head_sums = head_sums / lax.dynamic_slice(scale_all, (first_head,), (local,))
    head_all = lax.dynamic_update_slice(jnp.zeros((heads,), F32), head_sums, (first_head,))
    last = jnp.concatenate(
        [jnp.sum(one, axis=0) for one in (first_sums, gain_sums[:8], gain_sums[8:], mid_sums)]
        + [head_all]
    )
    last = Total(last, steps[0])
    rows_back = Rows(grad_in, micro_count, split)
    last.value = land(last.value, halves + beside)
    launch((), [last, rows_back] + ([] if parts > 1 else [rows_out]) + [one for one in halves + [o0] if one.steps])
    while last.steps:
        tail = [one for one in [last] + halves + [o0] if one.steps]
        for one in tail:
            one.end()
        launch((), tail)
    last.end()
    for one in halves + [o0]:
        if not hasattr(one, "total"):
            one.end()
    if parts == 1:
        rows_out.end()
    rows_back.end()
    block_out, grad_in = rows_out.result, rows_back.result
    vector = last.value
    d_totals, u_totals, o_totals, q_totals = (
        flush([d0, d1]), flush([u0, u1]), flush([o0]), flush(halves)
    )
    down_grad = jnp.concatenate(d_totals, axis=1).T
    up_grad = jnp.concatenate(u_totals, axis=1)
    out_grad = o_totals[0].T
    qkv_grad = jnp.concatenate(q_totals, axis=2)
    gains_sum = vector[: 3 * width].reshape(3, width)
    mid_own = lax.dynamic_slice(vector, (3 * width + tensor_rank * local_hidden,), (local_hidden,))
    scale_own = lax.dynamic_slice(
        vector, (3 * width + tensor_count * local_hidden + tensor_rank * local_heads,), (local_heads,)
    )
    return (
        block_out,
        grad_in,
        gains_sum,
        qkv_grad,
        scale_own,
        out_grad,
        up_grad,
        mid_own,
        down_grad,
    )


def solution(mesh):
    in_specs = (
        P(None, ("batch", "tensor"), None),
        P(None, "batch", None),
        P(),
        P(None, "batch", "tensor"),
        P("tensor"),
        P("tensor", "batch"),
        P("batch", "tensor"),
        P("tensor"),
        P("tensor", "batch"),
        P(None, ("batch", "tensor"), None),
    )
    out_specs = (
        P(None, ("batch", "tensor"), None),
        P(None, ("batch", "tensor"), None),
        P(),
        P(None, "batch", "tensor"),
        P("tensor"),
        P("tensor", "batch"),
        P("batch", "tensor"),
        P("tensor"),
        P("tensor", "batch"),
    )
    return jax.shard_map(body, mesh=mesh, in_specs=in_specs, out_specs=out_specs, check_vma=False)
```

```python
import functools
import math

import jax
import jax.numpy as jnp
from jax import lax
from jax.experimental import pallas as pl
from jax.experimental.pallas import tpu as pltpu
from jax.sharding import PartitionSpec as P

eps = 1e-05
SEQ_MOST = 512
F32 = jnp.float32
BF = jnp.bfloat16
ALL = ("batch", "tensor")
GELU_C = math.sqrt(2.0 / math.pi)
GELU_A = 0.044715
STEP = 64


def cost(us):
    return pl.CostEstimate(flops=int(us * 1e9), transcendentals=0, bytes_accessed=1 << 20)


def dotf(a, b, ca, cb):
    return lax.dot_general(a, b, (((ca,), (cb,)), ((), ())), preferred_element_type=F32)


def row_loop(rows, step, fn):
    def one(i, carry):
        fn(pl.multiple_of(i * step, step))
        return carry

    lax.fori_loop(0, rows // step, one, 0)


def normalize(values):
    centred = values - jnp.mean(values, axis=-1, keepdims=True)
    factor = lax.rsqrt(jnp.mean(centred * centred, axis=-1, keepdims=True) + eps)
    return (centred * factor, factor)


def norm_back(unit, factor, grad):
    return factor * (
        grad
        - jnp.mean(grad, axis=-1, keepdims=True)
        - unit * jnp.mean(grad * unit, axis=-1, keepdims=True)
    )


def fold8(values):
    rows, width = values.shape
    return jnp.sum(values.reshape(rows // 8, 8, width), axis=0)


def bits_of(count):
    return count.bit_length() - 1


def gather_steps(batch_count, tensor_count, tensor_first):
    tensor = [("tensor", 1 << k) for k in range(bits_of(tensor_count))]
    plane = [("batch", 2)]
    far = [("batch", 1 << k) for k in reversed(range(2, bits_of(batch_count)))]
    return far + (tensor + plane if tensor_first else plane + tensor) + [("batch", 1)]


def place_table(steps, batch_count, tensor_count):
    batch = jnp.arange(batch_count * tensor_count, dtype=jnp.int32) // tensor_count
    tensor = jnp.arange(batch_count * tensor_count, dtype=jnp.int32) % tensor_count
    batch = jnp.bitwise_xor(batch, lax.axis_index("batch"))
    tensor = jnp.bitwise_xor(tensor, lax.axis_index("tensor"))
    place = jnp.zeros_like(batch)
    for k, (axis, flip) in enumerate(steps):
        apart = (jnp.bitwise_and(batch if axis == "batch" else tensor, flip) != 0).astype(jnp.int32)
        place = place + apart * (1 << k)
    return place


def swap(value, axis, flip):
    count = lax.axis_size(axis)
    return lax.ppermute(value, axis, [(i, i ^ flip) for i in range(count)])


def held(value, after):
    return lax.optimization_barrier((value, after))[0]


class Gather:
    def __init__(self, buffer, steps):
        self.own, self.steps, self.parts = buffer, list(steps), None

    def outgoing(self):
        return self.arrived if len(self.steps) == 1 else self.own

    def go(self, value):
        step = self.steps.pop(0)
        self.arrived = swap(value, *step)
        if not self.steps:
            self.parts[1] = value
        else:
            self.own = value
            if len(self.steps) == 1:
                self.parts = [value, None, swap(value, *self.steps[0]), None]

    def end(self):
        if self.parts is None:
            self.own = jnp.concatenate([self.own, self.arrived], axis=0)
        elif not self.steps:
            self.parts[3] = self.arrived

    def columns(self, start, count, steps):
        return Gather(self.own[..., start : start + count], steps)


class Scatter:
    def __init__(self, keep, send, steps):
        self.keep, self.send, self.steps = keep, send, list(reversed(steps))

    def outgoing(self):
        return (self.send, self.keep)

    def go(self, value):
        send, self.keep = value
        self.arrived = swap(send, *self.steps.pop(0))

    def end(self):
        keep, arrived = self.keep, self.arrived
        half = keep.shape[0] // 2
        if self.steps:
            self.send = (keep[half:].astype(F32) + arrived[half:].astype(F32)).astype(BF)
            self.keep = (keep[:half].astype(F32) + arrived[:half].astype(F32)).astype(BF)
        else:
            self.total = keep[0].astype(F32) + arrived[0].astype(F32)


def merged(chains):
    keep = jnp.concatenate([chain.keep for chain in chains], axis=-1)
    send = jnp.concatenate([chain.send for chain in chains], axis=-1)
    return Scatter(keep, send, list(reversed(chains[0].steps)))


class Total:
    def __init__(self, value, batch_count, tensor_count):
        self.value, self.grid_of = value, (batch_count, tensor_count)
        bits = [(flip, 0) for flip in (1 << k for k in range(2, bits_of(batch_count)))]
        plane = [(2, 0)] + [(0, 1 << k) for k in range(bits_of(tensor_count))]
        self.steps = [[(1, 0)]]
        for group in (plane, bits):
            if len(group) <= 2:
                spans = [(0, 0)]
                for flip in group:
                    spans += [(one[0] ^ flip[0], one[1] ^ flip[1]) for one in spans]
                self.steps.append(spans[1:])
            else:
                self.steps += [[flip] for flip in group]

    def outgoing(self):
        return self.value

    def go(self, value):
        batch_count, tensor_count = self.grid_of
        self.value, self.arrived = value, []
        for batch, tensor in self.steps.pop(0):
            pairs = [
                (b * tensor_count + t, (b ^ batch) * tensor_count + (t ^ tensor))
                for b in range(batch_count)
                for t in range(tensor_count)
            ]
            self.arrived.append(lax.ppermute(value, ALL, pairs))

    def end(self):
        for one in self.arrived:
            self.value = self.value + one


class Rows:
    def __init__(self, value, micro_count, split, cuts=1):
        self.value, self.micro_count, self.split, self.cuts = value, micro_count, split, cuts
        self.taken = value.ndim == 3
        self.steps = [None]
        self.rank = lax.axis_index("tensor")

    def pieces(self):
        if self.taken:
            return self.value
        return self.value.reshape(self.micro_count, -1, self.value.shape[1])

    def outgoing(self):
        if self.split > 1:
            return []
        sent = []
        for flip in range(1, self.micro_count):
            one = lax.dynamic_index_in_dim(self.pieces(), lax.bitwise_xor(self.rank, flip), 0)
            sent += [one[:, n * (one.shape[1] // self.cuts) :][:, : one.shape[1] // self.cuts] for n in range(self.cuts)]
        return sent

    def go(self, value):
        self.steps = []
        if self.split == 1:
            self.arrived = [
                swap(one, "tensor", n // self.cuts + 1) for n, one in enumerate(value)
            ]
        else:
            self.arrived = [
                lax.all_gather(self.value, "tensor", axis=1 if self.taken else 0, tiled=True)
            ]

    def end(self):
        if self.split == 1:
            pieces = self.pieces()
            out = lax.dynamic_update_slice(
                jnp.zeros_like(pieces),
                lax.dynamic_index_in_dim(pieces, self.rank, 0),
                (self.rank, 0, 0),
            )
            for n, one in enumerate(self.arrived):
                other = lax.bitwise_xor(self.rank, n // self.cuts + 1)
                out = lax.dynamic_update_slice(
                    out, one, (other, n % self.cuts * one.shape[1], 0)
                )
            self.result = out.reshape(-1, out.shape[2]) if self.taken else out
            return
        whole = self.arrived[0]
        width = whole.shape[-1]
        if self.taken:
            rows = self.value.shape[0] * self.value.shape[1]
            start = (self.rank // self.split, self.rank % self.split * rows, 0)
            self.result = lax.dynamic_slice(whole, start, (1, rows, width))[0]
        else:
            own = self.value.shape[0] // self.micro_count
            whole = whole.reshape(self.micro_count, -1, width)
            start = (0, self.rank * own, 0)
            self.result = lax.dynamic_slice(whole, start, (self.micro_count, own, width))


def launch(inputs, chains):
    inputs, values = lax.optimization_barrier((inputs, [chain.outgoing() for chain in chains]))
    for chain, value in zip(chains, values):
        chain.go(value)
    return inputs


def land(inputs, chains):
    inputs, values = lax.optimization_barrier((inputs, [chain.arrived for chain in chains]))
    for chain, value in zip(chains, values):
        chain.arrived = value
        chain.end()
    return inputs


def hop(chains, after=()):
    launch(after, chains)
    for chain in chains:
        chain.end()


def columns(parts, order_ref, batch_count, tensor_count, t, start, count, lead=None):
    for first, width, which, w_ref in parts:
        if first <= start < first + width:
            break
    pieces = []
    for b in range(batch_count):
        p = order_ref[(which * batch_count + b) * tensor_count + t]
        here = pl.ds(start - first, count)
        pieces.append(w_ref[p, :, here] if lead is None else w_ref[p, lead, :, here])
    return jnp.concatenate(pieces, axis=0)


def weights(*refs):
    out, first = [], 0
    for n, ref in enumerate(refs):
        out.append((first, ref.shape[-1], n % 2, ref))
        first += ref.shape[-1]
    return out


HBM = pl.BlockSpec(memory_space=pltpu.HBM)


def whole(chain):
    part = chain.parts[0].shape
    return pltpu.VMEM((4 * part[0],) + part[1:], BF)


def in_hbm(*values):
    return [pltpu.with_memory_space_constraint(value, pltpu.HBM) for value in values]


def parts_of(chains):
    return in_hbm(*[part for chain in chains for part in chain.parts])


def load_parts(refs, w, sem):
    count = w.shape[0] // 4
    for n in range(4):
        pltpu.make_async_copy(refs[n], w.at[pl.ds(n * count, count)], sem).start()


def wait_whole(w, sem):
    pltpu.make_async_copy(w, w, sem).wait()


def qkv_kernel(grid_of, factor, count, order_ref, x_ref, gain_ref, *refs):
    batch_count, tensor_count = grid_of
    w_hbm, refs = refs[: 4 * count], refs[4 * count :]
    turned_ref, q_ref, k_ref, v_ref, h1_ref = refs[:5]
    w_refs, sem = refs[5:-1], refs[-1]
    first = pl.program_id(0) == 0

    @pl.when(first)
    def _():
        for n in range(count):
            load_parts(w_hbm[4 * n : 4 * n + 4], w_refs[n], sem.at[n])

    def chunk(r):
        here = pl.ds(r, STEP)
        unit, _ = normalize(x_ref[here, :].astype(F32))
        h1_ref[here, :] = (unit * gain_ref[0:1, :]).astype(BF)

    row_loop(x_ref.shape[0], STEP, chunk)
    turned_ref[...] = h1_ref[...].T

    @pl.when(first)
    def _():
        for n in range(count):
            wait_whole(w_refs[n], sem.at[n])

    parts = weights(*w_refs)
    cols = sum(part[1] for part in parts)
    for c, out in enumerate((q_ref, k_ref, v_ref)):
        for t in range(tensor_count):
            for start, width, _, _ in parts:
                w = columns(parts, order_ref, batch_count, tensor_count, t, start, width, lead=c)
                value = dotf(h1_ref[...], w, 1, 0).astype(BF)
                here = slice(t * cols + start, t * cols + start + width)
                out[:, here] = value * BF(factor) if c == 0 else value


def project(orders, x, gains, chains, grid_of, factor):
    rows, width = x.shape
    block = min(256, rows)
    row = pl.BlockSpec((block, width), lambda i, e: (i, 0))
    return pl.pallas_call(
        functools.partial(qkv_kernel, grid_of, factor, len(chains)),
        grid_spec=pltpu.PrefetchScalarGridSpec(
            num_scalar_prefetch=1,
            grid=(rows // block,),
            in_specs=[row, pl.BlockSpec((3, width), lambda i, e: (0, 0))]
            + [HBM] * (4 * len(chains)),
            out_specs=[pl.BlockSpec((width, block), lambda i, e: (0, i))] + [row] * 3,
            scratch_shapes=[pltpu.VMEM((block, width), BF)]
            + [whole(chain) for chain in chains]
            + [pltpu.SemaphoreType.DMA((len(chains),))],
        ),
        out_shape=[pltpu.HBM((width, rows), BF)]
        + [pltpu.HBM((rows, width), BF)] * 3,
        compiler_params=pltpu.CompilerParams(vmem_limit_bytes=24 << 20),
        cost_estimate=cost(13),
        name="project",
    )(orders, *in_hbm(x), gains, *parts_of(chains))


def spans(rows, block):
    return [
        (first, max(0, (first - SEQ_MOST + 1) // block * block), first + block)
        for first in range(0, rows, block)
    ]


def fill_bias(ends_ref, bias, parts, block):
    for (first, low, high), ref in zip(parts, bias):
        shape = (high - low, block)
        keys = low + lax.broadcasted_iota(jnp.int32, shape, 0)
        queries = first + lax.broadcasted_iota(jnp.int32, shape, 1)
        start = jnp.zeros(shape, jnp.int32)
        for n in range(ends_ref.shape[0]):
            end = ends_ref[n]
            start = jnp.where(queries >= end, end, start)
        ref[...] = jnp.where((keys <= queries) & (keys >= start), 0.0, -1e30).astype(F32)


def attend_kernel(rows, block, ends_ref, q_ref, k_ref, v_ref, scale_ref, o_ref, lse_ref, *bias):
    parts = spans(rows, block)

    @pl.when(pl.program_id(0) == 0)
    def _():
        fill_bias(ends_ref, bias, parts, block)

    lower = lax.broadcasted_iota(jnp.int32, (1, 128), 1) < 64
    for n, (first, low, high) in enumerate(parts):
        q = q_ref[pl.ds(first, block), :]
        heads = []
        for h in range(2):
            own = jnp.where(lower if h == 0 else ~lower, q, jnp.zeros_like(q))
            s = dotf(k_ref[pl.ds(low, high - low), :], own, 1, 1) + bias[n][...]
            most = jnp.max(s, axis=0, keepdims=True)
            p = jnp.exp(s - most)
            total = jnp.sum(p, axis=0, keepdims=True)
            probs = (p * (1.0 / total)).astype(BF)
            lse_ref[0, pl.ds(h, 1), pl.ds(first, block)] = most + jnp.log(total)
            heads.append(dotf(probs, v_ref[pl.ds(low, high - low), :], 0, 0))
        out = jnp.where(lower, heads[0], heads[1]) * scale_ref[...]
        o_ref[pl.ds(first, block), :] = out.astype(BF)


def attend_back_kernel(
    rows, block, factor, ends_ref, q_ref, k_ref, v_ref, da_ref, lse_ref,
    dq_ref, dk_ref, dv_ref, inner_ref, dk_acc, dv_acc, *bias
):
    parts = spans(rows, block)

    @pl.when(pl.program_id(0) == 0)
    def _():
        fill_bias(ends_ref, bias, parts, block)

    lower = lax.broadcasted_iota(jnp.int32, (1, 128), 1) < 64
    dk_acc[...] = jnp.zeros_like(dk_acc)
    dv_acc[...] = jnp.zeros_like(dv_acc)
    for n, (first, low, high) in enumerate(parts):
        here = pl.ds(first, block)
        keys = pl.ds(low, high - low)
        q, da, k, v = q_ref[here, :], da_ref[here, :], k_ref[keys, :], v_ref[keys, :]
        heads = []
        for h in range(2):
            mask = lower if h == 0 else ~lower
            q_own = jnp.where(mask, q, jnp.zeros_like(q))
            da_own = jnp.where(mask, da, jnp.zeros_like(da))
            s = dotf(k, q_own, 1, 1) + bias[n][...]
            p = jnp.exp(s - lse_ref[0, pl.ds(h, 1), here])
            product = p * dotf(v, da_own, 1, 1)
            inner = jnp.sum(product, axis=0, keepdims=True)
            inner_ref[0, pl.ds(h, 1), here] = inner
            ds = (product - p * inner).astype(BF)
            dv_acc[keys, :] += dotf(p.astype(BF), da_own, 1, 0)
            dk_acc[keys, :] += dotf(ds, q_own, 1, 0)
            heads.append(dotf(ds, k, 0, 0))
        dq_ref[here, :] = (jnp.where(lower, heads[0], heads[1]) * factor).astype(BF)
    dk_ref[...] = dk_acc[...].astype(BF)
    dv_ref[...] = dv_acc[...].astype(BF)


def bias_shapes(rows, block):
    return [pltpu.VMEM((high - low, block), F32) for _, low, high in spans(rows, block)]


def pair_of(pairs, tensor_count, parts, n):
    if parts == 1:
        return pairs, lambda i: i
    per_tensor = pairs // tensor_count
    per = per_tensor // parts
    return pairs // parts, lambda i: i // per * per_tensor + n * per + i % per


def attend(q, k, v, scale_row, ends, tensor_count, parts, n, before_out, before_lse):
    rows, width = q.shape
    block = min(256, rows)
    pairs = width // 128
    steps, pair = pair_of(pairs, tensor_count, parts, n)
    col = pl.BlockSpec((rows, 128), lambda i, e: (0, pair(i)))
    earlier = [] if before_out is None else [before_out, before_lse]
    count = len(earlier)

    def kernel(ends_ref, q_ref, k_ref, v_ref, scale_ref, *refs):
        attend_kernel(rows, block, ends_ref, q_ref, k_ref, v_ref, scale_ref, *refs[count:])

    return pl.pallas_call(
        kernel,
        grid_spec=pltpu.PrefetchScalarGridSpec(
            num_scalar_prefetch=1,
            grid=(steps,),
            in_specs=[col, col, col, pl.BlockSpec((1, 128), lambda i, e: (0, pair(i)))]
            + [HBM] * count,
            out_specs=[col, pl.BlockSpec((1, 2, rows), lambda i, e: (pair(i), 0, 0))],
            scratch_shapes=bias_shapes(rows, block),
        ),
        out_shape=[
            pltpu.HBM((rows, width), BF),
            pltpu.HBM((pairs, 2, rows), F32),
        ],
        input_output_aliases={5 + j: j for j in range(count)},
        compiler_params=pltpu.CompilerParams(vmem_limit_bytes=32 << 20),
        cost_estimate=cost(24 / parts),
        name="attend",
    )(ends, *in_hbm(q, k, v), scale_row, *earlier)


def attend_back(q, k, v, da, lse, ends, factor, tensor_count, parts, n):
    rows, width = q.shape
    block = min(256, rows)
    pairs = width // 128
    steps, pair = pair_of(pairs, tensor_count, parts, n)
    col = pl.BlockSpec((rows, 128), lambda i, e: (0, pair(i)))
    out_col = pl.BlockSpec((rows, 128), lambda i, e: (0, i))
    out = pltpu.HBM((rows, width // parts), BF)
    return pl.pallas_call(
        functools.partial(attend_back_kernel, rows, block, factor),
        grid_spec=pltpu.PrefetchScalarGridSpec(
            num_scalar_prefetch=1,
            grid=(steps,),
            in_specs=[col] * 4 + [pl.BlockSpec((1, 2, rows), lambda i, e: (pair(i), 0, 0))],
            out_specs=[out_col] * 3 + [pl.BlockSpec((1, 2, rows), lambda i, e: (i, 0, 0))],
            scratch_shapes=[pltpu.VMEM((rows, 128), F32)] * 2 + bias_shapes(rows, block),
        ),
        out_shape=[out, out, out, pltpu.HBM((steps, 2, rows), F32)],
        compiler_params=pltpu.CompilerParams(vmem_limit_bytes=40 << 20),
        cost_estimate=cost(42 / parts),
        name="attend_back",
    )(ends, *in_hbm(q, k, v, da), lse)


def put_stats(ref, here, values):
    lane = lax.broadcasted_iota(jnp.int32, (1, 128), 1)
    out = values[-1]
    for n in reversed(range(len(values) - 1)):
        out = jnp.where(lane < 16 * (n + 1), values[n], out)
    ref[here, :] = jnp.broadcast_to(out, (values[0].shape[0], 128))


def hidden_kernel(
    grid_of, order_ref, scaled_ref, x_ref, gain_ref, mid_ref, a0, a1, a2, a3, b0, b1, b2, b3,
    unit_ref, turned_ref, hidden_ref, narrow_ref, stat_ref, act, norm_stat, wide, h3_ref, wa, wb, sem
):
    batch_count, tensor_count = grid_of
    block, width = x_ref.shape
    total = hidden_ref.shape[1]
    up_cols = total // tensor_count
    out_cols = width // tensor_count
    get = functools.partial(columns, weights(wa, wb), order_ref, batch_count, tensor_count)
    first = pl.program_id(0) == 0

    @pl.when(first)
    def _():
        load_parts((a0, a1, a2, a3), wa, sem.at[0])
        load_parts((b0, b1, b2, b3), wb, sem.at[1])
        wait_whole(wa, sem.at[0])

    mixed = None
    for t in range(tensor_count):
        part = dotf(scaled_ref[:, t * out_cols : (t + 1) * out_cols], get(t, 0, out_cols), 1, 1)
        mixed = part if mixed is None else mixed + part
    wide[...] = mixed

    def norms(r):
        here = pl.ds(r, STEP)
        unit, factor = normalize(wide[here, :])
        unit_ref[here, :] = unit
        resid = x_ref[here, :].astype(F32) + unit * gain_ref[1:2, :]
        mean3 = jnp.mean(resid, axis=-1, keepdims=True)
        centred = resid - mean3
        factor3 = lax.rsqrt(jnp.mean(centred * centred, axis=-1, keepdims=True) + eps)
        h3_ref[here, :] = (centred * factor3 * gain_ref[2:3, :]).astype(BF)
        put_stats(norm_stat, here, [factor, mean3, factor3])

    row_loop(block, STEP, norms)
    turned_ref[...] = h3_ref[...].T

    @pl.when(first)
    def _():
        wait_whole(wb, sem.at[1])

    chunk = min(256, up_cols // 2)
    sums = jnp.zeros((block, 128), F32)
    squares = jnp.zeros((block, 128), F32)
    for c in range(total // chunk):
        t, off = divmod(c * chunk, up_cols)
        h = dotf(h3_ref[...], get(t, out_cols + off, chunk), 1, 0)
        hidden_ref[:, c * chunk : (c + 1) * chunk] = h
        half = 0.5 * jnp.tanh(h * (GELU_C + (GELU_C * GELU_A) * (h * h))) + 0.5
        a = h * half
        act[:, c * chunk : (c + 1) * chunk] = a
        for j in range(chunk // 128):
            piece = a[:, j * 128 : (j + 1) * 128]
            sums += piece
            squares += piece * piece
    mean = jnp.sum(sums, axis=1, keepdims=True) / total
    spread = jnp.sum(squares, axis=1, keepdims=True) / total - mean * mean
    scale = lax.rsqrt(spread + eps)
    before = norm_stat[...]
    put_stats(stat_ref, slice(None), [mean, scale, before[:, 0:1], before[:, 16:17], before[:, 32:33]])

    def narrow(r):
        here = pl.ds(r, STEP)
        m = stat_ref[here, 0:1]
        s = stat_ref[here, 16:17]
        narrow_ref[here, :] = ((act[here, :] - m) * s * mid_ref[...]).astype(BF)

    row_loop(block, STEP, narrow)


def hidden_forward(orders, scaled, x, gains, mid_row, wa, wb, grid_of, share, earlier):
    rows, width = x.shape
    block = min(256, rows)
    total = mid_row.shape[1]
    blocks = rows // block // share[1]
    first = share[0] * blocks
    row = pl.BlockSpec((block, width), lambda i, e: (first + i, 0))
    wide = pl.BlockSpec((block, total), lambda i, e: (first + i, 0))

    def kernel(order_ref, *refs):
        hidden_kernel(grid_of, order_ref, *refs[:12], *refs[12 + len(earlier) :])

    return pl.pallas_call(
        kernel,
        grid_spec=pltpu.PrefetchScalarGridSpec(
            num_scalar_prefetch=1,
            grid=(blocks,),
            in_specs=[
                row,
                row,
                pl.BlockSpec((3, width), lambda i, e: (0, 0)),
                pl.BlockSpec((1, total), lambda i, e: (0, 0)),
            ]
            + [HBM] * (8 + len(earlier)),
            out_specs=[row, pl.BlockSpec((width, block), lambda i, e: (0, first + i)), wide, wide]
            + [pl.BlockSpec((block, 128), lambda i, e: (first + i, 0))],
            scratch_shapes=[
                pltpu.VMEM((block, total), F32),
                pltpu.VMEM((block, 128), F32),
                pltpu.VMEM((block, width), F32),
                pltpu.VMEM((block, width), BF),
                whole(wa),
                whole(wb),
                pltpu.SemaphoreType.DMA((2,)),
            ],
        ),
        out_shape=[
            pltpu.HBM((rows, width), F32),
            pltpu.HBM((width, rows), BF),
            pltpu.HBM((rows, total), F32),
            pltpu.HBM((rows, total), BF),
            pltpu.HBM((rows, 128), F32),
        ],
        input_output_aliases={13 + n: n for n in range(len(earlier))},
        compiler_params=pltpu.CompilerParams(vmem_limit_bytes=44 << 20),
        cost_estimate=cost(30 / share[1]),
        name="hidden_forward",
    )(orders, *in_hbm(scaled, x), gains, mid_row, *parts_of((wa, wb)), *earlier)


def feed_kernel(grid_of, order_ref, narrow_ref, unit_ref, x_ref, gain_ref, a0, a1, a2, a3, b0, b1, b2, b3, out_ref, wa, wb, sem):
    batch_count, tensor_count = grid_of
    up_cols = narrow_ref.shape[1] // tensor_count
    parts = weights(wa, wb)

    @pl.when(pl.program_id(0) == 0)
    def _():
        load_parts((a0, a1, a2, a3), wa, sem.at[0])
        load_parts((b0, b1, b2, b3), wb, sem.at[1])
        wait_whole(wa, sem.at[0])
        wait_whole(wb, sem.at[1])

    out = x_ref[...].astype(F32) + unit_ref[...] * gain_ref[1:2, :]
    for start, width, _, _ in parts:
        for t in range(tensor_count):
            w = columns(parts, order_ref, batch_count, tensor_count, t, start, width)
            off = t * up_cols + start
            out += dotf(narrow_ref[:, off : off + width], w, 1, 1)
    out_ref[...] = out.astype(BF)


def feed_forward(orders, narrow, unit, x, gains, wa, wb, grid_of):
    rows, width = x.shape
    block = min(256, rows)
    total = narrow.shape[1]
    row = pl.BlockSpec((block, width), lambda i, e: (i, 0))
    return pl.pallas_call(
        functools.partial(feed_kernel, grid_of),
        grid_spec=pltpu.PrefetchScalarGridSpec(
            num_scalar_prefetch=1,
            grid=(rows // block,),
            in_specs=[pl.BlockSpec((block, total), lambda i, e: (i, 0)), row, row]
            + [pl.BlockSpec((3, width), lambda i, e: (0, 0))]
            + [HBM] * 8,
            out_specs=row,
            scratch_shapes=[whole(wa), whole(wb), pltpu.SemaphoreType.DMA((2,))],
        ),
        out_shape=pltpu.HBM((rows, width), BF),
        compiler_params=pltpu.CompilerParams(vmem_limit_bytes=28 << 20),
        cost_estimate=cost(14),
        name="feed_forward",
    )(orders, *in_hbm(narrow, unit, x), gains, *parts_of((wa, wb)))


def back_kernel(
    grid_of, order_ref, hidden_ref, stat_ref, unit_ref, x_ref, cot_ref, gain_ref, mid_ref,
    scale_ref, da0, da1, da2, da3, db0, db1, db2, db3, a0, a1, a2, a3, b0, b1, b2, b3, dhidden_ref, dresid_ref, turned_ref, dattended_ref,
    gains_ref, dmid_ref, grad, unit_s, slope_s, wide, dmixed_ref, wda, wdb, wa, wb, sem
):
    batch_count, tensor_count = grid_of
    block, width = x_ref.shape
    total = hidden_ref.shape[1]
    up_cols = total // tensor_count
    out_cols = width // tensor_count
    get = functools.partial(columns, weights(wa, wb), order_ref, batch_count, tensor_count)
    get_down = functools.partial(columns, weights(wda, wdb), order_ref, batch_count, tensor_count)
    first = pl.program_id(0) == 0

    @pl.when(first)
    def _():
        load_parts((da0, da1, da2, da3), wda, sem.at[0])
        load_parts((db0, db1, db2, db3), wdb, sem.at[1])
        load_parts((a0, a1, a2, a3), wa, sem.at[2])
        load_parts((b0, b1, b2, b3), wb, sem.at[3])
        gains_ref[...] = jnp.zeros_like(gains_ref)
        dmid_ref[...] = jnp.zeros_like(dmid_ref)
        wait_whole(wda, sem.at[0])
        wait_whole(wdb, sem.at[1])

    chunk = min(256, up_cols // 2)
    mean = stat_ref[:, 0:1]
    scale = stat_ref[:, 16:17]
    back_sum = jnp.zeros((block, 128), F32)
    back_inner = jnp.zeros((block, 128), F32)
    for c in range(total // chunk):
        t, off = divmod(c * chunk, up_cols)
        here = slice(c * chunk, (c + 1) * chunk)
        dn = dotf(cot_ref[...], get_down(t, off, chunk), 1, 0)
        h = hidden_ref[:, here]
        square = h * h
        half = 0.5 * jnp.tanh(h * (GELU_C + (GELU_C * GELU_A) * square)) + 0.5
        a = h * half
        slope_s[:, here] = half + a * (1.0 - half) * (
            2.0 * GELU_C + (6.0 * GELU_C * GELU_A) * square
        )
        unit = (a - mean) * scale
        unit_s[:, here] = unit
        dmid_ref[:, here] += fold8(dn * unit)
        g = dn * mid_ref[:, here]
        grad[:, here] = g
        inner = g * unit
        for j in range(chunk // 128):
            back_sum += g[:, j * 128 : (j + 1) * 128]
            back_inner += inner[:, j * 128 : (j + 1) * 128]
    sum_col = jnp.sum(back_sum, axis=1, keepdims=True) / total
    inner_col = jnp.sum(back_inner, axis=1, keepdims=True) / total

    @pl.when(first)
    def _():
        wait_whole(wa, sem.at[2])
        wait_whole(wb, sem.at[3])

    dh3 = None
    for c in range(total // chunk):
        t, off = divmod(c * chunk, up_cols)
        here = slice(c * chunk, (c + 1) * chunk)
        act_grad = scale * (grad[:, here] - sum_col - unit_s[:, here] * inner_col)
        dhidden = (act_grad * slope_s[:, here]).astype(BF)
        dhidden_ref[:, here] = dhidden
        part = dotf(dhidden, get(t, out_cols + off, chunk), 1, 1)
        dh3 = part if dh3 is None else dh3 + part
    wide[...] = dh3

    def back(r):
        here = pl.ds(r, STEP)
        unit = unit_ref[here, :]
        resid = x_ref[here, :].astype(F32) + unit * gain_ref[1:2, :]
        unit3 = (resid - stat_ref[here, 48:49]) * stat_ref[here, 64:65]
        third = wide[here, :]
        gains_ref[8:16, :] += fold8(third * unit3)
        dresid = cot_ref[here, :].astype(F32) + norm_back(
            unit3, stat_ref[here, 64:65], third * gain_ref[2:3, :]
        )
        dresid_ref[here, :] = dresid
        gains_ref[0:8, :] += fold8(dresid * unit)
        dmixed = norm_back(unit, stat_ref[here, 32:33], dresid * gain_ref[1:2, :])
        dmixed_ref[here, :] = dmixed.astype(BF)

    row_loop(block, STEP, back)
    turned_ref[...] = dmixed_ref[...].T
    for t in range(tensor_count):
        here = slice(t * out_cols, (t + 1) * out_cols)
        dscaled = dotf(dmixed_ref[...], get(t, 0, out_cols), 1, 0)
        dattended_ref[:, here] = (dscaled * scale_ref[:, here]).astype(BF)


def feed_back(orders, hidden, stat, unit, x, cot, gains, mid_row, scale_row, wda, wdb, wa, wb, grid_of):
    rows, width = x.shape
    block = min(256, rows)
    total = mid_row.shape[1]
    row = pl.BlockSpec((block, width), lambda i, e: (i, 0))
    wide = pl.BlockSpec((block, total), lambda i, e: (i, 0))
    return pl.pallas_call(
        functools.partial(back_kernel, grid_of),
        grid_spec=pltpu.PrefetchScalarGridSpec(
            num_scalar_prefetch=1,
            grid=(rows // block,),
            in_specs=[
                wide,
                pl.BlockSpec((block, 128), lambda i, e: (i, 0)),
                row,
                row,
                row,
                pl.BlockSpec((3, width), lambda i, e: (0, 0)),
                pl.BlockSpec((1, total), lambda i, e: (0, 0)),
                pl.BlockSpec((1, width), lambda i, e: (0, 0)),
            ]
            + [HBM] * 16,
            out_specs=[
                wide,
                row,
                pl.BlockSpec((width, block), lambda i, e: (0, i)),
                row,
                pl.BlockSpec((16, width), lambda i, e: (0, 0)),
                pl.BlockSpec((8, total), lambda i, e: (0, 0)),
            ],
            scratch_shapes=[
                pltpu.VMEM((block, total), F32),
                pltpu.VMEM((block, total), F32),
                pltpu.VMEM((block, total), F32),
                pltpu.VMEM((block, width), F32),
                pltpu.VMEM((block, width), BF),
            ]
            + [whole(chain) for chain in (wda, wdb, wa, wb)]
            + [pltpu.SemaphoreType.DMA((4,))],
        ),
        out_shape=[
            pltpu.HBM((rows, total), BF),
            pltpu.HBM((rows, width), F32),
            pltpu.HBM((width, rows), BF),
            pltpu.HBM((rows, width), BF),
            pltpu.HBM((16, width), F32),
            pltpu.HBM((8, total), F32),
        ],
        compiler_params=pltpu.CompilerParams(vmem_limit_bytes=60 << 20),
        cost_estimate=cost(60),
        name="feed_back",
    )(
        orders, *in_hbm(hidden, stat, unit, x, cot), gains, mid_row, scale_row,
        *parts_of((wda, wdb, wa, wb)),
    )


def grad_kernel(grid_of, count, turn, order_ref, a_ref, *refs):
    batch_count, tensor_count = grid_of
    b_refs, keep_ref, send_ref = refs[:count], refs[count], refs[count + 1]
    tensor = pl.program_id(1)
    if turn:
        turned = refs[count + 2]

        @pl.when((pl.program_id(0) == 0) & (tensor == 0))
        def _():
            turned[...] = a_ref[...].T

        a_ref = turned
    half = batch_count * tensor_count // 2
    height = keep_ref.shape[-2]
    second = order_ref[0] >= half
    for c, b_ref in enumerate(b_refs):
        acc = dotf(a_ref[...], b_ref[...], 1, 0).astype(BF)
        for core in range(2):

            @pl.when(second if core else jnp.logical_not(second))
            def _(acc=acc, core=core, c=c):
                for b in range(batch_count):
                    place = lax.bitwise_and(order_ref[b * tensor_count + tensor], half - 1)
                    ref = keep_ref if b % 2 == core else send_ref
                    ref[(place,) if count == 1 else (place, c)] = acc[b * height : (b + 1) * height]


def weight_grad(order, a, bs, grid_of, start, cols, name, turn=False):
    batch_count, tensor_count = grid_of
    width, rows = a.shape[::-1] if turn else a.shape
    part = bs[0].shape[1] // tensor_count
    chunk = min(512, cols)
    per = part // chunk
    height = width // batch_count
    count = len(bs)
    lead = (batch_count * tensor_count // 2,) + (() if count == 1 else (count,)) + (height,)
    zeros = (0,) * len(lead)
    out_spec = pl.BlockSpec(lead + (chunk,), lambda i, t, e: zeros + (i,))
    out = pltpu.HBM(lead + (cols,), BF)
    b_spec = pl.BlockSpec((rows, chunk), lambda i, t, e: (0, t * per + start // chunk + i))
    return pl.pallas_call(
        functools.partial(grad_kernel, grid_of, count, turn),
        grid_spec=pltpu.PrefetchScalarGridSpec(
            num_scalar_prefetch=1,
            grid=(cols // chunk, tensor_count),
            in_specs=[pl.BlockSpec(a.shape, lambda i, t, e: (0, 0))] + [b_spec] * count,
            out_specs=[out_spec, out_spec],
            scratch_shapes=[pltpu.VMEM((width, rows), BF)] if turn else [],
        ),
        out_shape=[out, out],
        compiler_params=pltpu.CompilerParams(vmem_limit_bytes=36 << 20),
        cost_estimate=cost(2.4 * count * cols * tensor_count / 1024),
        name=name,
    )(order, *in_hbm(a, *bs))


def input_kernel(grid_of, count, order_ref, *refs):
    batch_count, tensor_count = grid_of
    grads, refs = refs[: 3 * count], refs[3 * count :]
    x_ref, dresid_ref, gain_ref = refs[:3]
    w_hbm, refs = refs[3 : 3 + 4 * count], refs[3 + 4 * count :]
    out_ref, dgain_ref, wide = refs[:3]
    w_refs, sem = refs[3:-1], refs[-1]
    first = pl.program_id(0) == 0

    @pl.when(first)
    def _():
        for n in range(count):
            load_parts(w_hbm[4 * n : 4 * n + 4], w_refs[n], sem.at[n])
        dgain_ref[...] = jnp.zeros_like(dgain_ref)
        for n in range(count):
            wait_whole(w_refs[n], sem.at[n])

    parts = weights(*w_refs)
    total = None
    for n, (start, width, _, _) in enumerate(parts):
        for c in range(3):
            for t in range(tensor_count):
                w = columns(parts, order_ref, batch_count, tensor_count, t, start, width, lead=c)
                part = dotf(grads[3 * n + c][:, t * width : (t + 1) * width], w, 1, 1)
                total = part if total is None else total + part
    wide[...] = total

    def back(r):
        here = pl.ds(r, STEP)
        unit, factor = normalize(x_ref[here, :].astype(F32))
        grad = wide[here, :]
        dgain_ref[...] += fold8(grad * unit)
        out = dresid_ref[here, :] + norm_back(unit, factor, grad * gain_ref[0:1, :])
        out_ref[here, :] = out.astype(BF)

    row_loop(x_ref.shape[0], STEP, back)


def input_grad(orders, grads, x, dresid, gains, chains, grid_of):
    rows, width = x.shape
    block = min(256, rows)
    row = pl.BlockSpec((block, width), lambda i, e: (i, 0))
    part = pl.BlockSpec((block, width // len(chains)), lambda i, e: (i, 0))
    return pl.pallas_call(
        functools.partial(input_kernel, grid_of, len(chains)),
        grid_spec=pltpu.PrefetchScalarGridSpec(
            num_scalar_prefetch=1,
            grid=(rows // block,),
            in_specs=[part] * len(grads)
            + [row, row, pl.BlockSpec((3, width), lambda i, e: (0, 0))]
            + [HBM] * (4 * len(chains)),
            out_specs=[row, pl.BlockSpec((8, width), lambda i, e: (0, 0))],
            scratch_shapes=[pltpu.VMEM((block, width), F32)]
            + [whole(chain) for chain in chains]
            + [pltpu.SemaphoreType.DMA((len(chains),))],
        ),
        out_shape=[
            pltpu.HBM((rows, width), BF),
            pltpu.HBM((8, width), F32),
        ],
        compiler_params=pltpu.CompilerParams(vmem_limit_bytes=32 << 20),
        cost_estimate=cost(15),
        name="input_grad",
    )(orders, *in_hbm(*grads, x, dresid), gains, *parts_of(chains))


def gather_vector(value, tensor_count):
    rank = lax.axis_index("tensor")
    out = jnp.zeros((tensor_count,) + value.shape, value.dtype)
    for flip in range(tensor_count):
        part = value if flip == 0 else swap(value, "tensor", flip)
        out = lax.dynamic_update_slice(out, part[None], (lax.bitwise_xor(rank, flip), 0))
    return out


def body(
    block_in,
    lengths,
    norm_gains,
    qkv_weight,
    head_scale,
    out_weight,
    up_weight,
    mid_gain,
    down_weight,
    cotangent,
):
    tensor_count = lax.axis_size("tensor")
    batch_count = lax.axis_size("batch")
    tensor_rank = lax.axis_index("tensor")
    batch_rank = lax.axis_index("batch")
    micro_count, own_rows, width = block_in.shape
    if tensor_count % micro_count:
        raise NotImplementedError
    split = tensor_count // micro_count
    micro = tensor_rank // split
    local_heads = head_scale.shape[0]
    heads = local_heads * tensor_count
    head_size = width // heads
    local_hidden = mid_gain.shape[0]
    factor = head_size ** (-0.5)
    grid_of = (batch_count, tensor_count)
    half_cols = local_hidden // 2
    qkv_cols = width // tensor_count
    parts = 2 if qkv_cols % 256 == 0 and split == 1 else 1
    steps = [gather_steps(batch_count, tensor_count, first) for first in (True, False)]
    tables = [place_table(one, batch_count, tensor_count) for one in steps]
    orders = jnp.concatenate(tables)
    far = len(steps[0]) - 2 - bits_of(tensor_count)
    near = bits_of(tensor_count) + 1

    def more(chains, count):
        for _ in range(count):
            hop(chains)

    part_cols = qkv_cols // parts
    up_chunk = min(256, local_hidden // 2)
    out_cols = out_weight.shape[0]
    cut = out_cols + ((local_hidden - out_cols) // 2) // up_chunk * up_chunk
    rows_in = Rows(block_in, micro_count, split)
    qkv = Gather(qkv_weight[None], steps[0])
    launch((), [rows_in, qkv])
    qkv.end()
    for _ in range(far - 1):
        hop([qkv])
    qkv_chains = [
        qkv.columns(n * part_cols, part_cols, steps[n % 2][far:]) for n in range(parts)
    ]
    launch(rows_in.arrived, qkv_chains)
    vectors = gather_vector(
        held(jnp.concatenate([mid_gain, head_scale]), rows_in.arrived), tensor_count
    )
    out_up = Gather(
        held(jnp.concatenate([out_weight.T, up_weight], axis=1)[None], qkv.arrived), steps[0]
    )
    hop([out_up])
    for n in range(near - 1):
        for chain in qkv_chains:
            chain.end()
        launch((), qkv_chains)
    for _ in range(far - 1):
        hop([out_up])
    for chain in qkv_chains:
        chain.end()
    down = Gather(held(down_weight.T[None], out_up.arrived), steps[0])
    wa = out_up.columns(0, cut, steps[0][far:])
    wb = out_up.columns(cut, out_weight.shape[0] + local_hidden - cut, steps[1][far:])
    rows_in.end()
    x = launch(rows_in.result, qkv_chains)
    for chain in qkv_chains:
        chain.end()
    x = launch(x, [wa, wb])

    mid_row = vectors[:, :local_hidden].reshape(1, -1)
    scale_all = vectors[:, local_hidden:].reshape(-1)
    scale_row = jnp.repeat(scale_all, head_size)[None]
    own_lengths = lax.dynamic_index_in_dim(lengths[:, 0], micro, 0, keepdims=False)
    ends = jnp.cumsum(own_lengths).astype(jnp.int32)

    def spread(value):
        if split == 1:
            return value
        groups = [[m * split + s for s in range(split)] for m in range(micro_count)]
        return lax.all_to_all(value, "tensor", 1, 0, tiled=True, axis_index_groups=groups)

    def collect(value):
        if split == 1:
            return value
        groups = [[m * split + s for s in range(split)] for m in range(micro_count)]
        return lax.all_to_all(value, "tensor", 0, 1, tiled=True, axis_index_groups=groups)

    h1, q, k, v = project(orders, x, norm_gains, qkv_chains, grid_of, factor)
    q, k, v = land((q, k, v), [wa, wb])
    q, k, v = spread(q), spread(k), spread(v)
    more([wa, wb], near - 2)
    q = launch(q, [wa, wb, down])
    part = width // split
    scale_part = lax.dynamic_slice(scale_row, (0, tensor_rank % split * part), (1, part))
    scaled, lse = None, None
    for n in range(parts):
        scaled, lse = attend(q, k, v, scale_part, ends, tensor_count, parts, n, scaled, lse)
        if n == 0:
            scaled = land(scaled, [down])
            more([down], far - 2)
            scaled = launch(scaled, [down])
    scaled = land(scaled, [wa, wb, down])
    down_cut = half_cols + (up_chunk if half_cols % 1024 == 0 else 0)
    wda = down.columns(0, down_cut, steps[0][far:])
    wdb = down.columns(down_cut, local_hidden - down_cut, steps[1][far:])
    rows_cot = Rows(cotangent, micro_count, split)
    scaled = launch(scaled, [wa, wb])
    scaled = land(scaled, [wa, wb])
    scaled = collect(launch(scaled, [wda, wdb, rows_cot]))
    forward = []
    shares = 2 if x.shape[0] % 512 == 0 else 1
    for n in range(shares):
        if n:
            forward[0] = land(forward[0], [wda, wdb])
            more([wda, wdb], near - 2)
            forward[0] = launch(forward[0], [wda, wdb])
        forward = list(
            hidden_forward(orders, scaled, x, norm_gains, mid_row, wa, wb, grid_of, (n, shares), forward)
        )
    unit, h3, hidden, narrow, stat = forward
    if shares == 1:
        narrow = land(narrow, [wda, wdb])
        more([wda, wdb], near - 2)
        narrow = launch(narrow, [wda, wdb])
    unit, h3, hidden, narrow, stat = land([unit, h3, hidden, narrow, stat], [rows_cot, wda, wdb])
    cot = rows_cot.result

    def grad_half(n, a, b, name, turn=False):
        keep, send = weight_grad(tables[n], a, [b], grid_of, n * half_cols, half_cols, name, turn)
        return Scatter(keep, send, steps[n])

    def flush(chains):
        for chain in chains:
            while chain.steps:
                hop([chain])
        return [chain.total for chain in chains]

    cot_held = launch(cot, [wda, wdb])
    d0 = grad_half(0, cot_held, narrow, "grad_down", True)
    cot_held = launch(cot_held, [d0])
    d1 = grad_half(1, cot_held, narrow, "grad_down", True)
    d1.keep, d1.send = land((d1.keep, d1.send), [d0, wda, wdb])
    hidden = launch(hidden, [d1, d0])
    hidden = land(hidden, [d1])
    hidden = launch(hidden, [d1])
    back = feed_back(
        orders, hidden, stat, unit, x, cot, norm_gains, mid_row, scale_row, wda, wdb, wa, wb, grid_of
    )
    dhidden, dresid, dmixed, dattended, gain_sums, mid_sums = land(back, [d0, d1])
    more([d0, d1], near - 2)
    dhidden = launch(dhidden, [d0, d1])
    u0 = grad_half(0, h3, dhidden, "grad_up")
    u0.keep, u0.send = land((u0.keep, u0.send), [d0, d1])
    down_sum = merged([d0, d1])
    dhidden = launch(dhidden, [u0, down_sum])
    u1 = grad_half(1, h3, dhidden, "grad_up")
    u1.keep, u1.send = land((u1.keep, u1.send), [u0, down_sum])
    dmixed = launch(dmixed, [u1] + ([down_sum] if down_sum.steps else []))
    keep, send = weight_grad(
        tables[0], dmixed, [scaled], grid_of, 0, out_weight.shape[0], "grad_out"
    )
    o0 = Scatter(keep, send, steps[0])
    flying = [u1, down_sum] if far > 1 else [u1]
    o0.keep, o0.send = land((o0.keep, o0.send), flying)
    da = launch(spread(dattended), [u0, u1, o0])
    halves, grads, inners = [], [], []
    for n in range(parts):
        *three, inner = attend_back(q, k, v, da, lse, ends, factor, tensor_count, parts, n)
        inners.append(inner)
        if n == 0:
            three = land(three, [u0, u1, o0])
            narrow = launch(narrow, [u0, u1])
            block_out = feed_forward(orders, narrow, unit, x, norm_gains, wda, wdb, grid_of)
            block_out = land(block_out, [u0, u1])
            more([u0, u1], near - 2)
            up_sum = merged([u0, u1])
            rows_out = Rows(block_out, micro_count, split)
            three = [collect(one) for one in three]
            three = launch(three, [up_sum, o0])
            flying = [up_sum, o0]
        else:
            three = land(three, flying)
            flying = [o0]
            three = launch(three, flying)
        keep, send = weight_grad(tables[n % 2], h1, three, grid_of, 0, part_cols, "grad_qkv")
        halves.append(Scatter(keep, send, steps[n % 2]))
        grads += three
        halves[-1].keep, halves[-1].send = land((halves[-1].keep, halves[-1].send), flying)
        if n < parts - 1:
            flying = [halves[0], up_sum, o0, rows_out]
            da = launch(da, flying)
    q_last = halves[-1]
    dresid = launch(dresid, [q_last])
    dresid = land(dresid, [q_last])
    beside = halves + [o0] + ([] if parts > 1 else [rows_out])
    dresid = launch(dresid, beside)
    grad_in, first_sums = input_grad(orders, grads, x, dresid, norm_gains, qkv_chains, grid_of)
    grad_in, first_sums = land((grad_in, first_sums), beside)
    local = heads // split
    if parts == 1:
        head_sums = jnp.sum(inners[0], axis=-1).reshape(-1)
    else:
        shaped = [jnp.sum(one, axis=-1).reshape(tensor_count, -1) for one in inners]
        head_sums = jnp.concatenate(shaped, axis=1).reshape(-1)
    first_head = tensor_rank % split * local
    head_sums = head_sums / lax.dynamic_slice(scale_all, (first_head,), (local,))
    head_all = lax.dynamic_update_slice(jnp.zeros((heads,), F32), head_sums, (first_head,))
    last = jnp.concatenate(
        [jnp.sum(one, axis=0) for one in (first_sums, gain_sums[:8], gain_sums[8:], mid_sums)]
        + [head_all]
    )
    last = Total(last, batch_count, tensor_count)
    rows_back = Rows(grad_in, micro_count, split, 2)
    tail = [last] + halves + ([o0] if o0.steps else [])
    launch((), tail + [rows_back])
    for one in tail:
        one.end()
    if parts > 1:
        halves = [merged(halves)]
    after = ()
    while last.steps:
        tail = [one for one in [last] + halves + [o0] if one.steps]
        launch(after, tail)
        for one in tail:
            one.end()
        after = rows_back.arrived[:1]
    rows_back.end()
    block_out, grad_in = rows_out.result, rows_back.result
    d_totals, u_totals, o_totals, q_totals = (
        flush([down_sum]), flush([up_sum]), flush([o0]), flush(halves)
    )
    down_grad = d_totals[0].T
    up_grad = u_totals[0]
    out_grad = o_totals[0].T
    qkv_grad = q_totals[0]
    vector = last.value
    d_totals, u_totals, o_totals, q_totals = (
        flush([d0, d1]), flush([u0, u1]), flush([o0]), flush(halves)
    )
    gains_sum = vector[: 3 * width].reshape(3, width)
    mid_own = lax.dynamic_slice(vector, (3 * width + tensor_rank * local_hidden,), (local_hidden,))
    scale_own = lax.dynamic_slice(
        vector, (3 * width + tensor_count * local_hidden + tensor_rank * local_heads,), (local_heads,)
    )
    return (
        block_out,
        grad_in,
        gains_sum,
        qkv_grad,
        scale_own,
        out_grad,
        up_grad,
        mid_own,
        down_grad,
    )


def solution(mesh):
    in_specs = (
        P(None, ("batch", "tensor"), None),
        P(None, "batch", None),
        P(),
        P(None, "batch", "tensor"),
        P("tensor"),
        P("tensor", "batch"),
        P("batch", "tensor"),
        P("tensor"),
        P("tensor", "batch"),
        P(None, ("batch", "tensor"), None),
    )
    out_specs = (
        P(None, ("batch", "tensor"), None),
        P(None, ("batch", "tensor"), None),
        P(),
        P(None, "batch", "tensor"),
        P("tensor"),
        P("tensor", "batch"),
        P("batch", "tensor"),
        P("tensor"),
        P("tensor", "batch"),
    )
    return jax.shard_map(body, mesh=mesh, in_specs=in_specs, out_specs=out_specs, check_vma=False)
```

```python
import functools
import math

import jax
import jax.numpy as jnp
from jax import lax
from jax.experimental import pallas as pl
from jax.experimental.pallas import tpu as pltpu
from jax.sharding import PartitionSpec as P

eps = 1e-05
SEQ_MOST = 512
F32 = jnp.float32
BF = jnp.bfloat16
ALL = ("batch", "tensor")
GELU_C = math.sqrt(2.0 / math.pi)
GELU_A = 0.044715
STEP = 256


def cost(us):
    return pl.CostEstimate(flops=int(us * 1e9), transcendentals=0, bytes_accessed=1 << 20)


def dotf(a, b, ca, cb):
    return lax.dot_general(a, b, (((ca,), (cb,)), ((), ())), preferred_element_type=F32)


def row_loop(rows, step, fn):
    def one(i, carry):
        fn(pl.multiple_of(i * step, step))
        return carry

    lax.fori_loop(0, rows // step, one, 0)


def normalize(values):
    centred = values - jnp.mean(values, axis=-1, keepdims=True)
    factor = lax.rsqrt(jnp.mean(centred * centred, axis=-1, keepdims=True) + eps)
    return (centred * factor, factor)


def norm_back(unit, factor, grad):
    return factor * (
        grad
        - jnp.mean(grad, axis=-1, keepdims=True)
        - unit * jnp.mean(grad * unit, axis=-1, keepdims=True)
    )


def fold8(values):
    rows, width = values.shape
    return jnp.sum(values.reshape(rows // 8, 8, width), axis=0)


def bits_of(count):
    return count.bit_length() - 1


def gather_steps(batch_count, tensor_count, tensor_first):
    tensor = [("tensor", 1 << k) for k in range(bits_of(tensor_count))]
    plane = [("batch", 2)]
    far = [("batch", 1 << k) for k in reversed(range(2, bits_of(batch_count)))]
    return far + (tensor + plane if tensor_first else plane + tensor) + [("batch", 1)]


def place_table(steps, batch_count, tensor_count):
    batch = jnp.arange(batch_count * tensor_count, dtype=jnp.int32) // tensor_count
    tensor = jnp.arange(batch_count * tensor_count, dtype=jnp.int32) % tensor_count
    batch = jnp.bitwise_xor(batch, lax.axis_index("batch"))
    tensor = jnp.bitwise_xor(tensor, lax.axis_index("tensor"))
    place = jnp.zeros_like(batch)
    for k, (axis, flip) in enumerate(steps):
        apart = (jnp.bitwise_and(batch if axis == "batch" else tensor, flip) != 0).astype(jnp.int32)
        place = place + apart * (1 << k)
    return place


def swap(value, axis, flip):
    count = lax.axis_size(axis)
    return lax.ppermute(value, axis, [(i, i ^ flip) for i in range(count)])


def held(value, after):
    return lax.optimization_barrier((value, after))[0]


class Gather:
    def __init__(self, buffer, steps):
        self.own, self.steps, self.parts = buffer, list(steps), None

    def outgoing(self):
        return self.arrived if len(self.steps) == 1 else self.own

    def go(self, value):
        step = self.steps.pop(0)
        self.arrived = swap(value, *step)
        if not self.steps:
            self.parts[1] = value
        else:
            self.own = value
            if len(self.steps) == 1:
                self.parts = [value, None, swap(value, *self.steps[0]), None]

    def end(self):
        if self.parts is None:
            self.own = jnp.concatenate([self.own, self.arrived], axis=0)
        elif not self.steps:
            self.parts[3] = self.arrived

    def columns(self, start, count, steps):
        return Gather(self.own[..., start : start + count], steps)


class Scatter:
    def __init__(self, keep, send, steps):
        self.keep, self.send, self.steps = keep, send, list(reversed(steps))

    def outgoing(self):
        return (self.send, self.keep)

    def go(self, value):
        send, self.keep = value
        self.arrived = swap(send, *self.steps.pop(0))

    def end(self):
        keep, arrived = self.keep, self.arrived
        half = keep.shape[0] // 2
        if self.steps:
            self.send = (keep[half:].astype(F32) + arrived[half:].astype(F32)).astype(BF)
            self.keep = (keep[:half].astype(F32) + arrived[:half].astype(F32)).astype(BF)
        else:
            self.total = keep[0].astype(F32) + arrived[0].astype(F32)


def merged(chains):
    keep = jnp.concatenate([chain.keep for chain in chains], axis=-1)
    send = jnp.concatenate([chain.send for chain in chains], axis=-1)
    return Scatter(keep, send, list(reversed(chains[0].steps)))


class Total:
    def __init__(self, value, batch_count, tensor_count):
        self.value, self.grid_of = value, (batch_count, tensor_count)
        bits = [(flip, 0) for flip in (1 << k for k in range(2, bits_of(batch_count)))]
        plane = [(2, 0)] + [(0, 1 << k) for k in range(bits_of(tensor_count))]
        self.steps = [[(1, 0)]]
        for group in (plane, bits):
            if len(group) <= 2:
                spans = [(0, 0)]
                for flip in group:
                    spans += [(one[0] ^ flip[0], one[1] ^ flip[1]) for one in spans]
                self.steps.append(spans[1:])
            else:
                self.steps += [[flip] for flip in group]

    def outgoing(self):
        return self.value

    def go(self, value):
        batch_count, tensor_count = self.grid_of
        self.value, self.arrived = value, []
        for batch, tensor in self.steps.pop(0):
            pairs = [
                (b * tensor_count + t, (b ^ batch) * tensor_count + (t ^ tensor))
                for b in range(batch_count)
                for t in range(tensor_count)
            ]
            self.arrived.append(lax.ppermute(value, ALL, pairs))

    def end(self):
        for one in self.arrived:
            self.value = self.value + one


class Rows:
    def __init__(self, value, micro_count, split, cuts=1):
        self.value, self.micro_count, self.split, self.cuts = value, micro_count, split, cuts
        self.taken = value.ndim == 3
        self.steps = [None]
        self.rank = lax.axis_index("tensor")

    def pieces(self):
        if self.taken:
            return self.value
        return self.value.reshape(self.micro_count, -1, self.value.shape[1])

    def outgoing(self):
        if self.split > 1:
            return []
        sent = []
        for flip in range(1, self.micro_count):
            one = lax.dynamic_index_in_dim(self.pieces(), lax.bitwise_xor(self.rank, flip), 0)
            sent += [one[:, n * (one.shape[1] // self.cuts) :][:, : one.shape[1] // self.cuts] for n in range(self.cuts)]
        return sent

    def go(self, value):
        self.steps = []
        if self.split == 1:
            self.arrived = [
                swap(one, "tensor", n // self.cuts + 1) for n, one in enumerate(value)
            ]
        else:
            self.arrived = [
                lax.all_gather(self.value, "tensor", axis=1 if self.taken else 0, tiled=True)
            ]

    def end(self):
        if self.split == 1:
            pieces = self.pieces()
            out = lax.dynamic_update_slice(
                jnp.zeros_like(pieces),
                lax.dynamic_index_in_dim(pieces, self.rank, 0),
                (self.rank, 0, 0),
            )
            for n, one in enumerate(self.arrived):
                other = lax.bitwise_xor(self.rank, n // self.cuts + 1)
                out = lax.dynamic_update_slice(
                    out, one, (other, n % self.cuts * one.shape[1], 0)
                )
            self.result = out.reshape(-1, out.shape[2]) if self.taken else out
            return
        whole = self.arrived[0]
        width = whole.shape[-1]
        if self.taken:
            rows = self.value.shape[0] * self.value.shape[1]
            start = (self.rank // self.split, self.rank % self.split * rows, 0)
            self.result = lax.dynamic_slice(whole, start, (1, rows, width))[0]
        else:
            own = self.value.shape[0] // self.micro_count
            whole = whole.reshape(self.micro_count, -1, width)
            start = (0, self.rank * own, 0)
            self.result = lax.dynamic_slice(whole, start, (self.micro_count, own, width))


def launch(inputs, chains):
    inputs, values = lax.optimization_barrier((inputs, [chain.outgoing() for chain in chains]))
    for chain, value in zip(chains, values):
        chain.go(value)
    return inputs


def land(inputs, chains):
    inputs, values = lax.optimization_barrier((inputs, [chain.arrived for chain in chains]))
    for chain, value in zip(chains, values):
        chain.arrived = value
        chain.end()
    return inputs


def hop(chains, after=()):
    launch(after, chains)
    for chain in chains:
        chain.end()


def columns(parts, order_ref, batch_count, tensor_count, t, start, count, lead=None):
    for first, width, which, w_ref in parts:
        if first <= start < first + width:
            break
    pieces = []
    for b in range(batch_count):
        p = order_ref[(which * batch_count + b) * tensor_count + t]
        here = pl.ds(start - first, count)
        pieces.append(w_ref[p, :, here] if lead is None else w_ref[p, lead, :, here])
    return jnp.concatenate(pieces, axis=0)


def weights(*refs):
    out, first = [], 0
    for n, ref in enumerate(refs):
        out.append((first, ref.shape[-1], n % 2, ref))
        first += ref.shape[-1]
    return out


HBM = pl.BlockSpec(memory_space=pltpu.HBM)


def whole(chain):
    part = chain.parts[0].shape
    return pltpu.VMEM((4 * part[0],) + part[1:], BF)


def in_hbm(*values):
    return [pltpu.with_memory_space_constraint(value, pltpu.HBM) for value in values]


def parts_of(chains):
    return in_hbm(*[part for chain in chains for part in chain.parts])


def load_parts(refs, w, sem):
    count = w.shape[0] // 4
    for n in range(4):
        pltpu.make_async_copy(refs[n], w.at[pl.ds(n * count, count)], sem).start()


def wait_whole(w, sem):
    pltpu.make_async_copy(w, w, sem).wait()


def qkv_kernel(grid_of, factor, count, order_ref, x_ref, gain_ref, *refs):
    batch_count, tensor_count = grid_of
    w_hbm, refs = refs[: 4 * count], refs[4 * count :]
    turned_ref, q_ref, k_ref, v_ref, h1_ref = refs[:5]
    w_refs, sem = refs[5:-1], refs[-1]
    first = pl.program_id(0) == 0

    @pl.when(first)
    def _():
        for n in range(count):
            load_parts(w_hbm[4 * n : 4 * n + 4], w_refs[n], sem.at[n])

    def chunk(r):
        here = pl.ds(r, STEP)
        unit, _ = normalize(x_ref[here, :].astype(F32))
        h1_ref[here, :] = (unit * gain_ref[0:1, :]).astype(BF)

    row_loop(x_ref.shape[0], STEP, chunk)
    turned_ref[...] = h1_ref[...].T

    @pl.when(first)
    def _():
        for n in range(count):
            wait_whole(w_refs[n], sem.at[n])

    parts = weights(*w_refs)
    cols = sum(part[1] for part in parts)
    for c, out in enumerate((q_ref, k_ref, v_ref)):
        for t in range(tensor_count):
            for start, width, _, _ in parts:
                w = columns(parts, order_ref, batch_count, tensor_count, t, start, width, lead=c)
                value = dotf(h1_ref[...], w, 1, 0).astype(BF)
                here = slice(t * cols + start, t * cols + start + width)
                out[:, here] = value * BF(factor) if c == 0 else value


def project(orders, x, gains, chains, grid_of, factor):
    rows, width = x.shape
    block = min(256, rows)
    row = pl.BlockSpec((block, width), lambda i, e: (i, 0))
    return pl.pallas_call(
        functools.partial(qkv_kernel, grid_of, factor, len(chains)),
        grid_spec=pltpu.PrefetchScalarGridSpec(
            num_scalar_prefetch=1,
            grid=(rows // block,),
            in_specs=[row, pl.BlockSpec((3, width), lambda i, e: (0, 0))]
            + [HBM] * (4 * len(chains)),
            out_specs=[pl.BlockSpec((width, block), lambda i, e: (0, i))] + [row] * 3,
            scratch_shapes=[pltpu.VMEM((block, width), BF)]
            + [whole(chain) for chain in chains]
            + [pltpu.SemaphoreType.DMA((len(chains),))],
        ),
        out_shape=[pltpu.HBM((width, rows), BF)]
        + [pltpu.HBM((rows, width), BF)] * 3,
        compiler_params=pltpu.CompilerParams(vmem_limit_bytes=24 << 20),
        cost_estimate=cost(13),
        name="project",
    )(orders, *in_hbm(x), gains, *parts_of(chains))


def spans(rows, block):
    return [
        (first, max(0, (first - SEQ_MOST + 1) // block * block), first + block)
        for first in range(0, rows, block)
    ]


def fill_bias(ends_ref, bias, parts, block):
    for (first, low, high), ref in zip(parts, bias):
        shape = (high - low, block)
        keys = low + lax.broadcasted_iota(jnp.int32, shape, 0)
        queries = first + lax.broadcasted_iota(jnp.int32, shape, 1)
        start = jnp.zeros(shape, jnp.int32)
        for n in range(ends_ref.shape[0]):
            end = ends_ref[n]
            start = jnp.where(queries >= end, end, start)
        ref[...] = jnp.where((keys <= queries) & (keys >= start), 0.0, -1e30).astype(F32)


def attend_kernel(rows, block, ends_ref, q_ref, k_ref, v_ref, scale_ref, o_ref, lse_ref, *bias):
    parts = spans(rows, block)

    @pl.when(pl.program_id(0) == 0)
    def _():
        fill_bias(ends_ref, bias, parts, block)

    lower = lax.broadcasted_iota(jnp.int32, (1, 128), 1) < 64
    for n, (first, low, high) in enumerate(parts):
        q = q_ref[pl.ds(first, block), :]
        heads = []
        for h in range(2):
            own = jnp.where(lower if h == 0 else ~lower, q, jnp.zeros_like(q))
            s = dotf(k_ref[pl.ds(low, high - low), :], own, 1, 1) + bias[n][...]
            most = jnp.max(s, axis=0, keepdims=True)
            p = jnp.exp(s - most)
            total = jnp.sum(p, axis=0, keepdims=True)
            probs = (p * (1.0 / total)).astype(BF)
            lse_ref[0, pl.ds(h, 1), pl.ds(first, block)] = most + jnp.log(total)
            heads.append(dotf(probs, v_ref[pl.ds(low, high - low), :], 0, 0))
        out = jnp.where(lower, heads[0], heads[1]) * scale_ref[...]
        o_ref[pl.ds(first, block), :] = out.astype(BF)


def attend_back_kernel(
    rows, block, factor, ends_ref, q_ref, k_ref, v_ref, da_ref, lse_ref,
    dq_ref, dk_ref, dv_ref, inner_ref, dk_acc, dv_acc, *bias
):
    parts = spans(rows, block)

    @pl.when(pl.program_id(0) == 0)
    def _():
        fill_bias(ends_ref, bias, parts, block)

    lower = lax.broadcasted_iota(jnp.int32, (1, 128), 1) < 64
    dk_acc[...] = jnp.zeros_like(dk_acc)
    dv_acc[...] = jnp.zeros_like(dv_acc)
    for n, (first, low, high) in enumerate(parts):
        here = pl.ds(first, block)
        keys = pl.ds(low, high - low)
        q, da, k, v = q_ref[here, :], da_ref[here, :], k_ref[keys, :], v_ref[keys, :]
        heads = []
        for h in range(2):
            mask = lower if h == 0 else ~lower
            q_own = jnp.where(mask, q, jnp.zeros_like(q))
            da_own = jnp.where(mask, da, jnp.zeros_like(da))
            s = dotf(k, q_own, 1, 1) + bias[n][...]
            p = jnp.exp(s - lse_ref[0, pl.ds(h, 1), here])
            product = p * dotf(v, da_own, 1, 1)
            inner = jnp.sum(product, axis=0, keepdims=True)
            inner_ref[0, pl.ds(h, 1), here] = inner
            ds = (product - p * inner).astype(BF)
            dv_acc[keys, :] += dotf(p.astype(BF), da_own, 1, 0)
            dk_acc[keys, :] += dotf(ds, q_own, 1, 0)
            heads.append(dotf(ds, k, 0, 0))
        dq_ref[here, :] = (jnp.where(lower, heads[0], heads[1]) * factor).astype(BF)
    dk_ref[...] = dk_acc[...].astype(BF)
    dv_ref[...] = dv_acc[...].astype(BF)


def bias_shapes(rows, block):
    return [pltpu.VMEM((high - low, block), F32) for _, low, high in spans(rows, block)]


def pair_of(pairs, tensor_count, parts, n):
    if parts == 1:
        return pairs, lambda i: i
    per_tensor = pairs // tensor_count
    per = per_tensor // parts
    return pairs // parts, lambda i: i // per * per_tensor + n * per + i % per


def attend(q, k, v, scale_row, ends, tensor_count, parts, n, before_out, before_lse):
    rows, width = q.shape
    block = min(256, rows)
    pairs = width // 128
    steps, pair = pair_of(pairs, tensor_count, parts, n)
    col = pl.BlockSpec((rows, 128), lambda i, e: (0, pair(i)))
    earlier = [] if before_out is None else [before_out, before_lse]
    count = len(earlier)

    def kernel(ends_ref, q_ref, k_ref, v_ref, scale_ref, *refs):
        attend_kernel(rows, block, ends_ref, q_ref, k_ref, v_ref, scale_ref, *refs[count:])

    return pl.pallas_call(
        kernel,
        grid_spec=pltpu.PrefetchScalarGridSpec(
            num_scalar_prefetch=1,
            grid=(steps,),
            in_specs=[col, col, col, pl.BlockSpec((1, 128), lambda i, e: (0, pair(i)))]
            + [HBM] * count,
            out_specs=[col, pl.BlockSpec((1, 2, rows), lambda i, e: (pair(i), 0, 0))],
            scratch_shapes=bias_shapes(rows, block),
        ),
        out_shape=[
            pltpu.HBM((rows, width), BF),
            pltpu.HBM((pairs, 2, rows), F32),
        ],
        input_output_aliases={5 + j: j for j in range(count)},
        compiler_params=pltpu.CompilerParams(vmem_limit_bytes=32 << 20),
        cost_estimate=cost(24 / parts),
        name="attend",
    )(ends, *in_hbm(q, k, v), scale_row, *earlier)


def attend_back(q, k, v, da, lse, ends, factor, tensor_count, parts, n):
    rows, width = q.shape
    block = min(256, rows)
    pairs = width // 128
    steps, pair = pair_of(pairs, tensor_count, parts, n)
    col = pl.BlockSpec((rows, 128), lambda i, e: (0, pair(i)))
    out_col = pl.BlockSpec((rows, 128), lambda i, e: (0, i))
    out = pltpu.HBM((rows, width // parts), BF)
    return pl.pallas_call(
        functools.partial(attend_back_kernel, rows, block, factor),
        grid_spec=pltpu.PrefetchScalarGridSpec(
            num_scalar_prefetch=1,
            grid=(steps,),
            in_specs=[col] * 4 + [pl.BlockSpec((1, 2, rows), lambda i, e: (pair(i), 0, 0))],
            out_specs=[out_col] * 3 + [pl.BlockSpec((1, 2, rows), lambda i, e: (i, 0, 0))],
            scratch_shapes=[pltpu.VMEM((rows, 128), F32)] * 2 + bias_shapes(rows, block),
        ),
        out_shape=[out, out, out, pltpu.HBM((steps, 2, rows), F32)],
        compiler_params=pltpu.CompilerParams(vmem_limit_bytes=40 << 20),
        cost_estimate=cost(42 / parts),
        name="attend_back",
    )(ends, *in_hbm(q, k, v, da), lse)


def put_stats(ref, here, values):
    lane = lax.broadcasted_iota(jnp.int32, (1, 128), 1)
    out = values[-1]
    for n in reversed(range(len(values) - 1)):
        out = jnp.where(lane < 16 * (n + 1), values[n], out)
    ref[here, :] = jnp.broadcast_to(out, (values[0].shape[0], 128))


def hidden_kernel(
    grid_of, order_ref, scaled_ref, x_ref, gain_ref, mid_ref, a0, a1, a2, a3, b0, b1, b2, b3,
    unit_ref, turned_ref, hidden_ref, narrow_ref, stat_ref, act, norm_stat, wide, h3_ref, wa, wb, sem
):
    batch_count, tensor_count = grid_of
    block, width = x_ref.shape
    total = hidden_ref.shape[1]
    up_cols = total // tensor_count
    out_cols = width // tensor_count
    get = functools.partial(columns, weights(wa, wb), order_ref, batch_count, tensor_count)
    first = pl.program_id(0) == 0

    @pl.when(first)
    def _():
        load_parts((a0, a1, a2, a3), wa, sem.at[0])
        load_parts((b0, b1, b2, b3), wb, sem.at[1])
        wait_whole(wa, sem.at[0])

    mixed = None
    for t in range(tensor_count):
        part = dotf(scaled_ref[:, t * out_cols : (t + 1) * out_cols], get(t, 0, out_cols), 1, 1)
        mixed = part if mixed is None else mixed + part
    wide[...] = mixed

    def norms(r):
        here = pl.ds(r, STEP)
        unit, factor = normalize(wide[here, :])
        unit_ref[here, :] = unit
        resid = x_ref[here, :].astype(F32) + unit * gain_ref[1:2, :]
        mean3 = jnp.mean(resid, axis=-1, keepdims=True)
        centred = resid - mean3
        factor3 = lax.rsqrt(jnp.mean(centred * centred, axis=-1, keepdims=True) + eps)
        h3_ref[here, :] = (centred * factor3 * gain_ref[2:3, :]).astype(BF)
        put_stats(norm_stat, here, [factor, mean3, factor3])

    row_loop(block, STEP, norms)
    turned_ref[...] = h3_ref[...].T

    @pl.when(first)
    def _():
        wait_whole(wb, sem.at[1])

    chunk = min(256, up_cols // 2)
    sums = jnp.zeros((block, 128), F32)
    squares = jnp.zeros((block, 128), F32)
    for c in range(total // chunk):
        t, off = divmod(c * chunk, up_cols)
        h = dotf(h3_ref[...], get(t, out_cols + off, chunk), 1, 0)
        hidden_ref[:, c * chunk : (c + 1) * chunk] = h
        half = 0.5 * jnp.tanh(h * (GELU_C + (GELU_C * GELU_A) * (h * h))) + 0.5
        a = h * half
        act[:, c * chunk : (c + 1) * chunk] = a
        for j in range(chunk // 128):
            piece = a[:, j * 128 : (j + 1) * 128]
            sums += piece
            squares += piece * piece
    mean = jnp.sum(sums, axis=1, keepdims=True) / total
    spread = jnp.sum(squares, axis=1, keepdims=True) / total - mean * mean
    scale = lax.rsqrt(spread + eps)
    before = norm_stat[...]
    put_stats(stat_ref, slice(None), [mean, scale, before[:, 0:1], before[:, 16:17], before[:, 32:33]])

    def narrow(r):
        here = pl.ds(r, STEP)
        m = stat_ref[here, 0:1]
        s = stat_ref[here, 16:17]
        narrow_ref[here, :] = ((act[here, :] - m) * s * mid_ref[...]).astype(BF)

    row_loop(block, STEP, narrow)


def hidden_forward(orders, scaled, x, gains, mid_row, wa, wb, grid_of, share, earlier):
    rows, width = x.shape
    block = min(256, rows)
    total = mid_row.shape[1]
    blocks = rows // block // share[1]
    first = share[0] * blocks
    row = pl.BlockSpec((block, width), lambda i, e: (first + i, 0))
    wide = pl.BlockSpec((block, total), lambda i, e: (first + i, 0))

    def kernel(order_ref, *refs):
        hidden_kernel(grid_of, order_ref, *refs[:12], *refs[12 + len(earlier) :])

    return pl.pallas_call(
        kernel,
        grid_spec=pltpu.PrefetchScalarGridSpec(
            num_scalar_prefetch=1,
            grid=(blocks,),
            in_specs=[
                row,
                row,
                pl.BlockSpec((3, width), lambda i, e: (0, 0)),
                pl.BlockSpec((1, total), lambda i, e: (0, 0)),
            ]
            + [HBM] * (8 + len(earlier)),
            out_specs=[row, pl.BlockSpec((width, block), lambda i, e: (0, first + i)), wide, wide]
            + [pl.BlockSpec((block, 128), lambda i, e: (first + i, 0))],
            scratch_shapes=[
                pltpu.VMEM((block, total), F32),
                pltpu.VMEM((block, 128), F32),
                pltpu.VMEM((block, width), F32),
                pltpu.VMEM((block, width), BF),
                whole(wa),
                whole(wb),
                pltpu.SemaphoreType.DMA((2,)),
            ],
        ),
        out_shape=[
            pltpu.HBM((rows, width), F32),
            pltpu.HBM((width, rows), BF),
            pltpu.HBM((rows, total), F32),
            pltpu.HBM((rows, total), BF),
            pltpu.HBM((rows, 128), F32),
        ],
        input_output_aliases={13 + n: n for n in range(len(earlier))},
        compiler_params=pltpu.CompilerParams(vmem_limit_bytes=44 << 20),
        cost_estimate=cost(30 / share[1]),
        name="hidden_forward",
    )(orders, *in_hbm(scaled, x), gains, mid_row, *parts_of((wa, wb)), *earlier)


def feed_kernel(grid_of, order_ref, narrow_ref, unit_ref, x_ref, gain_ref, a0, a1, a2, a3, b0, b1, b2, b3, out_ref, wa, wb, sem):
    batch_count, tensor_count = grid_of
    up_cols = narrow_ref.shape[1] // tensor_count
    parts = weights(wa, wb)

    @pl.when(pl.program_id(0) == 0)
    def _():
        load_parts((a0, a1, a2, a3), wa, sem.at[0])
        load_parts((b0, b1, b2, b3), wb, sem.at[1])
        wait_whole(wa, sem.at[0])
        wait_whole(wb, sem.at[1])

    out = x_ref[...].astype(F32) + unit_ref[...] * gain_ref[1:2, :]
    for start, width, _, _ in parts:
        for t in range(tensor_count):
            w = columns(parts, order_ref, batch_count, tensor_count, t, start, width)
            off = t * up_cols + start
            out += dotf(narrow_ref[:, off : off + width], w, 1, 1)
    out_ref[...] = out.astype(BF)


def feed_forward(orders, narrow, unit, x, gains, wa, wb, grid_of):
    rows, width = x.shape
    block = min(256, rows)
    total = narrow.shape[1]
    row = pl.BlockSpec((block, width), lambda i, e: (i, 0))
    return pl.pallas_call(
        functools.partial(feed_kernel, grid_of),
        grid_spec=pltpu.PrefetchScalarGridSpec(
            num_scalar_prefetch=1,
            grid=(rows // block,),
            in_specs=[pl.BlockSpec((block, total), lambda i, e: (i, 0)), row, row]
            + [pl.BlockSpec((3, width), lambda i, e: (0, 0))]
            + [HBM] * 8,
            out_specs=row,
            scratch_shapes=[whole(wa), whole(wb), pltpu.SemaphoreType.DMA((2,))],
        ),
        out_shape=pltpu.HBM((rows, width), BF),
        compiler_params=pltpu.CompilerParams(vmem_limit_bytes=28 << 20),
        cost_estimate=cost(14),
        name="feed_forward",
    )(orders, *in_hbm(narrow, unit, x), gains, *parts_of((wa, wb)))


def back_kernel(
    grid_of, order_ref, hidden_ref, stat_ref, unit_ref, x_ref, cot_ref, gain_ref, mid_ref,
    scale_ref, da0, da1, da2, da3, db0, db1, db2, db3, a0, a1, a2, a3, b0, b1, b2, b3, dhidden_ref, dresid_ref, turned_ref, dattended_ref,
    gains_ref, dmid_ref, grad, unit_s, slope_s, wide, dmixed_ref, wda, wdb, wa, wb, sem
):
    batch_count, tensor_count = grid_of
    block, width = x_ref.shape
    total = hidden_ref.shape[1]
    up_cols = total // tensor_count
    out_cols = width // tensor_count
    get = functools.partial(columns, weights(wa, wb), order_ref, batch_count, tensor_count)
    get_down = functools.partial(columns, weights(wda, wdb), order_ref, batch_count, tensor_count)
    first = pl.program_id(0) == 0

    @pl.when(first)
    def _():
        load_parts((da0, da1, da2, da3), wda, sem.at[0])
        load_parts((db0, db1, db2, db3), wdb, sem.at[1])
        load_parts((a0, a1, a2, a3), wa, sem.at[2])
        load_parts((b0, b1, b2, b3), wb, sem.at[3])
        gains_ref[...] = jnp.zeros_like(gains_ref)
        dmid_ref[...] = jnp.zeros_like(dmid_ref)
        wait_whole(wda, sem.at[0])
        wait_whole(wdb, sem.at[1])

    chunk = min(256, up_cols // 2)
    mean = stat_ref[:, 0:1]
    scale = stat_ref[:, 16:17]
    back_sum = jnp.zeros((block, 128), F32)
    back_inner = jnp.zeros((block, 128), F32)
    for c in range(total // chunk):
        t, off = divmod(c * chunk, up_cols)
        here = slice(c * chunk, (c + 1) * chunk)
        dn = dotf(cot_ref[...], get_down(t, off, chunk), 1, 0)
        h = hidden_ref[:, here]
        square = h * h
        half = 0.5 * jnp.tanh(h * (GELU_C + (GELU_C * GELU_A) * square)) + 0.5
        a = h * half
        slope_s[:, here] = half + a * (1.0 - half) * (
            2.0 * GELU_C + (6.0 * GELU_C * GELU_A) * square
        )
        unit = (a - mean) * scale
        unit_s[:, here] = unit
        dmid_ref[:, here] += fold8(dn * unit)
        g = dn * mid_ref[:, here]
        grad[:, here] = g
        inner = g * unit
        for j in range(chunk // 128):
            back_sum += g[:, j * 128 : (j + 1) * 128]
            back_inner += inner[:, j * 128 : (j + 1) * 128]
    sum_col = jnp.sum(back_sum, axis=1, keepdims=True) / total
    inner_col = jnp.sum(back_inner, axis=1, keepdims=True) / total

    @pl.when(first)
    def _():
        wait_whole(wa, sem.at[2])
        wait_whole(wb, sem.at[3])

    dh3 = None
    for c in range(total // chunk):
        t, off = divmod(c * chunk, up_cols)
        here = slice(c * chunk, (c + 1) * chunk)
        act_grad = scale * (grad[:, here] - sum_col - unit_s[:, here] * inner_col)
        dhidden = (act_grad * slope_s[:, here]).astype(BF)
        dhidden_ref[:, here] = dhidden
        part = dotf(dhidden, get(t, out_cols + off, chunk), 1, 1)
        dh3 = part if dh3 is None else dh3 + part
    wide[...] = dh3

    def back(r):
        here = pl.ds(r, STEP)
        unit = unit_ref[here, :]
        resid = x_ref[here, :].astype(F32) + unit * gain_ref[1:2, :]
        unit3 = (resid - stat_ref[here, 48:49]) * stat_ref[here, 64:65]
        third = wide[here, :]
        gains_ref[8:16, :] += fold8(third * unit3)
        dresid = cot_ref[here, :].astype(F32) + norm_back(
            unit3, stat_ref[here, 64:65], third * gain_ref[2:3, :]
        )
        dresid_ref[here, :] = dresid
        gains_ref[0:8, :] += fold8(dresid * unit)
        dmixed = norm_back(unit, stat_ref[here, 32:33], dresid * gain_ref[1:2, :])
        dmixed_ref[here, :] = dmixed.astype(BF)

    row_loop(block, STEP, back)
    turned_ref[...] = dmixed_ref[...].T
    for t in range(tensor_count):
        here = slice(t * out_cols, (t + 1) * out_cols)
        dscaled = dotf(dmixed_ref[...], get(t, 0, out_cols), 1, 0)
        dattended_ref[:, here] = (dscaled * scale_ref[:, here]).astype(BF)


def feed_back(orders, hidden, stat, unit, x, cot, gains, mid_row, scale_row, wda, wdb, wa, wb, grid_of):
    rows, width = x.shape
    block = min(256, rows)
    total = mid_row.shape[1]
    row = pl.BlockSpec((block, width), lambda i, e: (i, 0))
    wide = pl.BlockSpec((block, total), lambda i, e: (i, 0))
    return pl.pallas_call(
        functools.partial(back_kernel, grid_of),
        grid_spec=pltpu.PrefetchScalarGridSpec(
            num_scalar_prefetch=1,
            grid=(rows // block,),
            in_specs=[
                wide,
                pl.BlockSpec((block, 128), lambda i, e: (i, 0)),
                row,
                row,
                row,
                pl.BlockSpec((3, width), lambda i, e: (0, 0)),
                pl.BlockSpec((1, total), lambda i, e: (0, 0)),
                pl.BlockSpec((1, width), lambda i, e: (0, 0)),
            ]
            + [HBM] * 16,
            out_specs=[
                wide,
                row,
                pl.BlockSpec((width, block), lambda i, e: (0, i)),
                row,
                pl.BlockSpec((16, width), lambda i, e: (0, 0)),
                pl.BlockSpec((8, total), lambda i, e: (0, 0)),
            ],
            scratch_shapes=[
                pltpu.VMEM((block, total), F32),
                pltpu.VMEM((block, total), F32),
                pltpu.VMEM((block, total), F32),
                pltpu.VMEM((block, width), F32),
                pltpu.VMEM((block, width), BF),
            ]
            + [whole(chain) for chain in (wda, wdb, wa, wb)]
            + [pltpu.SemaphoreType.DMA((4,))],
        ),
        out_shape=[
            pltpu.HBM((rows, total), BF),
            pltpu.HBM((rows, width), F32),
            pltpu.HBM((width, rows), BF),
            pltpu.HBM((rows, width), BF),
            pltpu.HBM((16, width), F32),
            pltpu.HBM((8, total), F32),
        ],
        compiler_params=pltpu.CompilerParams(vmem_limit_bytes=60 << 20),
        cost_estimate=cost(60),
        name="feed_back",
    )(
        orders, *in_hbm(hidden, stat, unit, x, cot), gains, mid_row, scale_row,
        *parts_of((wda, wdb, wa, wb)),
    )


def grad_kernel(grid_of, count, turn, order_ref, a_ref, *refs):
    batch_count, tensor_count = grid_of
    b_refs, keep_ref, send_ref = refs[:count], refs[count], refs[count + 1]
    tensor = pl.program_id(1)
    if turn:
        turned = refs[count + 2]

        @pl.when((pl.program_id(0) == 0) & (tensor == 0))
        def _():
            turned[...] = a_ref[...].T

        a_ref = turned
    half = batch_count * tensor_count // 2
    height = keep_ref.shape[-2]
    second = order_ref[0] >= half
    for c, b_ref in enumerate(b_refs):
        acc = dotf(a_ref[...], b_ref[...], 1, 0).astype(BF)
        for core in range(2):

            @pl.when(second if core else jnp.logical_not(second))
            def _(acc=acc, core=core, c=c):
                for b in range(batch_count):
                    place = lax.bitwise_and(order_ref[b * tensor_count + tensor], half - 1)
                    ref = keep_ref if b % 2 == core else send_ref
                    ref[(place,) if count == 1 else (place, c)] = acc[b * height : (b + 1) * height]


def weight_grad(order, a, bs, grid_of, start, cols, name, turn=False):
    batch_count, tensor_count = grid_of
    width, rows = a.shape[::-1] if turn else a.shape
    part = bs[0].shape[1] // tensor_count
    chunk = min(512, cols)
    per = part // chunk
    height = width // batch_count
    count = len(bs)
    lead = (batch_count * tensor_count // 2,) + (() if count == 1 else (count,)) + (height,)
    zeros = (0,) * len(lead)
    out_spec = pl.BlockSpec(lead + (chunk,), lambda i, t, e: zeros + (i,))
    out = pltpu.HBM(lead + (cols,), BF)
    b_spec = pl.BlockSpec((rows, chunk), lambda i, t, e: (0, t * per + start // chunk + i))
    return pl.pallas_call(
        functools.partial(grad_kernel, grid_of, count, turn),
        grid_spec=pltpu.PrefetchScalarGridSpec(
            num_scalar_prefetch=1,
            grid=(cols // chunk, tensor_count),
            in_specs=[pl.BlockSpec(a.shape, lambda i, t, e: (0, 0))] + [b_spec] * count,
            out_specs=[out_spec, out_spec],
            scratch_shapes=[pltpu.VMEM((width, rows), BF)] if turn else [],
        ),
        out_shape=[out, out],
        compiler_params=pltpu.CompilerParams(vmem_limit_bytes=36 << 20),
        cost_estimate=cost(2.4 * count * cols * tensor_count / 1024),
        name=name,
    )(order, *in_hbm(a, *bs))


def input_kernel(grid_of, count, order_ref, *refs):
    batch_count, tensor_count = grid_of
    grads, refs = refs[: 3 * count], refs[3 * count :]
    x_ref, dresid_ref, gain_ref = refs[:3]
    w_hbm, refs = refs[3 : 3 + 4 * count], refs[3 + 4 * count :]
    out_ref, dgain_ref, wide = refs[:3]
    w_refs, sem = refs[3:-1], refs[-1]
    first = pl.program_id(0) == 0

    @pl.when(first)
    def _():
        for n in range(count):
            load_parts(w_hbm[4 * n : 4 * n + 4], w_refs[n], sem.at[n])
        dgain_ref[...] = jnp.zeros_like(dgain_ref)
        for n in range(count):
            wait_whole(w_refs[n], sem.at[n])

    parts = weights(*w_refs)
    total = None
    for n, (start, width, _, _) in enumerate(parts):
        for c in range(3):
            for t in range(tensor_count):
                w = columns(parts, order_ref, batch_count, tensor_count, t, start, width, lead=c)
                part = dotf(grads[3 * n + c][:, t * width : (t + 1) * width], w, 1, 1)
                total = part if total is None else total + part
    wide[...] = total

    def back(r):
        here = pl.ds(r, STEP)
        unit, factor = normalize(x_ref[here, :].astype(F32))
        grad = wide[here, :]
        dgain_ref[...] += fold8(grad * unit)
        out = dresid_ref[here, :] + norm_back(unit, factor, grad * gain_ref[0:1, :])
        out_ref[here, :] = out.astype(BF)

    row_loop(x_ref.shape[0], STEP, back)


def input_grad(orders, grads, x, dresid, gains, chains, grid_of):
    rows, width = x.shape
    block = min(256, rows)
    row = pl.BlockSpec((block, width), lambda i, e: (i, 0))
    part = pl.BlockSpec((block, width // len(chains)), lambda i, e: (i, 0))
    return pl.pallas_call(
        functools.partial(input_kernel, grid_of, len(chains)),
        grid_spec=pltpu.PrefetchScalarGridSpec(
            num_scalar_prefetch=1,
            grid=(rows // block,),
            in_specs=[part] * len(grads)
            + [row, row, pl.BlockSpec((3, width), lambda i, e: (0, 0))]
            + [HBM] * (4 * len(chains)),
            out_specs=[row, pl.BlockSpec((8, width), lambda i, e: (0, 0))],
            scratch_shapes=[pltpu.VMEM((block, width), F32)]
            + [whole(chain) for chain in chains]
            + [pltpu.SemaphoreType.DMA((len(chains),))],
        ),
        out_shape=[
            pltpu.HBM((rows, width), BF),
            pltpu.HBM((8, width), F32),
        ],
        compiler_params=pltpu.CompilerParams(vmem_limit_bytes=32 << 20),
        cost_estimate=cost(15),
        name="input_grad",
    )(orders, *in_hbm(*grads, x, dresid), gains, *parts_of(chains))


def gather_vector(value, tensor_count):
    rank = lax.axis_index("tensor")
    out = jnp.zeros((tensor_count,) + value.shape, value.dtype)
    for flip in range(tensor_count):
        part = value if flip == 0 else swap(value, "tensor", flip)
        out = lax.dynamic_update_slice(out, part[None], (lax.bitwise_xor(rank, flip), 0))
    return out


def body(
    block_in,
    lengths,
    norm_gains,
    qkv_weight,
    head_scale,
    out_weight,
    up_weight,
    mid_gain,
    down_weight,
    cotangent,
):
    tensor_count = lax.axis_size("tensor")
    batch_count = lax.axis_size("batch")
    tensor_rank = lax.axis_index("tensor")
    batch_rank = lax.axis_index("batch")
    micro_count, own_rows, width = block_in.shape
    if tensor_count % micro_count:
        raise NotImplementedError
    split = tensor_count // micro_count
    micro = tensor_rank // split
    local_heads = head_scale.shape[0]
    heads = local_heads * tensor_count
    head_size = width // heads
    local_hidden = mid_gain.shape[0]
    factor = head_size ** (-0.5)
    grid_of = (batch_count, tensor_count)
    half_cols = local_hidden // 2
    qkv_cols = width // tensor_count
    parts = 2 if qkv_cols % 256 == 0 and split == 1 else 1
    steps = [gather_steps(batch_count, tensor_count, first) for first in (True, False)]
    tables = [place_table(one, batch_count, tensor_count) for one in steps]
    orders = jnp.concatenate(tables)
    far = len(steps[0]) - 2 - bits_of(tensor_count)
    near = bits_of(tensor_count) + 1

    def more(chains, count):
        for _ in range(count):
            hop(chains)

    part_cols = qkv_cols // parts
    up_chunk = min(256, local_hidden // 2)
    out_cols = out_weight.shape[0]
    cut = out_cols + ((local_hidden - out_cols) // 2) // up_chunk * up_chunk
    rows_in = Rows(block_in, micro_count, split)
    qkv = Gather(qkv_weight[None], steps[0])
    launch((), [rows_in, qkv])
    qkv.end()
    for _ in range(far - 1):
        hop([qkv])
    qkv_chains = [
        qkv.columns(n * part_cols, part_cols, steps[n % 2][far:]) for n in range(parts)
    ]
    launch(rows_in.arrived, qkv_chains)
    vectors = gather_vector(
        held(jnp.concatenate([mid_gain, head_scale]), rows_in.arrived), tensor_count
    )
    out_up = Gather(
        held(jnp.concatenate([out_weight.T, up_weight], axis=1)[None], qkv.arrived), steps[0]
    )
    hop([out_up])
    for n in range(near - 1):
        for chain in qkv_chains:
            chain.end()
        launch((), qkv_chains)
    for _ in range(far - 1):
        hop([out_up])
    for chain in qkv_chains:
        chain.end()
    down = Gather(held(down_weight.T[None], out_up.arrived), steps[0])
    wa = out_up.columns(0, cut, steps[0][far:])
    wb = out_up.columns(cut, out_weight.shape[0] + local_hidden - cut, steps[1][far:])
    rows_in.end()
    x = launch(rows_in.result, qkv_chains)
    for chain in qkv_chains:
        chain.end()
    x = launch(x, [wa, wb])

    mid_row = vectors[:, :local_hidden].reshape(1, -1)
    scale_all = vectors[:, local_hidden:].reshape(-1)
    scale_row = jnp.repeat(scale_all, head_size)[None]
    own_lengths = lax.dynamic_index_in_dim(lengths[:, 0], micro, 0, keepdims=False)
    ends = jnp.cumsum(own_lengths).astype(jnp.int32)

    def spread(value):
        if split == 1:
            return value
        groups = [[m * split + s for s in range(split)] for m in range(micro_count)]
        return lax.all_to_all(value, "tensor", 1, 0, tiled=True, axis_index_groups=groups)

    def collect(value):
        if split == 1:
            return value
        groups = [[m * split + s for s in range(split)] for m in range(micro_count)]
        return lax.all_to_all(value, "tensor", 0, 1, tiled=True, axis_index_groups=groups)

    h1, q, k, v = project(orders, x, norm_gains, qkv_chains, grid_of, factor)
    q, k, v = land((q, k, v), [wa, wb])
    q, k, v = spread(q), spread(k), spread(v)
    more([wa, wb], near - 2)
    q = launch(q, [wa, wb, down])
    part = width // split
    scale_part = lax.dynamic_slice(scale_row, (0, tensor_rank % split * part), (1, part))
    scaled, lse = None, None
    for n in range(parts):
        scaled, lse = attend(q, k, v, scale_part, ends, tensor_count, parts, n, scaled, lse)
        if n == 0:
            scaled = land(scaled, [down])
            more([down], far - 2)
            scaled = launch(scaled, [down])
    scaled = land(scaled, [wa, wb, down])
    down_cut = half_cols
    wda = down.columns(0, down_cut, steps[0][far:])
    wdb = down.columns(down_cut, local_hidden - down_cut, steps[1][far:])
    rows_cot = Rows(cotangent, micro_count, split)
    scaled = launch(scaled, [wa, wb])
    scaled = land(scaled, [wa, wb])
    scaled = collect(launch(scaled, [wda, wdb, rows_cot]))
    forward = []
    shares = 2 if x.shape[0] % 512 == 0 else 1
    for n in range(shares):
        if n:
            forward[0] = land(forward[0], [wda, wdb])
            more([wda, wdb], near - 2)
            forward[0] = launch(forward[0], [wda, wdb])
        forward = list(
            hidden_forward(orders, scaled, x, norm_gains, mid_row, wa, wb, grid_of, (n, shares), forward)
        )
    unit, h3, hidden, narrow, stat = forward
    if shares == 1:
        narrow = land(narrow, [wda, wdb])
        more([wda, wdb], near - 2)
        narrow = launch(narrow, [wda, wdb])
    unit, h3, hidden, narrow, stat = land([unit, h3, hidden, narrow, stat], [rows_cot, wda])
    cot = rows_cot.result

    def grad_half(n, a, b, name, turn=False):
        keep, send = weight_grad(tables[n], a, [b], grid_of, n * half_cols, half_cols, name, turn)
        return Scatter(keep, send, steps[n])

    def flush(chains):
        for chain in chains:
            while chain.steps:
                hop([chain])
        return [chain.total for chain in chains]

    cot_held = launch(cot, [wda])
    d0 = grad_half(0, cot_held, narrow, "grad_down", True)
    d0.keep, d0.send = land((d0.keep, d0.send), [wdb])
    cot_held = launch(cot_held, [d0, wdb])
    d1 = grad_half(1, cot_held, narrow, "grad_down", True)
    d1.keep, d1.send = land((d1.keep, d1.send), [d0, wda, wdb])
    hidden = launch(hidden, [d1, d0])
    hidden = land(hidden, [d1])
    hidden = launch(hidden, [d1])
    back = feed_back(
        orders, hidden, stat, unit, x, cot, norm_gains, mid_row, scale_row, wda, wdb, wa, wb, grid_of
    )
    dhidden, dresid, dmixed, dattended, gain_sums, mid_sums = land(back, [d0, d1])
    more([d0, d1], near - 2)
    dhidden = launch(dhidden, [d0, d1])
    u0 = grad_half(0, h3, dhidden, "grad_up")
    u0.keep, u0.send = land((u0.keep, u0.send), [d0, d1])
    down_sum = merged([d0, d1])
    dhidden = launch(dhidden, [u0, down_sum])
    u1 = grad_half(1, h3, dhidden, "grad_up")
    u1.keep, u1.send = land((u1.keep, u1.send), [u0, down_sum])
    dmixed = launch(dmixed, [u1])
    keep, send = weight_grad(
        tables[0], dmixed, [scaled], grid_of, 0, out_weight.shape[0], "grad_out"
    )
    o0 = Scatter(keep, send, steps[0])
    o0.keep, o0.send = land((o0.keep, o0.send), [u1])
    flying = [u0, u1, o0] + ([down_sum] if down_sum.steps else [])
    da = launch(spread(dattended), flying)
    halves, grads, inners = [], [], []
    for n in range(parts):
        *three, inner = attend_back(q, k, v, da, lse, ends, factor, tensor_count, parts, n)
        inners.append(inner)
        if n == 0:
            three = land(three, flying)
            narrow = launch(narrow, [u0, u1])
            block_out = feed_forward(orders, narrow, unit, x, norm_gains, wda, wdb, grid_of)
            block_out = land(block_out, [u0, u1])
            more([u0, u1], near - 2)
            up_sum = merged([u0, u1])
            rows_out = Rows(block_out, micro_count, split, 2)
            three = [collect(one) for one in three]
            three = launch(three, [up_sum, o0])
            flying = [up_sum, o0]
        else:
            three = land(three, flying)
            three, first_out = lax.optimization_barrier((three, rows_out.arrived[0]))
            rows_out.arrived[0] = first_out
            flying = [o0]
            three = launch(three, flying)
        keep, send = weight_grad(tables[n % 2], h1, three, grid_of, 0, part_cols, "grad_qkv")
        halves.append(Scatter(keep, send, steps[n % 2]))
        grads += three
        halves[-1].keep, halves[-1].send = land((halves[-1].keep, halves[-1].send), flying)
        if n < parts - 1:
            flying = [halves[0], up_sum, o0]
            da = launch(da, flying + [rows_out])
    q_last = halves[-1]
    if parts > 1:
        q_last.keep, q_last.send, rows_out.arrived = lax.optimization_barrier(
            (q_last.keep, q_last.send, rows_out.arrived)
        )
        rows_out.end()
    dresid = launch(dresid, [q_last])
    dresid = land(dresid, [q_last])
    beside = halves + [o0] + ([] if parts > 1 else [rows_out])
    dresid = launch(dresid, beside)
    grad_in, first_sums = input_grad(orders, grads, x, dresid, norm_gains, qkv_chains, grid_of)
    grad_in, first_sums = land((grad_in, first_sums), beside)
    local = heads // split
    if parts == 1:
        head_sums = jnp.sum(inners[0], axis=-1).reshape(-1)
    else:
        shaped = [jnp.sum(one, axis=-1).reshape(tensor_count, -1) for one in inners]
        head_sums = jnp.concatenate(shaped, axis=1).reshape(-1)
    first_head = tensor_rank % split * local
    head_sums = head_sums / lax.dynamic_slice(scale_all, (first_head,), (local,))
    head_all = lax.dynamic_update_slice(jnp.zeros((heads,), F32), head_sums, (first_head,))
    last = jnp.concatenate(
        [jnp.sum(one, axis=0) for one in (first_sums, gain_sums[:8], gain_sums[8:], mid_sums)]
        + [head_all]
    )
    last = Total(last, batch_count, tensor_count)
    rows_back = Rows(grad_in, micro_count, split, 2)
    tail = [last] + halves + ([o0] if o0.steps else [])
    launch((), tail + [rows_back])
    for one in tail:
        one.end()
    if parts > 1:
        halves = [merged(halves)]
    after = ()
    while last.steps:
        tail = [one for one in [last] + halves + [o0] if one.steps]
        launch(after, tail)
        for one in tail:
            one.end()
    rows_back.end()
    block_out, grad_in = rows_out.result, rows_back.result
    d_totals, u_totals, o_totals, q_totals = (
        flush([down_sum]), flush([up_sum]), flush([o0]), flush(halves)
    )
    down_grad = d_totals[0].T
    up_grad = u_totals[0]
    out_grad = o_totals[0].T
    qkv_grad = q_totals[0]
    vector = last.value
    d_totals, u_totals, o_totals, q_totals = (
        flush([d0, d1]), flush([u0, u1]), flush([o0]), flush(halves)
    )
    gains_sum = vector[: 3 * width].reshape(3, width)
    mid_own = lax.dynamic_slice(vector, (3 * width + tensor_rank * local_hidden,), (local_hidden,))
    scale_own = lax.dynamic_slice(
        vector, (3 * width + tensor_count * local_hidden + tensor_rank * local_heads,), (local_heads,)
    )
    return (
        block_out,
        grad_in,
        gains_sum,
        qkv_grad,
        scale_own,
        out_grad,
        up_grad,
        mid_own,
        down_grad,
    )


def solution(mesh):
    in_specs = (
        P(None, ("batch", "tensor"), None),
        P(None, "batch", None),
        P(),
        P(None, "batch", "tensor"),
        P("tensor"),
        P("tensor", "batch"),
        P("batch", "tensor"),
        P("tensor"),
        P("tensor", "batch"),
        P(None, ("batch", "tensor"), None),
    )
    out_specs = (
        P(None, ("batch", "tensor"), None),
        P(None, ("batch", "tensor"), None),
        P(),
        P(None, "batch", "tensor"),
        P("tensor"),
        P("tensor", "batch"),
        P("batch", "tensor"),
        P("tensor"),
        P("tensor", "batch"),
    )
    return jax.shard_map(body, mesh=mesh, in_specs=in_specs, out_specs=out_specs, check_vma=False)
```

```python
import functools
import math

import jax
import jax.numpy as jnp
from jax import lax
from jax.experimental import pallas as pl
from jax.experimental.pallas import tpu as pltpu
from jax.sharding import PartitionSpec as P

eps = 1e-05
SEQ_MOST = 512
F32 = jnp.float32
BF = jnp.bfloat16
ALL = ("batch", "tensor")
GELU_C = math.sqrt(2.0 / math.pi)
GELU_A = 0.044715
STEP = 256


def cost(us):
    return pl.CostEstimate(flops=int(us * 1e9), transcendentals=0, bytes_accessed=1 << 20)


def dotf(a, b, ca, cb):
    return lax.dot_general(a, b, (((ca,), (cb,)), ((), ())), preferred_element_type=F32)


def row_loop(rows, step, fn):
    def one(i, carry):
        fn(pl.multiple_of(i * step, step))
        return carry

    lax.fori_loop(0, rows // step, one, 0)


def normalize(values):
    centred = values - jnp.mean(values, axis=-1, keepdims=True)
    factor = lax.rsqrt(jnp.mean(centred * centred, axis=-1, keepdims=True) + eps)
    return (centred * factor, factor)


def norm_back(unit, factor, grad):
    return factor * (
        grad
        - jnp.mean(grad, axis=-1, keepdims=True)
        - unit * jnp.mean(grad * unit, axis=-1, keepdims=True)
    )


def fold8(values):
    rows, width = values.shape
    return jnp.sum(values.reshape(rows // 8, 8, width), axis=0)


def bits_of(count):
    return count.bit_length() - 1


def gather_steps(batch_count, tensor_count, tensor_first):
    tensor = [("tensor", 1 << k) for k in range(bits_of(tensor_count))]
    plane = [("batch", 2)]
    far = [("batch", 1 << k) for k in reversed(range(2, bits_of(batch_count)))]
    return far + (tensor + plane if tensor_first else plane + tensor) + [("batch", 1)]


def place_table(steps, batch_count, tensor_count):
    batch = jnp.arange(batch_count * tensor_count, dtype=jnp.int32) // tensor_count
    tensor = jnp.arange(batch_count * tensor_count, dtype=jnp.int32) % tensor_count
    batch = jnp.bitwise_xor(batch, lax.axis_index("batch"))
    tensor = jnp.bitwise_xor(tensor, lax.axis_index("tensor"))
    place = jnp.zeros_like(batch)
    for k, (axis, flip) in enumerate(steps):
        apart = (jnp.bitwise_and(batch if axis == "batch" else tensor, flip) != 0).astype(jnp.int32)
        place = place + apart * (1 << k)
    return place


def swap(value, axis, flip):
    count = lax.axis_size(axis)
    return lax.ppermute(value, axis, [(i, i ^ flip) for i in range(count)])


def held(value, after):
    return lax.optimization_barrier((value, after))[0]


class Gather:
    def __init__(self, buffer, steps):
        self.own, self.steps, self.parts = buffer, list(steps), None

    def outgoing(self):
        return self.arrived if len(self.steps) == 1 else self.own

    def go(self, value):
        step = self.steps.pop(0)
        self.arrived = swap(value, *step)
        if not self.steps:
            self.parts[1] = value
        else:
            self.own = value
            if len(self.steps) == 1:
                self.parts = [value, None, swap(value, *self.steps[0]), None]

    def end(self):
        if self.parts is None:
            self.own = jnp.concatenate([self.own, self.arrived], axis=0)
        elif not self.steps:
            self.parts[3] = self.arrived

    def columns(self, start, count, steps):
        return Gather(self.own[..., start : start + count], steps)


class Scatter:
    def __init__(self, keep, send, steps):
        self.keep, self.send, self.steps = keep, send, list(reversed(steps))

    def outgoing(self):
        return (self.send, self.keep)

    def go(self, value):
        send, self.keep = value
        self.arrived = swap(send, *self.steps.pop(0))

    def end(self):
        keep, arrived = self.keep, self.arrived
        half = keep.shape[0] // 2
        if self.steps:
            self.send = (keep[half:].astype(F32) + arrived[half:].astype(F32)).astype(BF)
            self.keep = (keep[:half].astype(F32) + arrived[:half].astype(F32)).astype(BF)
        else:
            self.total = keep[0].astype(F32) + arrived[0].astype(F32)


def merged(chains):
    keep = jnp.concatenate([chain.keep for chain in chains], axis=-1)
    send = jnp.concatenate([chain.send for chain in chains], axis=-1)
    return Scatter(keep, send, list(reversed(chains[0].steps)))


class Total:
    def __init__(self, value, batch_count, tensor_count):
        self.value, self.grid_of = value, (batch_count, tensor_count)
        bits = [(flip, 0) for flip in (1 << k for k in range(2, bits_of(batch_count)))]
        plane = [(2, 0)] + [(0, 1 << k) for k in range(bits_of(tensor_count))]
        self.steps = [[(1, 0)]]
        for group in (plane, bits):
            if len(group) <= 2:
                spans = [(0, 0)]
                for flip in group:
                    spans += [(one[0] ^ flip[0], one[1] ^ flip[1]) for one in spans]
                self.steps.append(spans[1:])
            else:
                self.steps += [[flip] for flip in group]

    def outgoing(self):
        return self.value

    def go(self, value):
        batch_count, tensor_count = self.grid_of
        self.value, self.arrived = value, []
        for batch, tensor in self.steps.pop(0):
            pairs = [
                (b * tensor_count + t, (b ^ batch) * tensor_count + (t ^ tensor))
                for b in range(batch_count)
                for t in range(tensor_count)
            ]
            self.arrived.append(lax.ppermute(value, ALL, pairs))

    def end(self):
        for one in self.arrived:
            self.value = self.value + one


class Rows:
    def __init__(self, value, micro_count, split, cuts=1):
        self.value, self.micro_count, self.split, self.cuts = value, micro_count, split, cuts
        self.taken = value.ndim == 3
        self.steps = [None]
        self.rank = lax.axis_index("tensor")

    def pieces(self):
        if self.taken:
            return self.value
        return self.value.reshape(self.micro_count, -1, self.value.shape[1])

    def outgoing(self):
        if self.split > 1:
            return []
        sent = []
        for flip in range(1, self.micro_count):
            one = lax.dynamic_index_in_dim(self.pieces(), lax.bitwise_xor(self.rank, flip), 0)
            sent += [one[:, n * (one.shape[1] // self.cuts) :][:, : one.shape[1] // self.cuts] for n in range(self.cuts)]
        return sent

    def go(self, value):
        self.steps = []
        if self.split == 1:
            self.arrived = [
                swap(one, "tensor", n // self.cuts + 1) for n, one in enumerate(value)
            ]
        else:
            self.arrived = [
                lax.all_gather(self.value, "tensor", axis=1 if self.taken else 0, tiled=True)
            ]

    def end(self):
        if self.split == 1:
            pieces = self.pieces()
            out = lax.dynamic_update_slice(
                jnp.zeros_like(pieces),
                lax.dynamic_index_in_dim(pieces, self.rank, 0),
                (self.rank, 0, 0),
            )
            for n, one in enumerate(self.arrived):
                other = lax.bitwise_xor(self.rank, n // self.cuts + 1)
                out = lax.dynamic_update_slice(
                    out, one, (other, n % self.cuts * one.shape[1], 0)
                )
            self.result = out.reshape(-1, out.shape[2]) if self.taken else out
            return
        whole = self.arrived[0]
        width = whole.shape[-1]
        if self.taken:
            rows = self.value.shape[0] * self.value.shape[1]
            start = (self.rank // self.split, self.rank % self.split * rows, 0)
            self.result = lax.dynamic_slice(whole, start, (1, rows, width))[0]
        else:
            own = self.value.shape[0] // self.micro_count
            whole = whole.reshape(self.micro_count, -1, width)
            start = (0, self.rank * own, 0)
            self.result = lax.dynamic_slice(whole, start, (self.micro_count, own, width))


def launch(inputs, chains):
    inputs, values = lax.optimization_barrier((inputs, [chain.outgoing() for chain in chains]))
    for chain, value in zip(chains, values):
        chain.go(value)
    return inputs


def land(inputs, chains):
    inputs, values = lax.optimization_barrier((inputs, [chain.arrived for chain in chains]))
    for chain, value in zip(chains, values):
        chain.arrived = value
        chain.end()
    return inputs


def hop(chains, after=()):
    launch(after, chains)
    for chain in chains:
        chain.end()


def columns(parts, order_ref, batch_count, tensor_count, t, start, count, lead=None):
    for first, width, which, w_ref in parts:
        if first <= start < first + width:
            break
    pieces = []
    for b in range(batch_count):
        p = order_ref[(which * batch_count + b) * tensor_count + t]
        here = pl.ds(start - first, count)
        pieces.append(w_ref[p, :, here] if lead is None else w_ref[p, lead, :, here])
    return jnp.concatenate(pieces, axis=0)


def weights(*refs):
    out, first = [], 0
    for n, ref in enumerate(refs):
        out.append((first, ref.shape[-1], n % 2, ref))
        first += ref.shape[-1]
    return out


HBM = pl.BlockSpec(memory_space=pltpu.HBM)


def whole(chain):
    part = chain.parts[0].shape
    return pltpu.VMEM((4 * part[0],) + part[1:], BF)


def in_hbm(*values):
    return [pltpu.with_memory_space_constraint(value, pltpu.HBM) for value in values]


def parts_of(chains):
    return in_hbm(*[part for chain in chains for part in chain.parts])


def load_parts(refs, w, sem):
    count = w.shape[0] // 4
    for n in range(4):
        pltpu.make_async_copy(refs[n], w.at[pl.ds(n * count, count)], sem).start()


def wait_whole(w, sem):
    pltpu.make_async_copy(w, w, sem).wait()


def qkv_kernel(grid_of, factor, count, order_ref, x_ref, gain_ref, *refs):
    batch_count, tensor_count = grid_of
    w_hbm, refs = refs[: 4 * count], refs[4 * count :]
    turned_ref, q_ref, k_ref, v_ref, h1_ref = refs[:5]
    w_refs, sem = refs[5:-1], refs[-1]
    first = pl.program_id(0) == 0

    @pl.when(first)
    def _():
        for n in range(count):
            load_parts(w_hbm[4 * n : 4 * n + 4], w_refs[n], sem.at[n])

    def chunk(r):
        here = pl.ds(r, STEP)
        unit, _ = normalize(x_ref[here, :].astype(F32))
        h1_ref[here, :] = (unit * gain_ref[0:1, :]).astype(BF)

    row_loop(x_ref.shape[0], STEP, chunk)
    turned_ref[...] = h1_ref[...].T

    parts = weights(*w_refs)
    cols = sum(part[1] for part in parts)
    for n, (start, width, _, _) in enumerate(parts):

        @pl.when(first)
        def _(n=n):
            wait_whole(w_refs[n], sem.at[n])

        for c, out in enumerate((q_ref, k_ref, v_ref)):
            for t in range(tensor_count):
                w = columns(parts, order_ref, batch_count, tensor_count, t, start, width, lead=c)
                value = dotf(h1_ref[...], w, 1, 0).astype(BF)
                here = slice(t * cols + start, t * cols + start + width)
                out[:, here] = value * BF(factor) if c == 0 else value


def project(orders, x, gains, chains, grid_of, factor):
    rows, width = x.shape
    block = min(256, rows)
    row = pl.BlockSpec((block, width), lambda i, e: (i, 0))
    return pl.pallas_call(
        functools.partial(qkv_kernel, grid_of, factor, len(chains)),
        grid_spec=pltpu.PrefetchScalarGridSpec(
            num_scalar_prefetch=1,
            grid=(rows // block,),
            in_specs=[row, pl.BlockSpec((3, width), lambda i, e: (0, 0))]
            + [HBM] * (4 * len(chains)),
            out_specs=[pl.BlockSpec((width, block), lambda i, e: (0, i))] + [row] * 3,
            scratch_shapes=[pltpu.VMEM((block, width), BF)]
            + [whole(chain) for chain in chains]
            + [pltpu.SemaphoreType.DMA((len(chains),))],
        ),
        out_shape=[pltpu.HBM((width, rows), BF)]
        + [pltpu.HBM((rows, width), BF)] * 3,
        compiler_params=pltpu.CompilerParams(vmem_limit_bytes=24 << 20),
        cost_estimate=cost(13),
        name="project",
    )(orders, *in_hbm(x), gains, *parts_of(chains))


def spans(rows, block):
    return [
        (first, max(0, (first - SEQ_MOST + 1) // block * block), first + block)
        for first in range(0, rows, block)
    ]


def fill_bias(ends_ref, bias, parts, block):
    for (first, low, high), ref in zip(parts, bias):
        shape = (high - low, block)
        keys = low + lax.broadcasted_iota(jnp.int32, shape, 0)
        queries = first + lax.broadcasted_iota(jnp.int32, shape, 1)
        start = jnp.zeros(shape, jnp.int32)
        for n in range(ends_ref.shape[0]):
            end = ends_ref[n]
            start = jnp.where(queries >= end, end, start)
        ref[...] = jnp.where((keys <= queries) & (keys >= start), 0.0, -1e30).astype(F32)


def attend_kernel(rows, block, ends_ref, q_ref, k_ref, v_ref, scale_ref, o_ref, lse_ref, *bias):
    parts = spans(rows, block)

    @pl.when(pl.program_id(0) == 0)
    def _():
        fill_bias(ends_ref, bias, parts, block)

    lower = lax.broadcasted_iota(jnp.int32, (1, 128), 1) < 64
    for n, (first, low, high) in enumerate(parts):
        q = q_ref[pl.ds(first, block), :]
        heads = []
        for h in range(2):
            own = jnp.where(lower if h == 0 else ~lower, q, jnp.zeros_like(q))
            s = dotf(k_ref[pl.ds(low, high - low), :], own, 1, 1) + bias[n][...]
            most = jnp.max(s, axis=0, keepdims=True)
            p = jnp.exp(s - most)
            total = jnp.sum(p, axis=0, keepdims=True)
            probs = (p * (1.0 / total)).astype(BF)
            lse_ref[0, pl.ds(h, 1), pl.ds(first, block)] = most + jnp.log(total)
            heads.append(dotf(probs, v_ref[pl.ds(low, high - low), :], 0, 0))
        out = jnp.where(lower, heads[0], heads[1]) * scale_ref[...]
        o_ref[pl.ds(first, block), :] = out.astype(BF)


def attend_back_kernel(
    rows, block, factor, ends_ref, q_ref, k_ref, v_ref, da_ref, lse_ref,
    dq_ref, dk_ref, dv_ref, inner_ref, dk_acc, dv_acc, *bias
):
    parts = spans(rows, block)

    @pl.when(pl.program_id(0) == 0)
    def _():
        fill_bias(ends_ref, bias, parts, block)

    lower = lax.broadcasted_iota(jnp.int32, (1, 128), 1) < 64
    dk_acc[...] = jnp.zeros_like(dk_acc)
    dv_acc[...] = jnp.zeros_like(dv_acc)
    for n, (first, low, high) in enumerate(parts):
        here = pl.ds(first, block)
        keys = pl.ds(low, high - low)
        q, da, k, v = q_ref[here, :], da_ref[here, :], k_ref[keys, :], v_ref[keys, :]
        heads = []
        for h in range(2):
            mask = lower if h == 0 else ~lower
            q_own = jnp.where(mask, q, jnp.zeros_like(q))
            da_own = jnp.where(mask, da, jnp.zeros_like(da))
            s = dotf(k, q_own, 1, 1) + bias[n][...]
            p = jnp.exp(s - lse_ref[0, pl.ds(h, 1), here])
            product = p * dotf(v, da_own, 1, 1)
            inner = jnp.sum(product, axis=0, keepdims=True)
            inner_ref[0, pl.ds(h, 1), here] = inner
            ds = (product - p * inner).astype(BF)
            dv_acc[keys, :] += dotf(p.astype(BF), da_own, 1, 0)
            dk_acc[keys, :] += dotf(ds, q_own, 1, 0)
            heads.append(dotf(ds, k, 0, 0))
        dq_ref[here, :] = (jnp.where(lower, heads[0], heads[1]) * factor).astype(BF)
    dk_ref[...] = dk_acc[...].astype(BF)
    dv_ref[...] = dv_acc[...].astype(BF)


def bias_shapes(rows, block):
    return [pltpu.VMEM((high - low, block), F32) for _, low, high in spans(rows, block)]


def pair_of(pairs, tensor_count, parts, n):
    if parts == 1:
        return pairs, lambda i: i
    per_tensor = pairs // tensor_count
    per = per_tensor // parts
    return pairs // parts, lambda i: i // per * per_tensor + n * per + i % per


def attend(q, k, v, scale_row, ends, tensor_count, parts, n, before_out, before_lse):
    rows, width = q.shape
    block = min(256, rows)
    pairs = width // 128
    steps, pair = pair_of(pairs, tensor_count, parts, n)
    col = pl.BlockSpec((rows, 128), lambda i, e: (0, pair(i)))
    earlier = [] if before_out is None else [before_out, before_lse]
    count = len(earlier)

    def kernel(ends_ref, q_ref, k_ref, v_ref, scale_ref, *refs):
        attend_kernel(rows, block, ends_ref, q_ref, k_ref, v_ref, scale_ref, *refs[count:])

    return pl.pallas_call(
        kernel,
        grid_spec=pltpu.PrefetchScalarGridSpec(
            num_scalar_prefetch=1,
            grid=(steps,),
            in_specs=[col, col, col, pl.BlockSpec((1, 128), lambda i, e: (0, pair(i)))]
            + [HBM] * count,
            out_specs=[col, pl.BlockSpec((1, 2, rows), lambda i, e: (pair(i), 0, 0))],
            scratch_shapes=bias_shapes(rows, block),
        ),
        out_shape=[
            pltpu.HBM((rows, width), BF),
            pltpu.HBM((pairs, 2, rows), F32),
        ],
        input_output_aliases={5 + j: j for j in range(count)},
        compiler_params=pltpu.CompilerParams(vmem_limit_bytes=32 << 20),
        cost_estimate=cost(24 / parts),
        name="attend",
    )(ends, *in_hbm(q, k, v), scale_row, *earlier)


def attend_back(q, k, v, da, lse, ends, factor, tensor_count, parts, n):
    rows, width = q.shape
    block = min(256, rows)
    pairs = width // 128
    steps, pair = pair_of(pairs, tensor_count, parts, n)
    col = pl.BlockSpec((rows, 128), lambda i, e: (0, pair(i)))
    out_col = pl.BlockSpec((rows, 128), lambda i, e: (0, i))
    out = pltpu.HBM((rows, width // parts), BF)
    return pl.pallas_call(
        functools.partial(attend_back_kernel, rows, block, factor),
        grid_spec=pltpu.PrefetchScalarGridSpec(
            num_scalar_prefetch=1,
            grid=(steps,),
            in_specs=[col] * 4 + [pl.BlockSpec((1, 2, rows), lambda i, e: (pair(i), 0, 0))],
            out_specs=[out_col] * 3 + [pl.BlockSpec((1, 2, rows), lambda i, e: (i, 0, 0))],
            scratch_shapes=[pltpu.VMEM((rows, 128), F32)] * 2 + bias_shapes(rows, block),
        ),
        out_shape=[out, out, out, pltpu.HBM((steps, 2, rows), F32)],
        compiler_params=pltpu.CompilerParams(vmem_limit_bytes=40 << 20),
        cost_estimate=cost(42 / parts),
        name="attend_back",
    )(ends, *in_hbm(q, k, v, da), lse)


def put_stats(ref, here, values):
    lane = lax.broadcasted_iota(jnp.int32, (1, 128), 1)
    out = values[-1]
    for n in reversed(range(len(values) - 1)):
        out = jnp.where(lane < 16 * (n + 1), values[n], out)
    ref[here, :] = jnp.broadcast_to(out, (values[0].shape[0], 128))


def hidden_kernel(
    grid_of, order_ref, scaled_ref, x_ref, gain_ref, mid_ref, a0, a1, a2, a3, b0, b1, b2, b3,
    unit_ref, turned_ref, hidden_ref, narrow_ref, stat_ref, act, norm_stat, wide, h3_ref, wa, wb, sem
):
    batch_count, tensor_count = grid_of
    block, width = x_ref.shape
    total = hidden_ref.shape[1]
    up_cols = total // tensor_count
    out_cols = width // tensor_count
    get = functools.partial(columns, weights(wa, wb), order_ref, batch_count, tensor_count)
    first = pl.program_id(0) == 0

    @pl.when(first)
    def _():
        load_parts((a0, a1, a2, a3), wa, sem.at[0])
        load_parts((b0, b1, b2, b3), wb, sem.at[1])
        wait_whole(wa, sem.at[0])

    mixed = None
    for t in range(tensor_count):
        part = dotf(scaled_ref[:, t * out_cols : (t + 1) * out_cols], get(t, 0, out_cols), 1, 1)
        mixed = part if mixed is None else mixed + part
    wide[...] = mixed

    def norms(r):
        here = pl.ds(r, STEP)
        unit, factor = normalize(wide[here, :])
        unit_ref[here, :] = unit
        resid = x_ref[here, :].astype(F32) + unit * gain_ref[1:2, :]
        mean3 = jnp.mean(resid, axis=-1, keepdims=True)
        centred = resid - mean3
        factor3 = lax.rsqrt(jnp.mean(centred * centred, axis=-1, keepdims=True) + eps)
        h3_ref[here, :] = (centred * factor3 * gain_ref[2:3, :]).astype(BF)
        put_stats(norm_stat, here, [factor, mean3, factor3])

    row_loop(block, STEP, norms)
    turned_ref[...] = h3_ref[...].T

    @pl.when(first)
    def _():
        wait_whole(wb, sem.at[1])

    chunk = min(256, up_cols // 2)
    sums = jnp.zeros((block, 128), F32)
    squares = jnp.zeros((block, 128), F32)
    for c in range(total // chunk):
        t, off = divmod(c * chunk, up_cols)
        h = dotf(h3_ref[...], get(t, out_cols + off, chunk), 1, 0)
        hidden_ref[:, c * chunk : (c + 1) * chunk] = h
        half = 0.5 * jnp.tanh(h * (GELU_C + (GELU_C * GELU_A) * (h * h))) + 0.5
        a = h * half
        act[:, c * chunk : (c + 1) * chunk] = a
        for j in range(chunk // 128):
            piece = a[:, j * 128 : (j + 1) * 128]
            sums += piece
            squares += piece * piece
    mean = jnp.sum(sums, axis=1, keepdims=True) / total
    spread = jnp.sum(squares, axis=1, keepdims=True) / total - mean * mean
    scale = lax.rsqrt(spread + eps)
    before = norm_stat[...]
    put_stats(stat_ref, slice(None), [mean, scale, before[:, 0:1], before[:, 16:17], before[:, 32:33]])

    def narrow(r):
        here = pl.ds(r, STEP)
        m = stat_ref[here, 0:1]
        s = stat_ref[here, 16:17]
        narrow_ref[here, :] = ((act[here, :] - m) * s * mid_ref[...]).astype(BF)

    row_loop(block, STEP, narrow)


def hidden_forward(orders, scaled, x, gains, mid_row, wa, wb, grid_of, share, earlier):
    rows, width = x.shape
    block = min(256, rows)
    total = mid_row.shape[1]
    blocks = rows // block // share[1]
    first = share[0] * blocks
    row = pl.BlockSpec((block, width), lambda i, e: (first + i, 0))
    wide = pl.BlockSpec((block, total), lambda i, e: (first + i, 0))

    def kernel(order_ref, *refs):
        hidden_kernel(grid_of, order_ref, *refs[:12], *refs[12 + len(earlier) :])

    return pl.pallas_call(
        kernel,
        grid_spec=pltpu.PrefetchScalarGridSpec(
            num_scalar_prefetch=1,
            grid=(blocks,),
            in_specs=[
                row,
                row,
                pl.BlockSpec((3, width), lambda i, e: (0, 0)),
                pl.BlockSpec((1, total), lambda i, e: (0, 0)),
            ]
            + [HBM] * (8 + len(earlier)),
            out_specs=[row, pl.BlockSpec((width, block), lambda i, e: (0, first + i)), wide, wide]
            + [pl.BlockSpec((block, 128), lambda i, e: (first + i, 0))],
            scratch_shapes=[
                pltpu.VMEM((block, total), F32),
                pltpu.VMEM((block, 128), F32),
                pltpu.VMEM((block, width), F32),
                pltpu.VMEM((block, width), BF),
                whole(wa),
                whole(wb),
                pltpu.SemaphoreType.DMA((2,)),
            ],
        ),
        out_shape=[
            pltpu.HBM((rows, width), F32),
            pltpu.HBM((width, rows), BF),
            pltpu.HBM((rows, total), F32),
            pltpu.HBM((rows, total), BF),
            pltpu.HBM((rows, 128), F32),
        ],
        input_output_aliases={13 + n: n for n in range(len(earlier))},
        compiler_params=pltpu.CompilerParams(vmem_limit_bytes=44 << 20),
        cost_estimate=cost(30 / share[1]),
        name="hidden_forward",
    )(orders, *in_hbm(scaled, x), gains, mid_row, *parts_of((wa, wb)), *earlier)


def feed_kernel(grid_of, order_ref, narrow_ref, unit_ref, x_ref, gain_ref, a0, a1, a2, a3, b0, b1, b2, b3, out_ref, wa, wb, sem):
    batch_count, tensor_count = grid_of
    up_cols = narrow_ref.shape[1] // tensor_count
    parts = weights(wa, wb)

    @pl.when(pl.program_id(0) == 0)
    def _():
        load_parts((a0, a1, a2, a3), wa, sem.at[0])
        load_parts((b0, b1, b2, b3), wb, sem.at[1])

    out = x_ref[...].astype(F32) + unit_ref[...] * gain_ref[1:2, :]
    for n, (start, width, _, w_ref) in enumerate(parts):

        @pl.when(pl.program_id(0) == 0)
        def _(n=n, w_ref=w_ref):
            wait_whole(w_ref, sem.at[n])

        for t in range(tensor_count):
            w = columns(parts, order_ref, batch_count, tensor_count, t, start, width)
            off = t * up_cols + start
            out += dotf(narrow_ref[:, off : off + width], w, 1, 1)
    out_ref[...] = out.astype(BF)


def feed_forward(orders, narrow, unit, x, gains, wa, wb, grid_of):
    rows, width = x.shape
    block = min(256, rows)
    total = narrow.shape[1]
    row = pl.BlockSpec((block, width), lambda i, e: (i, 0))
    return pl.pallas_call(
        functools.partial(feed_kernel, grid_of),
        grid_spec=pltpu.PrefetchScalarGridSpec(
            num_scalar_prefetch=1,
            grid=(rows // block,),
            in_specs=[pl.BlockSpec((block, total), lambda i, e: (i, 0)), row, row]
            + [pl.BlockSpec((3, width), lambda i, e: (0, 0))]
            + [HBM] * 8,
            out_specs=row,
            scratch_shapes=[whole(wa), whole(wb), pltpu.SemaphoreType.DMA((2,))],
        ),
        out_shape=pltpu.HBM((rows, width), BF),
        compiler_params=pltpu.CompilerParams(vmem_limit_bytes=28 << 20),
        cost_estimate=cost(14),
        name="feed_forward",
    )(orders, *in_hbm(narrow, unit, x), gains, *parts_of((wa, wb)))


def back_kernel(
    grid_of, order_ref, hidden_ref, stat_ref, unit_ref, x_ref, cot_ref, gain_ref, mid_ref,
    scale_ref, da0, da1, da2, da3, db0, db1, db2, db3, a0, a1, a2, a3, b0, b1, b2, b3, dhidden_ref, dresid_ref, turned_ref, dattended_ref,
    gains_ref, dmid_ref, grad, unit_s, slope_s, wide, dmixed_ref, wda, wdb, wa, wb, sem
):
    batch_count, tensor_count = grid_of
    block, width = x_ref.shape
    total = hidden_ref.shape[1]
    up_cols = total // tensor_count
    out_cols = width // tensor_count
    get = functools.partial(columns, weights(wa, wb), order_ref, batch_count, tensor_count)
    get_down = functools.partial(columns, weights(wda, wdb), order_ref, batch_count, tensor_count)
    first = pl.program_id(0) == 0

    @pl.when(first)
    def _():
        load_parts((da0, da1, da2, da3), wda, sem.at[0])
        load_parts((db0, db1, db2, db3), wdb, sem.at[1])
        load_parts((a0, a1, a2, a3), wa, sem.at[2])
        load_parts((b0, b1, b2, b3), wb, sem.at[3])
        gains_ref[...] = jnp.zeros_like(gains_ref)
        dmid_ref[...] = jnp.zeros_like(dmid_ref)
        wait_whole(wda, sem.at[0])

    chunk = min(256, up_cols // 2)
    mean = stat_ref[:, 0:1]
    scale = stat_ref[:, 16:17]
    back_sum = jnp.zeros((block, 128), F32)
    back_inner = jnp.zeros((block, 128), F32)
    turns = [divmod(c * chunk, up_cols) for c in range(total // chunk)]
    turns.sort(key=lambda turn: turn[1] >= wda.shape[2])
    waited = False
    for t, off in turns:
        if off >= wda.shape[2] and not waited:
            waited = True

            @pl.when(first)
            def _():
                wait_whole(wdb, sem.at[1])

        here = slice(t * up_cols + off, t * up_cols + off + chunk)
        dn = dotf(cot_ref[...], get_down(t, off, chunk), 1, 0)
        h = hidden_ref[:, here]
        square = h * h
        half = 0.5 * jnp.tanh(h * (GELU_C + (GELU_C * GELU_A) * square)) + 0.5
        a = h * half
        slope_s[:, here] = half + a * (1.0 - half) * (
            2.0 * GELU_C + (6.0 * GELU_C * GELU_A) * square
        )
        unit = (a - mean) * scale
        unit_s[:, here] = unit
        dmid_ref[:, here] += fold8(dn * unit)
        g = dn * mid_ref[:, here]
        grad[:, here] = g
        inner = g * unit
        for j in range(chunk // 128):
            back_sum += g[:, j * 128 : (j + 1) * 128]
            back_inner += inner[:, j * 128 : (j + 1) * 128]
    sum_col = jnp.sum(back_sum, axis=1, keepdims=True) / total
    inner_col = jnp.sum(back_inner, axis=1, keepdims=True) / total

    @pl.when(first)
    def _():
        wait_whole(wa, sem.at[2])
        wait_whole(wb, sem.at[3])

    dh3 = None
    for c in range(total // chunk):
        t, off = divmod(c * chunk, up_cols)
        here = slice(c * chunk, (c + 1) * chunk)
        act_grad = scale * (grad[:, here] - sum_col - unit_s[:, here] * inner_col)
        dhidden = (act_grad * slope_s[:, here]).astype(BF)
        dhidden_ref[:, here] = dhidden
        part = dotf(dhidden, get(t, out_cols + off, chunk), 1, 1)
        dh3 = part if dh3 is None else dh3 + part
    wide[...] = dh3

    def back(r):
        here = pl.ds(r, STEP)
        unit = unit_ref[here, :]
        resid = x_ref[here, :].astype(F32) + unit * gain_ref[1:2, :]
        unit3 = (resid - stat_ref[here, 48:49]) * stat_ref[here, 64:65]
        third = wide[here, :]
        gains_ref[8:16, :] += fold8(third * unit3)
        dresid = cot_ref[here, :].astype(F32) + norm_back(
            unit3, stat_ref[here, 64:65], third * gain_ref[2:3, :]
        )
        dresid_ref[here, :] = dresid
        gains_ref[0:8, :] += fold8(dresid * unit)
        dmixed = norm_back(unit, stat_ref[here, 32:33], dresid * gain_ref[1:2, :])
        dmixed_ref[here, :] = dmixed.astype(BF)

    row_loop(block, STEP, back)
    turned_ref[...] = dmixed_ref[...].T
    for t in range(tensor_count):
        here = slice(t * out_cols, (t + 1) * out_cols)
        dscaled = dotf(dmixed_ref[...], get(t, 0, out_cols), 1, 0)
        dattended_ref[:, here] = (dscaled * scale_ref[:, here]).astype(BF)


def feed_back(orders, hidden, stat, unit, x, cot, gains, mid_row, scale_row, wda, wdb, wa, wb, grid_of):
    rows, width = x.shape
    block = min(256, rows)
    total = mid_row.shape[1]
    row = pl.BlockSpec((block, width), lambda i, e: (i, 0))
    wide = pl.BlockSpec((block, total), lambda i, e: (i, 0))
    return pl.pallas_call(
        functools.partial(back_kernel, grid_of),
        grid_spec=pltpu.PrefetchScalarGridSpec(
            num_scalar_prefetch=1,
            grid=(rows // block,),
            in_specs=[
                wide,
                pl.BlockSpec((block, 128), lambda i, e: (i, 0)),
                row,
                row,
                row,
                pl.BlockSpec((3, width), lambda i, e: (0, 0)),
                pl.BlockSpec((1, total), lambda i, e: (0, 0)),
                pl.BlockSpec((1, width), lambda i, e: (0, 0)),
            ]
            + [HBM] * 16,
            out_specs=[
                wide,
                row,
                pl.BlockSpec((width, block), lambda i, e: (0, i)),
                row,
                pl.BlockSpec((16, width), lambda i, e: (0, 0)),
                pl.BlockSpec((8, total), lambda i, e: (0, 0)),
            ],
            scratch_shapes=[
                pltpu.VMEM((block, total), F32),
                pltpu.VMEM((block, total), F32),
                pltpu.VMEM((block, total), F32),
                pltpu.VMEM((block, width), F32),
                pltpu.VMEM((block, width), BF),
            ]
            + [whole(chain) for chain in (wda, wdb, wa, wb)]
            + [pltpu.SemaphoreType.DMA((4,))],
        ),
        out_shape=[
            pltpu.HBM((rows, total), BF),
            pltpu.HBM((rows, width), F32),
            pltpu.HBM((width, rows), BF),
            pltpu.HBM((rows, width), BF),
            pltpu.HBM((16, width), F32),
            pltpu.HBM((8, total), F32),
        ],
        compiler_params=pltpu.CompilerParams(vmem_limit_bytes=60 << 20),
        cost_estimate=cost(60),
        name="feed_back",
    )(
        orders, *in_hbm(hidden, stat, unit, x, cot), gains, mid_row, scale_row,
        *parts_of((wda, wdb, wa, wb)),
    )


def grad_kernel(grid_of, count, turn, chunk, order_ref, a_ref, *refs):
    batch_count, tensor_count = grid_of
    b_refs, keep_ref, send_ref = refs[:count], refs[count], refs[count + 1]
    tensor = pl.program_id(1)
    if turn:
        turned = refs[count + 2]

        @pl.when((pl.program_id(0) == 0) & (tensor == 0))
        def _():
            turned[...] = a_ref[...].T

        a_ref = turned
    half = batch_count * tensor_count // 2
    height = keep_ref.shape[-2]
    second = order_ref[0] >= half
    for c, b_ref in enumerate(b_refs):
        acc = dotf(a_ref[...], b_ref[...], 1, 0).astype(BF)
        for core in range(2):

            @pl.when(second if core else jnp.logical_not(second))
            def _(acc=acc, core=core, c=c):
                for b in range(batch_count):
                    place = lax.bitwise_and(order_ref[b * tensor_count + tensor], half - 1)
                    ref = keep_ref if b % 2 == core else send_ref
                    at = (place,) if count == 1 else (place, c)
                    if chunk:
                        start = pl.multiple_of(pl.program_id(0) * chunk, chunk)
                        at += (slice(None), pl.ds(start, chunk))
                    ref[at] = acc[b * height : (b + 1) * height]


def weight_grad(order, a, bs, grid_of, start, cols, name, turn=False, near=False):
    batch_count, tensor_count = grid_of
    width, rows = a.shape[::-1] if turn else a.shape
    part = bs[0].shape[1] // tensor_count
    chunk = min(512, cols)
    per = part // chunk
    height = width // batch_count
    count = len(bs)
    lead = (batch_count * tensor_count // 2,) + (() if count == 1 else (count,)) + (height,)
    zeros = (0,) * len(lead)
    if near:
        out_spec = pl.BlockSpec(memory_space=pltpu.VMEM)
        out = pltpu.VMEM(lead + (cols,), BF)
    else:
        out_spec = pl.BlockSpec(lead + (chunk,), lambda i, t, e: zeros + (i,))
        out = pltpu.HBM(lead + (cols,), BF)
    b_spec = pl.BlockSpec((rows, chunk), lambda i, t, e: (0, t * per + start // chunk + i))
    return pl.pallas_call(
        functools.partial(grad_kernel, grid_of, count, turn, chunk if near else None),
        grid_spec=pltpu.PrefetchScalarGridSpec(
            num_scalar_prefetch=1,
            grid=(cols // chunk, tensor_count),
            in_specs=[pl.BlockSpec(a.shape, lambda i, t, e: (0, 0))] + [b_spec] * count,
            out_specs=[out_spec, out_spec],
            scratch_shapes=[pltpu.VMEM((width, rows), BF)] if turn else [],
        ),
        out_shape=[out, out],
        compiler_params=pltpu.CompilerParams(vmem_limit_bytes=36 << 20),
        cost_estimate=cost(2.4 * count * cols * tensor_count / 1024),
        name=name,
    )(order, *in_hbm(a, *bs))


def input_kernel(grid_of, count, order_ref, *refs):
    batch_count, tensor_count = grid_of
    grads, refs = refs[: 3 * count], refs[3 * count :]
    x_ref, dresid_ref, gain_ref = refs[:3]
    w_hbm, refs = refs[3 : 3 + 4 * count], refs[3 + 4 * count :]
    out_ref, dgain_ref, wide = refs[:3]
    w_refs, sem = refs[3:-1], refs[-1]
    first = pl.program_id(0) == 0

    @pl.when(first)
    def _():
        for n in range(count):
            load_parts(w_hbm[4 * n : 4 * n + 4], w_refs[n], sem.at[n])
        dgain_ref[...] = jnp.zeros_like(dgain_ref)

    parts = weights(*w_refs)
    total = None
    for n, (start, width, _, _) in enumerate(parts):

        @pl.when(first)
        def _(n=n):
            wait_whole(w_refs[n], sem.at[n])

        for c in range(3):
            for t in range(tensor_count):
                w = columns(parts, order_ref, batch_count, tensor_count, t, start, width, lead=c)
                part = dotf(grads[3 * n + c][:, t * width : (t + 1) * width], w, 1, 1)
                total = part if total is None else total + part
    wide[...] = total

    def back(r):
        here = pl.ds(r, STEP)
        unit, factor = normalize(x_ref[here, :].astype(F32))
        grad = wide[here, :]
        dgain_ref[...] += fold8(grad * unit)
        out = dresid_ref[here, :] + norm_back(unit, factor, grad * gain_ref[0:1, :])
        out_ref[here, :] = out.astype(BF)

    row_loop(x_ref.shape[0], STEP, back)


def input_grad(orders, grads, x, dresid, gains, chains, grid_of):
    rows, width = x.shape
    block = min(256, rows)
    row = pl.BlockSpec((block, width), lambda i, e: (i, 0))
    part = pl.BlockSpec((block, width // len(chains)), lambda i, e: (i, 0))
    return pl.pallas_call(
        functools.partial(input_kernel, grid_of, len(chains)),
        grid_spec=pltpu.PrefetchScalarGridSpec(
            num_scalar_prefetch=1,
            grid=(rows // block,),
            in_specs=[part] * len(grads)
            + [row, row, pl.BlockSpec((3, width), lambda i, e: (0, 0))]
            + [HBM] * (4 * len(chains)),
            out_specs=[row, pl.BlockSpec((8, width), lambda i, e: (0, 0))],
            scratch_shapes=[pltpu.VMEM((block, width), F32)]
            + [whole(chain) for chain in chains]
            + [pltpu.SemaphoreType.DMA((len(chains),))],
        ),
        out_shape=[
            pltpu.HBM((rows, width), BF),
            pltpu.HBM((8, width), F32),
        ],
        compiler_params=pltpu.CompilerParams(vmem_limit_bytes=32 << 20),
        cost_estimate=cost(15),
        name="input_grad",
    )(orders, *in_hbm(*grads, x, dresid), gains, *parts_of(chains))


def gather_vector(value, tensor_count):
    rank = lax.axis_index("tensor")
    out = jnp.zeros((tensor_count,) + value.shape, value.dtype)
    for flip in range(tensor_count):
        part = value if flip == 0 else swap(value, "tensor", flip)
        out = lax.dynamic_update_slice(out, part[None], (lax.bitwise_xor(rank, flip), 0))
    return out


def body(
    block_in,
    lengths,
    norm_gains,
    qkv_weight,
    head_scale,
    out_weight,
    up_weight,
    mid_gain,
    down_weight,
    cotangent,
):
    tensor_count = lax.axis_size("tensor")
    batch_count = lax.axis_size("batch")
    tensor_rank = lax.axis_index("tensor")
    batch_rank = lax.axis_index("batch")
    micro_count, own_rows, width = block_in.shape
    if tensor_count % micro_count:
        raise NotImplementedError
    split = tensor_count // micro_count
    micro = tensor_rank // split
    local_heads = head_scale.shape[0]
    heads = local_heads * tensor_count
    head_size = width // heads
    local_hidden = mid_gain.shape[0]
    factor = head_size ** (-0.5)
    grid_of = (batch_count, tensor_count)
    half_cols = local_hidden // 2
    qkv_cols = width // tensor_count
    parts = 2 if qkv_cols % 256 == 0 and split == 1 else 1
    steps = [gather_steps(batch_count, tensor_count, first) for first in (True, False)]
    tables = [place_table(one, batch_count, tensor_count) for one in steps]
    orders = jnp.concatenate(tables)
    far = len(steps[0]) - 2 - bits_of(tensor_count)
    near = bits_of(tensor_count) + 1

    def more(chains, count):
        for _ in range(count):
            hop(chains)

    part_cols = qkv_cols // parts
    up_chunk = min(256, local_hidden // 2)
    out_cols = out_weight.shape[0]
    cut = out_cols + ((local_hidden - out_cols) // 2) // up_chunk * up_chunk
    rows_in = Rows(block_in, micro_count, split)
    qkv = Gather(qkv_weight[None], steps[0])
    launch((), [rows_in, qkv])
    qkv.end()
    for _ in range(far - 1):
        hop([qkv])
    qkv_chains = [
        qkv.columns(n * part_cols, part_cols, steps[n % 2][far:]) for n in range(parts)
    ]
    launch(rows_in.arrived, qkv_chains)
    vectors = gather_vector(
        held(jnp.concatenate([mid_gain, head_scale]), rows_in.arrived), tensor_count
    )
    out_up = Gather(
        held(jnp.concatenate([out_weight.T, up_weight], axis=1)[None], qkv.arrived), steps[0]
    )
    hop([out_up])
    for n in range(near - 1):
        for chain in qkv_chains:
            chain.end()
        launch((), qkv_chains)
    for _ in range(far - 1):
        hop([out_up])
    for chain in qkv_chains:
        chain.end()
    down = Gather(held(down_weight.T[None], out_up.arrived), steps[0])
    wa = out_up.columns(0, cut, steps[0][far:])
    wb = out_up.columns(cut, out_weight.shape[0] + local_hidden - cut, steps[1][far:])
    rows_in.end()
    x = launch(rows_in.result, qkv_chains)
    for chain in qkv_chains:
        chain.end()
    x = launch(x, [wa, wb])

    mid_row = vectors[:, :local_hidden].reshape(1, -1)
    scale_all = vectors[:, local_hidden:].reshape(-1)
    scale_row = jnp.repeat(scale_all, head_size)[None]
    own_lengths = lax.dynamic_index_in_dim(lengths[:, 0], micro, 0, keepdims=False)
    ends = jnp.cumsum(own_lengths).astype(jnp.int32)

    def spread(value):
        if split == 1:
            return value
        groups = [[m * split + s for s in range(split)] for m in range(micro_count)]
        return lax.all_to_all(value, "tensor", 1, 0, tiled=True, axis_index_groups=groups)

    def collect(value):
        if split == 1:
            return value
        groups = [[m * split + s for s in range(split)] for m in range(micro_count)]
        return lax.all_to_all(value, "tensor", 0, 1, tiled=True, axis_index_groups=groups)

    h1, q, k, v = project(orders, x, norm_gains, qkv_chains, grid_of, factor)
    q, k, v = land((q, k, v), [wa, wb])
    q, k, v = spread(q), spread(k), spread(v)
    more([wa, wb], near - 2)
    q = launch(q, [wa, wb, down])
    part = width // split
    scale_part = lax.dynamic_slice(scale_row, (0, tensor_rank % split * part), (1, part))
    scaled, lse = None, None
    for n in range(parts):
        scaled, lse = attend(q, k, v, scale_part, ends, tensor_count, parts, n, scaled, lse)
        if n == 0:
            scaled = land(scaled, [down])
            more([down], far - 2)
            scaled = launch(scaled, [down])
    scaled = land(scaled, [wa, wb, down])
    down_cut = half_cols
    wda = down.columns(0, down_cut, steps[0][far:])
    wdb = down.columns(down_cut, local_hidden - down_cut, steps[1][far:])
    rows_cot = Rows(cotangent, micro_count, split)
    scaled = launch(scaled, [wa, wb])
    scaled = land(scaled, [wa, wb])
    scaled = collect(launch(scaled, [wda, wdb, rows_cot]))
    forward = []
    shares = 2 if x.shape[0] % 512 == 0 else 1
    for n in range(shares):
        if n:
            forward[0] = land(forward[0], [wda, wdb])
            more([wda, wdb], near - 2)
            forward[0] = launch(forward[0], [wda, wdb])
        forward = list(
            hidden_forward(orders, scaled, x, norm_gains, mid_row, wa, wb, grid_of, (n, shares), forward)
        )
    unit, h3, hidden, narrow, stat = forward
    if shares == 1:
        narrow = land(narrow, [wda, wdb])
        more([wda, wdb], near - 2)
        narrow = launch(narrow, [wda, wdb])
    unit, h3, hidden, narrow, stat = land([unit, h3, hidden, narrow, stat], [rows_cot, wda])
    cot = rows_cot.result

    def grad_half(n, a, b, name, turn=False):
        keep, send = weight_grad(
            tables[n], a, [b], grid_of, n * half_cols, half_cols, name, turn, not turn
        )
        return Scatter(keep, send, steps[n])

    def flush(chains):
        for chain in chains:
            while chain.steps:
                hop([chain])
        return [chain.total for chain in chains]

    cot_held = launch(cot, [wda])
    d0 = grad_half(0, cot_held, narrow, "grad_down", True)
    d0.keep, d0.send = land((d0.keep, d0.send), [wdb])
    cot_held = launch(cot_held, [d0, wdb])
    d1 = grad_half(1, cot_held, narrow, "grad_down", True)
    d1.keep, d1.send = land((d1.keep, d1.send), [d0, wda, wdb])
    hidden = launch(hidden, [d1, d0])
    hidden = land(hidden, [d1])
    hidden = launch(hidden, [d1])
    back = feed_back(
        orders, hidden, stat, unit, x, cot, norm_gains, mid_row, scale_row, wda, wdb, wa, wb, grid_of
    )
    dhidden, dresid, dmixed, dattended, gain_sums, mid_sums = land(back, [d0, d1])
    more([d0, d1], near - 2)
    dhidden = launch(dhidden, [d0, d1])
    u0 = grad_half(0, h3, dhidden, "grad_up")
    u0.keep, u0.send = land((u0.keep, u0.send), [d0, d1])
    down_sum = merged([d0, d1])
    dhidden = launch(dhidden, [u0, down_sum])
    u1 = grad_half(1, h3, dhidden, "grad_up")
    u1.keep, u1.send = land((u1.keep, u1.send), [u0, down_sum])
    dmixed = launch(dmixed, [u1])
    keep, send = weight_grad(
        tables[0], dmixed, [scaled], grid_of, 0, out_weight.shape[0], "grad_out", near=True
    )
    o0 = Scatter(keep, send, steps[0])
    o0.keep, o0.send = land((o0.keep, o0.send), [u1])
    flying = [u0, u1, o0] + ([down_sum] if down_sum.steps else [])
    da = launch(spread(dattended), flying)
    halves, grads, inners = [], [], []
    for n in range(parts):
        *three, inner = attend_back(q, k, v, da, lse, ends, factor, tensor_count, parts, n)
        inners.append(inner)
        if n == 0:
            three = land(three, flying)
            narrow = launch(narrow, [u0, u1])
            block_out = feed_forward(orders, narrow, unit, x, norm_gains, wda, wdb, grid_of)
            block_out = land(block_out, [u0, u1])
            more([u0, u1], near - 2)
            up_sum = merged([u0, u1])
            rows_out = Rows(block_out, micro_count, split, 2)
            three = [collect(one) for one in three]
            three = launch(three, [up_sum, o0])
            flying = [up_sum, o0]
        else:
            three = land(three, flying)
            three, first_out = lax.optimization_barrier((three, rows_out.arrived[0]))
            rows_out.arrived[0] = first_out
            flying = [o0]
            three = launch(three, flying)
        keep, send = weight_grad(tables[n % 2], h1, three, grid_of, 0, part_cols, "grad_qkv", near=True)
        halves.append(Scatter(keep, send, steps[n % 2]))
        grads += three
        halves[-1].keep, halves[-1].send = land((halves[-1].keep, halves[-1].send), flying)
        if n < parts - 1:
            flying = [halves[0], up_sum, o0]
            da = launch(da, flying + [rows_out])
    q_last = halves[-1]
    if parts > 1:
        q_last.keep, q_last.send, rows_out.arrived = lax.optimization_barrier(
            (q_last.keep, q_last.send, rows_out.arrived)
        )
        rows_out.end()
    dresid = launch(dresid, [q_last])
    dresid = land(dresid, [q_last])
    beside = halves + [o0] + ([] if parts > 1 else [rows_out])
    dresid = launch(dresid, beside)
    grad_in, first_sums = input_grad(orders, grads, x, dresid, norm_gains, qkv_chains, grid_of)
    grad_in, first_sums = land((grad_in, first_sums), beside)
    local = heads // split
    if parts == 1:
        head_sums = jnp.sum(inners[0], axis=-1).reshape(-1)
    else:
        shaped = [jnp.sum(one, axis=-1).reshape(tensor_count, -1) for one in inners]
        head_sums = jnp.concatenate(shaped, axis=1).reshape(-1)
    first_head = tensor_rank % split * local
    head_sums = head_sums / lax.dynamic_slice(scale_all, (first_head,), (local,))
    head_all = lax.dynamic_update_slice(jnp.zeros((heads,), F32), head_sums, (first_head,))
    last = jnp.concatenate(
        [jnp.sum(one, axis=0) for one in (first_sums, gain_sums[:8], gain_sums[8:], mid_sums)]
        + [head_all]
    )
    last = Total(last, batch_count, tensor_count)
    rows_back = Rows(grad_in, micro_count, split, 2)
    tail = halves + ([o0] if o0.steps else [])
    launch((), tail + [last])
    last.end()
    launch((), [last])
    land((), tail + [last])
    if parts > 1:
        halves = [merged(halves)]
    sent = rows_back.outgoing()
    tail = [one for one in halves + [o0, last] if one.steps]
    values, sent = lax.optimization_barrier(([one.outgoing() for one in tail], sent))
    for one, value in zip(tail, values):
        one.go(value)
    rows_back.go(sent)
    for one in tail:
        one.end()
    while last.steps:
        hop([last])
    tail = [one for one in halves + [o0] if one.steps]
    launch((), tail)
    arrived = [one.arrived for one in tail]
    rows_back.arrived = held(rows_back.arrived, arrived)
    last.value = held(last.value, arrived)
    for one in tail:
        one.end()
    rows_back.end()
    block_out, grad_in = rows_out.result, rows_back.result
    d_totals, u_totals, o_totals, q_totals = (
        flush([down_sum]), flush([up_sum]), flush([o0]), flush(halves)
    )
    down_grad = d_totals[0].T
    up_grad = u_totals[0]
    out_grad = o_totals[0].T
    qkv_grad = q_totals[0]
    vector = last.value
    d_totals, u_totals, o_totals, q_totals = (
        flush([d0, d1]), flush([u0, u1]), flush([o0]), flush(halves)
    )
    gains_sum = vector[: 3 * width].reshape(3, width)
    mid_own = lax.dynamic_slice(vector, (3 * width + tensor_rank * local_hidden,), (local_hidden,))
    scale_own = lax.dynamic_slice(
        vector, (3 * width + tensor_count * local_hidden + tensor_rank * local_heads,), (local_heads,)
    )
    return (
        block_out,
        grad_in,
        gains_sum,
        qkv_grad,
        scale_own,
        out_grad,
        up_grad,
        mid_own,
        down_grad,
    )


def solution(mesh):
    in_specs = (
        P(None, ("batch", "tensor"), None),
        P(None, "batch", None),
        P(),
        P(None, "batch", "tensor"),
        P("tensor"),
        P("tensor", "batch"),
        P("batch", "tensor"),
        P("tensor"),
        P("tensor", "batch"),
        P(None, ("batch", "tensor"), None),
    )
    out_specs = (
        P(None, ("batch", "tensor"), None),
        P(None, ("batch", "tensor"), None),
        P(),
        P(None, "batch", "tensor"),
        P("tensor"),
        P("tensor", "batch"),
        P("batch", "tensor"),
        P("tensor"),
        P("tensor", "batch"),
    )
    return jax.shard_map(body, mesh=mesh, in_specs=in_specs, out_specs=out_specs, check_vma=False)
```

```python
import functools
import math

import jax
import jax.numpy as jnp
from jax import lax
from jax.experimental import pallas as pl
from jax.experimental.pallas import tpu as pltpu
from jax.sharding import PartitionSpec as P

eps = 1e-05
SEQ_MOST = 512
F32 = jnp.float32
BF = jnp.bfloat16
ALL = ("batch", "tensor")
GELU_C = math.sqrt(2.0 / math.pi)
GELU_A = 0.044715
STEP = 256


def cost(us):
    return pl.CostEstimate(flops=int(us * 1e9), transcendentals=0, bytes_accessed=1 << 20)


def dotf(a, b, ca, cb):
    return lax.dot_general(a, b, (((ca,), (cb,)), ((), ())), preferred_element_type=F32)


def row_loop(rows, step, fn):
    def one(i, carry):
        fn(pl.multiple_of(i * step, step))
        return carry

    lax.fori_loop(0, rows // step, one, 0)


def normalize(values):
    centred = values - jnp.mean(values, axis=-1, keepdims=True)
    factor = lax.rsqrt(jnp.mean(centred * centred, axis=-1, keepdims=True) + eps)
    return (centred * factor, factor)


def norm_back(unit, factor, grad):
    return factor * (
        grad
        - jnp.mean(grad, axis=-1, keepdims=True)
        - unit * jnp.mean(grad * unit, axis=-1, keepdims=True)
    )


def fold8(values):
    rows, width = values.shape
    return jnp.sum(values.reshape(rows // 8, 8, width), axis=0)


def bits_of(count):
    return count.bit_length() - 1


def gather_steps(batch_count, tensor_count, tensor_first):
    tensor = [("tensor", 1 << k) for k in range(bits_of(tensor_count))]
    plane = [("batch", 2)]
    far = [("batch", 1 << k) for k in reversed(range(2, bits_of(batch_count)))]
    return far + (tensor + plane if tensor_first else plane + tensor) + [("batch", 1)]


def place_table(steps, batch_count, tensor_count):
    batch = jnp.arange(batch_count * tensor_count, dtype=jnp.int32) // tensor_count
    tensor = jnp.arange(batch_count * tensor_count, dtype=jnp.int32) % tensor_count
    batch = jnp.bitwise_xor(batch, lax.axis_index("batch"))
    tensor = jnp.bitwise_xor(tensor, lax.axis_index("tensor"))
    place = jnp.zeros_like(batch)
    for k, (axis, flip) in enumerate(steps):
        apart = (jnp.bitwise_and(batch if axis == "batch" else tensor, flip) != 0).astype(jnp.int32)
        place = place + apart * (1 << k)
    return place


def swap(value, axis, flip):
    count = lax.axis_size(axis)
    return lax.ppermute(value, axis, [(i, i ^ flip) for i in range(count)])


def held(value, after):
    return lax.optimization_barrier((value, after))[0]


class Gather:
    def __init__(self, buffer, steps):
        self.own, self.steps, self.parts = buffer, list(steps), None

    def outgoing(self):
        return self.arrived if len(self.steps) == 1 else self.own

    def go(self, value):
        step = self.steps.pop(0)
        self.arrived = swap(value, *step)
        if not self.steps:
            self.parts[1] = value
        else:
            self.own = value
            if len(self.steps) == 1:
                self.parts = [value, None, swap(value, *self.steps[0]), None]

    def end(self):
        if self.parts is None:
            self.own = jnp.concatenate([self.own, self.arrived], axis=0)
        elif not self.steps:
            self.parts[3] = self.arrived

    def columns(self, start, count, steps):
        return Gather(self.own[..., start : start + count], steps)


class Scatter:
    def __init__(self, keep, send, steps):
        self.keep, self.send, self.steps = keep, send, list(reversed(steps))

    def outgoing(self):
        return (self.send, self.keep)

    def go(self, value):
        send, self.keep = value
        self.arrived = swap(send, *self.steps.pop(0))

    def end(self):
        keep, arrived = self.keep, self.arrived
        half = keep.shape[0] // 2
        if self.steps:
            self.send = (keep[half:].astype(F32) + arrived[half:].astype(F32)).astype(BF)
            self.keep = (keep[:half].astype(F32) + arrived[:half].astype(F32)).astype(BF)
        else:
            self.total = keep[0].astype(F32) + arrived[0].astype(F32)


def merged(chains):
    keep = jnp.concatenate([chain.keep for chain in chains], axis=-1)
    send = jnp.concatenate([chain.send for chain in chains], axis=-1)
    return Scatter(keep, send, list(reversed(chains[0].steps)))


class Total:
    def __init__(self, value, batch_count, tensor_count):
        self.value, self.grid_of = value, (batch_count, tensor_count)
        bits = [(flip, 0) for flip in (1 << k for k in range(2, bits_of(batch_count)))]
        plane = [(2, 0)] + [(0, 1 << k) for k in range(bits_of(tensor_count))]
        self.steps = [[(1, 0)]]
        for group in (plane, bits):
            if len(group) <= 2:
                spans = [(0, 0)]
                for flip in group:
                    spans += [(one[0] ^ flip[0], one[1] ^ flip[1]) for one in spans]
                self.steps.append(spans[1:])
            else:
                self.steps += [[flip] for flip in group]

    def outgoing(self):
        return self.value

    def go(self, value):
        batch_count, tensor_count = self.grid_of
        self.value, self.arrived = value, []
        for batch, tensor in self.steps.pop(0):
            pairs = [
                (b * tensor_count + t, (b ^ batch) * tensor_count + (t ^ tensor))
                for b in range(batch_count)
                for t in range(tensor_count)
            ]
            self.arrived.append(lax.ppermute(value, ALL, pairs))

    def end(self):
        for one in self.arrived:
            self.value = self.value + one


class Rows:
    def __init__(self, value, micro_count, split, cuts=1):
        self.value, self.micro_count, self.split, self.cuts = value, micro_count, split, cuts
        self.taken = value.ndim == 3
        self.steps = [None]
        self.rank = lax.axis_index("tensor")

    def pieces(self):
        if self.taken:
            return self.value
        return self.value.reshape(self.micro_count, -1, self.value.shape[1])

    def outgoing(self):
        if self.split > 1:
            return []
        sent = []
        for flip in range(1, self.micro_count):
            one = lax.dynamic_index_in_dim(self.pieces(), lax.bitwise_xor(self.rank, flip), 0)
            sent += [one[:, n * (one.shape[1] // self.cuts) :][:, : one.shape[1] // self.cuts] for n in range(self.cuts)]
        return sent

    def go(self, value):
        self.steps = []
        if self.split == 1:
            self.arrived = [
                swap(one, "tensor", n // self.cuts + 1) for n, one in enumerate(value)
            ]
        else:
            self.arrived = [
                lax.all_gather(self.value, "tensor", axis=1 if self.taken else 0, tiled=True)
            ]

    def end(self):
        if self.split == 1:
            pieces = self.pieces()
            out = lax.dynamic_update_slice(
                jnp.zeros_like(pieces),
                lax.dynamic_index_in_dim(pieces, self.rank, 0),
                (self.rank, 0, 0),
            )
            for n, one in enumerate(self.arrived):
                other = lax.bitwise_xor(self.rank, n // self.cuts + 1)
                out = lax.dynamic_update_slice(
                    out, one, (other, n % self.cuts * one.shape[1], 0)
                )
            self.result = out.reshape(-1, out.shape[2]) if self.taken else out
            return
        whole = self.arrived[0]
        width = whole.shape[-1]
        if self.taken:
            rows = self.value.shape[0] * self.value.shape[1]
            start = (self.rank // self.split, self.rank % self.split * rows, 0)
            self.result = lax.dynamic_slice(whole, start, (1, rows, width))[0]
        else:
            own = self.value.shape[0] // self.micro_count
            whole = whole.reshape(self.micro_count, -1, width)
            start = (0, self.rank * own, 0)
            self.result = lax.dynamic_slice(whole, start, (self.micro_count, own, width))


def launch(inputs, chains):
    inputs, values = lax.optimization_barrier((inputs, [chain.outgoing() for chain in chains]))
    for chain, value in zip(chains, values):
        chain.go(value)
    return inputs


def land(inputs, chains):
    inputs, values = lax.optimization_barrier((inputs, [chain.arrived for chain in chains]))
    for chain, value in zip(chains, values):
        chain.arrived = value
        chain.end()
    return inputs


def hop(chains, after=()):
    launch(after, chains)
    for chain in chains:
        chain.end()


def columns(parts, order_ref, batch_count, tensor_count, t, start, count, lead=None):
    for first, width, which, w_ref in parts:
        if first <= start < first + width:
            break
    pieces = []
    for b in range(batch_count):
        p = order_ref[(which * batch_count + b) * tensor_count + t]
        here = pl.ds(start - first, count)
        pieces.append(w_ref[p, :, here] if lead is None else w_ref[p, lead, :, here])
    return jnp.concatenate(pieces, axis=0)


def weights(*refs):
    out, first = [], 0
    for n, ref in enumerate(refs):
        out.append((first, ref.shape[-1], n % 2, ref))
        first += ref.shape[-1]
    return out


HBM = pl.BlockSpec(memory_space=pltpu.HBM)


def whole(chain):
    part = chain.parts[0].shape
    return pltpu.VMEM((4 * part[0],) + part[1:], BF)


def in_hbm(*values):
    return [pltpu.with_memory_space_constraint(value, pltpu.HBM) for value in values]


def parts_of(chains):
    return in_hbm(*[part for chain in chains for part in chain.parts])


def load_parts(refs, w, sem):
    count = w.shape[0] // 4
    for n in range(4):
        pltpu.make_async_copy(refs[n], w.at[pl.ds(n * count, count)], sem).start()


def wait_whole(w, sem):
    pltpu.make_async_copy(w, w, sem).wait()


def qkv_kernel(grid_of, factor, count, order_ref, x_ref, gain_ref, *refs):
    batch_count, tensor_count = grid_of
    w_hbm, refs = refs[: 4 * count], refs[4 * count :]
    turned_ref, q_ref, k_ref, v_ref, h1_ref = refs[:5]
    w_refs, sem = refs[5:-1], refs[-1]
    first = pl.program_id(0) == 0

    @pl.when(first)
    def _():
        for n in range(count):
            load_parts(w_hbm[4 * n : 4 * n + 4], w_refs[n], sem.at[n])

    def chunk(r):
        here = pl.ds(r, STEP)
        unit, _ = normalize(x_ref[here, :].astype(F32))
        h1_ref[here, :] = (unit * gain_ref[0:1, :]).astype(BF)

    row_loop(x_ref.shape[0], STEP, chunk)
    turned_ref[...] = h1_ref[...].T

    parts = weights(*w_refs)
    cols = sum(part[1] for part in parts)
    for n, (start, width, _, _) in enumerate(parts):

        @pl.when(first)
        def _(n=n):
            wait_whole(w_refs[n], sem.at[n])

        for c, out in enumerate((q_ref, k_ref, v_ref)):
            for t in range(tensor_count):
                w = columns(parts, order_ref, batch_count, tensor_count, t, start, width, lead=c)
                value = dotf(h1_ref[...], w, 1, 0).astype(BF)
                here = slice(t * cols + start, t * cols + start + width)
                out[:, here] = value * BF(factor) if c == 0 else value


def project(orders, x, gains, chains, grid_of, factor):
    rows, width = x.shape
    block = min(256, rows)
    row = pl.BlockSpec((block, width), lambda i, e: (i, 0))
    return pl.pallas_call(
        functools.partial(qkv_kernel, grid_of, factor, len(chains)),
        grid_spec=pltpu.PrefetchScalarGridSpec(
            num_scalar_prefetch=1,
            grid=(rows // block,),
            in_specs=[row, pl.BlockSpec((3, width), lambda i, e: (0, 0))]
            + [HBM] * (4 * len(chains)),
            out_specs=[pl.BlockSpec((width, block), lambda i, e: (0, i))] + [row] * 3,
            scratch_shapes=[pltpu.VMEM((block, width), BF)]
            + [whole(chain) for chain in chains]
            + [pltpu.SemaphoreType.DMA((len(chains),))],
        ),
        out_shape=[pltpu.HBM((width, rows), BF)]
        + [pltpu.HBM((rows, width), BF)] * 3,
        compiler_params=pltpu.CompilerParams(vmem_limit_bytes=24 << 20),
        cost_estimate=cost(13),
        name="project",
    )(orders, *in_hbm(x), gains, *parts_of(chains))


def spans(rows, block):
    return [
        (first, max(0, (first - SEQ_MOST + 1) // block * block), first + block)
        for first in range(0, rows, block)
    ]


def fill_bias(ends_ref, bias, parts, block):
    for (first, low, high), ref in zip(parts, bias):
        shape = (high - low, block)
        keys = low + lax.broadcasted_iota(jnp.int32, shape, 0)
        queries = first + lax.broadcasted_iota(jnp.int32, shape, 1)
        start = jnp.zeros(shape, jnp.int32)
        for n in range(ends_ref.shape[0]):
            end = ends_ref[n]
            start = jnp.where(queries >= end, end, start)
        ref[...] = jnp.where((keys <= queries) & (keys >= start), 0.0, -1e30).astype(F32)


def attend_kernel(rows, block, ends_ref, q_ref, k_ref, v_ref, scale_ref, o_ref, lse_ref, *bias):
    parts = spans(rows, block)

    @pl.when(pl.program_id(0) == 0)
    def _():
        fill_bias(ends_ref, bias, parts, block)

    lower = lax.broadcasted_iota(jnp.int32, (1, 128), 1) < 64
    for n, (first, low, high) in enumerate(parts):
        q = q_ref[pl.ds(first, block), :]
        heads = []
        for h in range(2):
            own = jnp.where(lower if h == 0 else ~lower, q, jnp.zeros_like(q))
            s = dotf(k_ref[pl.ds(low, high - low), :], own, 1, 1) + bias[n][...]
            most = jnp.max(s, axis=0, keepdims=True)
            p = jnp.exp(s - most)
            total = jnp.sum(p, axis=0, keepdims=True)
            probs = (p * (1.0 / total)).astype(BF)
            lse_ref[0, pl.ds(h, 1), pl.ds(first, block)] = most + jnp.log(total)
            heads.append(dotf(probs, v_ref[pl.ds(low, high - low), :], 0, 0))
        out = jnp.where(lower, heads[0], heads[1]) * scale_ref[...]
        o_ref[pl.ds(first, block), :] = out.astype(BF)


def attend_back_kernel(
    rows, block, factor, ends_ref, q_ref, k_ref, v_ref, da_ref, lse_ref,
    dq_ref, dk_ref, dv_ref, inner_ref, dk_acc, dv_acc, *bias
):
    parts = spans(rows, block)

    @pl.when(pl.program_id(0) == 0)
    def _():
        fill_bias(ends_ref, bias, parts, block)

    lower = lax.broadcasted_iota(jnp.int32, (1, 128), 1) < 64
    dk_acc[...] = jnp.zeros_like(dk_acc)
    dv_acc[...] = jnp.zeros_like(dv_acc)
    for n, (first, low, high) in enumerate(parts):
        here = pl.ds(first, block)
        keys = pl.ds(low, high - low)
        q, da, k, v = q_ref[here, :], da_ref[here, :], k_ref[keys, :], v_ref[keys, :]
        probs, scores, q_own, da_own, k_own = [], [], [], [], []
        for h in range(2):
            mask = lower if h == 0 else ~lower
            q_own.append(jnp.where(mask, q, jnp.zeros_like(q)))
            da_own.append(jnp.where(mask, da, jnp.zeros_like(da)))
            k_own.append(jnp.where(mask, k, jnp.zeros_like(k)))
            s = dotf(k, q_own[h], 1, 1) + bias[n][...]
            p = jnp.exp(s - lse_ref[0, pl.ds(h, 1), here])
            product = p * dotf(v, da_own[h], 1, 1)
            inner = jnp.sum(product, axis=0, keepdims=True)
            inner_ref[0, pl.ds(h, 1), here] = inner
            scores.append((product - p * inner).astype(BF))
            probs.append(p.astype(BF))
        dv_acc[keys, :] += dotf(
            jnp.concatenate(probs, axis=1), jnp.concatenate(da_own, axis=0), 1, 0
        )
        dk_acc[keys, :] += dotf(
            jnp.concatenate(scores, axis=1), jnp.concatenate(q_own, axis=0), 1, 0
        )
        dq = dotf(jnp.concatenate(scores, axis=0), jnp.concatenate(k_own, axis=0), 0, 0)
        dq_ref[here, :] = (dq * factor).astype(BF)
    dk_ref[...] = dk_acc[...].astype(BF)
    dv_ref[...] = dv_acc[...].astype(BF)


def bias_shapes(rows, block):
    return [pltpu.VMEM((high - low, block), F32) for _, low, high in spans(rows, block)]


def pair_of(pairs, tensor_count, parts, n):
    if parts == 1:
        return pairs, lambda i: i
    per_tensor = pairs // tensor_count
    per = per_tensor // parts
    return pairs // parts, lambda i: i // per * per_tensor + n * per + i % per


def attend(q, k, v, scale_row, ends, tensor_count, parts, n, before_out, before_lse):
    rows, width = q.shape
    block = min(256, rows)
    pairs = width // 128
    steps, pair = pair_of(pairs, tensor_count, parts, n)
    col = pl.BlockSpec((rows, 128), lambda i, e: (0, pair(i)))
    earlier = [] if before_out is None else [before_out, before_lse]
    count = len(earlier)

    def kernel(ends_ref, q_ref, k_ref, v_ref, scale_ref, *refs):
        attend_kernel(rows, block, ends_ref, q_ref, k_ref, v_ref, scale_ref, *refs[count:])

    return pl.pallas_call(
        kernel,
        grid_spec=pltpu.PrefetchScalarGridSpec(
            num_scalar_prefetch=1,
            grid=(steps,),
            in_specs=[col, col, col, pl.BlockSpec((1, 128), lambda i, e: (0, pair(i)))]
            + [HBM] * count,
            out_specs=[col, pl.BlockSpec((1, 2, rows), lambda i, e: (pair(i), 0, 0))],
            scratch_shapes=bias_shapes(rows, block),
        ),
        out_shape=[
            pltpu.HBM((rows, width), BF),
            pltpu.HBM((pairs, 2, rows), F32),
        ],
        input_output_aliases={5 + j: j for j in range(count)},
        compiler_params=pltpu.CompilerParams(vmem_limit_bytes=32 << 20),
        cost_estimate=cost(24 / parts),
        name="attend",
    )(ends, *in_hbm(q, k, v), scale_row, *earlier)


def attend_back(q, k, v, da, lse, ends, factor, tensor_count, parts, n):
    rows, width = q.shape
    block = min(256, rows)
    pairs = width // 128
    steps, pair = pair_of(pairs, tensor_count, parts, n)
    col = pl.BlockSpec((rows, 128), lambda i, e: (0, pair(i)))
    out_col = pl.BlockSpec((rows, 128), lambda i, e: (0, i))
    out = pltpu.HBM((rows, width // parts), BF)
    return pl.pallas_call(
        functools.partial(attend_back_kernel, rows, block, factor),
        grid_spec=pltpu.PrefetchScalarGridSpec(
            num_scalar_prefetch=1,
            grid=(steps,),
            in_specs=[col] * 4 + [pl.BlockSpec((1, 2, rows), lambda i, e: (pair(i), 0, 0))],
            out_specs=[out_col] * 3 + [pl.BlockSpec((1, 2, rows), lambda i, e: (i, 0, 0))],
            scratch_shapes=[pltpu.VMEM((rows, 128), F32)] * 2 + bias_shapes(rows, block),
        ),
        out_shape=[out, out, out, pltpu.HBM((steps, 2, rows), F32)],
        compiler_params=pltpu.CompilerParams(vmem_limit_bytes=40 << 20),
        cost_estimate=cost(42 / parts),
        name="attend_back",
    )(ends, *in_hbm(q, k, v, da), lse)


def put_stats(ref, here, values):
    lane = lax.broadcasted_iota(jnp.int32, (1, 128), 1)
    out = values[-1]
    for n in reversed(range(len(values) - 1)):
        out = jnp.where(lane < 16 * (n + 1), values[n], out)
    ref[here, :] = jnp.broadcast_to(out, (values[0].shape[0], 128))


def hidden_kernel(
    grid_of, order_ref, scaled_ref, x_ref, gain_ref, mid_ref, a0, a1, a2, a3, b0, b1, b2, b3,
    unit_ref, turned_ref, hidden_ref, narrow_ref, stat_ref, act, norm_stat, wide, h3_ref, wa, wb, sem
):
    batch_count, tensor_count = grid_of
    block, width = x_ref.shape
    total = hidden_ref.shape[1]
    up_cols = total // tensor_count
    out_cols = width // tensor_count
    get = functools.partial(columns, weights(wa, wb), order_ref, batch_count, tensor_count)
    first = pl.program_id(0) == 0

    @pl.when(first)
    def _():
        load_parts((a0, a1, a2, a3), wa, sem.at[0])
        load_parts((b0, b1, b2, b3), wb, sem.at[1])
        wait_whole(wa, sem.at[0])

    mixed = None
    for t in range(tensor_count):
        part = dotf(scaled_ref[:, t * out_cols : (t + 1) * out_cols], get(t, 0, out_cols), 1, 1)
        mixed = part if mixed is None else mixed + part
    wide[...] = mixed

    def norms(r):
        here = pl.ds(r, STEP)
        unit, factor = normalize(wide[here, :])
        unit_ref[here, :] = unit
        resid = x_ref[here, :].astype(F32) + unit * gain_ref[1:2, :]
        mean3 = jnp.mean(resid, axis=-1, keepdims=True)
        centred = resid - mean3
        factor3 = lax.rsqrt(jnp.mean(centred * centred, axis=-1, keepdims=True) + eps)
        h3_ref[here, :] = (centred * factor3 * gain_ref[2:3, :]).astype(BF)
        put_stats(norm_stat, here, [factor, mean3, factor3])

    row_loop(block, STEP, norms)
    turned_ref[...] = h3_ref[...].T

    @pl.when(first)
    def _():
        wait_whole(wb, sem.at[1])

    chunk = min(256, up_cols // 2)
    sums = jnp.zeros((block, 128), F32)
    squares = jnp.zeros((block, 128), F32)
    for c in range(total // chunk):
        t, off = divmod(c * chunk, up_cols)
        h = dotf(h3_ref[...], get(t, out_cols + off, chunk), 1, 0)
        hidden_ref[:, c * chunk : (c + 1) * chunk] = h
        half = 0.5 * jnp.tanh(h * (GELU_C + (GELU_C * GELU_A) * (h * h))) + 0.5
        a = h * half
        act[:, c * chunk : (c + 1) * chunk] = a
        for j in range(chunk // 128):
            piece = a[:, j * 128 : (j + 1) * 128]
            sums += piece
            squares += piece * piece
    mean = jnp.sum(sums, axis=1, keepdims=True) / total
    spread = jnp.sum(squares, axis=1, keepdims=True) / total - mean * mean
    scale = lax.rsqrt(spread + eps)
    before = norm_stat[...]
    put_stats(stat_ref, slice(None), [mean, scale, before[:, 0:1], before[:, 16:17], before[:, 32:33]])

    def narrow(r):
        here = pl.ds(r, STEP)
        m = stat_ref[here, 0:1]
        s = stat_ref[here, 16:17]
        narrow_ref[here, :] = ((act[here, :] - m) * s * mid_ref[...]).astype(BF)

    row_loop(block, STEP, narrow)


def hidden_forward(orders, scaled, x, gains, mid_row, wa, wb, grid_of, share, earlier):
    rows, width = x.shape
    block = min(256, rows)
    total = mid_row.shape[1]
    blocks = rows // block // share[1]
    first = share[0] * blocks
    row = pl.BlockSpec((block, width), lambda i, e: (first + i, 0))
    wide = pl.BlockSpec((block, total), lambda i, e: (first + i, 0))

    def kernel(order_ref, *refs):
        hidden_kernel(grid_of, order_ref, *refs[:12], *refs[12 + len(earlier) :])

    return pl.pallas_call(
        kernel,
        grid_spec=pltpu.PrefetchScalarGridSpec(
            num_scalar_prefetch=1,
            grid=(blocks,),
            in_specs=[
                row,
                row,
                pl.BlockSpec((3, width), lambda i, e: (0, 0)),
                pl.BlockSpec((1, total), lambda i, e: (0, 0)),
            ]
            + [HBM] * (8 + len(earlier)),
            out_specs=[row, pl.BlockSpec((width, block), lambda i, e: (0, first + i)), wide, wide]
            + [pl.BlockSpec((block, 128), lambda i, e: (first + i, 0))],
            scratch_shapes=[
                pltpu.VMEM((block, total), F32),
                pltpu.VMEM((block, 128), F32),
                pltpu.VMEM((block, width), F32),
                pltpu.VMEM((block, width), BF),
                whole(wa),
                whole(wb),
                pltpu.SemaphoreType.DMA((2,)),
            ],
        ),
        out_shape=[
            pltpu.HBM((rows, width), F32),
            pltpu.HBM((width, rows), BF),
            pltpu.HBM((rows, total), F32),
            pltpu.HBM((rows, total), BF),
            pltpu.HBM((rows, 128), F32),
        ],
        input_output_aliases={13 + n: n for n in range(len(earlier))},
        compiler_params=pltpu.CompilerParams(vmem_limit_bytes=44 << 20),
        cost_estimate=cost(30 / share[1]),
        name="hidden_forward",
    )(orders, *in_hbm(scaled, x), gains, mid_row, *parts_of((wa, wb)), *earlier)


def feed_kernel(grid_of, order_ref, narrow_ref, unit_ref, x_ref, gain_ref, a0, a1, a2, a3, b0, b1, b2, b3, out_ref, wa, wb, sem):
    batch_count, tensor_count = grid_of
    up_cols = narrow_ref.shape[1] // tensor_count
    parts = weights(wa, wb)

    @pl.when(pl.program_id(0) == 0)
    def _():
        load_parts((a0, a1, a2, a3), wa, sem.at[0])
        load_parts((b0, b1, b2, b3), wb, sem.at[1])

    out = x_ref[...].astype(F32) + unit_ref[...] * gain_ref[1:2, :]
    for n, (start, width, _, w_ref) in enumerate(parts):

        @pl.when(pl.program_id(0) == 0)
        def _(n=n, w_ref=w_ref):
            wait_whole(w_ref, sem.at[n])

        for t in range(tensor_count):
            w = columns(parts, order_ref, batch_count, tensor_count, t, start, width)
            off = t * up_cols + start
            out += dotf(narrow_ref[:, off : off + width], w, 1, 1)
    out_ref[...] = out.astype(BF)


def feed_forward(orders, narrow, unit, x, gains, wa, wb, grid_of):
    rows, width = x.shape
    block = min(256, rows)
    total = narrow.shape[1]
    row = pl.BlockSpec((block, width), lambda i, e: (i, 0))
    return pl.pallas_call(
        functools.partial(feed_kernel, grid_of),
        grid_spec=pltpu.PrefetchScalarGridSpec(
            num_scalar_prefetch=1,
            grid=(rows // block,),
            in_specs=[pl.BlockSpec((block, total), lambda i, e: (i, 0)), row, row]
            + [pl.BlockSpec((3, width), lambda i, e: (0, 0))]
            + [HBM] * 8,
            out_specs=row,
            scratch_shapes=[whole(wa), whole(wb), pltpu.SemaphoreType.DMA((2,))],
        ),
        out_shape=pltpu.HBM((rows, width), BF),
        compiler_params=pltpu.CompilerParams(vmem_limit_bytes=28 << 20),
        cost_estimate=cost(14),
        name="feed_forward",
    )(orders, *in_hbm(narrow, unit, x), gains, *parts_of((wa, wb)))


def back_kernel(
    grid_of, order_ref, hidden_ref, stat_ref, unit_ref, x_ref, cot_ref, gain_ref, mid_ref,
    scale_ref, da0, da1, da2, da3, db0, db1, db2, db3, a0, a1, a2, a3, b0, b1, b2, b3, dhidden_ref, dresid_ref, turned_ref, dattended_ref,
    gains_ref, dmid_ref, grad, unit_s, slope_s, wide, dmixed_ref, wda, wdb, wa, wb, sem
):
    batch_count, tensor_count = grid_of
    block, width = x_ref.shape
    total = hidden_ref.shape[1]
    up_cols = total // tensor_count
    out_cols = width // tensor_count
    get = functools.partial(columns, weights(wa, wb), order_ref, batch_count, tensor_count)
    get_down = functools.partial(columns, weights(wda, wdb), order_ref, batch_count, tensor_count)
    first = pl.program_id(0) == 0

    @pl.when(first)
    def _():
        load_parts((da0, da1, da2, da3), wda, sem.at[0])
        load_parts((db0, db1, db2, db3), wdb, sem.at[1])
        load_parts((a0, a1, a2, a3), wa, sem.at[2])
        load_parts((b0, b1, b2, b3), wb, sem.at[3])
        gains_ref[...] = jnp.zeros_like(gains_ref)
        dmid_ref[...] = jnp.zeros_like(dmid_ref)
        wait_whole(wda, sem.at[0])

    chunk = min(256, up_cols // 2)
    mean = stat_ref[:, 0:1]
    scale = stat_ref[:, 16:17]
    back_sum = jnp.zeros((block, 128), F32)
    back_inner = jnp.zeros((block, 128), F32)
    turns = [divmod(c * chunk, up_cols) for c in range(total // chunk)]
    turns.sort(key=lambda turn: turn[1] >= wda.shape[2])
    waited = False
    for t, off in turns:
        if off >= wda.shape[2] and not waited:
            waited = True

            @pl.when(first)
            def _():
                wait_whole(wdb, sem.at[1])

        here = slice(t * up_cols + off, t * up_cols + off + chunk)
        dn = dotf(cot_ref[...], get_down(t, off, chunk), 1, 0)
        h = hidden_ref[:, here]
        square = h * h
        half = 0.5 * jnp.tanh(h * (GELU_C + (GELU_C * GELU_A) * square)) + 0.5
        a = h * half
        slope_s[:, here] = half + a * (1.0 - half) * (
            2.0 * GELU_C + (6.0 * GELU_C * GELU_A) * square
        )
        unit = (a - mean) * scale
        unit_s[:, here] = unit
        dmid_ref[:, here] += fold8(dn * unit)
        g = dn * mid_ref[:, here]
        grad[:, here] = g
        inner = g * unit
        for j in range(chunk // 128):
            back_sum += g[:, j * 128 : (j + 1) * 128]
            back_inner += inner[:, j * 128 : (j + 1) * 128]
    sum_col = jnp.sum(back_sum, axis=1, keepdims=True) / total
    inner_col = jnp.sum(back_inner, axis=1, keepdims=True) / total

    @pl.when(first)
    def _():
        wait_whole(wa, sem.at[2])
        wait_whole(wb, sem.at[3])

    dh3 = None
    for c in range(total // chunk):
        t, off = divmod(c * chunk, up_cols)
        here = slice(c * chunk, (c + 1) * chunk)
        act_grad = scale * (grad[:, here] - sum_col - unit_s[:, here] * inner_col)
        dhidden = (act_grad * slope_s[:, here]).astype(BF)
        dhidden_ref[:, here] = dhidden
        part = dotf(dhidden, get(t, out_cols + off, chunk), 1, 1)
        dh3 = part if dh3 is None else dh3 + part
    wide[...] = dh3

    def back(r):
        here = pl.ds(r, STEP)
        unit = unit_ref[here, :]
        resid = x_ref[here, :].astype(F32) + unit * gain_ref[1:2, :]
        unit3 = (resid - stat_ref[here, 48:49]) * stat_ref[here, 64:65]
        third = wide[here, :]
        gains_ref[8:16, :] += fold8(third * unit3)
        dresid = cot_ref[here, :].astype(F32) + norm_back(
            unit3, stat_ref[here, 64:65], third * gain_ref[2:3, :]
        )
        dresid_ref[here, :] = dresid
        gains_ref[0:8, :] += fold8(dresid * unit)
        dmixed = norm_back(unit, stat_ref[here, 32:33], dresid * gain_ref[1:2, :])
        dmixed_ref[here, :] = dmixed.astype(BF)

    row_loop(block, STEP, back)
    turned_ref[...] = dmixed_ref[...].T
    for t in range(tensor_count):
        here = slice(t * out_cols, (t + 1) * out_cols)
        dscaled = dotf(dmixed_ref[...], get(t, 0, out_cols), 1, 0)
        dattended_ref[:, here] = (dscaled * scale_ref[:, here]).astype(BF)


def feed_back(orders, hidden, stat, unit, x, cot, gains, mid_row, scale_row, wda, wdb, wa, wb, grid_of):
    rows, width = x.shape
    block = min(256, rows)
    total = mid_row.shape[1]
    row = pl.BlockSpec((block, width), lambda i, e: (i, 0))
    wide = pl.BlockSpec((block, total), lambda i, e: (i, 0))
    return pl.pallas_call(
        functools.partial(back_kernel, grid_of),
        grid_spec=pltpu.PrefetchScalarGridSpec(
            num_scalar_prefetch=1,
            grid=(rows // block,),
            in_specs=[
                wide,
                pl.BlockSpec((block, 128), lambda i, e: (i, 0)),
                row,
                row,
                row,
                pl.BlockSpec((3, width), lambda i, e: (0, 0)),
                pl.BlockSpec((1, total), lambda i, e: (0, 0)),
                pl.BlockSpec((1, width), lambda i, e: (0, 0)),
            ]
            + [HBM] * 16,
            out_specs=[
                wide,
                row,
                pl.BlockSpec((width, block), lambda i, e: (0, i)),
                row,
                pl.BlockSpec((16, width), lambda i, e: (0, 0)),
                pl.BlockSpec((8, total), lambda i, e: (0, 0)),
            ],
            scratch_shapes=[
                pltpu.VMEM((block, total), F32),
                pltpu.VMEM((block, total), F32),
                pltpu.VMEM((block, total), F32),
                pltpu.VMEM((block, width), F32),
                pltpu.VMEM((block, width), BF),
            ]
            + [whole(chain) for chain in (wda, wdb, wa, wb)]
            + [pltpu.SemaphoreType.DMA((4,))],
        ),
        out_shape=[
            pltpu.HBM((rows, total), BF),
            pltpu.HBM((rows, width), F32),
            pltpu.HBM((width, rows), BF),
            pltpu.HBM((rows, width), BF),
            pltpu.HBM((16, width), F32),
            pltpu.HBM((8, total), F32),
        ],
        compiler_params=pltpu.CompilerParams(vmem_limit_bytes=60 << 20),
        cost_estimate=cost(60),
        name="feed_back",
    )(
        orders, *in_hbm(hidden, stat, unit, x, cot), gains, mid_row, scale_row,
        *parts_of((wda, wdb, wa, wb)),
    )


def grad_kernel(grid_of, count, turn, chunk, order_ref, a_ref, *refs):
    batch_count, tensor_count = grid_of
    b_refs, keep_ref, send_ref = refs[:count], refs[count], refs[count + 1]
    tensor = pl.program_id(1)
    if turn:
        turned = refs[count + 2]

        @pl.when((pl.program_id(0) == 0) & (tensor == 0))
        def _():
            turned[...] = a_ref[...].T

        a_ref = turned
    half = batch_count * tensor_count // 2
    height = keep_ref.shape[-2]
    second = order_ref[0] >= half
    for c, b_ref in enumerate(b_refs):
        acc = dotf(a_ref[...], b_ref[...], 1, 0).astype(BF)
        for core in range(2):

            @pl.when(second if core else jnp.logical_not(second))
            def _(acc=acc, core=core, c=c):
                for b in range(batch_count):
                    place = lax.bitwise_and(order_ref[b * tensor_count + tensor], half - 1)
                    ref = keep_ref if b % 2 == core else send_ref
                    at = (place,) if count == 1 else (place, c)
                    if chunk:
                        start = pl.multiple_of(pl.program_id(0) * chunk, chunk)
                        at += (slice(None), pl.ds(start, chunk))
                    ref[at] = acc[b * height : (b + 1) * height]


def weight_grad(order, a, bs, grid_of, start, cols, name, turn=False, near=False):
    batch_count, tensor_count = grid_of
    width, rows = a.shape[::-1] if turn else a.shape
    part = bs[0].shape[1] // tensor_count
    chunk = min(512, cols)
    per = part // chunk
    height = width // batch_count
    count = len(bs)
    lead = (batch_count * tensor_count // 2,) + (() if count == 1 else (count,)) + (height,)
    zeros = (0,) * len(lead)
    if near:
        out_spec = pl.BlockSpec(memory_space=pltpu.VMEM)
        out = pltpu.VMEM(lead + (cols,), BF)
    else:
        out_spec = pl.BlockSpec(lead + (chunk,), lambda i, t, e: zeros + (i,))
        out = pltpu.HBM(lead + (cols,), BF)
    b_spec = pl.BlockSpec((rows, chunk), lambda i, t, e: (0, t * per + start // chunk + i))
    return pl.pallas_call(
        functools.partial(grad_kernel, grid_of, count, turn, chunk if near else None),
        grid_spec=pltpu.PrefetchScalarGridSpec(
            num_scalar_prefetch=1,
            grid=(cols // chunk, tensor_count),
            in_specs=[pl.BlockSpec(a.shape, lambda i, t, e: (0, 0))] + [b_spec] * count,
            out_specs=[out_spec, out_spec],
            scratch_shapes=[pltpu.VMEM((width, rows), BF)] if turn else [],
        ),
        out_shape=[out, out],
        compiler_params=pltpu.CompilerParams(vmem_limit_bytes=36 << 20),
        cost_estimate=cost(2.4 * count * cols * tensor_count / 1024),
        name=name,
    )(order, *in_hbm(a, *bs))


def input_kernel(grid_of, count, order_ref, *refs):
    batch_count, tensor_count = grid_of
    grads, refs = refs[: 3 * count], refs[3 * count :]
    x_ref, dresid_ref, gain_ref = refs[:3]
    w_hbm, refs = refs[3 : 3 + 4 * count], refs[3 + 4 * count :]
    out_ref, dgain_ref, wide = refs[:3]
    w_refs, sem = refs[3:-1], refs[-1]
    first = pl.program_id(0) == 0

    @pl.when(first)
    def _():
        for n in range(count):
            load_parts(w_hbm[4 * n : 4 * n + 4], w_refs[n], sem.at[n])
        dgain_ref[...] = jnp.zeros_like(dgain_ref)

    parts = weights(*w_refs)
    total = None
    for n, (start, width, _, _) in enumerate(parts):

        @pl.when(first)
        def _(n=n):
            wait_whole(w_refs[n], sem.at[n])

        for c in range(3):
            for t in range(tensor_count):
                w = columns(parts, order_ref, batch_count, tensor_count, t, start, width, lead=c)
                part = dotf(grads[3 * n + c][:, t * width : (t + 1) * width], w, 1, 1)
                total = part if total is None else total + part
    wide[...] = total

    def back(r):
        here = pl.ds(r, STEP)
        unit, factor = normalize(x_ref[here, :].astype(F32))
        grad = wide[here, :]
        dgain_ref[...] += fold8(grad * unit)
        out = dresid_ref[here, :] + norm_back(unit, factor, grad * gain_ref[0:1, :])
        out_ref[here, :] = out.astype(BF)

    row_loop(x_ref.shape[0], STEP, back)


def input_grad(orders, grads, x, dresid, gains, chains, grid_of):
    rows, width = x.shape
    block = min(256, rows)
    row = pl.BlockSpec((block, width), lambda i, e: (i, 0))
    part = pl.BlockSpec((block, width // len(chains)), lambda i, e: (i, 0))
    return pl.pallas_call(
        functools.partial(input_kernel, grid_of, len(chains)),
        grid_spec=pltpu.PrefetchScalarGridSpec(
            num_scalar_prefetch=1,
            grid=(rows // block,),
            in_specs=[part] * len(grads)
            + [row, row, pl.BlockSpec((3, width), lambda i, e: (0, 0))]
            + [HBM] * (4 * len(chains)),
            out_specs=[row, pl.BlockSpec((8, width), lambda i, e: (0, 0))],
            scratch_shapes=[pltpu.VMEM((block, width), F32)]
            + [whole(chain) for chain in chains]
            + [pltpu.SemaphoreType.DMA((len(chains),))],
        ),
        out_shape=[
            pltpu.HBM((rows, width), BF),
            pltpu.HBM((8, width), F32),
        ],
        compiler_params=pltpu.CompilerParams(vmem_limit_bytes=32 << 20),
        cost_estimate=cost(15),
        name="input_grad",
    )(orders, *in_hbm(*grads, x, dresid), gains, *parts_of(chains))


def gather_vector(value, tensor_count):
    rank = lax.axis_index("tensor")
    out = jnp.zeros((tensor_count,) + value.shape, value.dtype)
    for flip in range(tensor_count):
        part = value if flip == 0 else swap(value, "tensor", flip)
        out = lax.dynamic_update_slice(out, part[None], (lax.bitwise_xor(rank, flip), 0))
    return out


def body(
    block_in,
    lengths,
    norm_gains,
    qkv_weight,
    head_scale,
    out_weight,
    up_weight,
    mid_gain,
    down_weight,
    cotangent,
):
    tensor_count = lax.axis_size("tensor")
    batch_count = lax.axis_size("batch")
    tensor_rank = lax.axis_index("tensor")
    batch_rank = lax.axis_index("batch")
    micro_count, own_rows, width = block_in.shape
    if tensor_count % micro_count:
        raise NotImplementedError
    split = tensor_count // micro_count
    micro = tensor_rank // split
    local_heads = head_scale.shape[0]
    heads = local_heads * tensor_count
    head_size = width // heads
    local_hidden = mid_gain.shape[0]
    factor = head_size ** (-0.5)
    grid_of = (batch_count, tensor_count)
    half_cols = local_hidden // 2
    qkv_cols = width // tensor_count
    parts = 2 if qkv_cols % 256 == 0 and split == 1 else 1
    steps = [gather_steps(batch_count, tensor_count, first) for first in (True, False)]
    tables = [place_table(one, batch_count, tensor_count) for one in steps]
    orders = jnp.concatenate(tables)
    far = len(steps[0]) - 2 - bits_of(tensor_count)
    near = bits_of(tensor_count) + 1

    def more(chains, count):
        for _ in range(count):
            hop(chains)

    part_cols = qkv_cols // parts
    up_chunk = min(256, local_hidden // 2)
    out_cols = out_weight.shape[0]
    cut = out_cols + ((local_hidden - out_cols) // 2) // up_chunk * up_chunk
    rows_in = Rows(block_in, micro_count, split)
    qkv = Gather(qkv_weight[None], steps[0])
    launch((), [rows_in, qkv])
    qkv.end()
    for _ in range(far - 1):
        hop([qkv])
    qkv_chains = [
        qkv.columns(n * part_cols, part_cols, steps[n % 2][far:]) for n in range(parts)
    ]
    launch(rows_in.arrived, qkv_chains)
    vectors = gather_vector(
        held(jnp.concatenate([mid_gain, head_scale]), rows_in.arrived), tensor_count
    )
    out_up = Gather(
        held(jnp.concatenate([out_weight.T, up_weight], axis=1)[None], qkv.arrived), steps[0]
    )
    hop([out_up])
    for n in range(near - 1):
        for chain in qkv_chains:
            chain.end()
        launch((), qkv_chains)
    for _ in range(far - 1):
        hop([out_up])
    for chain in qkv_chains:
        chain.end()
    down = Gather(held(down_weight.T[None], out_up.arrived), steps[0])
    wa = out_up.columns(0, cut, steps[0][far:])
    wb = out_up.columns(cut, out_weight.shape[0] + local_hidden - cut, steps[1][far:])
    rows_in.end()
    x = launch(rows_in.result, qkv_chains)
    for chain in qkv_chains:
        chain.end()
    x = launch(x, [wa, wb])

    mid_row = vectors[:, :local_hidden].reshape(1, -1)
    scale_all = vectors[:, local_hidden:].reshape(-1)
    scale_row = jnp.repeat(scale_all, head_size)[None]
    own_lengths = lax.dynamic_index_in_dim(lengths[:, 0], micro, 0, keepdims=False)
    ends = jnp.cumsum(own_lengths).astype(jnp.int32)

    def spread(value):
        if split == 1:
            return value
        groups = [[m * split + s for s in range(split)] for m in range(micro_count)]
        return lax.all_to_all(value, "tensor", 1, 0, tiled=True, axis_index_groups=groups)

    def collect(value):
        if split == 1:
            return value
        groups = [[m * split + s for s in range(split)] for m in range(micro_count)]
        return lax.all_to_all(value, "tensor", 0, 1, tiled=True, axis_index_groups=groups)

    h1, q, k, v = project(orders, x, norm_gains, qkv_chains, grid_of, factor)
    q, k, v = land((q, k, v), [wa, wb])
    q, k, v = spread(q), spread(k), spread(v)
    more([wa, wb], near - 2)
    q = launch(q, [wa, wb, down])
    part = width // split
    scale_part = lax.dynamic_slice(scale_row, (0, tensor_rank % split * part), (1, part))
    scaled, lse = None, None
    for n in range(parts):
        scaled, lse = attend(q, k, v, scale_part, ends, tensor_count, parts, n, scaled, lse)
        if n == 0:
            scaled = land(scaled, [down])
            more([down], far - 2)
            scaled = launch(scaled, [down])
    scaled = land(scaled, [wa, wb, down])
    down_cut = half_cols
    wda = down.columns(0, down_cut, steps[0][far:])
    wdb = down.columns(down_cut, local_hidden - down_cut, steps[1][far:])
    rows_cot = Rows(cotangent, micro_count, split)
    scaled = launch(scaled, [wa, wb])
    scaled = land(scaled, [wa, wb])
    scaled = collect(launch(scaled, [wda, wdb, rows_cot]))
    forward = []
    shares = 2 if x.shape[0] % 512 == 0 else 1
    for n in range(shares):
        if n:
            forward[0] = land(forward[0], [wda, wdb])
            more([wda, wdb], near - 2)
            forward[0] = launch(forward[0], [wda, wdb])
        forward = list(
            hidden_forward(orders, scaled, x, norm_gains, mid_row, wa, wb, grid_of, (n, shares), forward)
        )
    unit, h3, hidden, narrow, stat = forward
    if shares == 1:
        narrow = land(narrow, [wda, wdb])
        more([wda, wdb], near - 2)
        narrow = launch(narrow, [wda, wdb])
    unit, h3, hidden, narrow, stat = land([unit, h3, hidden, narrow, stat], [rows_cot, wda])
    cot = rows_cot.result

    def grad_half(n, a, b, name, turn=False):
        keep, send = weight_grad(
            tables[n], a, [b], grid_of, n * half_cols, half_cols, name, turn, True
        )
        return Scatter(keep, send, steps[n])

    def flush(chains):
        for chain in chains:
            while chain.steps:
                hop([chain])
        return [chain.total for chain in chains]

    cot_held = launch(cot, [wda])
    d0 = grad_half(0, cot_held, narrow, "grad_down", True)
    d0.keep, d0.send = land((d0.keep, d0.send), [wdb])
    cot_held = launch(cot_held, [d0, wdb])
    d1 = grad_half(1, cot_held, narrow, "grad_down", True)
    d1.keep, d1.send = land((d1.keep, d1.send), [d0, wda, wdb])
    hidden = launch(hidden, [d1, d0])
    hidden = land(hidden, [d1])
    hidden = launch(hidden, [d1])
    back = feed_back(
        orders, hidden, stat, unit, x, cot, norm_gains, mid_row, scale_row, wda, wdb, wa, wb, grid_of
    )
    dhidden, dresid, dmixed, dattended, gain_sums, mid_sums = land(back, [d0, d1])
    more([d0, d1], near - 2)
    dhidden = launch(dhidden, [d0, d1])
    u0 = grad_half(0, h3, dhidden, "grad_up")
    u0.keep, u0.send = land((u0.keep, u0.send), [d0, d1])
    down_sum = merged([d0, d1])
    dhidden = launch(dhidden, [u0, down_sum])
    u1 = grad_half(1, h3, dhidden, "grad_up")
    u1.keep, u1.send = land((u1.keep, u1.send), [u0, down_sum])
    dmixed = launch(dmixed, [u1])
    keep, send = weight_grad(
        tables[0], dmixed, [scaled], grid_of, 0, out_weight.shape[0], "grad_out", near=True
    )
    o0 = Scatter(keep, send, steps[0])
    o0.keep, o0.send = land((o0.keep, o0.send), [u1])
    flying = [u0, u1, o0] + ([down_sum] if down_sum.steps else [])
    da = launch(spread(dattended), flying)
    halves, grads, inners = [], [], []
    for n in range(parts):
        *three, inner = attend_back(q, k, v, da, lse, ends, factor, tensor_count, parts, n)
        inners.append(inner)
        if n == 0:
            three = land(three, flying)
            narrow = launch(narrow, [u0, u1])
            block_out = feed_forward(orders, narrow, unit, x, norm_gains, wda, wdb, grid_of)
            block_out = land(block_out, [u0, u1])
            more([u0, u1], near - 2)
            up_sum = merged([u0, u1])
            rows_out = Rows(block_out, micro_count, split, 2)
            three = [collect(one) for one in three]
            three = launch(three, [up_sum, o0])
            flying = [up_sum, o0]
        else:
            three = land(three, flying)
            three, first_out = lax.optimization_barrier((three, rows_out.arrived[0]))
            rows_out.arrived[0] = first_out
            flying = [o0]
            three = launch(three, flying)
        keep, send = weight_grad(tables[n % 2], h1, three, grid_of, 0, part_cols, "grad_qkv", near=True)
        halves.append(Scatter(keep, send, steps[n % 2]))
        grads += three
        halves[-1].keep, halves[-1].send = land((halves[-1].keep, halves[-1].send), flying)
        if n < parts - 1:
            flying = [halves[0], up_sum, o0]
            da = launch(da, flying + [rows_out])
    q_last = halves[-1]
    if parts > 1:
        q_last.keep, q_last.send, rows_out.arrived = lax.optimization_barrier(
            (q_last.keep, q_last.send, rows_out.arrived)
        )
    dresid = launch(dresid, [q_last])
    dresid = land(dresid, [q_last])
    beside = halves + [o0] + ([] if parts > 1 else [rows_out])
    dresid = launch(dresid, beside)
    grad_in, first_sums = input_grad(orders, grads, x, dresid, norm_gains, qkv_chains, grid_of)
    grad_in, first_sums = land((grad_in, first_sums), beside)
    local = heads // split
    if parts == 1:
        head_sums = jnp.sum(inners[0], axis=-1).reshape(-1)
    else:
        shaped = [jnp.sum(one, axis=-1).reshape(tensor_count, -1) for one in inners]
        head_sums = jnp.concatenate(shaped, axis=1).reshape(-1)
    first_head = tensor_rank % split * local
    head_sums = head_sums / lax.dynamic_slice(scale_all, (first_head,), (local,))
    head_all = lax.dynamic_update_slice(jnp.zeros((heads,), F32), head_sums, (first_head,))
    last = jnp.concatenate(
        [jnp.sum(one, axis=0) for one in (first_sums, gain_sums[:8], gain_sums[8:], mid_sums)]
        + [head_all]
    )
    last = Total(last, batch_count, tensor_count)
    rows_back = Rows(grad_in, micro_count, split, 2)
    tail = halves + ([o0] if o0.steps else [])
    launch((), tail + [last])
    last.end()
    launch((), [last])
    land((), tail + [last])
    if parts > 1:
        halves = [merged(halves)]
    sent = rows_back.outgoing()
    tail = [one for one in halves + [o0, last] if one.steps]
    values, sent = lax.optimization_barrier(([one.outgoing() for one in tail], sent))
    for one, value in zip(tail, values):
        one.go(value)
    rows_back.go(sent)
    rows_out.arrived = held(rows_out.arrived, [one.arrived for one in tail])
    for one in tail:
        one.end()
    while last.steps:
        hop([last])
    tail = [one for one in halves + [o0] if one.steps]
    launch((), tail)
    arrived = [one.arrived for one in tail]
    rows_back.arrived = held(rows_back.arrived, arrived)
    last.value = held(last.value, arrived)
    for one in tail:
        one.end()
    rows_out.end()
    rows_back.end()
    block_out, grad_in = rows_out.result, rows_back.result
    d_totals, u_totals, o_totals, q_totals = (
        flush([down_sum]), flush([up_sum]), flush([o0]), flush(halves)
    )
    down_grad = d_totals[0].T
    up_grad = u_totals[0]
    out_grad = o_totals[0].T
    qkv_grad = q_totals[0]
    vector = last.value
    d_totals, u_totals, o_totals, q_totals = (
        flush([d0, d1]), flush([u0, u1]), flush([o0]), flush(halves)
    )
    gains_sum = vector[: 3 * width].reshape(3, width)
    mid_own = lax.dynamic_slice(vector, (3 * width + tensor_rank * local_hidden,), (local_hidden,))
    scale_own = lax.dynamic_slice(
        vector, (3 * width + tensor_count * local_hidden + tensor_rank * local_heads,), (local_heads,)
    )
    return (
        block_out,
        grad_in,
        gains_sum,
        qkv_grad,
        scale_own,
        out_grad,
        up_grad,
        mid_own,
        down_grad,
    )


def solution(mesh):
    in_specs = (
        P(None, ("batch", "tensor"), None),
        P(None, "batch", None),
        P(),
        P(None, "batch", "tensor"),
        P("tensor"),
        P("tensor", "batch"),
        P("batch", "tensor"),
        P("tensor"),
        P("tensor", "batch"),
        P(None, ("batch", "tensor"), None),
    )
    out_specs = (
        P(None, ("batch", "tensor"), None),
        P(None, ("batch", "tensor"), None),
        P(),
        P(None, "batch", "tensor"),
        P("tensor"),
        P("tensor", "batch"),
        P("batch", "tensor"),
        P("tensor"),
        P("tensor", "batch"),
    )
    return jax.shard_map(body, mesh=mesh, in_specs=in_specs, out_specs=out_specs, check_vma=False)
```

```python
import functools
import math

import jax
import jax.numpy as jnp
from jax import lax
from jax.experimental import pallas as pl
from jax.experimental.pallas import tpu as pltpu
from jax.sharding import PartitionSpec as P

eps = 1e-05
SEQ_MOST = 512
F32 = jnp.float32
BF = jnp.bfloat16
ALL = ("batch", "tensor")
GELU_C = math.sqrt(2.0 / math.pi)
GELU_A = 0.044715
STEP = 256


def cost(us):
    return pl.CostEstimate(flops=int(us * 1e9), transcendentals=0, bytes_accessed=1 << 20)


def dotf(a, b, ca, cb):
    return lax.dot_general(a, b, (((ca,), (cb,)), ((), ())), preferred_element_type=F32)


def row_loop(rows, step, fn):
    def one(i, carry):
        fn(pl.multiple_of(i * step, step))
        return carry

    lax.fori_loop(0, rows // step, one, 0)


def normalize(values):
    centred = values - jnp.mean(values, axis=-1, keepdims=True)
    factor = lax.rsqrt(jnp.mean(centred * centred, axis=-1, keepdims=True) + eps)
    return (centred * factor, factor)


def norm_back(unit, factor, grad):
    return factor * (
        grad
        - jnp.mean(grad, axis=-1, keepdims=True)
        - unit * jnp.mean(grad * unit, axis=-1, keepdims=True)
    )


def fold8(values):
    rows, width = values.shape
    return jnp.sum(values.reshape(rows // 8, 8, width), axis=0)


def bits_of(count):
    return count.bit_length() - 1


def gather_steps(batch_count, tensor_count, tensor_first):
    tensor = [("tensor", 1 << k) for k in range(bits_of(tensor_count))]
    plane = [("batch", 2)]
    far = [("batch", 1 << k) for k in reversed(range(2, bits_of(batch_count)))]
    return far + (tensor + plane if tensor_first else plane + tensor) + [("batch", 1)]


def place_table(steps, batch_count, tensor_count):
    batch = jnp.arange(batch_count * tensor_count, dtype=jnp.int32) // tensor_count
    tensor = jnp.arange(batch_count * tensor_count, dtype=jnp.int32) % tensor_count
    batch = jnp.bitwise_xor(batch, lax.axis_index("batch"))
    tensor = jnp.bitwise_xor(tensor, lax.axis_index("tensor"))
    place = jnp.zeros_like(batch)
    for k, (axis, flip) in enumerate(steps):
        apart = (jnp.bitwise_and(batch if axis == "batch" else tensor, flip) != 0).astype(jnp.int32)
        place = place + apart * (1 << k)
    return place


def swap(value, axis, flip):
    count = lax.axis_size(axis)
    return lax.ppermute(value, axis, [(i, i ^ flip) for i in range(count)])


def held(value, after):
    return lax.optimization_barrier((value, after))[0]


class Gather:
    def __init__(self, buffer, steps):
        self.own, self.steps, self.parts = buffer, list(steps), None

    def outgoing(self):
        return self.arrived if len(self.steps) == 1 else self.own

    def go(self, value):
        step = self.steps.pop(0)
        self.arrived = swap(value, *step)
        if not self.steps:
            self.parts[1] = value
        else:
            self.own = value
            if len(self.steps) == 1:
                self.parts = [value, None, swap(value, *self.steps[0]), None]

    def end(self):
        if self.parts is None:
            self.own = jnp.concatenate([self.own, self.arrived], axis=0)
        elif not self.steps:
            self.parts[3] = self.arrived

    def columns(self, start, count, steps):
        return Gather(self.own[..., start : start + count], steps)


class Scatter:
    def __init__(self, keep, send, steps):
        self.keep, self.send, self.steps = keep, send, list(reversed(steps))

    def outgoing(self):
        return (self.send, self.keep)

    def go(self, value):
        send, self.keep = value
        self.arrived = swap(send, *self.steps.pop(0))

    def end(self):
        keep, arrived = self.keep, self.arrived
        half = keep.shape[0] // 2
        if self.steps:
            self.send = (keep[half:].astype(F32) + arrived[half:].astype(F32)).astype(BF)
            self.keep = (keep[:half].astype(F32) + arrived[:half].astype(F32)).astype(BF)
        else:
            self.total = keep[0].astype(F32) + arrived[0].astype(F32)


def merged(chains):
    keep = jnp.concatenate([chain.keep for chain in chains], axis=-1)
    send = jnp.concatenate([chain.send for chain in chains], axis=-1)
    return Scatter(keep, send, list(reversed(chains[0].steps)))


class Total:
    def __init__(self, value, batch_count, tensor_count):
        self.value, self.grid_of = value, (batch_count, tensor_count)
        bits = [(flip, 0) for flip in (1 << k for k in range(2, bits_of(batch_count)))]
        plane = [(2, 0)] + [(0, 1 << k) for k in range(bits_of(tensor_count))]
        self.steps = [[(1, 0)]]
        for group in (plane, bits):
            if len(group) <= 2:
                spans = [(0, 0)]
                for flip in group:
                    spans += [(one[0] ^ flip[0], one[1] ^ flip[1]) for one in spans]
                self.steps.append(spans[1:])
            else:
                self.steps += [[flip] for flip in group]

    def outgoing(self):
        return self.value

    def go(self, value):
        batch_count, tensor_count = self.grid_of
        self.value, self.arrived = value, []
        for batch, tensor in self.steps.pop(0):
            pairs = [
                (b * tensor_count + t, (b ^ batch) * tensor_count + (t ^ tensor))
                for b in range(batch_count)
                for t in range(tensor_count)
            ]
            self.arrived.append(lax.ppermute(value, ALL, pairs))

    def end(self):
        for one in self.arrived:
            self.value = self.value + one


class Rows:
    def __init__(self, value, micro_count, split, cuts=1):
        self.value, self.micro_count, self.split, self.cuts = value, micro_count, split, cuts
        self.taken = value.ndim == 3
        self.steps = [None]
        self.rank = lax.axis_index("tensor")

    def pieces(self):
        if self.taken:
            return self.value
        return self.value.reshape(self.micro_count, -1, self.value.shape[1])

    def outgoing(self):
        if self.split > 1:
            return []
        sent = []
        for flip in range(1, self.micro_count):
            one = lax.dynamic_index_in_dim(self.pieces(), lax.bitwise_xor(self.rank, flip), 0)
            sent += [one[:, n * (one.shape[1] // self.cuts) :][:, : one.shape[1] // self.cuts] for n in range(self.cuts)]
        return sent

    def go(self, value):
        self.steps = []
        if self.split == 1:
            self.arrived = [
                swap(one, "tensor", n // self.cuts + 1) for n, one in enumerate(value)
            ]
        else:
            self.arrived = [
                lax.all_gather(self.value, "tensor", axis=1 if self.taken else 0, tiled=True)
            ]

    def end(self):
        if self.split == 1:
            pieces = self.pieces()
            out = lax.dynamic_update_slice(
                jnp.zeros_like(pieces),
                lax.dynamic_index_in_dim(pieces, self.rank, 0),
                (self.rank, 0, 0),
            )
            for n, one in enumerate(self.arrived):
                other = lax.bitwise_xor(self.rank, n // self.cuts + 1)
                out = lax.dynamic_update_slice(
                    out, one, (other, n % self.cuts * one.shape[1], 0)
                )
            self.result = out.reshape(-1, out.shape[2]) if self.taken else out
            return
        whole = self.arrived[0]
        width = whole.shape[-1]
        if self.taken:
            rows = self.value.shape[0] * self.value.shape[1]
            start = (self.rank // self.split, self.rank % self.split * rows, 0)
            self.result = lax.dynamic_slice(whole, start, (1, rows, width))[0]
        else:
            own = self.value.shape[0] // self.micro_count
            whole = whole.reshape(self.micro_count, -1, width)
            start = (0, self.rank * own, 0)
            self.result = lax.dynamic_slice(whole, start, (self.micro_count, own, width))


def launch(inputs, chains):
    inputs, values = lax.optimization_barrier((inputs, [chain.outgoing() for chain in chains]))
    for chain, value in zip(chains, values):
        chain.go(value)
    return inputs


def land(inputs, chains):
    inputs, values = lax.optimization_barrier((inputs, [chain.arrived for chain in chains]))
    for chain, value in zip(chains, values):
        chain.arrived = value
        chain.end()
    return inputs


def hop(chains, after=()):
    launch(after, chains)
    for chain in chains:
        chain.end()


def columns(parts, order_ref, batch_count, tensor_count, t, start, count, lead=None):
    for first, width, which, w_ref in parts:
        if first <= start < first + width:
            break
    pieces = []
    for b in range(batch_count):
        p = order_ref[(which * batch_count + b) * tensor_count + t]
        here = pl.ds(start - first, count)
        pieces.append(w_ref[p, :, here] if lead is None else w_ref[p, lead, :, here])
    return jnp.concatenate(pieces, axis=0)


def weights(*refs):
    out, first = [], 0
    for n, ref in enumerate(refs):
        out.append((first, ref.shape[-1], n % 2, ref))
        first += ref.shape[-1]
    return out


HBM = pl.BlockSpec(memory_space=pltpu.HBM)


def whole(chain):
    part = chain.parts[0].shape
    return pltpu.VMEM((4 * part[0],) + part[1:], BF)


def in_hbm(*values):
    return [pltpu.with_memory_space_constraint(value, pltpu.HBM) for value in values]


def parts_of(chains):
    return in_hbm(*[part for chain in chains for part in chain.parts])


def load_parts(refs, w, sem):
    count = w.shape[0] // 4
    for n in range(4):
        pltpu.make_async_copy(refs[n], w.at[pl.ds(n * count, count)], sem).start()


def wait_whole(w, sem):
    pltpu.make_async_copy(w, w, sem).wait()


def qkv_kernel(grid_of, factor, count, order_ref, x_ref, gain_ref, *refs):
    batch_count, tensor_count = grid_of
    w_hbm, refs = refs[: 4 * count], refs[4 * count :]
    turned_ref, q_ref, k_ref, v_ref, h1_ref = refs[:5]
    w_refs, sem = refs[5:-1], refs[-1]
    first = pl.program_id(0) == 0

    @pl.when(first)
    def _():
        for n in range(count):
            load_parts(w_hbm[4 * n : 4 * n + 4], w_refs[n], sem.at[n])

    def chunk(r):
        here = pl.ds(r, STEP)
        unit, _ = normalize(x_ref[here, :].astype(F32))
        h1_ref[here, :] = (unit * gain_ref[0:1, :]).astype(BF)

    row_loop(x_ref.shape[0], STEP, chunk)
    turned_ref[...] = h1_ref[...].T

    parts = weights(*w_refs)
    cols = sum(part[1] for part in parts)
    for n, (start, width, _, _) in enumerate(parts):

        @pl.when(first)
        def _(n=n):
            wait_whole(w_refs[n], sem.at[n])

        for c, out in enumerate((q_ref, k_ref, v_ref)):
            for t in range(tensor_count):
                w = columns(parts, order_ref, batch_count, tensor_count, t, start, width, lead=c)
                value = dotf(h1_ref[...], w, 1, 0).astype(BF)
                here = slice(t * cols + start, t * cols + start + width)
                out[:, here] = value * BF(factor) if c == 0 else value


def project(orders, x, gains, chains, grid_of, factor):
    rows, width = x.shape
    block = min(256, rows)
    row = pl.BlockSpec((block, width), lambda i, e: (i, 0))
    return pl.pallas_call(
        functools.partial(qkv_kernel, grid_of, factor, len(chains)),
        grid_spec=pltpu.PrefetchScalarGridSpec(
            num_scalar_prefetch=1,
            grid=(rows // block,),
            in_specs=[row, pl.BlockSpec((3, width), lambda i, e: (0, 0))]
            + [HBM] * (4 * len(chains)),
            out_specs=[pl.BlockSpec((width, block), lambda i, e: (0, i))] + [row] * 3,
            scratch_shapes=[pltpu.VMEM((block, width), BF)]
            + [whole(chain) for chain in chains]
            + [pltpu.SemaphoreType.DMA((len(chains),))],
        ),
        out_shape=[pltpu.HBM((width, rows), BF)]
        + [pltpu.HBM((rows, width), BF)] * 3,
        compiler_params=pltpu.CompilerParams(vmem_limit_bytes=24 << 20),
        cost_estimate=cost(13),
        name="project",
    )(orders, *in_hbm(x), gains, *parts_of(chains))


def spans(rows, block):
    return [
        (first, max(0, (first - SEQ_MOST + 1) // block * block), first + block)
        for first in range(0, rows, block)
    ]


def fill_bias(ends_ref, bias, parts, block):
    for (first, low, high), ref in zip(parts, bias):
        shape = (high - low, block)
        keys = low + lax.broadcasted_iota(jnp.int32, shape, 0)
        queries = first + lax.broadcasted_iota(jnp.int32, shape, 1)
        start = jnp.zeros(shape, jnp.int32)
        for n in range(ends_ref.shape[0]):
            end = ends_ref[n]
            start = jnp.where(queries >= end, end, start)
        ref[...] = jnp.where((keys <= queries) & (keys >= start), 0.0, -1e30).astype(F32)


def attend_kernel(rows, block, ends_ref, q_ref, k_ref, v_ref, scale_ref, o_ref, lse_ref, *bias):
    parts = spans(rows, block)

    @pl.when(pl.program_id(0) == 0)
    def _():
        fill_bias(ends_ref, bias, parts, block)

    lower = lax.broadcasted_iota(jnp.int32, (1, 128), 1) < 64
    for n, (first, low, high) in enumerate(parts):
        q = q_ref[pl.ds(first, block), :]
        heads = []
        for h in range(2):
            own = jnp.where(lower if h == 0 else ~lower, q, jnp.zeros_like(q))
            s = dotf(k_ref[pl.ds(low, high - low), :], own, 1, 1) + bias[n][...]
            most = jnp.max(s, axis=0, keepdims=True)
            p = jnp.exp(s - most)
            total = jnp.sum(p, axis=0, keepdims=True)
            probs = (p * (1.0 / total)).astype(BF)
            lse_ref[0, pl.ds(h, 1), pl.ds(first, block)] = most + jnp.log(total)
            heads.append(dotf(probs, v_ref[pl.ds(low, high - low), :], 0, 0))
        out = jnp.where(lower, heads[0], heads[1]) * scale_ref[...]
        o_ref[pl.ds(first, block), :] = out.astype(BF)


def attend_back_kernel(
    rows, block, factor, ends_ref, q_ref, k_ref, v_ref, da_ref, lse_ref,
    dq_ref, dk_ref, dv_ref, inner_ref, dk_acc, dv_acc, *bias
):
    parts = spans(rows, block)

    @pl.when(pl.program_id(0) == 0)
    def _():
        fill_bias(ends_ref, bias, parts, block)

    lower = lax.broadcasted_iota(jnp.int32, (1, 128), 1) < 64
    dk_acc[...] = jnp.zeros_like(dk_acc)
    dv_acc[...] = jnp.zeros_like(dv_acc)
    for n, (first, low, high) in enumerate(parts):
        here = pl.ds(first, block)
        keys = pl.ds(low, high - low)
        q, da, k, v = q_ref[here, :], da_ref[here, :], k_ref[keys, :], v_ref[keys, :]
        probs, scores, q_own, da_own, k_own = [], [], [], [], []
        for h in range(2):
            mask = lower if h == 0 else ~lower
            q_own.append(jnp.where(mask, q, jnp.zeros_like(q)))
            da_own.append(jnp.where(mask, da, jnp.zeros_like(da)))
            k_own.append(jnp.where(mask, k, jnp.zeros_like(k)))
            s = dotf(k, q_own[h], 1, 1) + bias[n][...]
            p = jnp.exp(s - lse_ref[0, pl.ds(h, 1), here])
            product = p * dotf(v, da_own[h], 1, 1)
            inner = jnp.sum(product, axis=0, keepdims=True)
            inner_ref[0, pl.ds(h, 1), here] = inner
            scores.append((product - p * inner).astype(BF))
            probs.append(p.astype(BF))
        dv_acc[keys, :] += dotf(
            jnp.concatenate(probs, axis=1), jnp.concatenate(da_own, axis=0), 1, 0
        )
        dk_acc[keys, :] += dotf(
            jnp.concatenate(scores, axis=1), jnp.concatenate(q_own, axis=0), 1, 0
        )
        dq = dotf(jnp.concatenate(scores, axis=0), jnp.concatenate(k_own, axis=0), 0, 0)
        dq_ref[here, :] = (dq * factor).astype(BF)
    dk_ref[...] = dk_acc[...].astype(BF)
    dv_ref[...] = dv_acc[...].astype(BF)


def bias_shapes(rows, block):
    return [pltpu.VMEM((high - low, block), F32) for _, low, high in spans(rows, block)]


def pair_of(pairs, tensor_count, parts, n):
    if parts == 1:
        return pairs, lambda i: i
    per_tensor = pairs // tensor_count
    per = per_tensor // parts
    return pairs // parts, lambda i: i // per * per_tensor + n * per + i % per


def attend(q, k, v, scale_row, ends, tensor_count, parts, n, before_out, before_lse):
    rows, width = q.shape
    block = min(256, rows)
    pairs = width // 128
    steps, pair = pair_of(pairs, tensor_count, parts, n)
    col = pl.BlockSpec((rows, 128), lambda i, e: (0, pair(i)))
    earlier = [] if before_out is None else [before_out, before_lse]
    count = len(earlier)

    def kernel(ends_ref, q_ref, k_ref, v_ref, scale_ref, *refs):
        attend_kernel(rows, block, ends_ref, q_ref, k_ref, v_ref, scale_ref, *refs[count:])

    return pl.pallas_call(
        kernel,
        grid_spec=pltpu.PrefetchScalarGridSpec(
            num_scalar_prefetch=1,
            grid=(steps,),
            in_specs=[col, col, col, pl.BlockSpec((1, 128), lambda i, e: (0, pair(i)))]
            + [HBM] * count,
            out_specs=[col, pl.BlockSpec((1, 2, rows), lambda i, e: (pair(i), 0, 0))],
            scratch_shapes=bias_shapes(rows, block),
        ),
        out_shape=[
            pltpu.HBM((rows, width), BF),
            pltpu.HBM((pairs, 2, rows), F32),
        ],
        input_output_aliases={5 + j: j for j in range(count)},
        compiler_params=pltpu.CompilerParams(vmem_limit_bytes=32 << 20),
        cost_estimate=cost(24 / parts),
        name="attend",
    )(ends, *in_hbm(q, k, v), scale_row, *earlier)


def attend_back(q, k, v, da, lse, ends, factor, tensor_count, parts, n):
    rows, width = q.shape
    block = min(256, rows)
    pairs = width // 128
    steps, pair = pair_of(pairs, tensor_count, parts, n)
    col = pl.BlockSpec((rows, 128), lambda i, e: (0, pair(i)))
    out_col = pl.BlockSpec((rows, 128), lambda i, e: (0, i))
    out = pltpu.HBM((rows, width // parts), BF)
    return pl.pallas_call(
        functools.partial(attend_back_kernel, rows, block, factor),
        grid_spec=pltpu.PrefetchScalarGridSpec(
            num_scalar_prefetch=1,
            grid=(steps,),
            in_specs=[col] * 4 + [pl.BlockSpec((1, 2, rows), lambda i, e: (pair(i), 0, 0))],
            out_specs=[out_col] * 3 + [pl.BlockSpec((1, 2, rows), lambda i, e: (i, 0, 0))],
            scratch_shapes=[pltpu.VMEM((rows, 128), F32)] * 2 + bias_shapes(rows, block),
        ),
        out_shape=[out, out, out, pltpu.HBM((steps, 2, rows), F32)],
        compiler_params=pltpu.CompilerParams(vmem_limit_bytes=40 << 20),
        cost_estimate=cost(42 / parts),
        name="attend_back",
    )(ends, *in_hbm(q, k, v, da), lse)


def put_stats(ref, here, values):
    lane = lax.broadcasted_iota(jnp.int32, (1, 128), 1)
    out = values[-1]
    for n in reversed(range(len(values) - 1)):
        out = jnp.where(lane < 16 * (n + 1), values[n], out)
    ref[here, :] = jnp.broadcast_to(out, (values[0].shape[0], 128))


def hidden_kernel(
    grid_of, order_ref, scaled_ref, x_ref, gain_ref, mid_ref, a0, a1, a2, a3, b0, b1, b2, b3,
    unit_ref, turned_ref, hidden_ref, narrow_ref, stat_ref, act, norm_stat, wide, h3_ref, wa, wb, sem
):
    batch_count, tensor_count = grid_of
    block, width = x_ref.shape
    total = hidden_ref.shape[1]
    up_cols = total // tensor_count
    out_cols = width // tensor_count
    get = functools.partial(columns, weights(wa, wb), order_ref, batch_count, tensor_count)
    first = pl.program_id(0) == 0

    @pl.when(first)
    def _():
        load_parts((a0, a1, a2, a3), wa, sem.at[0])
        load_parts((b0, b1, b2, b3), wb, sem.at[1])
        wait_whole(wa, sem.at[0])

    mixed = None
    for t in range(tensor_count):
        part = dotf(scaled_ref[:, t * out_cols : (t + 1) * out_cols], get(t, 0, out_cols), 1, 1)
        mixed = part if mixed is None else mixed + part
    wide[...] = mixed

    def norms(r):
        here = pl.ds(r, STEP)
        unit, factor = normalize(wide[here, :])
        unit_ref[here, :] = unit
        resid = x_ref[here, :].astype(F32) + unit * gain_ref[1:2, :]
        mean3 = jnp.mean(resid, axis=-1, keepdims=True)
        centred = resid - mean3
        factor3 = lax.rsqrt(jnp.mean(centred * centred, axis=-1, keepdims=True) + eps)
        h3_ref[here, :] = (centred * factor3 * gain_ref[2:3, :]).astype(BF)
        put_stats(norm_stat, here, [factor, mean3, factor3])

    row_loop(block, STEP, norms)
    turned_ref[...] = h3_ref[...].T

    @pl.when(first)
    def _():
        wait_whole(wb, sem.at[1])

    chunk = min(256, up_cols // 2)
    sums = jnp.zeros((block, 128), F32)
    squares = jnp.zeros((block, 128), F32)
    for c in range(total // chunk):
        t, off = divmod(c * chunk, up_cols)
        h = dotf(h3_ref[...], get(t, out_cols + off, chunk), 1, 0)
        hidden_ref[:, c * chunk : (c + 1) * chunk] = h
        half = 0.5 * jnp.tanh(h * (GELU_C + (GELU_C * GELU_A) * (h * h))) + 0.5
        a = h * half
        act[:, c * chunk : (c + 1) * chunk] = a
        for j in range(chunk // 128):
            piece = a[:, j * 128 : (j + 1) * 128]
            sums += piece
            squares += piece * piece
    mean = jnp.sum(sums, axis=1, keepdims=True) / total
    spread = jnp.sum(squares, axis=1, keepdims=True) / total - mean * mean
    scale = lax.rsqrt(spread + eps)
    before = norm_stat[...]
    put_stats(stat_ref, slice(None), [mean, scale, before[:, 0:1], before[:, 16:17], before[:, 32:33]])

    def narrow(r):
        here = pl.ds(r, STEP)
        m = stat_ref[here, 0:1]
        s = stat_ref[here, 16:17]
        narrow_ref[here, :] = ((act[here, :] - m) * s * mid_ref[...]).astype(BF)

    row_loop(block, STEP, narrow)


def hidden_forward(orders, scaled, x, gains, mid_row, wa, wb, grid_of, share, earlier):
    rows, width = x.shape
    block = min(256, rows)
    total = mid_row.shape[1]
    blocks = rows // block // share[1]
    first = share[0] * blocks
    row = pl.BlockSpec((block, width), lambda i, e: (first + i, 0))
    wide = pl.BlockSpec((block, total), lambda i, e: (first + i, 0))

    def kernel(order_ref, *refs):
        hidden_kernel(grid_of, order_ref, *refs[:12], *refs[12 + len(earlier) :])

    return pl.pallas_call(
        kernel,
        grid_spec=pltpu.PrefetchScalarGridSpec(
            num_scalar_prefetch=1,
            grid=(blocks,),
            in_specs=[
                row,
                row,
                pl.BlockSpec((3, width), lambda i, e: (0, 0)),
                pl.BlockSpec((1, total), lambda i, e: (0, 0)),
            ]
            + [HBM] * (8 + len(earlier)),
            out_specs=[row, pl.BlockSpec((width, block), lambda i, e: (0, first + i)), wide, wide]
            + [pl.BlockSpec((block, 128), lambda i, e: (first + i, 0))],
            scratch_shapes=[
                pltpu.VMEM((block, total), F32),
                pltpu.VMEM((block, 128), F32),
                pltpu.VMEM((block, width), F32),
                pltpu.VMEM((block, width), BF),
                whole(wa),
                whole(wb),
                pltpu.SemaphoreType.DMA((2,)),
            ],
        ),
        out_shape=[
            pltpu.HBM((rows, width), F32),
            pltpu.HBM((width, rows), BF),
            pltpu.HBM((rows, total), F32),
            pltpu.HBM((rows, total), BF),
            pltpu.HBM((rows, 128), F32),
        ],
        input_output_aliases={13 + n: n for n in range(len(earlier))},
        compiler_params=pltpu.CompilerParams(vmem_limit_bytes=44 << 20),
        cost_estimate=cost(30 / share[1]),
        name="hidden_forward",
    )(orders, *in_hbm(scaled, x), gains, mid_row, *parts_of((wa, wb)), *earlier)


def feed_kernel(grid_of, order_ref, narrow_ref, unit_ref, x_ref, gain_ref, a0, a1, a2, a3, b0, b1, b2, b3, out_ref, wa, wb, sem):
    batch_count, tensor_count = grid_of
    up_cols = narrow_ref.shape[1] // tensor_count
    parts = weights(wa, wb)

    @pl.when(pl.program_id(0) == 0)
    def _():
        load_parts((a0, a1, a2, a3), wa, sem.at[0])
        load_parts((b0, b1, b2, b3), wb, sem.at[1])

    out = x_ref[...].astype(F32) + unit_ref[...] * gain_ref[1:2, :]
    for n, (start, width, _, w_ref) in enumerate(parts):

        @pl.when(pl.program_id(0) == 0)
        def _(n=n, w_ref=w_ref):
            wait_whole(w_ref, sem.at[n])

        for t in range(tensor_count):
            w = columns(parts, order_ref, batch_count, tensor_count, t, start, width)
            off = t * up_cols + start
            out += dotf(narrow_ref[:, off : off + width], w, 1, 1)
    out_ref[...] = out.astype(BF)


def feed_forward(orders, narrow, unit, x, gains, wa, wb, grid_of):
    rows, width = x.shape
    block = min(256, rows)
    total = narrow.shape[1]
    row = pl.BlockSpec((block, width), lambda i, e: (i, 0))
    return pl.pallas_call(
        functools.partial(feed_kernel, grid_of),
        grid_spec=pltpu.PrefetchScalarGridSpec(
            num_scalar_prefetch=1,
            grid=(rows // block,),
            in_specs=[pl.BlockSpec((block, total), lambda i, e: (i, 0)), row, row]
            + [pl.BlockSpec((3, width), lambda i, e: (0, 0))]
            + [HBM] * 8,
            out_specs=row,
            scratch_shapes=[whole(wa), whole(wb), pltpu.SemaphoreType.DMA((2,))],
        ),
        out_shape=pltpu.HBM((rows, width), BF),
        compiler_params=pltpu.CompilerParams(vmem_limit_bytes=28 << 20),
        cost_estimate=cost(14),
        name="feed_forward",
    )(orders, *in_hbm(narrow, unit, x), gains, *parts_of((wa, wb)))


def back_kernel(
    grid_of, order_ref, hidden_ref, stat_ref, unit_ref, x_ref, cot_ref, gain_ref, mid_ref,
    scale_ref, da0, da1, da2, da3, db0, db1, db2, db3, a0, a1, a2, a3, b0, b1, b2, b3, dhidden_ref, dresid_ref, turned_ref, dattended_ref,
    gains_ref, dmid_ref, grad, unit_s, slope_s, wide, dmixed_ref, wda, wdb, wa, wb, sem
):
    batch_count, tensor_count = grid_of
    block, width = x_ref.shape
    total = hidden_ref.shape[1]
    up_cols = total // tensor_count
    out_cols = width // tensor_count
    get = functools.partial(columns, weights(wa, wb), order_ref, batch_count, tensor_count)
    get_down = functools.partial(columns, weights(wda, wdb), order_ref, batch_count, tensor_count)
    first = pl.program_id(0) == 0

    @pl.when(first)
    def _():
        load_parts((da0, da1, da2, da3), wda, sem.at[0])
        load_parts((db0, db1, db2, db3), wdb, sem.at[1])
        load_parts((a0, a1, a2, a3), wa, sem.at[2])
        load_parts((b0, b1, b2, b3), wb, sem.at[3])
        gains_ref[...] = jnp.zeros_like(gains_ref)
        dmid_ref[...] = jnp.zeros_like(dmid_ref)
        wait_whole(wda, sem.at[0])

    chunk = min(256, up_cols // 2)
    mean = stat_ref[:, 0:1]
    scale = stat_ref[:, 16:17]
    back_sum = jnp.zeros((block, 128), F32)
    back_inner = jnp.zeros((block, 128), F32)
    turns = [divmod(c * chunk, up_cols) for c in range(total // chunk)]
    turns.sort(key=lambda turn: turn[1] >= wda.shape[2])
    waited = False
    for t, off in turns:
        if off >= wda.shape[2] and not waited:
            waited = True

            @pl.when(first)
            def _():
                wait_whole(wdb, sem.at[1])

        here = slice(t * up_cols + off, t * up_cols + off + chunk)
        dn = dotf(cot_ref[...], get_down(t, off, chunk), 1, 0)
        h = hidden_ref[:, here]
        square = h * h
        half = 0.5 * jnp.tanh(h * (GELU_C + (GELU_C * GELU_A) * square)) + 0.5
        a = h * half
        slope_s[:, here] = half + a * (1.0 - half) * (
            2.0 * GELU_C + (6.0 * GELU_C * GELU_A) * square
        )
        unit = (a - mean) * scale
        unit_s[:, here] = unit
        dmid_ref[:, here] += fold8(dn * unit)
        g = dn * mid_ref[:, here]
        grad[:, here] = g
        inner = g * unit
        for j in range(chunk // 128):
            back_sum += g[:, j * 128 : (j + 1) * 128]
            back_inner += inner[:, j * 128 : (j + 1) * 128]
    sum_col = jnp.sum(back_sum, axis=1, keepdims=True) / total
    inner_col = jnp.sum(back_inner, axis=1, keepdims=True) / total

    @pl.when(first)
    def _():
        wait_whole(wa, sem.at[2])
        wait_whole(wb, sem.at[3])

    dh3 = None
    for c in range(total // chunk):
        t, off = divmod(c * chunk, up_cols)
        here = slice(c * chunk, (c + 1) * chunk)
        act_grad = scale * (grad[:, here] - sum_col - unit_s[:, here] * inner_col)
        dhidden = (act_grad * slope_s[:, here]).astype(BF)
        dhidden_ref[:, here] = dhidden
        part = dotf(dhidden, get(t, out_cols + off, chunk), 1, 1)
        dh3 = part if dh3 is None else dh3 + part
    wide[...] = dh3

    def back(r):
        here = pl.ds(r, STEP)
        unit = unit_ref[here, :]
        resid = x_ref[here, :].astype(F32) + unit * gain_ref[1:2, :]
        unit3 = (resid - stat_ref[here, 48:49]) * stat_ref[here, 64:65]
        third = wide[here, :]
        gains_ref[8:16, :] += fold8(third * unit3)
        dresid = cot_ref[here, :].astype(F32) + norm_back(
            unit3, stat_ref[here, 64:65], third * gain_ref[2:3, :]
        )
        dresid_ref[here, :] = dresid
        gains_ref[0:8, :] += fold8(dresid * unit)
        dmixed = norm_back(unit, stat_ref[here, 32:33], dresid * gain_ref[1:2, :])
        dmixed_ref[here, :] = dmixed.astype(BF)

    row_loop(block, STEP, back)
    turned_ref[...] = dmixed_ref[...].T
    for t in range(tensor_count):
        here = slice(t * out_cols, (t + 1) * out_cols)
        dscaled = dotf(dmixed_ref[...], get(t, 0, out_cols), 1, 0)
        dattended_ref[:, here] = (dscaled * scale_ref[:, here]).astype(BF)


def feed_back(orders, hidden, stat, unit, x, cot, gains, mid_row, scale_row, wda, wdb, wa, wb, grid_of):
    rows, width = x.shape
    block = min(256, rows)
    total = mid_row.shape[1]
    row = pl.BlockSpec((block, width), lambda i, e: (i, 0))
    wide = pl.BlockSpec((block, total), lambda i, e: (i, 0))
    return pl.pallas_call(
        functools.partial(back_kernel, grid_of),
        grid_spec=pltpu.PrefetchScalarGridSpec(
            num_scalar_prefetch=1,
            grid=(rows // block,),
            in_specs=[
                wide,
                pl.BlockSpec((block, 128), lambda i, e: (i, 0)),
                row,
                row,
                row,
                pl.BlockSpec((3, width), lambda i, e: (0, 0)),
                pl.BlockSpec((1, total), lambda i, e: (0, 0)),
                pl.BlockSpec((1, width), lambda i, e: (0, 0)),
            ]
            + [HBM] * 16,
            out_specs=[
                wide,
                row,
                pl.BlockSpec((width, block), lambda i, e: (0, i)),
                row,
                pl.BlockSpec((16, width), lambda i, e: (0, 0)),
                pl.BlockSpec((8, total), lambda i, e: (0, 0)),
            ],
            scratch_shapes=[
                pltpu.VMEM((block, total), F32),
                pltpu.VMEM((block, total), F32),
                pltpu.VMEM((block, total), F32),
                pltpu.VMEM((block, width), F32),
                pltpu.VMEM((block, width), BF),
            ]
            + [whole(chain) for chain in (wda, wdb, wa, wb)]
            + [pltpu.SemaphoreType.DMA((4,))],
        ),
        out_shape=[
            pltpu.HBM((rows, total), BF),
            pltpu.HBM((rows, width), F32),
            pltpu.HBM((width, rows), BF),
            pltpu.HBM((rows, width), BF),
            pltpu.HBM((16, width), F32),
            pltpu.HBM((8, total), F32),
        ],
        compiler_params=pltpu.CompilerParams(vmem_limit_bytes=60 << 20),
        cost_estimate=cost(60),
        name="feed_back",
    )(
        orders, *in_hbm(hidden, stat, unit, x, cot), gains, mid_row, scale_row,
        *parts_of((wda, wdb, wa, wb)),
    )


def grad_kernel(grid_of, count, turn, chunk, order_ref, a_ref, *refs):
    batch_count, tensor_count = grid_of
    b_refs, keep_ref, send_ref = refs[:count], refs[count], refs[count + 1]
    tensor = pl.program_id(1)
    if turn:
        turned = refs[count + 2]

        @pl.when((pl.program_id(0) == 0) & (tensor == 0))
        def _():
            turned[...] = a_ref[...].T

        a_ref = turned
    half = batch_count * tensor_count // 2
    height = keep_ref.shape[-2]
    second = order_ref[0] >= half
    for c, b_ref in enumerate(b_refs):
        acc = dotf(a_ref[...], b_ref[...], 1, 0).astype(BF)
        for core in range(2):

            @pl.when(second if core else jnp.logical_not(second))
            def _(acc=acc, core=core, c=c):
                for b in range(batch_count):
                    place = lax.bitwise_and(order_ref[b * tensor_count + tensor], half - 1)
                    ref = keep_ref if b % 2 == core else send_ref
                    at = (place,) if count == 1 else (place, c)
                    if chunk:
                        start = pl.multiple_of(pl.program_id(0) * chunk, chunk)
                        at += (slice(None), pl.ds(start, chunk))
                    ref[at] = acc[b * height : (b + 1) * height]


def weight_grad(order, a, bs, grid_of, start, cols, name, turn=False, near=False):
    batch_count, tensor_count = grid_of
    width, rows = a.shape[::-1] if turn else a.shape
    part = bs[0].shape[1] // tensor_count
    chunk = min(512, cols)
    per = part // chunk
    height = width // batch_count
    count = len(bs)
    lead = (batch_count * tensor_count // 2,) + (() if count == 1 else (count,)) + (height,)
    zeros = (0,) * len(lead)
    if near:
        out_spec = pl.BlockSpec(memory_space=pltpu.VMEM)
        out = pltpu.VMEM(lead + (cols,), BF)
    else:
        out_spec = pl.BlockSpec(lead + (chunk,), lambda i, t, e: zeros + (i,))
        out = pltpu.HBM(lead + (cols,), BF)
    b_spec = pl.BlockSpec((rows, chunk), lambda i, t, e: (0, t * per + start // chunk + i))
    return pl.pallas_call(
        functools.partial(grad_kernel, grid_of, count, turn, chunk if near else None),
        grid_spec=pltpu.PrefetchScalarGridSpec(
            num_scalar_prefetch=1,
            grid=(cols // chunk, tensor_count),
            in_specs=[pl.BlockSpec(a.shape, lambda i, t, e: (0, 0))] + [b_spec] * count,
            out_specs=[out_spec, out_spec],
            scratch_shapes=[pltpu.VMEM((width, rows), BF)] if turn else [],
        ),
        out_shape=[out, out],
        compiler_params=pltpu.CompilerParams(vmem_limit_bytes=36 << 20),
        cost_estimate=cost(2.4 * count * cols * tensor_count / 1024),
        name=name,
    )(order, *in_hbm(a, *bs))


def input_kernel(grid_of, count, order_ref, *refs):
    batch_count, tensor_count = grid_of
    grads, refs = refs[: 3 * count], refs[3 * count :]
    x_ref, dresid_ref, gain_ref = refs[:3]
    w_hbm, refs = refs[3 : 3 + 4 * count], refs[3 + 4 * count :]
    out_ref, dgain_ref, wide = refs[:3]
    w_refs, sem = refs[3:-1], refs[-1]
    first = pl.program_id(0) == 0

    @pl.when(first)
    def _():
        for n in range(count):
            load_parts(w_hbm[4 * n : 4 * n + 4], w_refs[n], sem.at[n])
        dgain_ref[...] = jnp.zeros_like(dgain_ref)

    parts = weights(*w_refs)
    total = None
    for n, (start, width, _, _) in enumerate(parts):

        @pl.when(first)
        def _(n=n):
            wait_whole(w_refs[n], sem.at[n])

        for c in range(3):
            for t in range(tensor_count):
                w = columns(parts, order_ref, batch_count, tensor_count, t, start, width, lead=c)
                part = dotf(grads[3 * n + c][:, t * width : (t + 1) * width], w, 1, 1)
                total = part if total is None else total + part
    wide[...] = total

    def back(r):
        here = pl.ds(r, STEP)
        unit, factor = normalize(x_ref[here, :].astype(F32))
        grad = wide[here, :]
        dgain_ref[...] += fold8(grad * unit)
        out = dresid_ref[here, :] + norm_back(unit, factor, grad * gain_ref[0:1, :])
        out_ref[here, :] = out.astype(BF)

    row_loop(x_ref.shape[0], STEP, back)


def input_grad(orders, grads, x, dresid, gains, chains, grid_of):
    rows, width = x.shape
    block = min(256, rows)
    row = pl.BlockSpec((block, width), lambda i, e: (i, 0))
    part = pl.BlockSpec((block, width // len(chains)), lambda i, e: (i, 0))
    return pl.pallas_call(
        functools.partial(input_kernel, grid_of, len(chains)),
        grid_spec=pltpu.PrefetchScalarGridSpec(
            num_scalar_prefetch=1,
            grid=(rows // block,),
            in_specs=[part] * len(grads)
            + [row, row, pl.BlockSpec((3, width), lambda i, e: (0, 0))]
            + [HBM] * (4 * len(chains)),
            out_specs=[row, pl.BlockSpec((8, width), lambda i, e: (0, 0))],
            scratch_shapes=[pltpu.VMEM((block, width), F32)]
            + [whole(chain) for chain in chains]
            + [pltpu.SemaphoreType.DMA((len(chains),))],
        ),
        out_shape=[
            pltpu.HBM((rows, width), BF),
            pltpu.HBM((8, width), F32),
        ],
        compiler_params=pltpu.CompilerParams(vmem_limit_bytes=32 << 20),
        cost_estimate=cost(15),
        name="input_grad",
    )(orders, *in_hbm(*grads, x, dresid), gains, *parts_of(chains))


def gather_vector(value, tensor_count):
    rank = lax.axis_index("tensor")
    out = jnp.zeros((tensor_count,) + value.shape, value.dtype)
    for flip in range(tensor_count):
        part = value if flip == 0 else swap(value, "tensor", flip)
        out = lax.dynamic_update_slice(out, part[None], (lax.bitwise_xor(rank, flip), 0))
    return out


def body(
    block_in,
    lengths,
    norm_gains,
    qkv_weight,
    head_scale,
    out_weight,
    up_weight,
    mid_gain,
    down_weight,
    cotangent,
):
    tensor_count = lax.axis_size("tensor")
    batch_count = lax.axis_size("batch")
    tensor_rank = lax.axis_index("tensor")
    batch_rank = lax.axis_index("batch")
    micro_count, own_rows, width = block_in.shape
    if tensor_count % micro_count:
        raise NotImplementedError
    split = tensor_count // micro_count
    micro = tensor_rank // split
    local_heads = head_scale.shape[0]
    heads = local_heads * tensor_count
    head_size = width // heads
    local_hidden = mid_gain.shape[0]
    factor = head_size ** (-0.5)
    grid_of = (batch_count, tensor_count)
    half_cols = local_hidden // 2
    qkv_cols = width // tensor_count
    parts = 2 if qkv_cols % 256 == 0 and split == 1 else 1
    steps = [gather_steps(batch_count, tensor_count, first) for first in (True, False)]
    tables = [place_table(one, batch_count, tensor_count) for one in steps]
    orders = jnp.concatenate(tables)
    far = len(steps[0]) - 2 - bits_of(tensor_count)
    near = bits_of(tensor_count) + 1

    def more(chains, count):
        for _ in range(count):
            hop(chains)

    part_cols = qkv_cols // parts
    up_chunk = min(256, local_hidden // 2)
    out_cols = out_weight.shape[0]
    cut = out_cols + ((local_hidden - out_cols) // 2) // up_chunk * up_chunk
    rows_in = Rows(block_in, micro_count, split)
    qkv = Gather(qkv_weight[None], steps[0])
    launch((), [rows_in, qkv])
    qkv.end()
    for _ in range(far - 1):
        hop([qkv])
    qkv_chains = [
        qkv.columns(n * part_cols, part_cols, steps[n % 2][far:]) for n in range(parts)
    ]
    launch(rows_in.arrived, qkv_chains)
    vectors = gather_vector(
        held(jnp.concatenate([mid_gain, head_scale]), rows_in.arrived), tensor_count
    )
    out_up = Gather(
        held(jnp.concatenate([out_weight.T, up_weight], axis=1)[None], qkv.arrived), steps[0]
    )
    hop([out_up])
    for n in range(near - 1):
        for chain in qkv_chains:
            chain.end()
        launch((), qkv_chains)
    for _ in range(far - 1):
        hop([out_up])
    for chain in qkv_chains:
        chain.end()
    down = Gather(held(down_weight.T[None], out_up.arrived), steps[0])
    wa = out_up.columns(0, cut, steps[0][far:])
    wb = out_up.columns(cut, out_weight.shape[0] + local_hidden - cut, steps[1][far:])
    rows_in.end()
    x = launch(rows_in.result, qkv_chains)
    for chain in qkv_chains:
        chain.end()
    x = launch(x, [wa, wb, down])

    mid_row = vectors[:, :local_hidden].reshape(1, -1)
    scale_all = vectors[:, local_hidden:].reshape(-1)
    scale_row = jnp.repeat(scale_all, head_size)[None]
    own_lengths = lax.dynamic_index_in_dim(lengths[:, 0], micro, 0, keepdims=False)
    ends = jnp.cumsum(own_lengths).astype(jnp.int32)

    def spread(value):
        if split == 1:
            return value
        groups = [[m * split + s for s in range(split)] for m in range(micro_count)]
        return lax.all_to_all(value, "tensor", 1, 0, tiled=True, axis_index_groups=groups)

    def collect(value):
        if split == 1:
            return value
        groups = [[m * split + s for s in range(split)] for m in range(micro_count)]
        return lax.all_to_all(value, "tensor", 0, 1, tiled=True, axis_index_groups=groups)

    h1, q, k, v = project(orders, x, norm_gains, qkv_chains, grid_of, factor)
    q, k, v = land((q, k, v), [wa, wb, down])
    more([down], far - 2)
    q, k, v = spread(q), spread(k), spread(v)
    more([wa, wb], near - 2)
    q = launch(q, [wa, wb, down])
    part = width // split
    scale_part = lax.dynamic_slice(scale_row, (0, tensor_rank % split * part), (1, part))
    scaled, lse = attend(q, k, v, scale_part, ends, tensor_count, 1, 0, None, None)
    scaled = land(scaled, [wa, wb, down])
    down_cut = half_cols
    wda = down.columns(0, down_cut, steps[0][far:])
    wdb = down.columns(down_cut, local_hidden - down_cut, steps[1][far:])
    rows_cot = Rows(cotangent, micro_count, split)
    scaled = launch(scaled, [wa, wb])
    scaled = land(scaled, [wa, wb])
    scaled = collect(launch(scaled, [wda, wdb, rows_cot]))
    forward = []
    shares = 2 if x.shape[0] % 512 == 0 else 1
    for n in range(shares):
        if n:
            forward[0] = land(forward[0], [wda, wdb])
            more([wda, wdb], near - 2)
            forward[0] = launch(forward[0], [wda, wdb])
        forward = list(
            hidden_forward(orders, scaled, x, norm_gains, mid_row, wa, wb, grid_of, (n, shares), forward)
        )
    unit, h3, hidden, narrow, stat = forward
    if shares == 1:
        narrow = land(narrow, [wda, wdb])
        more([wda, wdb], near - 2)
        narrow = launch(narrow, [wda, wdb])
    unit, h3, hidden, narrow, stat = land([unit, h3, hidden, narrow, stat], [rows_cot, wda])
    cot = rows_cot.result

    def grad_half(n, a, b, name, turn=False):
        keep, send = weight_grad(
            tables[n], a, [b], grid_of, n * half_cols, half_cols, name, turn, True
        )
        return Scatter(keep, send, steps[n])

    def flush(chains):
        for chain in chains:
            while chain.steps:
                hop([chain])
        return [chain.total for chain in chains]

    cot_held = launch(cot, [wda])
    d0 = grad_half(0, cot_held, narrow, "grad_down", True)
    d0.keep, d0.send = land((d0.keep, d0.send), [wdb])
    cot_held = launch(cot_held, [d0, wdb])
    d1 = grad_half(1, cot_held, narrow, "grad_down", True)
    d1.keep, d1.send = land((d1.keep, d1.send), [d0, wda, wdb])
    hidden = launch(hidden, [d1, d0])
    hidden = land(hidden, [d1])
    hidden = launch(hidden, [d1])
    back = feed_back(
        orders, hidden, stat, unit, x, cot, norm_gains, mid_row, scale_row, wda, wdb, wa, wb, grid_of
    )
    dhidden, dresid, dmixed, dattended, gain_sums, mid_sums = land(back, [d0, d1])
    more([d0, d1], near - 2)
    dhidden = launch(dhidden, [d0, d1])
    u0 = grad_half(0, h3, dhidden, "grad_up")
    u0.keep, u0.send = land((u0.keep, u0.send), [d0, d1])
    down_sum = merged([d0, d1])
    dhidden = launch(dhidden, [u0, down_sum])
    u1 = grad_half(1, h3, dhidden, "grad_up")
    u1.keep, u1.send = land((u1.keep, u1.send), [u0, down_sum])
    dmixed = launch(dmixed, [u1])
    keep, send = weight_grad(
        tables[0], dmixed, [scaled], grid_of, 0, out_weight.shape[0], "grad_out", near=True
    )
    o0 = Scatter(keep, send, steps[0])
    o0.keep, o0.send = land((o0.keep, o0.send), [u1])
    flying = [u0, u1, o0] + ([down_sum] if down_sum.steps else [])
    da = launch(spread(dattended), flying)
    halves, grads, inners = [], [], []
    for n in range(parts):
        *three, inner = attend_back(q, k, v, da, lse, ends, factor, tensor_count, parts, n)
        inners.append(inner)
        if n == 0:
            three = land(three, flying)
            narrow = launch(narrow, [u0, u1])
            block_out = feed_forward(orders, narrow, unit, x, norm_gains, wda, wdb, grid_of)
            block_out = land(block_out, [u0, u1])
            more([u0, u1], near - 2)
            up_sum = merged([u0, u1])
            rows_out = Rows(block_out, micro_count, split, 2)
            three = [collect(one) for one in three]
            three = launch(three, [up_sum, o0])
            flying = [up_sum, o0]
        else:
            three = land(three, flying)
            three, first_out = lax.optimization_barrier((three, rows_out.arrived[0]))
            rows_out.arrived[0] = first_out
            flying = [o0]
            three = launch(three, flying)
        keep, send = weight_grad(tables[n % 2], h1, three, grid_of, 0, part_cols, "grad_qkv", near=True)
        halves.append(Scatter(keep, send, steps[n % 2]))
        grads += three
        halves[-1].keep, halves[-1].send = land((halves[-1].keep, halves[-1].send), flying)
        if n < parts - 1:
            flying = [halves[0], up_sum, o0]
            da = launch(da, flying + [rows_out])
    q_last = halves[-1]
    if parts > 1:
        q_last.keep, q_last.send, rows_out.arrived = lax.optimization_barrier(
            (q_last.keep, q_last.send, rows_out.arrived)
        )
    dresid = launch(dresid, [q_last])
    dresid = land(dresid, [q_last])
    beside = halves + [o0] + ([] if parts > 1 else [rows_out])
    dresid = launch(dresid, beside)
    grad_in, first_sums = input_grad(orders, grads, x, dresid, norm_gains, qkv_chains, grid_of)
    grad_in, first_sums = land((grad_in, first_sums), beside)
    local = heads // split
    if parts == 1:
        head_sums = jnp.sum(inners[0], axis=-1).reshape(-1)
    else:
        shaped = [jnp.sum(one, axis=-1).reshape(tensor_count, -1) for one in inners]
        head_sums = jnp.concatenate(shaped, axis=1).reshape(-1)
    first_head = tensor_rank % split * local
    head_sums = head_sums / lax.dynamic_slice(scale_all, (first_head,), (local,))
    head_all = lax.dynamic_update_slice(jnp.zeros((heads,), F32), head_sums, (first_head,))
    last = jnp.concatenate(
        [jnp.sum(one, axis=0) for one in (first_sums, gain_sums[:8], gain_sums[8:], mid_sums)]
        + [head_all]
    )
    last = Total(last, batch_count, tensor_count)
    rows_back = Rows(grad_in, micro_count, split, 2)
    tail = halves + ([o0] if o0.steps else [])
    launch((), tail + [last])
    last.end()
    launch((), [last])
    land((), tail + [last])
    if parts > 1:
        halves = [merged(halves)]
    sent = rows_back.outgoing()
    tail = [one for one in halves + [o0, last] if one.steps]
    values, sent = lax.optimization_barrier(([one.outgoing() for one in tail], sent))
    for one, value in zip(tail, values):
        one.go(value)
    rows_back.go(sent)
    for one in tail:
        one.end()
    while last.steps:
        hop([last])
    tail = [one for one in halves + [o0] if one.steps]
    launch((), tail)
    arrived = [one.arrived for one in tail]
    rows_back.arrived = held(rows_back.arrived, arrived)
    last.value = held(last.value, arrived)
    for one in tail:
        one.end()
    rows_out.arrived = held(rows_out.arrived, arrived)
    rows_out.end()
    rows_back.end()
    block_out, grad_in = rows_out.result, rows_back.result
    d_totals, u_totals, o_totals, q_totals = (
        flush([down_sum]), flush([up_sum]), flush([o0]), flush(halves)
    )
    down_grad = d_totals[0].T
    up_grad = u_totals[0]
    out_grad = o_totals[0].T
    qkv_grad = q_totals[0]
    vector = last.value
    d_totals, u_totals, o_totals, q_totals = (
        flush([d0, d1]), flush([u0, u1]), flush([o0]), flush(halves)
    )
    gains_sum = vector[: 3 * width].reshape(3, width)
    mid_own = lax.dynamic_slice(vector, (3 * width + tensor_rank * local_hidden,), (local_hidden,))
    scale_own = lax.dynamic_slice(
        vector, (3 * width + tensor_count * local_hidden + tensor_rank * local_heads,), (local_heads,)
    )
    return (
        block_out,
        grad_in,
        gains_sum,
        qkv_grad,
        scale_own,
        out_grad,
        up_grad,
        mid_own,
        down_grad,
    )


def solution(mesh):
    in_specs = (
        P(None, ("batch", "tensor"), None),
        P(None, "batch", None),
        P(),
        P(None, "batch", "tensor"),
        P("tensor"),
        P("tensor", "batch"),
        P("batch", "tensor"),
        P("tensor"),
        P("tensor", "batch"),
        P(None, ("batch", "tensor"), None),
    )
    out_specs = (
        P(None, ("batch", "tensor"), None),
        P(None, ("batch", "tensor"), None),
        P(),
        P(None, "batch", "tensor"),
        P("tensor"),
        P("tensor", "batch"),
        P("batch", "tensor"),
        P("tensor"),
        P("tensor", "batch"),
    )
    return jax.shard_map(body, mesh=mesh, in_specs=in_specs, out_specs=out_specs, check_vma=False)
```

```python
import functools
import math

import jax
import jax.numpy as jnp
from jax import lax
from jax.experimental import pallas as pl
from jax.experimental.pallas import tpu as pltpu
from jax.sharding import PartitionSpec as P

eps = 1e-05
SEQ_MOST = 512
F32 = jnp.float32
BF = jnp.bfloat16
ALL = ("batch", "tensor")
GELU_C = math.sqrt(2.0 / math.pi)
GELU_A = 0.044715
STEP = 256


def cost(us):
    return pl.CostEstimate(flops=int(us * 1e9), transcendentals=0, bytes_accessed=1 << 20)


def dotf(a, b, ca, cb):
    return lax.dot_general(a, b, (((ca,), (cb,)), ((), ())), preferred_element_type=F32)


def row_loop(rows, step, fn):
    def one(i, carry):
        fn(pl.multiple_of(i * step, step))
        return carry

    lax.fori_loop(0, rows // step, one, 0)


def normalize(values):
    centred = values - jnp.mean(values, axis=-1, keepdims=True)
    factor = lax.rsqrt(jnp.mean(centred * centred, axis=-1, keepdims=True) + eps)
    return (centred * factor, factor)


def norm_back(unit, factor, grad):
    return factor * (
        grad
        - jnp.mean(grad, axis=-1, keepdims=True)
        - unit * jnp.mean(grad * unit, axis=-1, keepdims=True)
    )


def fold8(values):
    rows, width = values.shape
    return jnp.sum(values.reshape(rows // 8, 8, width), axis=0)


def bits_of(count):
    return count.bit_length() - 1


def gather_steps(batch_count, tensor_count, tensor_first):
    tensor = [("tensor", 1 << k) for k in range(bits_of(tensor_count))]
    plane = [("batch", 2)]
    far = [("batch", 1 << k) for k in reversed(range(2, bits_of(batch_count)))]
    return far + (tensor + plane if tensor_first else plane + tensor) + [("batch", 1)]


def place_table(steps, batch_count, tensor_count):
    batch = jnp.arange(batch_count * tensor_count, dtype=jnp.int32) // tensor_count
    tensor = jnp.arange(batch_count * tensor_count, dtype=jnp.int32) % tensor_count
    batch = jnp.bitwise_xor(batch, lax.axis_index("batch"))
    tensor = jnp.bitwise_xor(tensor, lax.axis_index("tensor"))
    place = jnp.zeros_like(batch)
    for k, (axis, flip) in enumerate(steps):
        apart = (jnp.bitwise_and(batch if axis == "batch" else tensor, flip) != 0).astype(jnp.int32)
        place = place + apart * (1 << k)
    return place


def swap(value, axis, flip):
    count = lax.axis_size(axis)
    return lax.ppermute(value, axis, [(i, i ^ flip) for i in range(count)])


def held(value, after):
    return lax.optimization_barrier((value, after))[0]


class Gather:
    def __init__(self, buffer, steps):
        self.own, self.steps, self.parts = buffer, list(steps), None

    def outgoing(self):
        return self.arrived if len(self.steps) == 1 else self.own

    def go(self, value):
        step = self.steps.pop(0)
        self.arrived = swap(value, *step)
        if not self.steps:
            self.parts[1] = value
        else:
            self.own = value
            if len(self.steps) == 1:
                self.parts = [value, None, swap(value, *self.steps[0]), None]

    def end(self):
        if self.parts is None:
            self.own = jnp.concatenate([self.own, self.arrived], axis=0)
        elif not self.steps:
            self.parts[3] = self.arrived

    def columns(self, start, count, steps):
        return Gather(self.own[..., start : start + count], steps)


class Scatter:
    def __init__(self, keep, send, steps):
        self.keep, self.send, self.steps = keep, send, list(reversed(steps))

    def outgoing(self):
        return (self.send, self.keep)

    def go(self, value):
        send, self.keep = value
        self.arrived = swap(send, *self.steps.pop(0))

    def end(self):
        keep, arrived = self.keep, self.arrived
        half = keep.shape[0] // 2
        if self.steps:
            self.send = (keep[half:].astype(F32) + arrived[half:].astype(F32)).astype(BF)
            self.keep = (keep[:half].astype(F32) + arrived[:half].astype(F32)).astype(BF)
        else:
            self.total = keep[0].astype(F32) + arrived[0].astype(F32)


def merged(chains):
    keep = jnp.concatenate([chain.keep for chain in chains], axis=-1)
    send = jnp.concatenate([chain.send for chain in chains], axis=-1)
    return Scatter(keep, send, list(reversed(chains[0].steps)))


class Total:
    def __init__(self, value, batch_count, tensor_count):
        self.value, self.grid_of = value, (batch_count, tensor_count)
        bits = [(flip, 0) for flip in (1 << k for k in range(2, bits_of(batch_count)))]
        plane = [(2, 0)] + [(0, 1 << k) for k in range(bits_of(tensor_count))]
        self.steps = [[(1, 0)]]
        for group in (plane, bits):
            if len(group) <= 2:
                spans = [(0, 0)]
                for flip in group:
                    spans += [(one[0] ^ flip[0], one[1] ^ flip[1]) for one in spans]
                self.steps.append(spans[1:])
            else:
                self.steps += [[flip] for flip in group]

    def outgoing(self):
        return self.value

    def go(self, value):
        batch_count, tensor_count = self.grid_of
        self.value, self.arrived = value, []
        for batch, tensor in self.steps.pop(0):
            pairs = [
                (b * tensor_count + t, (b ^ batch) * tensor_count + (t ^ tensor))
                for b in range(batch_count)
                for t in range(tensor_count)
            ]
            self.arrived.append(lax.ppermute(value, ALL, pairs))

    def end(self):
        for one in self.arrived:
            self.value = self.value + one


class Rows:
    def __init__(self, value, micro_count, split, cuts=1):
        self.value, self.micro_count, self.split, self.cuts = value, micro_count, split, cuts
        self.taken = value.ndim == 3
        self.steps = [None]
        self.rank = lax.axis_index("tensor")

    def pieces(self):
        if self.taken:
            return self.value
        return self.value.reshape(self.micro_count, -1, self.value.shape[1])

    def outgoing(self):
        if self.split > 1:
            return []
        sent = []
        for flip in range(1, self.micro_count):
            one = lax.dynamic_index_in_dim(self.pieces(), lax.bitwise_xor(self.rank, flip), 0)
            sent += [one[:, n * (one.shape[1] // self.cuts) :][:, : one.shape[1] // self.cuts] for n in range(self.cuts)]
        return sent

    def go(self, value):
        self.steps = []
        if self.split == 1:
            self.arrived = [
                swap(one, "tensor", n // self.cuts + 1) for n, one in enumerate(value)
            ]
        else:
            self.arrived = [
                lax.all_gather(self.value, "tensor", axis=1 if self.taken else 0, tiled=True)
            ]

    def end(self):
        if self.split == 1:
            pieces = self.pieces()
            out = lax.dynamic_update_slice(
                jnp.zeros_like(pieces),
                lax.dynamic_index_in_dim(pieces, self.rank, 0),
                (self.rank, 0, 0),
            )
            for n, one in enumerate(self.arrived):
                other = lax.bitwise_xor(self.rank, n // self.cuts + 1)
                out = lax.dynamic_update_slice(
                    out, one, (other, n % self.cuts * one.shape[1], 0)
                )
            self.result = out.reshape(-1, out.shape[2]) if self.taken else out
            return
        whole = self.arrived[0]
        width = whole.shape[-1]
        if self.taken:
            rows = self.value.shape[0] * self.value.shape[1]
            start = (self.rank // self.split, self.rank % self.split * rows, 0)
            self.result = lax.dynamic_slice(whole, start, (1, rows, width))[0]
        else:
            own = self.value.shape[0] // self.micro_count
            whole = whole.reshape(self.micro_count, -1, width)
            start = (0, self.rank * own, 0)
            self.result = lax.dynamic_slice(whole, start, (self.micro_count, own, width))


def launch(inputs, chains):
    inputs, values = lax.optimization_barrier((inputs, [chain.outgoing() for chain in chains]))
    for chain, value in zip(chains, values):
        chain.go(value)
    return inputs


def land(inputs, chains):
    inputs, values = lax.optimization_barrier((inputs, [chain.arrived for chain in chains]))
    for chain, value in zip(chains, values):
        chain.arrived = value
        chain.end()
    return inputs


def hop(chains, after=()):
    launch(after, chains)
    for chain in chains:
        chain.end()


def columns(parts, order_ref, batch_count, tensor_count, t, start, count, lead=None):
    for first, width, which, w_ref in parts:
        if first <= start < first + width:
            break
    pieces = []
    for b in range(batch_count):
        p = order_ref[(which * batch_count + b) * tensor_count + t]
        here = pl.ds(start - first, count)
        pieces.append(w_ref[p, :, here] if lead is None else w_ref[p, lead, :, here])
    return jnp.concatenate(pieces, axis=0)


def weights(*refs):
    out, first = [], 0
    for n, ref in enumerate(refs):
        out.append((first, ref.shape[-1], n % 2, ref))
        first += ref.shape[-1]
    return out


HBM = pl.BlockSpec(memory_space=pltpu.HBM)


def whole(chain):
    part = chain.parts[0].shape
    return pltpu.VMEM((4 * part[0],) + part[1:], BF)


def in_hbm(*values):
    return [pltpu.with_memory_space_constraint(value, pltpu.HBM) for value in values]


def parts_of(chains):
    return in_hbm(*[part for chain in chains for part in chain.parts])


def load_parts(refs, w, sem):
    count = w.shape[0] // 4
    for n in range(4):
        pltpu.make_async_copy(refs[n], w.at[pl.ds(n * count, count)], sem).start()


def wait_whole(w, sem):
    pltpu.make_async_copy(w, w, sem).wait()


def qkv_kernel(grid_of, factor, count, order_ref, x_ref, gain_ref, *refs):
    batch_count, tensor_count = grid_of
    w_hbm, refs = refs[: 4 * count], refs[4 * count :]
    turned_ref, q_ref, k_ref, v_ref, h1_ref = refs[:5]
    w_refs, sem = refs[5:-1], refs[-1]
    first = pl.program_id(0) == 0

    @pl.when(first)
    def _():
        for n in range(count):
            load_parts(w_hbm[4 * n : 4 * n + 4], w_refs[n], sem.at[n])

    def chunk(r):
        here = pl.ds(r, STEP)
        unit, _ = normalize(x_ref[here, :].astype(F32))
        h1_ref[here, :] = (unit * gain_ref[0:1, :]).astype(BF)

    row_loop(x_ref.shape[0], STEP, chunk)
    turned_ref[...] = h1_ref[...].T

    parts = weights(*w_refs)
    cols = sum(part[1] for part in parts)
    for n, (start, width, _, _) in enumerate(parts):

        @pl.when(first)
        def _(n=n):
            wait_whole(w_refs[n], sem.at[n])

        for c, out in enumerate((q_ref, k_ref, v_ref)):
            for t in range(tensor_count):
                w = columns(parts, order_ref, batch_count, tensor_count, t, start, width, lead=c)
                value = dotf(h1_ref[...], w, 1, 0).astype(BF)
                here = slice(t * cols + start, t * cols + start + width)
                out[:, here] = value * BF(factor) if c == 0 else value


def project(orders, x, gains, chains, grid_of, factor):
    rows, width = x.shape
    block = min(256, rows)
    row = pl.BlockSpec((block, width), lambda i, e: (i, 0))
    return pl.pallas_call(
        functools.partial(qkv_kernel, grid_of, factor, len(chains)),
        grid_spec=pltpu.PrefetchScalarGridSpec(
            num_scalar_prefetch=1,
            grid=(rows // block,),
            in_specs=[row, pl.BlockSpec((3, width), lambda i, e: (0, 0))]
            + [HBM] * (4 * len(chains)),
            out_specs=[pl.BlockSpec((width, block), lambda i, e: (0, i))] + [row] * 3,
            scratch_shapes=[pltpu.VMEM((block, width), BF)]
            + [whole(chain) for chain in chains]
            + [pltpu.SemaphoreType.DMA((len(chains),))],
        ),
        out_shape=[pltpu.HBM((width, rows), BF)]
        + [pltpu.HBM((rows, width), BF)] * 3,
        compiler_params=pltpu.CompilerParams(vmem_limit_bytes=24 << 20),
        cost_estimate=cost(13),
        name="project",
    )(orders, *in_hbm(x), gains, *parts_of(chains))


def spans(rows, block):
    return [
        (first, max(0, (first - SEQ_MOST + 1) // block * block), first + block)
        for first in range(0, rows, block)
    ]


def fill_bias(ends_ref, bias, parts, block):
    for (first, low, high), ref in zip(parts, bias):
        shape = (high - low, block)
        keys = low + lax.broadcasted_iota(jnp.int32, shape, 0)
        queries = first + lax.broadcasted_iota(jnp.int32, shape, 1)
        start = jnp.zeros(shape, jnp.int32)
        for n in range(ends_ref.shape[0]):
            end = ends_ref[n]
            start = jnp.where(queries >= end, end, start)
        ref[...] = jnp.where((keys <= queries) & (keys >= start), 0.0, -1e30).astype(F32)


def attend_kernel(rows, block, ends_ref, q_ref, k_ref, v_ref, scale_ref, o_ref, lse_ref, *bias):
    parts = spans(rows, block)

    @pl.when(pl.program_id(0) == 0)
    def _():
        fill_bias(ends_ref, bias, parts, block)

    lower = lax.broadcasted_iota(jnp.int32, (1, 128), 1) < 64
    for n, (first, low, high) in enumerate(parts):
        q = q_ref[pl.ds(first, block), :]
        heads = []
        for h in range(2):
            own = jnp.where(lower if h == 0 else ~lower, q, jnp.zeros_like(q))
            s = dotf(k_ref[pl.ds(low, high - low), :], own, 1, 1) + bias[n][...]
            most = jnp.max(s, axis=0, keepdims=True)
            p = jnp.exp(s - most)
            total = jnp.sum(p, axis=0, keepdims=True)
            probs = (p * (1.0 / total)).astype(BF)
            lse_ref[0, pl.ds(h, 1), pl.ds(first, block)] = most + jnp.log(total)
            heads.append(dotf(probs, v_ref[pl.ds(low, high - low), :], 0, 0))
        out = jnp.where(lower, heads[0], heads[1]) * scale_ref[...]
        o_ref[pl.ds(first, block), :] = out.astype(BF)


def attend_back_kernel(
    rows, block, factor, ends_ref, q_ref, k_ref, v_ref, da_ref, lse_ref,
    dq_ref, dk_ref, dv_ref, inner_ref, dk_acc, dv_acc, *bias
):
    parts = spans(rows, block)

    @pl.when(pl.program_id(0) == 0)
    def _():
        fill_bias(ends_ref, bias, parts, block)

    lower = lax.broadcasted_iota(jnp.int32, (1, 128), 1) < 64
    dk_acc[...] = jnp.zeros_like(dk_acc)
    dv_acc[...] = jnp.zeros_like(dv_acc)
    for n, (first, low, high) in enumerate(parts):
        here = pl.ds(first, block)
        keys = pl.ds(low, high - low)
        q, da, k, v = q_ref[here, :], da_ref[here, :], k_ref[keys, :], v_ref[keys, :]
        probs, scores, q_own, da_own, k_own = [], [], [], [], []
        for h in range(2):
            mask = lower if h == 0 else ~lower
            q_own.append(jnp.where(mask, q, jnp.zeros_like(q)))
            da_own.append(jnp.where(mask, da, jnp.zeros_like(da)))
            k_own.append(jnp.where(mask, k, jnp.zeros_like(k)))
            s = dotf(k, q_own[h], 1, 1) + bias[n][...]
            p = jnp.exp(s - lse_ref[0, pl.ds(h, 1), here])
            product = p * dotf(v, da_own[h], 1, 1)
            inner = jnp.sum(product, axis=0, keepdims=True)
            inner_ref[0, pl.ds(h, 1), here] = inner
            scores.append((product - p * inner).astype(BF))
            probs.append(p.astype(BF))
        dv_acc[keys, :] += dotf(
            jnp.concatenate(probs, axis=1), jnp.concatenate(da_own, axis=0), 1, 0
        )
        dk_acc[keys, :] += dotf(
            jnp.concatenate(scores, axis=1), jnp.concatenate(q_own, axis=0), 1, 0
        )
        dq = dotf(jnp.concatenate(scores, axis=0), jnp.concatenate(k_own, axis=0), 0, 0)
        dq_ref[here, :] = (dq * factor).astype(BF)
    dk_ref[...] = dk_acc[...].astype(BF)
    dv_ref[...] = dv_acc[...].astype(BF)


def bias_shapes(rows, block):
    return [pltpu.VMEM((high - low, block), F32) for _, low, high in spans(rows, block)]


def pair_of(pairs, tensor_count, parts, n):
    if parts == 1:
        return pairs, lambda i: i
    per_tensor = pairs // tensor_count
    per = per_tensor // parts
    return pairs // parts, lambda i: i // per * per_tensor + n * per + i % per


def attend(q, k, v, scale_row, ends, tensor_count, parts, n, before_out, before_lse):
    rows, width = q.shape
    block = min(256, rows)
    pairs = width // 128
    steps, pair = pair_of(pairs, tensor_count, parts, n)
    col = pl.BlockSpec((rows, 128), lambda i, e: (0, pair(i)))
    earlier = [] if before_out is None else [before_out, before_lse]
    count = len(earlier)

    def kernel(ends_ref, q_ref, k_ref, v_ref, scale_ref, *refs):
        attend_kernel(rows, block, ends_ref, q_ref, k_ref, v_ref, scale_ref, *refs[count:])

    return pl.pallas_call(
        kernel,
        grid_spec=pltpu.PrefetchScalarGridSpec(
            num_scalar_prefetch=1,
            grid=(steps,),
            in_specs=[col, col, col, pl.BlockSpec((1, 128), lambda i, e: (0, pair(i)))]
            + [HBM] * count,
            out_specs=[col, pl.BlockSpec((1, 2, rows), lambda i, e: (pair(i), 0, 0))],
            scratch_shapes=bias_shapes(rows, block),
        ),
        out_shape=[
            pltpu.HBM((rows, width), BF),
            pltpu.HBM((pairs, 2, rows), F32),
        ],
        input_output_aliases={5 + j: j for j in range(count)},
        compiler_params=pltpu.CompilerParams(vmem_limit_bytes=32 << 20),
        cost_estimate=cost(24 / parts),
        name="attend",
    )(ends, *in_hbm(q, k, v), scale_row, *earlier)


def attend_back(q, k, v, da, lse, ends, factor, tensor_count, parts, n):
    rows, width = q.shape
    block = min(256, rows)
    pairs = width // 128
    steps, pair = pair_of(pairs, tensor_count, parts, n)
    col = pl.BlockSpec((rows, 128), lambda i, e: (0, pair(i)))
    out_col = pl.BlockSpec((rows, 128), lambda i, e: (0, i))
    out = pltpu.HBM((rows, width // parts), BF)
    return pl.pallas_call(
        functools.partial(attend_back_kernel, rows, block, factor),
        grid_spec=pltpu.PrefetchScalarGridSpec(
            num_scalar_prefetch=1,
            grid=(steps,),
            in_specs=[col] * 4 + [pl.BlockSpec((1, 2, rows), lambda i, e: (pair(i), 0, 0))],
            out_specs=[out_col] * 3 + [pl.BlockSpec((1, 2, rows), lambda i, e: (i, 0, 0))],
            scratch_shapes=[pltpu.VMEM((rows, 128), F32)] * 2 + bias_shapes(rows, block),
        ),
        out_shape=[out, out, out, pltpu.HBM((steps, 2, rows), F32)],
        compiler_params=pltpu.CompilerParams(vmem_limit_bytes=40 << 20),
        cost_estimate=cost(42 / parts),
        name="attend_back",
    )(ends, *in_hbm(q, k, v, da), lse)


def put_stats(ref, here, values):
    lane = lax.broadcasted_iota(jnp.int32, (1, 128), 1)
    out = values[-1]
    for n in reversed(range(len(values) - 1)):
        out = jnp.where(lane < 16 * (n + 1), values[n], out)
    ref[here, :] = jnp.broadcast_to(out, (values[0].shape[0], 128))


def hidden_kernel(
    grid_of, order_ref, scaled_ref, x_ref, gain_ref, mid_ref, a0, a1, a2, a3, b0, b1, b2, b3,
    unit_ref, turned_ref, hidden_ref, narrow_ref, stat_ref, act, norm_stat, wide, h3_ref, wa, wb, sem
):
    batch_count, tensor_count = grid_of
    block, width = x_ref.shape
    total = hidden_ref.shape[1]
    up_cols = total // tensor_count
    out_cols = width // tensor_count
    get = functools.partial(columns, weights(wa, wb), order_ref, batch_count, tensor_count)
    first = pl.program_id(0) == 0

    @pl.when(first)
    def _():
        load_parts((a0, a1, a2, a3), wa, sem.at[0])
        load_parts((b0, b1, b2, b3), wb, sem.at[1])
        wait_whole(wa, sem.at[0])

    mixed = None
    for t in range(tensor_count):
        part = dotf(scaled_ref[:, t * out_cols : (t + 1) * out_cols], get(t, 0, out_cols), 1, 1)
        mixed = part if mixed is None else mixed + part
    wide[...] = mixed

    def norms(r):
        here = pl.ds(r, STEP)
        unit, factor = normalize(wide[here, :])
        unit_ref[here, :] = unit
        resid = x_ref[here, :].astype(F32) + unit * gain_ref[1:2, :]
        mean3 = jnp.mean(resid, axis=-1, keepdims=True)
        centred = resid - mean3
        factor3 = lax.rsqrt(jnp.mean(centred * centred, axis=-1, keepdims=True) + eps)
        h3_ref[here, :] = (centred * factor3 * gain_ref[2:3, :]).astype(BF)
        put_stats(norm_stat, here, [factor, mean3, factor3])

    row_loop(block, STEP, norms)
    turned_ref[...] = h3_ref[...].T

    @pl.when(first)
    def _():
        wait_whole(wb, sem.at[1])

    chunk = min(256, up_cols // 2)
    sums = jnp.zeros((block, 128), F32)
    squares = jnp.zeros((block, 128), F32)
    for c in range(total // chunk):
        t, off = divmod(c * chunk, up_cols)
        h = dotf(h3_ref[...], get(t, out_cols + off, chunk), 1, 0)
        hidden_ref[:, c * chunk : (c + 1) * chunk] = h
        half = 0.5 * jnp.tanh(h * (GELU_C + (GELU_C * GELU_A) * (h * h))) + 0.5
        a = h * half
        act[:, c * chunk : (c + 1) * chunk] = a
        for j in range(chunk // 128):
            piece = a[:, j * 128 : (j + 1) * 128]
            sums += piece
            squares += piece * piece
    mean = jnp.sum(sums, axis=1, keepdims=True) / total
    spread = jnp.sum(squares, axis=1, keepdims=True) / total - mean * mean
    scale = lax.rsqrt(spread + eps)
    before = norm_stat[...]
    put_stats(stat_ref, slice(None), [mean, scale, before[:, 0:1], before[:, 16:17], before[:, 32:33]])

    def narrow(r):
        here = pl.ds(r, STEP)
        m = stat_ref[here, 0:1]
        s = stat_ref[here, 16:17]
        narrow_ref[here, :] = ((act[here, :] - m) * s * mid_ref[...]).astype(BF)

    row_loop(block, STEP, narrow)


def hidden_forward(orders, scaled, x, gains, mid_row, wa, wb, grid_of, share, earlier):
    rows, width = x.shape
    block = min(256, rows)
    total = mid_row.shape[1]
    blocks = rows // block // share[1]
    first = share[0] * blocks
    row = pl.BlockSpec((block, width), lambda i, e: (first + i, 0))
    wide = pl.BlockSpec((block, total), lambda i, e: (first + i, 0))

    def kernel(order_ref, *refs):
        hidden_kernel(grid_of, order_ref, *refs[:12], *refs[12 + len(earlier) :])

    return pl.pallas_call(
        kernel,
        grid_spec=pltpu.PrefetchScalarGridSpec(
            num_scalar_prefetch=1,
            grid=(blocks,),
            in_specs=[
                row,
                row,
                pl.BlockSpec((3, width), lambda i, e: (0, 0)),
                pl.BlockSpec((1, total), lambda i, e: (0, 0)),
            ]
            + [HBM] * (8 + len(earlier)),
            out_specs=[row, pl.BlockSpec((width, block), lambda i, e: (0, first + i)), wide, wide]
            + [pl.BlockSpec((block, 128), lambda i, e: (first + i, 0))],
            scratch_shapes=[
                pltpu.VMEM((block, total), F32),
                pltpu.VMEM((block, 128), F32),
                pltpu.VMEM((block, width), F32),
                pltpu.VMEM((block, width), BF),
                whole(wa),
                whole(wb),
                pltpu.SemaphoreType.DMA((2,)),
            ],
        ),
        out_shape=[
            pltpu.HBM((rows, width), F32),
            pltpu.HBM((width, rows), BF),
            pltpu.HBM((rows, total), F32),
            pltpu.HBM((rows, total), BF),
            pltpu.HBM((rows, 128), F32),
        ],
        input_output_aliases={13 + n: n for n in range(len(earlier))},
        compiler_params=pltpu.CompilerParams(vmem_limit_bytes=44 << 20),
        cost_estimate=cost(30 / share[1]),
        name="hidden_forward",
    )(orders, *in_hbm(scaled, x), gains, mid_row, *parts_of((wa, wb)), *earlier)


def feed_kernel(grid_of, order_ref, narrow_ref, unit_ref, x_ref, gain_ref, a0, a1, a2, a3, b0, b1, b2, b3, out_ref, wa, wb, sem):
    batch_count, tensor_count = grid_of
    up_cols = narrow_ref.shape[1] // tensor_count
    parts = weights(wa, wb)

    @pl.when(pl.program_id(0) == 0)
    def _():
        load_parts((a0, a1, a2, a3), wa, sem.at[0])
        load_parts((b0, b1, b2, b3), wb, sem.at[1])

    out = x_ref[...].astype(F32) + unit_ref[...] * gain_ref[1:2, :]
    for n, (start, width, _, w_ref) in enumerate(parts):

        @pl.when(pl.program_id(0) == 0)
        def _(n=n, w_ref=w_ref):
            wait_whole(w_ref, sem.at[n])

        for t in range(tensor_count):
            w = columns(parts, order_ref, batch_count, tensor_count, t, start, width)
            off = t * up_cols + start
            out += dotf(narrow_ref[:, off : off + width], w, 1, 1)
    out_ref[...] = out.astype(BF)


def feed_forward(orders, narrow, unit, x, gains, wa, wb, grid_of):
    rows, width = x.shape
    block = min(256, rows)
    total = narrow.shape[1]
    row = pl.BlockSpec((block, width), lambda i, e: (i, 0))
    return pl.pallas_call(
        functools.partial(feed_kernel, grid_of),
        grid_spec=pltpu.PrefetchScalarGridSpec(
            num_scalar_prefetch=1,
            grid=(rows // block,),
            in_specs=[pl.BlockSpec((block, total), lambda i, e: (i, 0)), row, row]
            + [pl.BlockSpec((3, width), lambda i, e: (0, 0))]
            + [HBM] * 8,
            out_specs=row,
            scratch_shapes=[whole(wa), whole(wb), pltpu.SemaphoreType.DMA((2,))],
        ),
        out_shape=pltpu.HBM((rows, width), BF),
        compiler_params=pltpu.CompilerParams(vmem_limit_bytes=28 << 20),
        cost_estimate=cost(14),
        name="feed_forward",
    )(orders, *in_hbm(narrow, unit, x), gains, *parts_of((wa, wb)))


def back_kernel(
    grid_of, order_ref, hidden_ref, stat_ref, unit_ref, x_ref, cot_ref, gain_ref, mid_ref,
    scale_ref, da0, da1, da2, da3, db0, db1, db2, db3, a0, a1, a2, a3, b0, b1, b2, b3, dhidden_ref, dresid_ref, turned_ref, dattended_ref,
    gains_ref, dmid_ref, grad, unit_s, slope_s, wide, dmixed_ref, wda, wdb, wa, wb, sem
):
    batch_count, tensor_count = grid_of
    block, width = x_ref.shape
    total = hidden_ref.shape[1]
    up_cols = total // tensor_count
    out_cols = width // tensor_count
    get = functools.partial(columns, weights(wa, wb), order_ref, batch_count, tensor_count)
    get_down = functools.partial(columns, weights(wda, wdb), order_ref, batch_count, tensor_count)
    first = pl.program_id(0) == 0

    @pl.when(first)
    def _():
        load_parts((da0, da1, da2, da3), wda, sem.at[0])
        load_parts((db0, db1, db2, db3), wdb, sem.at[1])
        load_parts((a0, a1, a2, a3), wa, sem.at[2])
        load_parts((b0, b1, b2, b3), wb, sem.at[3])
        gains_ref[...] = jnp.zeros_like(gains_ref)
        dmid_ref[...] = jnp.zeros_like(dmid_ref)
        wait_whole(wda, sem.at[0])

    chunk = min(256, up_cols // 2)
    mean = stat_ref[:, 0:1]
    scale = stat_ref[:, 16:17]
    back_sum = jnp.zeros((block, 128), F32)
    back_inner = jnp.zeros((block, 128), F32)
    turns = [divmod(c * chunk, up_cols) for c in range(total // chunk)]
    turns.sort(key=lambda turn: turn[1] >= wda.shape[2])
    waited = False
    for t, off in turns:
        if off >= wda.shape[2] and not waited:
            waited = True

            @pl.when(first)
            def _():
                wait_whole(wdb, sem.at[1])

        here = slice(t * up_cols + off, t * up_cols + off + chunk)
        dn = dotf(cot_ref[...], get_down(t, off, chunk), 1, 0)
        h = hidden_ref[:, here]
        square = h * h
        half = 0.5 * jnp.tanh(h * (GELU_C + (GELU_C * GELU_A) * square)) + 0.5
        a = h * half
        slope_s[:, here] = half + a * (1.0 - half) * (
            2.0 * GELU_C + (6.0 * GELU_C * GELU_A) * square
        )
        unit = (a - mean) * scale
        unit_s[:, here] = unit
        dmid_ref[:, here] += fold8(dn * unit)
        g = dn * mid_ref[:, here]
        grad[:, here] = g
        inner = g * unit
        for j in range(chunk // 128):
            back_sum += g[:, j * 128 : (j + 1) * 128]
            back_inner += inner[:, j * 128 : (j + 1) * 128]
    sum_col = jnp.sum(back_sum, axis=1, keepdims=True) / total
    inner_col = jnp.sum(back_inner, axis=1, keepdims=True) / total

    @pl.when(first)
    def _():
        wait_whole(wa, sem.at[2])
        wait_whole(wb, sem.at[3])

    dh3 = None
    for c in range(total // chunk):
        t, off = divmod(c * chunk, up_cols)
        here = slice(c * chunk, (c + 1) * chunk)
        act_grad = scale * (grad[:, here] - sum_col - unit_s[:, here] * inner_col)
        dhidden = (act_grad * slope_s[:, here]).astype(BF)
        dhidden_ref[:, here] = dhidden
        part = dotf(dhidden, get(t, out_cols + off, chunk), 1, 1)
        dh3 = part if dh3 is None else dh3 + part
    wide[...] = dh3

    def back(r):
        here = pl.ds(r, STEP)
        unit = unit_ref[here, :]
        resid = x_ref[here, :].astype(F32) + unit * gain_ref[1:2, :]
        unit3 = (resid - stat_ref[here, 48:49]) * stat_ref[here, 64:65]
        third = wide[here, :]
        gains_ref[8:16, :] += fold8(third * unit3)
        dresid = cot_ref[here, :].astype(F32) + norm_back(
            unit3, stat_ref[here, 64:65], third * gain_ref[2:3, :]
        )
        dresid_ref[here, :] = dresid
        gains_ref[0:8, :] += fold8(dresid * unit)
        dmixed = norm_back(unit, stat_ref[here, 32:33], dresid * gain_ref[1:2, :])
        dmixed_ref[here, :] = dmixed.astype(BF)

    row_loop(block, STEP, back)
    turned_ref[...] = dmixed_ref[...].T
    for t in range(tensor_count):
        here = slice(t * out_cols, (t + 1) * out_cols)
        dscaled = dotf(dmixed_ref[...], get(t, 0, out_cols), 1, 0)
        dattended_ref[:, here] = (dscaled * scale_ref[:, here]).astype(BF)


def feed_back(orders, hidden, stat, unit, x, cot, gains, mid_row, scale_row, wda, wdb, wa, wb, grid_of):
    rows, width = x.shape
    block = min(256, rows)
    total = mid_row.shape[1]
    row = pl.BlockSpec((block, width), lambda i, e: (i, 0))
    wide = pl.BlockSpec((block, total), lambda i, e: (i, 0))
    return pl.pallas_call(
        functools.partial(back_kernel, grid_of),
        grid_spec=pltpu.PrefetchScalarGridSpec(
            num_scalar_prefetch=1,
            grid=(rows // block,),
            in_specs=[
                wide,
                pl.BlockSpec((block, 128), lambda i, e: (i, 0)),
                row,
                row,
                row,
                pl.BlockSpec((3, width), lambda i, e: (0, 0)),
                pl.BlockSpec((1, total), lambda i, e: (0, 0)),
                pl.BlockSpec((1, width), lambda i, e: (0, 0)),
            ]
            + [HBM] * 16,
            out_specs=[
                wide,
                row,
                pl.BlockSpec((width, block), lambda i, e: (0, i)),
                row,
                pl.BlockSpec((16, width), lambda i, e: (0, 0)),
                pl.BlockSpec((8, total), lambda i, e: (0, 0)),
            ],
            scratch_shapes=[
                pltpu.VMEM((block, total), F32),
                pltpu.VMEM((block, total), F32),
                pltpu.VMEM((block, total), F32),
                pltpu.VMEM((block, width), F32),
                pltpu.VMEM((block, width), BF),
            ]
            + [whole(chain) for chain in (wda, wdb, wa, wb)]
            + [pltpu.SemaphoreType.DMA((4,))],
        ),
        out_shape=[
            pltpu.HBM((rows, total), BF),
            pltpu.HBM((rows, width), F32),
            pltpu.HBM((width, rows), BF),
            pltpu.HBM((rows, width), BF),
            pltpu.HBM((16, width), F32),
            pltpu.HBM((8, total), F32),
        ],
        compiler_params=pltpu.CompilerParams(vmem_limit_bytes=60 << 20),
        cost_estimate=cost(60),
        name="feed_back",
    )(
        orders, *in_hbm(hidden, stat, unit, x, cot), gains, mid_row, scale_row,
        *parts_of((wda, wdb, wa, wb)),
    )


def grad_kernel(grid_of, count, turn, chunk, order_ref, a_ref, *refs):
    batch_count, tensor_count = grid_of
    b_refs, keep_ref, send_ref = refs[:count], refs[count], refs[count + 1]
    tensor = pl.program_id(1)
    if turn:
        turned = refs[count + 2]

        @pl.when((pl.program_id(0) == 0) & (tensor == 0))
        def _():
            turned[...] = a_ref[...].T

        a_ref = turned
    half = batch_count * tensor_count // 2
    height = keep_ref.shape[-2]
    second = order_ref[0] >= half
    for c, b_ref in enumerate(b_refs):
        acc = dotf(a_ref[...], b_ref[...], 1, 0).astype(BF)
        for core in range(2):

            @pl.when(second if core else jnp.logical_not(second))
            def _(acc=acc, core=core, c=c):
                for b in range(batch_count):
                    place = lax.bitwise_and(order_ref[b * tensor_count + tensor], half - 1)
                    ref = keep_ref if b % 2 == core else send_ref
                    at = (place,) if count == 1 else (place, c)
                    if chunk:
                        start = pl.multiple_of(pl.program_id(0) * chunk, chunk)
                        at += (slice(None), pl.ds(start, chunk))
                    ref[at] = acc[b * height : (b + 1) * height]


def weight_grad(order, a, bs, grid_of, start, cols, name, turn=False, near=False):
    batch_count, tensor_count = grid_of
    width, rows = a.shape[::-1] if turn else a.shape
    part = bs[0].shape[1] // tensor_count
    chunk = min(512, cols)
    per = part // chunk
    height = width // batch_count
    count = len(bs)
    lead = (batch_count * tensor_count // 2,) + (() if count == 1 else (count,)) + (height,)
    zeros = (0,) * len(lead)
    if near:
        out_spec = pl.BlockSpec(memory_space=pltpu.VMEM)
        out = pltpu.VMEM(lead + (cols,), BF)
    else:
        out_spec = pl.BlockSpec(lead + (chunk,), lambda i, t, e: zeros + (i,))
        out = pltpu.HBM(lead + (cols,), BF)
    b_spec = pl.BlockSpec((rows, chunk), lambda i, t, e: (0, t * per + start // chunk + i))
    return pl.pallas_call(
        functools.partial(grad_kernel, grid_of, count, turn, chunk if near else None),
        grid_spec=pltpu.PrefetchScalarGridSpec(
            num_scalar_prefetch=1,
            grid=(cols // chunk, tensor_count),
            in_specs=[pl.BlockSpec(a.shape, lambda i, t, e: (0, 0))] + [b_spec] * count,
            out_specs=[out_spec, out_spec],
            scratch_shapes=[pltpu.VMEM((width, rows), BF)] if turn else [],
        ),
        out_shape=[out, out],
        compiler_params=pltpu.CompilerParams(vmem_limit_bytes=36 << 20),
        cost_estimate=cost(2.4 * count * cols * tensor_count / 1024),
        name=name,
    )(order, *in_hbm(a, *bs))


def input_kernel(grid_of, count, order_ref, *refs):
    batch_count, tensor_count = grid_of
    grads, refs = refs[: 3 * count], refs[3 * count :]
    x_ref, dresid_ref, gain_ref = refs[:3]
    w_hbm, refs = refs[3 : 3 + 4 * count], refs[3 + 4 * count :]
    out_ref, dgain_ref, wide = refs[:3]
    w_refs, sem = refs[3:-1], refs[-1]
    first = pl.program_id(0) == 0

    @pl.when(first)
    def _():
        for n in range(count):
            load_parts(w_hbm[4 * n : 4 * n + 4], w_refs[n], sem.at[n])
        dgain_ref[...] = jnp.zeros_like(dgain_ref)

    parts = weights(*w_refs)
    total = None
    for n, (start, width, _, _) in enumerate(parts):

        @pl.when(first)
        def _(n=n):
            wait_whole(w_refs[n], sem.at[n])

        for c in range(3):
            for t in range(tensor_count):
                w = columns(parts, order_ref, batch_count, tensor_count, t, start, width, lead=c)
                part = dotf(grads[3 * n + c][:, t * width : (t + 1) * width], w, 1, 1)
                total = part if total is None else total + part
    wide[...] = total

    def back(r):
        here = pl.ds(r, STEP)
        unit, factor = normalize(x_ref[here, :].astype(F32))
        grad = wide[here, :]
        dgain_ref[...] += fold8(grad * unit)
        out = dresid_ref[here, :] + norm_back(unit, factor, grad * gain_ref[0:1, :])
        out_ref[here, :] = out.astype(BF)

    row_loop(x_ref.shape[0], STEP, back)


def input_grad(orders, grads, x, dresid, gains, chains, grid_of):
    rows, width = x.shape
    block = min(256, rows)
    row = pl.BlockSpec((block, width), lambda i, e: (i, 0))
    part = pl.BlockSpec((block, width // len(chains)), lambda i, e: (i, 0))
    return pl.pallas_call(
        functools.partial(input_kernel, grid_of, len(chains)),
        grid_spec=pltpu.PrefetchScalarGridSpec(
            num_scalar_prefetch=1,
            grid=(rows // block,),
            in_specs=[part] * len(grads)
            + [row, row, pl.BlockSpec((3, width), lambda i, e: (0, 0))]
            + [HBM] * (4 * len(chains)),
            out_specs=[row, pl.BlockSpec((8, width), lambda i, e: (0, 0))],
            scratch_shapes=[pltpu.VMEM((block, width), F32)]
            + [whole(chain) for chain in chains]
            + [pltpu.SemaphoreType.DMA((len(chains),))],
        ),
        out_shape=[
            pltpu.HBM((rows, width), BF),
            pltpu.HBM((8, width), F32),
        ],
        compiler_params=pltpu.CompilerParams(vmem_limit_bytes=32 << 20),
        cost_estimate=cost(15),
        name="input_grad",
    )(orders, *in_hbm(*grads, x, dresid), gains, *parts_of(chains))


def gather_vector(value, tensor_count):
    rank = lax.axis_index("tensor")
    out = jnp.zeros((tensor_count,) + value.shape, value.dtype)
    for flip in range(tensor_count):
        part = value if flip == 0 else swap(value, "tensor", flip)
        out = lax.dynamic_update_slice(out, part[None], (lax.bitwise_xor(rank, flip), 0))
    return out


def body(
    block_in,
    lengths,
    norm_gains,
    qkv_weight,
    head_scale,
    out_weight,
    up_weight,
    mid_gain,
    down_weight,
    cotangent,
):
    tensor_count = lax.axis_size("tensor")
    batch_count = lax.axis_size("batch")
    tensor_rank = lax.axis_index("tensor")
    batch_rank = lax.axis_index("batch")
    micro_count, own_rows, width = block_in.shape
    if tensor_count % micro_count:
        raise NotImplementedError
    split = tensor_count // micro_count
    micro = tensor_rank // split
    local_heads = head_scale.shape[0]
    heads = local_heads * tensor_count
    head_size = width // heads
    local_hidden = mid_gain.shape[0]
    factor = head_size ** (-0.5)
    grid_of = (batch_count, tensor_count)
    half_cols = local_hidden // 2
    qkv_cols = width // tensor_count
    parts = 2 if qkv_cols % 256 == 0 and split == 1 else 1
    steps = [gather_steps(batch_count, tensor_count, first) for first in (True, False)]
    tables = [place_table(one, batch_count, tensor_count) for one in steps]
    orders = jnp.concatenate(tables)
    far = len(steps[0]) - 2 - bits_of(tensor_count)
    near = bits_of(tensor_count) + 1

    def more(chains, count):
        for _ in range(count):
            hop(chains)

    part_cols = qkv_cols // parts
    up_chunk = min(256, local_hidden // 2)
    out_cols = out_weight.shape[0]
    cut = out_cols + ((local_hidden - out_cols) // 2) // up_chunk * up_chunk
    rows_in = Rows(block_in, micro_count, split)
    qkv = Gather(qkv_weight[None], steps[0])
    launch((), [rows_in, qkv])
    qkv.end()
    for _ in range(far - 1):
        hop([qkv])
    qkv_chains = [
        qkv.columns(n * part_cols, part_cols, steps[n % 2][far:]) for n in range(parts)
    ]
    launch(rows_in.arrived, qkv_chains)
    vectors = gather_vector(
        held(jnp.concatenate([mid_gain, head_scale]), rows_in.arrived), tensor_count
    )
    out_up = Gather(
        held(jnp.concatenate([out_weight.T, up_weight], axis=1)[None], qkv.arrived), steps[0]
    )
    hop([out_up])
    for n in range(near - 1):
        for chain in qkv_chains:
            chain.end()
        launch((), qkv_chains)
    for _ in range(far - 1):
        hop([out_up])
    for chain in qkv_chains:
        chain.end()
    down = Gather(held(down_weight.T[None], out_up.arrived), steps[0])
    wa = out_up.columns(0, cut, steps[0][far:])
    wb = out_up.columns(cut, out_weight.shape[0] + local_hidden - cut, steps[1][far:])
    rows_in.end()
    x = launch(rows_in.result, qkv_chains)
    for chain in qkv_chains:
        chain.end()
    x = launch(x, [wa, wb, down])

    mid_row = vectors[:, :local_hidden].reshape(1, -1)
    scale_all = vectors[:, local_hidden:].reshape(-1)
    scale_row = jnp.repeat(scale_all, head_size)[None]
    own_lengths = lax.dynamic_index_in_dim(lengths[:, 0], micro, 0, keepdims=False)
    ends = jnp.cumsum(own_lengths).astype(jnp.int32)

    def spread(value):
        if split == 1:
            return value
        groups = [[m * split + s for s in range(split)] for m in range(micro_count)]
        return lax.all_to_all(value, "tensor", 1, 0, tiled=True, axis_index_groups=groups)

    def collect(value):
        if split == 1:
            return value
        groups = [[m * split + s for s in range(split)] for m in range(micro_count)]
        return lax.all_to_all(value, "tensor", 0, 1, tiled=True, axis_index_groups=groups)

    h1, q, k, v = project(orders, x, norm_gains, qkv_chains, grid_of, factor)
    q, k, v = land((q, k, v), [wa, wb, down])
    more([down], far - 2)
    q, k, v = spread(q), spread(k), spread(v)
    more([wa, wb], near - 2)
    q = launch(q, [wa, wb, down])
    part = width // split
    scale_part = lax.dynamic_slice(scale_row, (0, tensor_rank % split * part), (1, part))
    scaled, lse = attend(q, k, v, scale_part, ends, tensor_count, 1, 0, None, None)
    scaled = land(scaled, [wa, wb, down])
    down_cut = half_cols
    wda = down.columns(0, down_cut, steps[0][far:])
    wdb = down.columns(down_cut, local_hidden - down_cut, steps[1][far:])
    rows_cot = Rows(cotangent, micro_count, split)
    scaled = launch(scaled, [wa, wb])
    scaled = land(scaled, [wa, wb])
    scaled = collect(launch(scaled, [wda, wdb, rows_cot]))
    forward = []
    shares = 2 if x.shape[0] % 512 == 0 else 1
    for n in range(shares):
        if n:
            forward[0] = land(forward[0], [wda, wdb])
            more([wda, wdb], near - 2)
            forward[0] = launch(forward[0], [wda, wdb])
        forward = list(
            hidden_forward(orders, scaled, x, norm_gains, mid_row, wa, wb, grid_of, (n, shares), forward)
        )
    unit, h3, hidden, narrow, stat = forward
    if shares == 1:
        narrow = land(narrow, [wda, wdb])
        more([wda, wdb], near - 2)
        narrow = launch(narrow, [wda, wdb])
    unit, h3, hidden, narrow, stat = land([unit, h3, hidden, narrow, stat], [rows_cot, wda])
    cot = rows_cot.result

    def grad_half(n, a, b, name, turn=False):
        keep, send = weight_grad(
            tables[n], a, [b], grid_of, n * half_cols, half_cols, name, turn, True
        )
        return Scatter(keep, send, steps[n])

    def flush(chains):
        for chain in chains:
            while chain.steps:
                hop([chain])
        return [chain.total for chain in chains]

    cot_held = launch(cot, [wda])
    d0 = grad_half(0, cot_held, narrow, "grad_down", True)
    d0.keep, d0.send = land((d0.keep, d0.send), [wdb])
    cot_held = launch(cot_held, [d0, wdb])
    d1 = grad_half(1, cot_held, narrow, "grad_down", True)
    d1.keep, d1.send = land((d1.keep, d1.send), [d0, wda, wdb])
    hidden = launch(hidden, [d1, d0])
    hidden = land(hidden, [d1])
    hidden = launch(hidden, [d1])
    back = feed_back(
        orders, hidden, stat, unit, x, cot, norm_gains, mid_row, scale_row, wda, wdb, wa, wb, grid_of
    )
    dhidden, dresid, dmixed, dattended, gain_sums, mid_sums = land(back, [d0, d1])
    more([d0, d1], near - 2)
    dhidden = launch(dhidden, [d0, d1])
    u0 = grad_half(0, h3, dhidden, "grad_up")
    dhidden = launch(dhidden, [u0])
    u1 = grad_half(1, h3, dhidden, "grad_up")
    u1.keep, u1.send = land((u1.keep, u1.send), [u0, d0, d1])
    down_sum = merged([d0, d1])
    dmixed = launch(dmixed, [u1])
    keep, send = weight_grad(
        tables[0], dmixed, [scaled], grid_of, 0, out_weight.shape[0], "grad_out", near=True
    )
    o0 = Scatter(keep, send, steps[0])
    o0.keep, o0.send = land((o0.keep, o0.send), [u1])
    flying = [u0, u1, o0] + ([down_sum] if down_sum.steps else [])
    da = launch(spread(dattended), flying)
    halves, grads, inners = [], [], []
    for n in range(parts):
        *three, inner = attend_back(q, k, v, da, lse, ends, factor, tensor_count, parts, n)
        inners.append(inner)
        if n == 0:
            three = land(three, flying)
            beside = [u0, u1] + ([down_sum] if down_sum.steps else [])
            narrow = launch(narrow, beside)
            block_out = feed_forward(orders, narrow, unit, x, norm_gains, wda, wdb, grid_of)
            block_out = land(block_out, beside)
            more([u0, u1], near - 2)
            up_sum = merged([u0, u1])
            rows_out = Rows(block_out, micro_count, split, 2)
            three = [collect(one) for one in three]
            three = launch(three, [up_sum, o0])
            flying = [up_sum, o0]
        else:
            three = land(three, flying)
            three, first_out = lax.optimization_barrier((three, rows_out.arrived[0]))
            rows_out.arrived[0] = first_out
            flying = [o0]
            three = launch(three, flying)
        keep, send = weight_grad(tables[n % 2], h1, three, grid_of, 0, part_cols, "grad_qkv", near=True)
        halves.append(Scatter(keep, send, steps[n % 2]))
        grads += three
        halves[-1].keep, halves[-1].send = land((halves[-1].keep, halves[-1].send), flying)
        if n < parts - 1:
            flying = [halves[0], up_sum, o0]
            da = launch(da, flying + [rows_out])
    q_last = halves[-1]
    if parts > 1:
        q_last.keep, q_last.send, rows_out.arrived = lax.optimization_barrier(
            (q_last.keep, q_last.send, rows_out.arrived)
        )
    dresid = launch(dresid, [q_last])
    dresid = land(dresid, [q_last])
    beside = halves + [o0] + ([] if parts > 1 else [rows_out])
    dresid = launch(dresid, beside)
    grad_in, first_sums = input_grad(orders, grads, x, dresid, norm_gains, qkv_chains, grid_of)
    grad_in, first_sums = land((grad_in, first_sums), beside)
    local = heads // split
    if parts == 1:
        head_sums = jnp.sum(inners[0], axis=-1).reshape(-1)
    else:
        shaped = [jnp.sum(one, axis=-1).reshape(tensor_count, -1) for one in inners]
        head_sums = jnp.concatenate(shaped, axis=1).reshape(-1)
    first_head = tensor_rank % split * local
    head_sums = head_sums / lax.dynamic_slice(scale_all, (first_head,), (local,))
    head_all = lax.dynamic_update_slice(jnp.zeros((heads,), F32), head_sums, (first_head,))
    last = jnp.concatenate(
        [jnp.sum(one, axis=0) for one in (first_sums, gain_sums[:8], gain_sums[8:], mid_sums)]
        + [head_all]
    )
    last = Total(last, batch_count, tensor_count)
    rows_back = Rows(grad_in, micro_count, split, 2)
    tail = halves + ([o0] if o0.steps else [])
    launch((), tail + [last])
    last.end()
    launch((), [last])
    land((), tail + [last])
    if parts > 1:
        halves = [merged(halves)]
    sent = rows_back.outgoing()
    tail = [one for one in halves + [o0, last] if one.steps]
    values, sent = lax.optimization_barrier(([one.outgoing() for one in tail], sent))
    for one, value in zip(tail, values):
        one.go(value)
    rows_back.go(sent)
    for one in tail:
        one.end()
    while last.steps:
        hop([last])
    tail = [one for one in halves + [o0] if one.steps]
    launch((), tail)
    arrived = [one.arrived for one in tail]
    rows_back.arrived = held(rows_back.arrived, arrived)
    last.value = held(last.value, arrived)
    for one in tail:
        one.end()
    rows_out.arrived = held(rows_out.arrived, arrived)
    rows_out.end()
    rows_back.end()
    block_out, grad_in = rows_out.result, rows_back.result
    d_totals, u_totals, o_totals, q_totals = (
        flush([down_sum]), flush([up_sum]), flush([o0]), flush(halves)
    )
    down_grad = d_totals[0].T
    up_grad = u_totals[0]
    out_grad = o_totals[0].T
    qkv_grad = q_totals[0]
    vector = last.value
    d_totals, u_totals, o_totals, q_totals = (
        flush([d0, d1]), flush([u0, u1]), flush([o0]), flush(halves)
    )
    gains_sum = vector[: 3 * width].reshape(3, width)
    mid_own = lax.dynamic_slice(vector, (3 * width + tensor_rank * local_hidden,), (local_hidden,))
    scale_own = lax.dynamic_slice(
        vector, (3 * width + tensor_count * local_hidden + tensor_rank * local_heads,), (local_heads,)
    )
    return (
        block_out,
        grad_in,
        gains_sum,
        qkv_grad,
        scale_own,
        out_grad,
        up_grad,
        mid_own,
        down_grad,
    )


def solution(mesh):
    in_specs = (
        P(None, ("batch", "tensor"), None),
        P(None, "batch", None),
        P(),
        P(None, "batch", "tensor"),
        P("tensor"),
        P("tensor", "batch"),
        P("batch", "tensor"),
        P("tensor"),
        P("tensor", "batch"),
        P(None, ("batch", "tensor"), None),
    )
    out_specs = (
        P(None, ("batch", "tensor"), None),
        P(None, ("batch", "tensor"), None),
        P(),
        P(None, "batch", "tensor"),
        P("tensor"),
        P("tensor", "batch"),
        P("batch", "tensor"),
        P("tensor"),
        P("tensor", "batch"),
    )
    return jax.shard_map(body, mesh=mesh, in_specs=in_specs, out_specs=out_specs, check_vma=False)
```

```python
import functools
import math

import jax
import jax.numpy as jnp
from jax import lax
from jax.experimental import pallas as pl
from jax.experimental.pallas import tpu as pltpu
from jax.sharding import PartitionSpec as P

eps = 1e-05
SEQ_MOST = 512
F32 = jnp.float32
BF = jnp.bfloat16
ALL = ("batch", "tensor")
GELU_C = math.sqrt(2.0 / math.pi)
GELU_A = 0.044715
STEP = 256


def cost(us):
    return pl.CostEstimate(flops=int(us * 1e9), transcendentals=0, bytes_accessed=1 << 20)


def dotf(a, b, ca, cb):
    return lax.dot_general(a, b, (((ca,), (cb,)), ((), ())), preferred_element_type=F32)


def row_loop(rows, step, fn):
    def one(i, carry):
        fn(pl.multiple_of(i * step, step))
        return carry

    lax.fori_loop(0, rows // step, one, 0)


def normalize(values):
    centred = values - jnp.mean(values, axis=-1, keepdims=True)
    factor = lax.rsqrt(jnp.mean(centred * centred, axis=-1, keepdims=True) + eps)
    return (centred * factor, factor)


def norm_back(unit, factor, grad):
    return factor * (
        grad
        - jnp.mean(grad, axis=-1, keepdims=True)
        - unit * jnp.mean(grad * unit, axis=-1, keepdims=True)
    )


def fold8(values):
    rows, width = values.shape
    return jnp.sum(values.reshape(rows // 8, 8, width), axis=0)


def bits_of(count):
    return count.bit_length() - 1


def gather_steps(batch_count, tensor_count, tensor_first):
    tensor = [("tensor", 1 << k) for k in range(bits_of(tensor_count))]
    plane = [("batch", 2)]
    far = [("batch", 1 << k) for k in reversed(range(2, bits_of(batch_count)))]
    return far + (tensor + plane if tensor_first else plane + tensor) + [("batch", 1)]


def place_table(steps, batch_count, tensor_count):
    batch = jnp.arange(batch_count * tensor_count, dtype=jnp.int32) // tensor_count
    tensor = jnp.arange(batch_count * tensor_count, dtype=jnp.int32) % tensor_count
    batch = jnp.bitwise_xor(batch, lax.axis_index("batch"))
    tensor = jnp.bitwise_xor(tensor, lax.axis_index("tensor"))
    place = jnp.zeros_like(batch)
    for k, (axis, flip) in enumerate(steps):
        apart = (jnp.bitwise_and(batch if axis == "batch" else tensor, flip) != 0).astype(jnp.int32)
        place = place + apart * (1 << k)
    return place


def swap(value, axis, flip):
    count = lax.axis_size(axis)
    return lax.ppermute(value, axis, [(i, i ^ flip) for i in range(count)])


def held(value, after):
    return lax.optimization_barrier((value, after))[0]


class Gather:
    def __init__(self, buffer, steps):
        self.own, self.steps, self.parts = buffer, list(steps), None

    def outgoing(self):
        return self.arrived if len(self.steps) == 1 else self.own

    def go(self, value):
        step = self.steps.pop(0)
        self.arrived = swap(value, *step)
        if not self.steps:
            self.parts[1] = value
        else:
            self.own = value
            if len(self.steps) == 1:
                self.parts = [value, None, swap(value, *self.steps[0]), None]

    def end(self):
        if self.parts is None:
            self.own = jnp.concatenate([self.own, self.arrived], axis=0)
        elif not self.steps:
            self.parts[3] = self.arrived

    def columns(self, start, count, steps):
        return Gather(self.own[..., start : start + count], steps)


class Scatter:
    def __init__(self, keep, send, steps):
        self.keep, self.send, self.steps = keep, send, list(reversed(steps))

    def outgoing(self):
        return (self.send, self.keep)

    def go(self, value):
        send, self.keep = value
        self.arrived = swap(send, *self.steps.pop(0))

    def end(self):
        keep, arrived = self.keep, self.arrived
        half = keep.shape[0] // 2
        if self.steps:
            self.send = (keep[half:].astype(F32) + arrived[half:].astype(F32)).astype(BF)
            self.keep = (keep[:half].astype(F32) + arrived[:half].astype(F32)).astype(BF)
        else:
            self.total = keep[0].astype(F32) + arrived[0].astype(F32)


def merged(chains):
    keep = jnp.concatenate([chain.keep for chain in chains], axis=-1)
    send = jnp.concatenate([chain.send for chain in chains], axis=-1)
    return Scatter(keep, send, list(reversed(chains[0].steps)))


class Total:
    def __init__(self, value, batch_count, tensor_count):
        self.value, self.grid_of = value, (batch_count, tensor_count)
        bits = [(flip, 0) for flip in (1 << k for k in range(2, bits_of(batch_count)))]
        plane = [(2, 0)] + [(0, 1 << k) for k in range(bits_of(tensor_count))]
        self.steps = [[(1, 0)]]
        for group in (plane, bits):
            if len(group) <= 2:
                spans = [(0, 0)]
                for flip in group:
                    spans += [(one[0] ^ flip[0], one[1] ^ flip[1]) for one in spans]
                self.steps.append(spans[1:])
            else:
                self.steps += [[flip] for flip in group]

    def outgoing(self):
        return self.value

    def go(self, value):
        batch_count, tensor_count = self.grid_of
        self.value, self.arrived = value, []
        for batch, tensor in self.steps.pop(0):
            pairs = [
                (b * tensor_count + t, (b ^ batch) * tensor_count + (t ^ tensor))
                for b in range(batch_count)
                for t in range(tensor_count)
            ]
            self.arrived.append(lax.ppermute(value, ALL, pairs))

    def end(self):
        for one in self.arrived:
            self.value = self.value + one


class Rows:
    def __init__(self, value, micro_count, split, cuts=1):
        self.value, self.micro_count, self.split, self.cuts = value, micro_count, split, cuts
        self.taken = value.ndim == 3
        self.steps = [None]
        self.rank = lax.axis_index("tensor")

    def pieces(self):
        if self.taken:
            return self.value
        return self.value.reshape(self.micro_count, -1, self.value.shape[1])

    def outgoing(self):
        if self.split > 1:
            return []
        sent = []
        for flip in range(1, self.micro_count):
            one = lax.dynamic_index_in_dim(self.pieces(), lax.bitwise_xor(self.rank, flip), 0)
            sent += [one[:, n * (one.shape[1] // self.cuts) :][:, : one.shape[1] // self.cuts] for n in range(self.cuts)]
        return sent

    def go(self, value):
        self.steps = []
        if self.split == 1:
            self.arrived = [
                swap(one, "tensor", n // self.cuts + 1) for n, one in enumerate(value)
            ]
        else:
            self.arrived = [
                lax.all_gather(self.value, "tensor", axis=1 if self.taken else 0, tiled=True)
            ]

    def end(self):
        if self.split == 1:
            pieces = self.pieces()
            out = lax.dynamic_update_slice(
                jnp.zeros_like(pieces),
                lax.dynamic_index_in_dim(pieces, self.rank, 0),
                (self.rank, 0, 0),
            )
            for n, one in enumerate(self.arrived):
                other = lax.bitwise_xor(self.rank, n // self.cuts + 1)
                out = lax.dynamic_update_slice(
                    out, one, (other, n % self.cuts * one.shape[1], 0)
                )
            self.result = out.reshape(-1, out.shape[2]) if self.taken else out
            return
        whole = self.arrived[0]
        width = whole.shape[-1]
        if self.taken:
            rows = self.value.shape[0] * self.value.shape[1]
            start = (self.rank // self.split, self.rank % self.split * rows, 0)
            self.result = lax.dynamic_slice(whole, start, (1, rows, width))[0]
        else:
            own = self.value.shape[0] // self.micro_count
            whole = whole.reshape(self.micro_count, -1, width)
            start = (0, self.rank * own, 0)
            self.result = lax.dynamic_slice(whole, start, (self.micro_count, own, width))


def launch(inputs, chains):
    inputs, values = lax.optimization_barrier((inputs, [chain.outgoing() for chain in chains]))
    for chain, value in zip(chains, values):
        chain.go(value)
    return inputs


def land(inputs, chains):
    inputs, values = lax.optimization_barrier((inputs, [chain.arrived for chain in chains]))
    for chain, value in zip(chains, values):
        chain.arrived = value
        chain.end()
    return inputs


def hop(chains, after=()):
    launch(after, chains)
    for chain in chains:
        chain.end()


def columns(parts, order_ref, batch_count, tensor_count, t, start, count, lead=None):
    for first, width, which, w_ref in parts:
        if first <= start < first + width:
            break
    pieces = []
    for b in range(batch_count):
        p = order_ref[(which * batch_count + b) * tensor_count + t]
        here = pl.ds(start - first, count)
        pieces.append(w_ref[p, :, here] if lead is None else w_ref[p, lead, :, here])
    return jnp.concatenate(pieces, axis=0)


def weights(*refs):
    out, first = [], 0
    for n, ref in enumerate(refs):
        out.append((first, ref.shape[-1], n % 2, ref))
        first += ref.shape[-1]
    return out


HBM = pl.BlockSpec(memory_space=pltpu.HBM)


def whole(chain):
    part = chain.parts[0].shape
    return pltpu.VMEM((4 * part[0],) + part[1:], BF)


def in_hbm(*values):
    return [pltpu.with_memory_space_constraint(value, pltpu.HBM) for value in values]


def parts_of(chains):
    return in_hbm(*[part for chain in chains for part in chain.parts])


def load_parts(refs, w, sem):
    count = w.shape[0] // 4
    for n in range(4):
        pltpu.make_async_copy(refs[n], w.at[pl.ds(n * count, count)], sem).start()


def wait_whole(w, sem):
    pltpu.make_async_copy(w, w, sem).wait()


def qkv_kernel(grid_of, factor, count, order_ref, x_ref, gain_ref, *refs):
    batch_count, tensor_count = grid_of
    w_hbm, refs = refs[: 4 * count], refs[4 * count :]
    turned_ref, q_ref, k_ref, v_ref, h1_ref = refs[:5]
    w_refs, sem = refs[5:-1], refs[-1]
    first = pl.program_id(0) == 0

    @pl.when(first)
    def _():
        for n in range(count):
            load_parts(w_hbm[4 * n : 4 * n + 4], w_refs[n], sem.at[n])

    def chunk(r):
        here = pl.ds(r, STEP)
        unit, _ = normalize(x_ref[here, :].astype(F32))
        h1_ref[here, :] = (unit * gain_ref[0:1, :]).astype(BF)

    row_loop(x_ref.shape[0], STEP, chunk)
    turned_ref[...] = h1_ref[...].T

    parts = weights(*w_refs)
    cols = sum(part[1] for part in parts)
    for n, (start, width, _, _) in enumerate(parts):

        @pl.when(first)
        def _(n=n):
            wait_whole(w_refs[n], sem.at[n])

        for c, out in enumerate((q_ref, k_ref, v_ref)):
            for t in range(tensor_count):
                w = columns(parts, order_ref, batch_count, tensor_count, t, start, width, lead=c)
                value = dotf(h1_ref[...], w, 1, 0).astype(BF)
                here = slice(t * cols + start, t * cols + start + width)
                out[:, here] = value * BF(factor) if c == 0 else value


def project(orders, x, gains, chains, grid_of, factor):
    rows, width = x.shape
    block = min(256, rows)
    row = pl.BlockSpec((block, width), lambda i, e: (i, 0))
    return pl.pallas_call(
        functools.partial(qkv_kernel, grid_of, factor, len(chains)),
        grid_spec=pltpu.PrefetchScalarGridSpec(
            num_scalar_prefetch=1,
            grid=(rows // block,),
            in_specs=[row, pl.BlockSpec((3, width), lambda i, e: (0, 0))]
            + [HBM] * (4 * len(chains)),
            out_specs=[pl.BlockSpec((width, block), lambda i, e: (0, i))] + [row] * 3,
            scratch_shapes=[pltpu.VMEM((block, width), BF)]
            + [whole(chain) for chain in chains]
            + [pltpu.SemaphoreType.DMA((len(chains),))],
        ),
        out_shape=[pltpu.HBM((width, rows), BF)]
        + [pltpu.HBM((rows, width), BF)] * 3,
        compiler_params=pltpu.CompilerParams(vmem_limit_bytes=24 << 20),
        cost_estimate=cost(13),
        name="project",
    )(orders, *in_hbm(x), gains, *parts_of(chains))


def spans(rows, block):
    return [
        (first, max(0, (first - SEQ_MOST + 1) // block * block), first + block)
        for first in range(0, rows, block)
    ]


def fill_bias(ends_ref, bias, parts, block):
    for (first, low, high), ref in zip(parts, bias):
        shape = (high - low, block)
        keys = low + lax.broadcasted_iota(jnp.int32, shape, 0)
        queries = first + lax.broadcasted_iota(jnp.int32, shape, 1)
        start = jnp.zeros(shape, jnp.int32)
        for n in range(ends_ref.shape[0]):
            end = ends_ref[n]
            start = jnp.where(queries >= end, end, start)
        ref[...] = jnp.where((keys <= queries) & (keys >= start), 0.0, -1e30).astype(F32)


def attend_kernel(rows, block, ends_ref, q_ref, k_ref, v_ref, scale_ref, o_ref, lse_ref, *bias):
    parts = spans(rows, block)

    @pl.when(pl.program_id(0) == 0)
    def _():
        fill_bias(ends_ref, bias, parts, block)

    lower = lax.broadcasted_iota(jnp.int32, (1, 128), 1) < 64
    for n, (first, low, high) in enumerate(parts):
        q = q_ref[pl.ds(first, block), :]
        heads = []
        for h in range(2):
            own = jnp.where(lower if h == 0 else ~lower, q, jnp.zeros_like(q))
            s = dotf(k_ref[pl.ds(low, high - low), :], own, 1, 1) + bias[n][...]
            most = jnp.max(s, axis=0, keepdims=True)
            p = jnp.exp(s - most)
            total = jnp.sum(p, axis=0, keepdims=True)
            probs = (p * (1.0 / total)).astype(BF)
            lse_ref[0, pl.ds(h, 1), pl.ds(first, block)] = most + jnp.log(total)
            heads.append(dotf(probs, v_ref[pl.ds(low, high - low), :], 0, 0))
        out = jnp.where(lower, heads[0], heads[1]) * scale_ref[...]
        o_ref[pl.ds(first, block), :] = out.astype(BF)


def attend_back_kernel(
    rows, block, factor, ends_ref, q_ref, k_ref, v_ref, da_ref, lse_ref,
    dq_ref, dk_ref, dv_ref, inner_ref, dk_acc, dv_acc, *bias
):
    parts = spans(rows, block)

    @pl.when(pl.program_id(0) == 0)
    def _():
        fill_bias(ends_ref, bias, parts, block)

    lower = lax.broadcasted_iota(jnp.int32, (1, 128), 1) < 64
    dk_acc[...] = jnp.zeros_like(dk_acc)
    dv_acc[...] = jnp.zeros_like(dv_acc)
    for n, (first, low, high) in enumerate(parts):
        here = pl.ds(first, block)
        keys = pl.ds(low, high - low)
        q, da, k, v = q_ref[here, :], da_ref[here, :], k_ref[keys, :], v_ref[keys, :]
        probs, scores, q_own, da_own, k_own = [], [], [], [], []
        for h in range(2):
            mask = lower if h == 0 else ~lower
            q_own.append(jnp.where(mask, q, jnp.zeros_like(q)))
            da_own.append(jnp.where(mask, da, jnp.zeros_like(da)))
            k_own.append(jnp.where(mask, k, jnp.zeros_like(k)))
            s = dotf(k, q_own[h], 1, 1) + bias[n][...]
            p = jnp.exp(s - lse_ref[0, pl.ds(h, 1), here])
            product = p * dotf(v, da_own[h], 1, 1)
            inner = jnp.sum(product, axis=0, keepdims=True)
            inner_ref[0, pl.ds(h, 1), here] = inner
            scores.append((product - p * inner).astype(BF))
            probs.append(p.astype(BF))
        dv_acc[keys, :] += dotf(
            jnp.concatenate(probs, axis=1), jnp.concatenate(da_own, axis=0), 1, 0
        )
        dk_acc[keys, :] += dotf(
            jnp.concatenate(scores, axis=1), jnp.concatenate(q_own, axis=0), 1, 0
        )
        dq = dotf(jnp.concatenate(scores, axis=0), jnp.concatenate(k_own, axis=0), 0, 0)
        dq_ref[here, :] = (dq * factor).astype(BF)
    dk_ref[...] = dk_acc[...].astype(BF)
    dv_ref[...] = dv_acc[...].astype(BF)


def bias_shapes(rows, block):
    return [pltpu.VMEM((high - low, block), F32) for _, low, high in spans(rows, block)]


def pair_of(pairs, tensor_count, parts, n):
    if parts == 1:
        return pairs, lambda i: i
    per_tensor = pairs // tensor_count
    per = per_tensor // parts
    return pairs // parts, lambda i: i // per * per_tensor + n * per + i % per


def attend(q, k, v, scale_row, ends, tensor_count, parts, n, before_out, before_lse):
    rows, width = q.shape
    block = min(256, rows)
    pairs = width // 128
    steps, pair = pair_of(pairs, tensor_count, parts, n)
    col = pl.BlockSpec((rows, 128), lambda i, e: (0, pair(i)))
    earlier = [] if before_out is None else [before_out, before_lse]
    count = len(earlier)

    def kernel(ends_ref, q_ref, k_ref, v_ref, scale_ref, *refs):
        attend_kernel(rows, block, ends_ref, q_ref, k_ref, v_ref, scale_ref, *refs[count:])

    return pl.pallas_call(
        kernel,
        grid_spec=pltpu.PrefetchScalarGridSpec(
            num_scalar_prefetch=1,
            grid=(steps,),
            in_specs=[col, col, col, pl.BlockSpec((1, 128), lambda i, e: (0, pair(i)))]
            + [HBM] * count,
            out_specs=[col, pl.BlockSpec((1, 2, rows), lambda i, e: (pair(i), 0, 0))],
            scratch_shapes=bias_shapes(rows, block),
        ),
        out_shape=[
            pltpu.HBM((rows, width), BF),
            pltpu.HBM((pairs, 2, rows), F32),
        ],
        input_output_aliases={5 + j: j for j in range(count)},
        compiler_params=pltpu.CompilerParams(vmem_limit_bytes=32 << 20),
        cost_estimate=cost(24 / parts),
        name="attend",
    )(ends, *in_hbm(q, k, v), scale_row, *earlier)


def attend_back(q, k, v, da, lse, ends, factor, tensor_count, parts, n):
    rows, width = q.shape
    block = min(256, rows)
    pairs = width // 128
    steps, pair = pair_of(pairs, tensor_count, parts, n)
    col = pl.BlockSpec((rows, 128), lambda i, e: (0, pair(i)))
    out_col = pl.BlockSpec((rows, 128), lambda i, e: (0, i))
    out = pltpu.HBM((rows, width // parts), BF)
    return pl.pallas_call(
        functools.partial(attend_back_kernel, rows, block, factor),
        grid_spec=pltpu.PrefetchScalarGridSpec(
            num_scalar_prefetch=1,
            grid=(steps,),
            in_specs=[col] * 4 + [pl.BlockSpec((1, 2, rows), lambda i, e: (pair(i), 0, 0))],
            out_specs=[out_col] * 3 + [pl.BlockSpec((1, 2, rows), lambda i, e: (i, 0, 0))],
            scratch_shapes=[pltpu.VMEM((rows, 128), F32)] * 2 + bias_shapes(rows, block),
        ),
        out_shape=[out, out, out, pltpu.HBM((steps, 2, rows), F32)],
        compiler_params=pltpu.CompilerParams(vmem_limit_bytes=40 << 20),
        cost_estimate=cost(42 / parts),
        name="attend_back",
    )(ends, *in_hbm(q, k, v, da), lse)


def put_stats(ref, here, values):
    lane = lax.broadcasted_iota(jnp.int32, (1, 128), 1)
    out = values[-1]
    for n in reversed(range(len(values) - 1)):
        out = jnp.where(lane < 16 * (n + 1), values[n], out)
    ref[here, :] = jnp.broadcast_to(out, (values[0].shape[0], 128))


def hidden_kernel(
    grid_of, order_ref, scaled_ref, x_ref, gain_ref, mid_ref, a0, a1, a2, a3, b0, b1, b2, b3,
    unit_ref, turned_ref, hidden_ref, narrow_ref, stat_ref, act, norm_stat, wide, h3_ref, wa, wb, sem
):
    batch_count, tensor_count = grid_of
    block, width = x_ref.shape
    total = hidden_ref.shape[1]
    up_cols = total // tensor_count
    out_cols = width // tensor_count
    get = functools.partial(columns, weights(wa, wb), order_ref, batch_count, tensor_count)
    first = pl.program_id(0) == 0

    @pl.when(first)
    def _():
        load_parts((a0, a1, a2, a3), wa, sem.at[0])
        load_parts((b0, b1, b2, b3), wb, sem.at[1])
        wait_whole(wa, sem.at[0])

    mixed = None
    for t in range(tensor_count):
        part = dotf(scaled_ref[:, t * out_cols : (t + 1) * out_cols], get(t, 0, out_cols), 1, 1)
        mixed = part if mixed is None else mixed + part
    wide[...] = mixed

    def norms(r):
        here = pl.ds(r, STEP)
        unit, factor = normalize(wide[here, :])
        unit_ref[here, :] = unit
        resid = x_ref[here, :].astype(F32) + unit * gain_ref[1:2, :]
        mean3 = jnp.mean(resid, axis=-1, keepdims=True)
        centred = resid - mean3
        factor3 = lax.rsqrt(jnp.mean(centred * centred, axis=-1, keepdims=True) + eps)
        h3_ref[here, :] = (centred * factor3 * gain_ref[2:3, :]).astype(BF)
        put_stats(norm_stat, here, [factor, mean3, factor3])

    row_loop(block, STEP, norms)
    turned_ref[...] = h3_ref[...].T

    @pl.when(first)
    def _():
        wait_whole(wb, sem.at[1])

    chunk = min(256, up_cols // 2)
    sums = jnp.zeros((block, 128), F32)
    squares = jnp.zeros((block, 128), F32)
    for c in range(total // chunk):
        t, off = divmod(c * chunk, up_cols)
        h = dotf(h3_ref[...], get(t, out_cols + off, chunk), 1, 0)
        hidden_ref[:, c * chunk : (c + 1) * chunk] = h
        half = 0.5 * jnp.tanh(h * (GELU_C + (GELU_C * GELU_A) * (h * h))) + 0.5
        a = h * half
        act[:, c * chunk : (c + 1) * chunk] = a
        for j in range(chunk // 128):
            piece = a[:, j * 128 : (j + 1) * 128]
            sums += piece
            squares += piece * piece
    mean = jnp.sum(sums, axis=1, keepdims=True) / total
    spread = jnp.sum(squares, axis=1, keepdims=True) / total - mean * mean
    scale = lax.rsqrt(spread + eps)
    before = norm_stat[...]
    put_stats(stat_ref, slice(None), [mean, scale, before[:, 0:1], before[:, 16:17], before[:, 32:33]])

    def narrow(r):
        here = pl.ds(r, 64)
        m = stat_ref[here, 0:1]
        s = stat_ref[here, 16:17]
        narrow_ref[here, :] = ((act[here, :] - m) * s * mid_ref[...]).astype(BF)

    row_loop(block, 64, narrow)


def hidden_forward(orders, scaled, x, gains, mid_row, wa, wb, grid_of, share, earlier):
    rows, width = x.shape
    block = min(256, rows)
    total = mid_row.shape[1]
    blocks = rows // block // share[1]
    first = share[0] * blocks
    row = pl.BlockSpec((block, width), lambda i, e: (first + i, 0))
    wide = pl.BlockSpec((block, total), lambda i, e: (first + i, 0))

    def kernel(order_ref, *refs):
        hidden_kernel(grid_of, order_ref, *refs[:12], *refs[12 + len(earlier) :])

    return pl.pallas_call(
        kernel,
        grid_spec=pltpu.PrefetchScalarGridSpec(
            num_scalar_prefetch=1,
            grid=(blocks,),
            in_specs=[
                row,
                row,
                pl.BlockSpec((3, width), lambda i, e: (0, 0)),
                pl.BlockSpec((1, total), lambda i, e: (0, 0)),
            ]
            + [HBM] * (8 + len(earlier)),
            out_specs=[row, pl.BlockSpec((width, block), lambda i, e: (0, first + i)), wide, wide]
            + [pl.BlockSpec((block, 128), lambda i, e: (first + i, 0))],
            scratch_shapes=[
                pltpu.VMEM((block, total), F32),
                pltpu.VMEM((block, 128), F32),
                pltpu.VMEM((block, width), F32),
                pltpu.VMEM((block, width), BF),
                whole(wa),
                whole(wb),
                pltpu.SemaphoreType.DMA((2,)),
            ],
        ),
        out_shape=[
            pltpu.HBM((rows, width), F32),
            pltpu.HBM((width, rows), BF),
            pltpu.HBM((rows, total), F32),
            pltpu.HBM((rows, total), BF),
            pltpu.HBM((rows, 128), F32),
        ],
        input_output_aliases={13 + n: n for n in range(len(earlier))},
        compiler_params=pltpu.CompilerParams(vmem_limit_bytes=44 << 20),
        cost_estimate=cost(30 / share[1]),
        name="hidden_forward",
    )(orders, *in_hbm(scaled, x), gains, mid_row, *parts_of((wa, wb)), *earlier)


def feed_kernel(grid_of, order_ref, narrow_ref, unit_ref, x_ref, gain_ref, a0, a1, a2, a3, b0, b1, b2, b3, out_ref, wa, wb, sem):
    batch_count, tensor_count = grid_of
    up_cols = narrow_ref.shape[1] // tensor_count
    parts = weights(wa, wb)

    @pl.when(pl.program_id(0) == 0)
    def _():
        load_parts((a0, a1, a2, a3), wa, sem.at[0])
        load_parts((b0, b1, b2, b3), wb, sem.at[1])

    out = x_ref[...].astype(F32) + unit_ref[...] * gain_ref[1:2, :]
    for n, (start, width, _, w_ref) in enumerate(parts):

        @pl.when(pl.program_id(0) == 0)
        def _(n=n, w_ref=w_ref):
            wait_whole(w_ref, sem.at[n])

        for t in range(tensor_count):
            w = columns(parts, order_ref, batch_count, tensor_count, t, start, width)
            off = t * up_cols + start
            out += dotf(narrow_ref[:, off : off + width], w, 1, 1)
    out_ref[...] = out.astype(BF)


def feed_forward(orders, narrow, unit, x, gains, wa, wb, grid_of):
    rows, width = x.shape
    block = min(256, rows)
    total = narrow.shape[1]
    row = pl.BlockSpec((block, width), lambda i, e: (i, 0))
    return pl.pallas_call(
        functools.partial(feed_kernel, grid_of),
        grid_spec=pltpu.PrefetchScalarGridSpec(
            num_scalar_prefetch=1,
            grid=(rows // block,),
            in_specs=[pl.BlockSpec((block, total), lambda i, e: (i, 0)), row, row]
            + [pl.BlockSpec((3, width), lambda i, e: (0, 0))]
            + [HBM] * 8,
            out_specs=row,
            scratch_shapes=[whole(wa), whole(wb), pltpu.SemaphoreType.DMA((2,))],
        ),
        out_shape=pltpu.HBM((rows, width), BF),
        compiler_params=pltpu.CompilerParams(vmem_limit_bytes=28 << 20),
        cost_estimate=cost(14),
        name="feed_forward",
    )(orders, *in_hbm(narrow, unit, x), gains, *parts_of((wa, wb)))


def back_kernel(
    grid_of, order_ref, hidden_ref, stat_ref, unit_ref, x_ref, cot_ref, gain_ref, mid_ref,
    scale_ref, da0, da1, da2, da3, db0, db1, db2, db3, a0, a1, a2, a3, b0, b1, b2, b3, dhidden_ref, dresid_ref, turned_ref, dattended_ref,
    gains_ref, dmid_ref, grad, unit_s, slope_s, wide, dmixed_ref, wda, wdb, wa, wb, sem
):
    batch_count, tensor_count = grid_of
    block, width = x_ref.shape
    total = hidden_ref.shape[1]
    up_cols = total // tensor_count
    out_cols = width // tensor_count
    get = functools.partial(columns, weights(wa, wb), order_ref, batch_count, tensor_count)
    get_down = functools.partial(columns, weights(wda, wdb), order_ref, batch_count, tensor_count)
    first = pl.program_id(0) == 0

    @pl.when(first)
    def _():
        load_parts((da0, da1, da2, da3), wda, sem.at[0])
        load_parts((db0, db1, db2, db3), wdb, sem.at[1])
        load_parts((a0, a1, a2, a3), wa, sem.at[2])
        load_parts((b0, b1, b2, b3), wb, sem.at[3])
        gains_ref[...] = jnp.zeros_like(gains_ref)
        dmid_ref[...] = jnp.zeros_like(dmid_ref)
        wait_whole(wda, sem.at[0])

    chunk = min(256, up_cols // 2)
    mean = stat_ref[:, 0:1]
    scale = stat_ref[:, 16:17]
    back_sum = jnp.zeros((block, 128), F32)
    back_inner = jnp.zeros((block, 128), F32)
    turns = [divmod(c * chunk, up_cols) for c in range(total // chunk)]
    turns.sort(key=lambda turn: turn[1] >= wda.shape[2])
    waited = False
    for t, off in turns:
        if off >= wda.shape[2] and not waited:
            waited = True

            @pl.when(first)
            def _():
                wait_whole(wdb, sem.at[1])

        here = slice(t * up_cols + off, t * up_cols + off + chunk)
        dn = dotf(cot_ref[...], get_down(t, off, chunk), 1, 0)
        h = hidden_ref[:, here]
        square = h * h
        half = 0.5 * jnp.tanh(h * (GELU_C + (GELU_C * GELU_A) * square)) + 0.5
        a = h * half
        slope_s[:, here] = half + a * (1.0 - half) * (
            2.0 * GELU_C + (6.0 * GELU_C * GELU_A) * square
        )
        unit = (a - mean) * scale
        unit_s[:, here] = unit
        dmid_ref[:, here] += fold8(dn * unit)
        g = dn * mid_ref[:, here]
        grad[:, here] = g
        inner = g * unit
        for j in range(chunk // 128):
            back_sum += g[:, j * 128 : (j + 1) * 128]
            back_inner += inner[:, j * 128 : (j + 1) * 128]
    sum_col = jnp.sum(back_sum, axis=1, keepdims=True) / total
    inner_col = jnp.sum(back_inner, axis=1, keepdims=True) / total

    @pl.when(first)
    def _():
        wait_whole(wa, sem.at[2])
        wait_whole(wb, sem.at[3])

    dh3 = None
    for c in range(total // chunk):
        t, off = divmod(c * chunk, up_cols)
        here = slice(c * chunk, (c + 1) * chunk)
        act_grad = scale * (grad[:, here] - sum_col - unit_s[:, here] * inner_col)
        dhidden = (act_grad * slope_s[:, here]).astype(BF)
        dhidden_ref[:, here] = dhidden
        part = dotf(dhidden, get(t, out_cols + off, chunk), 1, 1)
        dh3 = part if dh3 is None else dh3 + part
    wide[...] = dh3

    def back(r):
        here = pl.ds(r, STEP)
        unit = unit_ref[here, :]
        resid = x_ref[here, :].astype(F32) + unit * gain_ref[1:2, :]
        unit3 = (resid - stat_ref[here, 48:49]) * stat_ref[here, 64:65]
        third = wide[here, :]
        gains_ref[8:16, :] += fold8(third * unit3)
        dresid = cot_ref[here, :].astype(F32) + norm_back(
            unit3, stat_ref[here, 64:65], third * gain_ref[2:3, :]
        )
        dresid_ref[here, :] = dresid
        gains_ref[0:8, :] += fold8(dresid * unit)
        dmixed = norm_back(unit, stat_ref[here, 32:33], dresid * gain_ref[1:2, :])
        dmixed_ref[here, :] = dmixed.astype(BF)

    row_loop(block, STEP, back)
    turned_ref[...] = dmixed_ref[...].T
    for t in range(tensor_count):
        here = slice(t * out_cols, (t + 1) * out_cols)
        dscaled = dotf(dmixed_ref[...], get(t, 0, out_cols), 1, 0)
        dattended_ref[:, here] = (dscaled * scale_ref[:, here]).astype(BF)


def feed_back(orders, hidden, stat, unit, x, cot, gains, mid_row, scale_row, wda, wdb, wa, wb, grid_of):
    rows, width = x.shape
    block = min(256, rows)
    total = mid_row.shape[1]
    row = pl.BlockSpec((block, width), lambda i, e: (i, 0))
    wide = pl.BlockSpec((block, total), lambda i, e: (i, 0))
    return pl.pallas_call(
        functools.partial(back_kernel, grid_of),
        grid_spec=pltpu.PrefetchScalarGridSpec(
            num_scalar_prefetch=1,
            grid=(rows // block,),
            in_specs=[
                wide,
                pl.BlockSpec((block, 128), lambda i, e: (i, 0)),
                row,
                row,
                row,
                pl.BlockSpec((3, width), lambda i, e: (0, 0)),
                pl.BlockSpec((1, total), lambda i, e: (0, 0)),
                pl.BlockSpec((1, width), lambda i, e: (0, 0)),
            ]
            + [HBM] * 16,
            out_specs=[
                wide,
                row,
                pl.BlockSpec((width, block), lambda i, e: (0, i)),
                row,
                pl.BlockSpec((16, width), lambda i, e: (0, 0)),
                pl.BlockSpec((8, total), lambda i, e: (0, 0)),
            ],
            scratch_shapes=[
                pltpu.VMEM((block, total), F32),
                pltpu.VMEM((block, total), F32),
                pltpu.VMEM((block, total), F32),
                pltpu.VMEM((block, width), F32),
                pltpu.VMEM((block, width), BF),
            ]
            + [whole(chain) for chain in (wda, wdb, wa, wb)]
            + [pltpu.SemaphoreType.DMA((4,))],
        ),
        out_shape=[
            pltpu.HBM((rows, total), BF),
            pltpu.HBM((rows, width), F32),
            pltpu.HBM((width, rows), BF),
            pltpu.HBM((rows, width), BF),
            pltpu.HBM((16, width), F32),
            pltpu.HBM((8, total), F32),
        ],
        compiler_params=pltpu.CompilerParams(vmem_limit_bytes=60 << 20),
        cost_estimate=cost(60),
        name="feed_back",
    )(
        orders, *in_hbm(hidden, stat, unit, x, cot), gains, mid_row, scale_row,
        *parts_of((wda, wdb, wa, wb)),
    )


def grad_kernel(grid_of, count, turn, chunk, order_ref, a_ref, *refs):
    batch_count, tensor_count = grid_of
    b_refs, keep_ref, send_ref = refs[:count], refs[count], refs[count + 1]
    tensor = pl.program_id(1)
    if turn:
        turned = refs[count + 2]

        @pl.when((pl.program_id(0) == 0) & (tensor == 0))
        def _():
            turned[...] = a_ref[...].T

        a_ref = turned
    half = batch_count * tensor_count // 2
    height = keep_ref.shape[-2]
    second = order_ref[0] >= half
    for c, b_ref in enumerate(b_refs):
        acc = dotf(a_ref[...], b_ref[...], 1, 0).astype(BF)
        for core in range(2):

            @pl.when(second if core else jnp.logical_not(second))
            def _(acc=acc, core=core, c=c):
                for b in range(batch_count):
                    place = lax.bitwise_and(order_ref[b * tensor_count + tensor], half - 1)
                    ref = keep_ref if b % 2 == core else send_ref
                    at = (place,) if count == 1 else (place, c)
                    if chunk:
                        start = pl.multiple_of(pl.program_id(0) * chunk, chunk)
                        at += (slice(None), pl.ds(start, chunk))
                    ref[at] = acc[b * height : (b + 1) * height]


def weight_grad(order, a, bs, grid_of, start, cols, name, turn=False, near=False):
    batch_count, tensor_count = grid_of
    width, rows = a.shape[::-1] if turn else a.shape
    part = bs[0].shape[1] // tensor_count
    chunk = min(512, cols)
    per = part // chunk
    height = width // batch_count
    count = len(bs)
    lead = (batch_count * tensor_count // 2,) + (() if count == 1 else (count,)) + (height,)
    zeros = (0,) * len(lead)
    if near:
        out_spec = pl.BlockSpec(memory_space=pltpu.VMEM)
        out = pltpu.VMEM(lead + (cols,), BF)
    else:
        out_spec = pl.BlockSpec(lead + (chunk,), lambda i, t, e: zeros + (i,))
        out = pltpu.HBM(lead + (cols,), BF)
    b_spec = pl.BlockSpec((rows, chunk), lambda i, t, e: (0, t * per + start // chunk + i))
    return pl.pallas_call(
        functools.partial(grad_kernel, grid_of, count, turn, chunk if near else None),
        grid_spec=pltpu.PrefetchScalarGridSpec(
            num_scalar_prefetch=1,
            grid=(cols // chunk, tensor_count),
            in_specs=[pl.BlockSpec(a.shape, lambda i, t, e: (0, 0))] + [b_spec] * count,
            out_specs=[out_spec, out_spec],
            scratch_shapes=[pltpu.VMEM((width, rows), BF)] if turn else [],
        ),
        out_shape=[out, out],
        compiler_params=pltpu.CompilerParams(vmem_limit_bytes=36 << 20),
        cost_estimate=cost(2.4 * count * cols * tensor_count / 1024),
        name=name,
    )(order, *in_hbm(a, *bs))


def input_kernel(grid_of, count, order_ref, *refs):
    batch_count, tensor_count = grid_of
    grads, refs = refs[: 3 * count], refs[3 * count :]
    x_ref, dresid_ref, gain_ref = refs[:3]
    w_hbm, refs = refs[3 : 3 + 4 * count], refs[3 + 4 * count :]
    out_ref, dgain_ref, wide = refs[:3]
    w_refs, sem = refs[3:-1], refs[-1]
    first = pl.program_id(0) == 0

    @pl.when(first)
    def _():
        for n in range(count):
            load_parts(w_hbm[4 * n : 4 * n + 4], w_refs[n], sem.at[n])
        dgain_ref[...] = jnp.zeros_like(dgain_ref)

    parts = weights(*w_refs)
    total = None
    for n, (start, width, _, _) in enumerate(parts):

        @pl.when(first)
        def _(n=n):
            wait_whole(w_refs[n], sem.at[n])

        for c in range(3):
            for t in range(tensor_count):
                w = columns(parts, order_ref, batch_count, tensor_count, t, start, width, lead=c)
                part = dotf(grads[3 * n + c][:, t * width : (t + 1) * width], w, 1, 1)
                total = part if total is None else total + part
    wide[...] = total

    def back(r):
        here = pl.ds(r, STEP)
        unit, factor = normalize(x_ref[here, :].astype(F32))
        grad = wide[here, :]
        dgain_ref[...] += fold8(grad * unit)
        out = dresid_ref[here, :] + norm_back(unit, factor, grad * gain_ref[0:1, :])
        out_ref[here, :] = out.astype(BF)

    row_loop(x_ref.shape[0], STEP, back)


def input_grad(orders, grads, x, dresid, gains, chains, grid_of):
    rows, width = x.shape
    block = min(256, rows)
    row = pl.BlockSpec((block, width), lambda i, e: (i, 0))
    part = pl.BlockSpec((block, width // len(chains)), lambda i, e: (i, 0))
    return pl.pallas_call(
        functools.partial(input_kernel, grid_of, len(chains)),
        grid_spec=pltpu.PrefetchScalarGridSpec(
            num_scalar_prefetch=1,
            grid=(rows // block,),
            in_specs=[part] * len(grads)
            + [row, row, pl.BlockSpec((3, width), lambda i, e: (0, 0))]
            + [HBM] * (4 * len(chains)),
            out_specs=[row, pl.BlockSpec((8, width), lambda i, e: (0, 0))],
            scratch_shapes=[pltpu.VMEM((block, width), F32)]
            + [whole(chain) for chain in chains]
            + [pltpu.SemaphoreType.DMA((len(chains),))],
        ),
        out_shape=[
            pltpu.HBM((rows, width), BF),
            pltpu.HBM((8, width), F32),
        ],
        compiler_params=pltpu.CompilerParams(vmem_limit_bytes=32 << 20),
        cost_estimate=cost(15),
        name="input_grad",
    )(orders, *in_hbm(*grads, x, dresid), gains, *parts_of(chains))


def gather_vector(value, tensor_count):
    rank = lax.axis_index("tensor")
    out = jnp.zeros((tensor_count,) + value.shape, value.dtype)
    for flip in range(tensor_count):
        part = value if flip == 0 else swap(value, "tensor", flip)
        out = lax.dynamic_update_slice(out, part[None], (lax.bitwise_xor(rank, flip), 0))
    return out


def body(
    block_in,
    lengths,
    norm_gains,
    qkv_weight,
    head_scale,
    out_weight,
    up_weight,
    mid_gain,
    down_weight,
    cotangent,
):
    tensor_count = lax.axis_size("tensor")
    batch_count = lax.axis_size("batch")
    tensor_rank = lax.axis_index("tensor")
    batch_rank = lax.axis_index("batch")
    micro_count, own_rows, width = block_in.shape
    if tensor_count % micro_count:
        raise NotImplementedError
    split = tensor_count // micro_count
    micro = tensor_rank // split
    local_heads = head_scale.shape[0]
    heads = local_heads * tensor_count
    head_size = width // heads
    local_hidden = mid_gain.shape[0]
    factor = head_size ** (-0.5)
    grid_of = (batch_count, tensor_count)
    half_cols = local_hidden // 2
    qkv_cols = width // tensor_count
    parts = 2 if qkv_cols % 256 == 0 and split == 1 else 1
    steps = [gather_steps(batch_count, tensor_count, first) for first in (True, False)]
    tables = [place_table(one, batch_count, tensor_count) for one in steps]
    orders = jnp.concatenate(tables)
    far = len(steps[0]) - 2 - bits_of(tensor_count)
    near = bits_of(tensor_count) + 1

    def more(chains, count):
        for _ in range(count):
            hop(chains)

    part_cols = qkv_cols // parts
    up_chunk = min(256, local_hidden // 2)
    out_cols = out_weight.shape[0]
    cut = out_cols + ((local_hidden - out_cols) // 2) // up_chunk * up_chunk
    rows_in = Rows(block_in, micro_count, split)
    qkv = Gather(qkv_weight[None], steps[0])
    launch((), [rows_in, qkv])
    qkv.end()
    for _ in range(far - 1):
        hop([qkv])
    qkv_chains = [
        qkv.columns(n * part_cols, part_cols, steps[n % 2][far:]) for n in range(parts)
    ]
    launch(rows_in.arrived, qkv_chains)
    vectors = gather_vector(
        held(jnp.concatenate([mid_gain, head_scale]), rows_in.arrived), tensor_count
    )
    out_up = Gather(
        held(jnp.concatenate([out_weight.T, up_weight], axis=1)[None], qkv.arrived), steps[0]
    )
    hop([out_up])
    for n in range(near - 1):
        for chain in qkv_chains:
            chain.end()
        launch((), qkv_chains)
    for _ in range(far - 1):
        hop([out_up])
    for chain in qkv_chains:
        chain.end()
    down = Gather(held(down_weight.T[None], out_up.arrived), steps[0])
    wa = out_up.columns(0, cut, steps[0][far:])
    wb = out_up.columns(cut, out_weight.shape[0] + local_hidden - cut, steps[1][far:])
    rows_in.end()
    x = launch(rows_in.result, qkv_chains)
    for chain in qkv_chains:
        chain.end()
    x = launch(x, [wa, wb, down])

    mid_row = vectors[:, :local_hidden].reshape(1, -1)
    scale_all = vectors[:, local_hidden:].reshape(-1)
    scale_row = jnp.repeat(scale_all, head_size)[None]
    own_lengths = lax.dynamic_index_in_dim(lengths[:, 0], micro, 0, keepdims=False)
    ends = jnp.cumsum(own_lengths).astype(jnp.int32)

    def spread(value):
        if split == 1:
            return value
        groups = [[m * split + s for s in range(split)] for m in range(micro_count)]
        return lax.all_to_all(value, "tensor", 1, 0, tiled=True, axis_index_groups=groups)

    def collect(value):
        if split == 1:
            return value
        groups = [[m * split + s for s in range(split)] for m in range(micro_count)]
        return lax.all_to_all(value, "tensor", 0, 1, tiled=True, axis_index_groups=groups)

    h1, q, k, v = project(orders, x, norm_gains, qkv_chains, grid_of, factor)
    q, k, v = land((q, k, v), [wa, wb, down])
    more([down], far - 2)
    q, k, v = spread(q), spread(k), spread(v)
    more([wa, wb], near - 2)
    q = launch(q, [wa, wb, down])
    part = width // split
    scale_part = lax.dynamic_slice(scale_row, (0, tensor_rank % split * part), (1, part))
    scaled, lse = attend(q, k, v, scale_part, ends, tensor_count, 1, 0, None, None)
    scaled = land(scaled, [wa, wb, down])
    down_cut = half_cols
    wda = down.columns(0, down_cut, steps[0][far:])
    wdb = down.columns(down_cut, local_hidden - down_cut, steps[1][far:])
    rows_cot = Rows(cotangent, micro_count, split)
    scaled = launch(scaled, [wa, wb])
    scaled = land(scaled, [wa, wb])
    scaled = collect(launch(scaled, [wda, wdb, rows_cot]))
    forward = []
    shares = 2 if x.shape[0] % 512 == 0 else 1
    for n in range(shares):
        if n:
            forward[0] = land(forward[0], [wda, wdb])
            more([wda, wdb], near - 2)
            forward[0] = launch(forward[0], [wda, wdb])
        forward = list(
            hidden_forward(orders, scaled, x, norm_gains, mid_row, wa, wb, grid_of, (n, shares), forward)
        )
    unit, h3, hidden, narrow, stat = forward
    if shares == 1:
        narrow = land(narrow, [wda, wdb])
        more([wda, wdb], near - 2)
        narrow = launch(narrow, [wda, wdb])
    unit, h3, hidden, narrow, stat = land([unit, h3, hidden, narrow, stat], [rows_cot, wda])
    cot = rows_cot.result

    def grad_half(n, a, b, name, turn=False):
        keep, send = weight_grad(
            tables[n], a, [b], grid_of, n * half_cols, half_cols, name, turn, True
        )
        return Scatter(keep, send, steps[n])

    def flush(chains):
        for chain in chains:
            while chain.steps:
                hop([chain])
        return [chain.total for chain in chains]

    cot_held = launch(cot, [wda])
    d0 = grad_half(0, cot_held, narrow, "grad_down", True)
    d0.keep, d0.send = land((d0.keep, d0.send), [wdb])
    cot_held = launch(cot_held, [d0, wdb])
    d1 = grad_half(1, cot_held, narrow, "grad_down", True)
    d1.keep, d1.send = land((d1.keep, d1.send), [d0, wda, wdb])
    hidden = launch(hidden, [d1, d0])
    hidden = land(hidden, [d1])
    hidden = launch(hidden, [d1])
    back = feed_back(
        orders, hidden, stat, unit, x, cot, norm_gains, mid_row, scale_row, wda, wdb, wa, wb, grid_of
    )
    dhidden, dresid, dmixed, dattended, gain_sums, mid_sums = land(back, [d0, d1])
    more([d0, d1], near - 2)
    dhidden = launch(dhidden, [d0, d1])
    u0 = grad_half(0, h3, dhidden, "grad_up")
    dhidden = launch(dhidden, [u0])
    u1 = grad_half(1, h3, dhidden, "grad_up")
    u1.keep, u1.send = land((u1.keep, u1.send), [u0, d0, d1])
    down_sum = merged([d0, d1])
    dmixed = launch(dmixed, [u1])
    keep, send = weight_grad(
        tables[0], dmixed, [scaled], grid_of, 0, out_weight.shape[0], "grad_out", near=True
    )
    o0 = Scatter(keep, send, steps[0])
    o0.keep, o0.send = land((o0.keep, o0.send), [u1])
    flying = [u0, u1, o0] + ([down_sum] if down_sum.steps else [])
    da = launch(spread(dattended), flying)
    halves, grads, inners = [], [], []
    for n in range(parts):
        *three, inner = attend_back(q, k, v, da, lse, ends, factor, tensor_count, parts, n)
        inners.append(inner)
        if n == 0:
            three = land(three, flying)
            beside = [u0, u1] + ([down_sum] if down_sum.steps else [])
            narrow = launch(narrow, beside)
            block_out = feed_forward(orders, narrow, unit, x, norm_gains, wda, wdb, grid_of)
            block_out = land(block_out, beside)
            more([u0, u1], near - 2)
            up_sum = merged([u0, u1])
            rows_out = Rows(block_out, micro_count, split, 2)
            three = [collect(one) for one in three]
            three = launch(three, [up_sum, o0])
            flying = [up_sum, o0]
        else:
            three = land(three, flying)
            three, first_out = lax.optimization_barrier((three, rows_out.arrived[0]))
            rows_out.arrived[0] = first_out
            flying = [o0]
            three = launch(three, flying)
        keep, send = weight_grad(tables[n % 2], h1, three, grid_of, 0, part_cols, "grad_qkv", near=True)
        halves.append(Scatter(keep, send, steps[n % 2]))
        grads += three
        halves[-1].keep, halves[-1].send = land((halves[-1].keep, halves[-1].send), flying)
        if n < parts - 1:
            flying = [halves[0], up_sum, o0]
            da = launch(da, flying + [rows_out])
    q_last = halves[-1]
    if parts > 1:
        q_last.keep, q_last.send, rows_out.arrived = lax.optimization_barrier(
            (q_last.keep, q_last.send, rows_out.arrived)
        )
    dresid = launch(dresid, [q_last])
    dresid = land(dresid, [q_last])
    beside = halves + [o0] + ([] if parts > 1 else [rows_out])
    dresid = launch(dresid, beside)
    grad_in, first_sums = input_grad(orders, grads, x, dresid, norm_gains, qkv_chains, grid_of)
    grad_in, first_sums = land((grad_in, first_sums), beside)
    local = heads // split
    if parts == 1:
        head_sums = jnp.sum(inners[0], axis=-1).reshape(-1)
    else:
        shaped = [jnp.sum(one, axis=-1).reshape(tensor_count, -1) for one in inners]
        head_sums = jnp.concatenate(shaped, axis=1).reshape(-1)
    first_head = tensor_rank % split * local
    head_sums = head_sums / lax.dynamic_slice(scale_all, (first_head,), (local,))
    head_all = lax.dynamic_update_slice(jnp.zeros((heads,), F32), head_sums, (first_head,))
    last = jnp.concatenate(
        [jnp.sum(one, axis=0) for one in (first_sums, gain_sums[:8], gain_sums[8:], mid_sums)]
        + [head_all]
    )
    last = Total(last, batch_count, tensor_count)
    rows_back = Rows(grad_in, micro_count, split, 2)
    tail = halves + ([o0] if o0.steps else [])
    launch((), tail + [last])
    last.end()
    launch((), [last])
    land((), tail + [last])
    if parts > 1:
        halves = [merged(halves)]
    sent = rows_back.outgoing()
    tail = [one for one in halves + [o0, last] if one.steps]
    values, sent = lax.optimization_barrier(([one.outgoing() for one in tail], sent))
    for one, value in zip(tail, values):
        one.go(value)
    rows_back.go(sent)
    for one in tail:
        one.end()
    while last.steps:
        hop([last])
    tail = [one for one in halves + [o0] if one.steps]
    launch((), tail)
    arrived = [one.arrived for one in tail]
    rows_back.arrived = held(rows_back.arrived, arrived)
    last.value = held(last.value, arrived)
    for one in tail:
        one.end()
    rows_out.arrived = held(rows_out.arrived, arrived)
    rows_out.end()
    rows_back.end()
    block_out, grad_in = rows_out.result, rows_back.result
    d_totals, u_totals, o_totals, q_totals = (
        flush([down_sum]), flush([up_sum]), flush([o0]), flush(halves)
    )
    down_grad = d_totals[0].T
    up_grad = u_totals[0]
    out_grad = o_totals[0].T
    qkv_grad = q_totals[0]
    vector = last.value
    d_totals, u_totals, o_totals, q_totals = (
        flush([d0, d1]), flush([u0, u1]), flush([o0]), flush(halves)
    )
    gains_sum = vector[: 3 * width].reshape(3, width)
    mid_own = lax.dynamic_slice(vector, (3 * width + tensor_rank * local_hidden,), (local_hidden,))
    scale_own = lax.dynamic_slice(
        vector, (3 * width + tensor_count * local_hidden + tensor_rank * local_heads,), (local_heads,)
    )
    return (
        block_out,
        grad_in,
        gains_sum,
        qkv_grad,
        scale_own,
        out_grad,
        up_grad,
        mid_own,
        down_grad,
    )


def solution(mesh):
    in_specs = (
        P(None, ("batch", "tensor"), None),
        P(None, "batch", None),
        P(),
        P(None, "batch", "tensor"),
        P("tensor"),
        P("tensor", "batch"),
        P("batch", "tensor"),
        P("tensor"),
        P("tensor", "batch"),
        P(None, ("batch", "tensor"), None),
    )
    out_specs = (
        P(None, ("batch", "tensor"), None),
        P(None, ("batch", "tensor"), None),
        P(),
        P(None, "batch", "tensor"),
        P("tensor"),
        P("tensor", "batch"),
        P("batch", "tensor"),
        P("tensor"),
        P("tensor", "batch"),
    )
    return jax.shard_map(body, mesh=mesh, in_specs=in_specs, out_specs=out_specs, check_vma=False)
```
